32 devices in a mesh: az: 4 (over y, x), ax: 4 (over z), pl: 2 (over core).
Axes of the slice: x: 2, y: 2, z: 4, core: 2. Of those that a mesh axis runs over, the one named last changes fastest.
Arguments:
- cells: float32 [2, 10, 32, 32768], P('pl', None, 'ax', 'az'), may hold values from 0.05 to 3, as said below
- speeds: float32 [2, 2, 32, 32768], P('pl', None, 'ax', 'az'), may hold values from -1 to 1
- supply: float32 [10, 4, 32768], P(None, 'ax', 'az'), may hold values from 0.25 to 2
- mix: float32 [9, 9], replicated, may hold values from -2 to 2
- prefactor: float32 [9], replicated, may hold values from 1 to 4
- activation: float32 [9], replicated, may hold values from 1 to 4
- heat: float32 [9], replicated, may hold values from 0.5 to 2
- inj_column: int32 [128, 1], P(('az', 'ax')), may hold values from 0 to 3; in each aligned block of 8 rows (0 to 7, 8 to 15, ...) at most 4 rows name the same one
- inj_slot: int32 [128], P(('az', 'ax')), may hold values from 0 to 7
- inj_open: int32 [128], P(('az', 'ax')), may hold values 0 or 1
Outputs:
- cells_next: float32 [2, 10, 32, 32768], P('pl', None, 'ax', 'az')
The draws below stay inside these ranges and needn't reach their ends.
Inputs may be any that keep to these rules, and one draw needn't show every extreme that they name: `cells`: the last component (temperature) is at least 0.25; species densities are positive. `inj_column`: within the 8 blocks of one device at most 4 name one column, a bound that some block reaches.
All inputs are finite; a program needn't handle non-finite values. No bound on the sum of `inj_open` on one device may be relied on, other than what follows from the above.
Results may differ from the reference program's by a relative error of at most 0.00005.
Values sent between devices are 32-bit elements; how exact they have to be, the bound alone decides.
No kernel may reach another device: no remote copies, remote signals or barrier semaphores. Data moves between devices by JAX's collectives and lax.ppermute only.
A program may use at most 128 MiB of HBM per device.

```python
import math
import jax
import jax.numpy as jnp
import numpy as np
from jax import lax

SPECIES = 9
NV = 10
NR = 64
CAX = 8
TB = 16
BPD = 8
TPC = 8
CAP = 4
NPB = 128
NAZ = 512
NAX = 32
N_AZ = 4
N_AX = 4


def draw_cells(key, part):
    key_spec = jax.random.fold_in(key, 11)
    key_temp = jax.random.fold_in(key, 23)
    spec_shape = (2, NV - 1, NAX, NAZ * NR)
    temp_shape = (2, 1, NAX, NAZ * NR)
    species = jnp.exp(jax.random.uniform(key_spec, spec_shape, jnp.float32, -2.3, 0.69))
    theta = jax.random.uniform(key_temp, temp_shape, jnp.float32, 0.3, 2.6)
    return jnp.concatenate([species, theta], axis=1)


def place_ends(values, stream_key, low, top_value):
    place = [jax.random.randint(jax.random.fold_in(stream_key, axis), (), 0, length) for axis, length in enumerate(values.shape)]
    main_axis = values.shape.index(max(values.shape))
    beside = place[:main_axis] + [(place[main_axis] + 1) % values.shape[main_axis]] + place[main_axis + 1:]
    return values.at[tuple(place)].set(low).at[tuple(beside)].set(top_value)


def level_of(key, dims, pieces, smallest, high):
    factor_of = 1.0
    for dim, parts in pieces:
        steps = jax.random.uniform(jax.random.fold_in(jax.random.fold_in(key, 6), dim), (parts,), jnp.float32, smallest / len(pieces), high / len(pieces))
        factor_of = factor_of * jnp.repeat(jnp.exp(steps), dims[dim] // parts).reshape((-1,) + (1,) * (len(dims) - 1 - dim))
    return factor_of


def shared_out(stream_key, own, number, rows, amount, top, limit, lean):
    order = jax.random.permutation(stream_key, amount)
    crowded, ordinary = load_shares(amount, rows * top, limit, lean, True), load_shares(amount, rows * top, limit, lean, False)
    places = jnp.arange(amount)

    def named(lengths, turn):
        used = int((lengths > 0).sum())
        fixed = max(1, used // 4)
        shifted = fixed + (places - fixed + turn * (used - fixed)) % max(1, amount - fixed)
        return jnp.zeros((amount,), jnp.int32).at[order[jnp.where(places < fixed, places, shifted)]].set(jnp.asarray(lengths, jnp.int32))

    lengths = jnp.where(number % 4 == 0, named(crowded, number // 4), named(ordinary, number - number // 4 - 1))
    mixed = jax.random.permutation(jax.random.fold_in(own, 3), amount)
    source_of, sink = mixed[0:amount // 2 * 2:2], mixed[1:amount // 2 * 2:2]
    slack = jnp.minimum(lengths[source_of] - 1, limit - lengths[sink]) // 2
    slack = jnp.where((source_of == order[0]) | (sink == order[0]) | (lengths[sink] == 0), 0, jnp.maximum(slack, 0))
    shifted = jax.random.randint(jax.random.fold_in(own, 4), (amount // 2,), 0, 1 << 20) % (slack + 1)
    lengths = lengths.at[source_of].add(-shifted).at[sink].add(shifted)
    items = jnp.searchsorted(jnp.cumsum(lengths), jnp.arange(rows * top), side="right").astype(jnp.int32)
    table = items.reshape(top, rows).T
    table = table[jax.random.permutation(jax.random.fold_in(own, 1), rows)]
    turn = jax.random.randint(jax.random.fold_in(own, 2), (rows, 1), 0, top)
    return jnp.take_along_axis(table, (jnp.arange(top)[None, :] + turn) % top, axis=1)


def load_shares(number_of, total, bound, skew, full):
    loads = [(1 << 20) // math.isqrt(standing ** skew) + 1 for standing in range(1, number_of + 1)]
    largest = bound if full else min(bound, max(-(-total // number_of), total * loads[0] // sum(loads)))
    least = 1 if total - largest >= number_of - 1 else 0
    holding, surplus = [largest] + [least] * (number_of - 1), total - largest - least * (number_of - 1)
    while surplus > 0:
        candidates = [i for i in range(1, number_of) if holding[i] < largest] or [i for i in range(1, number_of) if holding[i] < bound]
        pool, remaining = sum([loads[i] for i in candidates]), surplus
        for i in candidates:
            addition = min(bound - holding[i], max(1, remaining * loads[i] // pool), surplus)
            holding[i] = holding[i] + addition
            surplus = surplus - addition
    return np.array(holding)


def centred(rng, shape, scale, bound, kind=jnp.bfloat16):
    return jnp.clip(scale * jax.random.normal(rng, shape, jnp.float32), -bound, bound).astype(kind)


def setup_inputs(seed: int = 0) -> dict:
    arg_keys = jax.random.split(jax.random.key(seed), 11)
    cells = draw_cells(jax.random.fold_in(arg_keys[10], 71), 0)
    speeds = jnp.clip(jax.random.uniform(arg_keys[1], (2, 2, NAX, NAZ * NR), jnp.float32, -1.0, 1.0) * level_of(arg_keys[1], (2, 2, NAX, NAZ * NR), ((0, 2), (2, 4), (3, 4)), -0.4, 0.0), -1.0, 1.0)
    supply = jnp.clip(0.25 + 1.75 * jax.random.uniform(arg_keys[2], (NV, N_AX, NAZ * NR), jnp.float32) ** level_of(arg_keys[2], (NV, N_AX, NAZ * NR), ((1, 4), (2, 4)), -0.2, 0.2), 0.25, 2.0)
    mix = centred(arg_keys[3], (SPECIES, SPECIES), SPECIES ** -0.5, 2.0, jnp.float32)
    prefactor = jnp.clip(jnp.exp(jax.random.uniform(arg_keys[4], (SPECIES,), jnp.float32, math.log(1.0), math.log(4.0))), 1.0, 4.0)
    activation = jnp.clip(jax.random.uniform(arg_keys[5], (SPECIES,), jnp.float32, 1.0, 4.0), 1.0, 4.0)
    heat = jnp.clip(jax.random.uniform(arg_keys[6], (SPECIES,), jnp.float32, 0.5, 2.0), 0.5, 2.0)
    inj_column_keys = jax.random.split(jax.random.fold_in(arg_keys[7], 1), NPB // BPD)
    inj_column_turns = jax.random.permutation(jax.random.fold_in(arg_keys[7], 3), NPB // BPD)
    inj_column = jax.vmap(lambda own, number: shared_out(jax.random.fold_in(arg_keys[7], 2), own, number, BPD, N_AZ, 1, CAP, 2))(inj_column_keys, inj_column_turns).reshape((NPB, 1))
    inj_slot = place_ends(jax.random.randint(arg_keys[8], (NPB,), 0, TPC), jax.random.fold_in(arg_keys[8], 1), 0, TPC - 1).astype(jnp.int32)
    inj_open = place_ends((jax.random.randint(arg_keys[9], (NPB,), 0, 4) < 3).astype(jnp.int32), jax.random.fold_in(arg_keys[9], 1), 0, 1)
    return dict(cells=cells, speeds=speeds, supply=supply, mix=mix, prefactor=prefactor, activation=activation, heat=heat, inj_column=inj_column, inj_slot=inj_slot, inj_open=inj_open)


step_dt = 0.2
high = lax.Precision.HIGHEST


def divergence(field, vel, dim):
    count = field.shape[dim]
    lower = lax.slice_in_dim(field, 0, count - 1, axis=field.ndim + dim)
    upper = lax.slice_in_dim(field, 1, count, axis=field.ndim + dim)
    vel_low = lax.slice_in_dim(vel, 0, count - 1, axis=vel.ndim + dim)
    vel_up = lax.slice_in_dim(vel, 1, count, axis=vel.ndim + dim)
    flux = 0.5 * (vel_low * lower + vel_up * upper) - 0.5 * (upper - lower)
    faces = count - 1
    axis = flux.ndim + dim
    return lax.slice_in_dim(flux, 1, faces, axis=axis) - lax.slice_in_dim(flux, 0, faces - 1, axis=axis)


def reaction(state, mix, prefactor, activation, heat):
    species = state[:-1]
    theta = jnp.maximum(state[-1], 0.5)
    shape_k = (-1,) + (1,) * (species.ndim - 1)
    rate = prefactor.reshape(shape_k) * jnp.exp(-activation.reshape(shape_k) / theta[None]) * jnp.maximum(species, 0.0)
    dspec = jnp.einsum("vk,k...->v...", mix, rate, precision=high)
    dtheta = jnp.einsum("k,k...->...", heat, rate, precision=high)
    return jnp.concatenate([dspec, dtheta[None]], axis=0)


def tendency(state, q_az, u_az, q_ax, w_ax, mix, prefactor, activation, heat):
    return -(divergence(q_az, u_az, -2) + divergence(q_ax, w_ax, -3)) + reaction(state, mix, prefactor, activation, heat)


def wrap_az(field):
    return jnp.concatenate([field[..., -1:, :], field, field[..., :1, :]], axis=-2)


def full_rhs(chamber, plenum, u_ch, w_ch, u_pl, w_pl, supply_rows, open_map, mix, prefactor, activation, heat):
    faces = plenum[:, :, -1]
    faces = faces.reshape(NV, N_AX, N_AZ, BPD, TB * NR).transpose(0, 2, 1, 3, 4).reshape(NV, NPB, TB * NR)
    inlet = jnp.einsum("tb,vbx->vtx", open_map, faces, precision=high).reshape(NV, 1, NAZ, NR)
    q_ax = jnp.concatenate([inlet, chamber, chamber[:, -1:]], axis=1)
    zero_row = jnp.zeros((1, NAZ, NR), jnp.float32)
    w_ax = jnp.concatenate([zero_row, w_ch, zero_row], axis=0)
    rhs_ch = tendency(chamber, wrap_az(chamber), wrap_az(u_ch), q_ax, w_ax, mix, prefactor, activation, heat)
    cycle_top = chamber.reshape(NV, N_AX, CAX, NAZ, NR)[:, :, :1]
    p_ax = jnp.concatenate([supply_rows, plenum, cycle_top], axis=2)
    zero_cycle = jnp.zeros((N_AX, 1, NAZ, NR), jnp.float32)
    pw_ax = jnp.concatenate([zero_cycle, w_pl, zero_cycle], axis=1)
    rhs_pl = tendency(plenum, wrap_az(plenum), wrap_az(u_pl), p_ax, pw_ax, mix, prefactor, activation, heat)
    return rhs_ch, rhs_pl


def reference(cells, speeds, supply, mix, prefactor, activation, heat, inj_column, inj_slot, inj_open):
    chamber = cells[0].reshape(NV, NAX, NAZ, NR)
    plenum = cells[1].reshape(NV, N_AX, CAX, NAZ, NR)
    u_ch = speeds[0, 0].reshape(NAX, NAZ, NR)
    w_ch = speeds[0, 1].reshape(NAX, NAZ, NR)
    u_pl = speeds[1, 0].reshape(N_AX, CAX, NAZ, NR)
    w_pl = speeds[1, 1].reshape(N_AX, CAX, NAZ, NR)
    supply_rows = supply.reshape(NV, N_AX, 1, NAZ, NR)
    tile = inj_column[:, 0] * TPC + inj_slot
    tiles = jnp.arange(N_AZ * TPC, dtype=jnp.int32)
    open_map = (tiles[:, None] == tile[None, :]).astype(jnp.float32) * inj_open.astype(jnp.float32)[None, :]
    args = (mix, prefactor, activation, heat)
    k_ch, k_pl = full_rhs(chamber, plenum, u_ch, w_ch, u_pl, w_pl, supply_rows, open_map, *args)
    ch_one = chamber + step_dt * k_ch
    pl_one = plenum + step_dt * k_pl
    k2_ch, k2_pl = full_rhs(ch_one, pl_one, u_ch, w_ch, u_pl, w_pl, supply_rows, open_map, *args)
    ch_two = 0.5 * chamber + 0.5 * (ch_one + step_dt * k2_ch)
    pl_two = 0.5 * plenum + 0.5 * (pl_one + step_dt * k2_pl)
    return jnp.stack([ch_two.reshape(NV, NAX, NAZ * NR), pl_two.reshape(NV, NAX, NAZ * NR)], axis=0)
```

```python
import functools

import jax
import jax.numpy as jnp
from jax import lax
from jax.experimental import pallas as pl
from jax.experimental.pallas import tpu as pltpu
from jax.sharding import PartitionSpec as P

NV = 10
NS = 9
LANES = 128
CAX = 8
HALF = 64
AXES = ("az", "ax", "pl")
NJ = 4

f32 = jnp.float32


def roles():
    return lax.axis_index("az"), lax.axis_index("ax"), lax.axis_index("pl")


def low_half():
    return lax.broadcasted_iota(jnp.int32, (CAX, LANES), 1) < HALF


def extract(q_ref, vel_ref, col_ref, slot_ref, open_ref, out_refs, s_ref, own_ref, n_az):
    az, ax, plen = roles()
    n = q_ref.shape[1] // CAX
    for v in range(NV):
        s_ref[pl.ds(v * n, n), :] = q_ref[v, pl.ds(0, n, stride=CAX), :]

    @pl.when(plen == 0)
    def _():
        w_low = vel_ref[1, pl.ds(0, n, stride=CAX), :]
        w_top = vel_ref[1, pl.ds(CAX - 1, n, stride=CAX), :]
        even = ax % 2 == 0

        def put(up_ref, down_ref):
            for v in range(NV):
                up_ref[pl.ds(v * n, n), :] = (1.0 + w_top) * q_ref[v, pl.ds(CAX - 1, n, stride=CAX), :]
                down_ref[pl.ds(v * n, n), :] = (1.0 - w_low) * q_ref[v, pl.ds(0, n, stride=CAX), :]

        @pl.when(even)
        def _():
            put(out_refs[0], out_refs[1])

        @pl.when(jnp.logical_not(even))
        def _():
            put(out_refs[1], out_refs[0])

    @pl.when(plen == 1)
    def _():
        refs = (own_ref,) + tuple(out_refs)
        for ref in refs:
            ref[...] = jnp.zeros_like(ref)
        blocks = n // CAX
        for b in range(blocks):
            tile = slot_ref[b]
            for shift, ref in enumerate(refs):
                here = jnp.logical_and(col_ref[b] == (az + shift) % n_az, open_ref[b] != 0)

                @pl.when(here)
                def _(ref=ref, b=b, tile=tile):
                    for v in range(NV):
                        row = pl.multiple_of(v * n + tile * CAX, CAX)
                        ref[pl.ds(row, CAX), :] += q_ref[v, pl.ds(CAX * CAX * b + CAX - 1, CAX, stride=CAX), :]


def first_kernel(n_az, n_out, q_ref, vel_ref, col_ref, slot_ref, open_ref, *outs):
    out_refs, (s_ref, own_ref, er_ref, el_ref) = outs[:n_out], outs[n_out:]
    n = q_ref.shape[1] // CAX
    for v in range(NV):
        el_ref[pl.ds(v * CAX, CAX), :] = q_ref[v, pl.ds(0, CAX), :]
        er_ref[pl.ds(v * CAX, CAX), :] = q_ref[v, pl.ds((n - 1) * CAX, CAX), :]
    el_ref[pl.ds(NV * CAX, CAX), :] = vel_ref[0, pl.ds(0, CAX), :]
    er_ref[pl.ds(NV * CAX, CAX), :] = vel_ref[0, pl.ds((n - 1) * CAX, CAX), :]
    extract(q_ref, vel_ref, col_ref, slot_ref, open_ref, out_refs, s_ref, own_ref, n_az)


def source(state, mix_ref, pre_ref, act_ref, heat_ref):
    inv = 1.0 / jnp.maximum(state[NS], 0.5)
    rates = [pre_ref[k] * jnp.exp(-act_ref[k] * inv) * jnp.maximum(state[k], 0.0) for k in range(NS)]
    out = []
    for v in range(NV):
        acc = None
        for k in range(NS):
            term = (mix_ref[v, k] if v < NS else heat_ref[k]) * rates[k]
            acc = term if acc is None else acc + term
        out.append(0.2 * acc)
    return out


def choose_ghosts(q_ref, ra_ref, rb_ref, s_ref, supply_ref, lo_ref, hi_ref, n_ax):
    _, ax, plen = roles()
    n = q_ref.shape[1] // CAX
    even = ax % 2 == 0
    odd = jnp.logical_not(even)
    cham = plen == 0

    @pl.when(plen == 1)
    def _():
        lo_ref[...] = supply_ref[...]
        hi_ref[...] = s_ref[...]

    @pl.when(jnp.logical_and(cham, even))
    def _():
        hi_ref[...] = ra_ref[...]

    @pl.when(jnp.logical_and(cham, odd))
    def _():
        lo_ref[...] = ra_ref[...]

    @pl.when(jnp.logical_and(cham, ax == 0))
    def _():
        lo_ref[...] = jnp.zeros_like(lo_ref)

    @pl.when(jnp.logical_and(cham, jnp.logical_and(even, ax > 0)))
    def _():
        lo_ref[...] = rb_ref[...]

    @pl.when(jnp.logical_and(cham, jnp.logical_and(odd, ax < n_ax - 1)))
    def _():
        hi_ref[...] = rb_ref[...]

    @pl.when(jnp.logical_and(cham, ax == n_ax - 1))
    def _():
        for v in range(NV):
            hi_ref[pl.ds(v * n, n), :] = q_ref[v, pl.ds(CAX - 1, n, stride=CAX), :]


def advance(q_ref, vel_ref, hl_ref, hr_ref, ul, ur, lo_ref, hi_ref, mix_ref, pre_ref, act_ref, heat_ref, finish):
    n = q_ref.shape[1] // CAX
    left = low_half()
    sub = lax.broadcasted_iota(jnp.int32, (CAX, LANES), 0)
    bottom, top = sub == 0, sub == CAX - 1

    def column(ref, v, j0, head, tail):
        regs = [ref[v, pl.ds(pl.multiple_of((j0 + d) * CAX, CAX), CAX), :] for d in range(NJ)]
        before = ref[v, pl.ds(pl.multiple_of(jnp.maximum(j0 - 1, 0) * CAX, CAX), CAX), :]
        after = ref[v, pl.ds(pl.multiple_of(jnp.minimum(j0 + NJ, n - 1) * CAX, CAX), CAX), :]
        before = jnp.where(j0 == 0, head, before)
        after = jnp.where(j0 + NJ == n, tail, after)
        turned = [pltpu.roll(x, HALF, 1) for x in [before] + regs + [after]]
        lefts = [jnp.where(left, turned[d], turned[d + 1]) for d in range(NJ)]
        rights = [jnp.where(left, turned[d + 1], turned[d + 2]) for d in range(NJ)]
        return regs, lefts, rights

    def body(c, carry):
        j0 = c * NJ
        _, u_left, u_right = column(vel_ref, 0, j0, ul, ur)
        w = [vel_ref[1, pl.ds(pl.multiple_of((j0 + d) * CAX, CAX), CAX), :] for d in range(NJ)]
        al = [0.1 + 0.1 * x for x in u_left]
        ar = [0.1 - 0.1 * x for x in u_right]
        wu = [0.1 + 0.1 * x for x in w]
        wd = [0.1 - 0.1 * x for x in w]
        src = []
        for d in range(NJ):
            state = [q_ref[v, pl.ds(pl.multiple_of((j0 + d) * CAX, CAX), CAX), :] for v in range(NV)]
            src.append(source(state, mix_ref, pre_ref, act_ref, heat_ref))
        for v in range(NV):
            regs, lefts, rights = column(q_ref, v, j0, hl_ref[pl.ds(v * CAX, CAX), :], hr_ref[pl.ds(v * CAX, CAX), :])
            for d in range(NJ):
                lo = jnp.broadcast_to(lo_ref[pl.ds(v * n + j0 + d, 1), :], (CAX, LANES))
                hi = jnp.broadcast_to(hi_ref[pl.ds(v * n + j0 + d, 1), :], (CAX, LANES))
                below = jnp.where(bottom, 0.1 * lo, pltpu.roll(wu[d] * regs[d], 1, 0))
                above = jnp.where(top, 0.1 * hi, pltpu.roll(wd[d] * regs[d], CAX - 1, 0))
                new = (0.6 * regs[d] + src[d][v]) + (al[d] * lefts[d] + ar[d] * rights[d]) + (below + above)
                finish(j0 + d, v, new)
        return carry

    lax.fori_loop(0, n // NJ, body, 0)


def section_one_kernel(n_az, n_ax, n_out, q_ref, vel_ref, hl_ref, hr_ref, s_in_ref, supply_ref, own_in_ref,
                       col_ref, slot_ref, open_ref, mix_ref, pre_ref, act_ref, heat_ref, *rest):
    got, rest = rest[:n_out], rest[n_out:]
    out_refs, rest = rest[:n_out], rest[n_out:]
    q1_ref, tile_ref, s_ref, own_ref, er_ref, el_ref, lo_ref, hi_ref = rest
    n = q_ref.shape[1] // CAX
    _, _, plen = roles()
    choose_ghosts(q_ref, got[0], got[1], s_in_ref, supply_ref, lo_ref, hi_ref, n_ax)

    @pl.when(plen == 1)
    def _():
        total = own_in_ref[...]
        for ref in got:
            total = total + ref[...]
        tile_ref[...] = total

    def finish(j, v, new):
        q1_ref[v, pl.ds(pl.multiple_of(j * CAX, CAX), CAX), :] = new

    ul, ur = hl_ref[pl.ds(NV * CAX, CAX), :], hr_ref[pl.ds(NV * CAX, CAX), :]
    advance(q_ref, vel_ref, hl_ref, hr_ref, ul, ur, lo_ref, hi_ref, mix_ref, pre_ref, act_ref, heat_ref, finish)
    for v in range(NV):
        el_ref[pl.ds(v * CAX, CAX), :] = q1_ref[v, pl.ds(0, CAX), :]
        er_ref[pl.ds(v * CAX, CAX), :] = q1_ref[v, pl.ds((n - 1) * CAX, CAX), :]
    extract(q1_ref, vel_ref, col_ref, slot_ref, open_ref, out_refs, s_ref, own_ref, n_az)


def section_two_kernel(n_ax, q_ref, q1_ref, vel_ref, hl_ref, hr_ref, u_l_ref, u_r_ref, ra_ref, rb_ref, s_in_ref, supply_ref,
                       mix_ref, pre_ref, act_ref, heat_ref, out_ref, base_ref, row_ref, lo_ref, hi_ref):
    n = q_ref.shape[1] // CAX
    choose_ghosts(q1_ref, ra_ref, rb_ref, s_in_ref, supply_ref, lo_ref, hi_ref, n_ax)

    def finish(j, v, new):
        at = pl.ds(pl.multiple_of(j * CAX, CAX), CAX)
        out_ref[v, at, :] = 0.5 * q_ref[v, at, :] + 0.5 * new

    advance(q1_ref, vel_ref, hl_ref, hr_ref, u_l_ref[...], u_r_ref[...], lo_ref, hi_ref,
            mix_ref, pre_ref, act_ref, heat_ref, finish)
    row_ref[pl.ds(0, n), :] = vel_ref[0, pl.ds(0, n, stride=CAX), :]
    row_ref[pl.ds(n, n), :] = vel_ref[1, pl.ds(0, n, stride=CAX), :]
    w_next = vel_ref[1, pl.ds(1, n, stride=CAX), :]
    for v in range(NV):
        base_ref[pl.ds(v * n, n), :] = (
            0.5 * q_ref[v, pl.ds(0, n, stride=CAX), :]
            + 0.05 * ((1.0 - w_next) * q1_ref[v, pl.ds(1, n, stride=CAX), :]))


def last_kernel(part_ref, base_ref, row_ref, s1_ref, dq_ref, s_in_ref, f_in_ref, dl_ref, dr_ref, hl_ref, hr_ref,
                u_l_ref, u_r_ref, mix_ref, pre_ref, act_ref, heat_ref, out_ref):
    n = out_ref.shape[1] // CAX
    _, ax, plen = roles()
    out_ref[...] = part_ref[...]
    first = lax.broadcasted_iota(jnp.int32, (n, LANES), 0) == 0
    last = lax.broadcasted_iota(jnp.int32, (n, LANES), 0) == n - 1
    left = lax.broadcasted_iota(jnp.int32, (n, LANES), 1) < HALF

    def neighbours(x, head, tail):
        before = jnp.where(first, head, pltpu.roll(x, 1, 0))
        after = jnp.where(last, tail, pltpu.roll(x, n - 1, 0))
        mid = pltpu.roll(x, HALF, 1)
        return (jnp.where(left, pltpu.roll(before, HALF, 1), mid),
                jnp.where(left, mid, pltpu.roll(after, HALF, 1)))

    @pl.when(jnp.logical_and(ax == 0, plen == 0))
    def _():
        u = row_ref[pl.ds(0, n), :]
        w = row_ref[pl.ds(n, n), :]
        u_left, u_right = neighbours(u, u_l_ref[pl.ds(0, 1), :], u_r_ref[pl.ds(0, 1), :])
        state = [s1_ref[pl.ds(v * n, n), :] + dq_ref[pl.ds(v * n, n), :] for v in range(NV)]
        src = source(state, mix_ref, pre_ref, act_ref, heat_ref)
        for v in range(NV):
            head = hl_ref[pl.ds(v * CAX, 1), :] + dl_ref[pl.ds(v, 1), :]
            tail = hr_ref[pl.ds(v * CAX, 1), :] + dr_ref[pl.ds(v, 1), :]
            q_left, q_right = neighbours(state[v], head, tail)
            inlet = s_in_ref[pl.ds(v * n, n), :] + f_in_ref[pl.ds(v * n, n), :]
            new = 0.6 * state[v] + 0.1 * ((1.0 + u_left) * q_left + (1.0 - u_right) * q_right + inlet) + src[v]
            out_ref[v, pl.ds(0, n, stride=CAX), :] = base_ref[pl.ds(v * n, n), :] + 0.5 * new
            out_ref[v, pl.ds(1, n, stride=CAX), :] = (
                part_ref[v, pl.ds(1, n, stride=CAX), :] + 0.05 * ((1.0 + w) * dq_ref[pl.ds(v * n, n), :]))

    @pl.when(jnp.logical_and(ax == 0, plen == 1))
    def _():
        for v in range(NV):
            out_ref[v, pl.ds(CAX - 1, n, stride=CAX), :] = (
                part_ref[v, pl.ds(CAX - 1, n, stride=CAX), :] + 0.05 * s_in_ref[pl.ds(v * n, n), :])


def shape(*dims):
    return jax.ShapeDtypeStruct(dims, f32)


def call(kernel, inputs, kinds, outs, scratch=()):
    vmem = pl.BlockSpec(memory_space=pltpu.VMEM)
    smem = pl.BlockSpec(memory_space=pltpu.SMEM)
    return pl.pallas_call(
        kernel,
        in_specs=[smem if k == "s" else vmem for k in kinds],
        out_specs=[vmem] * len(outs),
        out_shape=outs,
        scratch_shapes=list(scratch),
        compiler_params=pltpu.CompilerParams(vmem_limit_bytes=56 * 1024 * 1024),
    )(*inputs)


def local(n_az, n_ax, cells, speeds, supply, mix, prefactor, activation, heat, inj_column, inj_slot, inj_open):
    size = cells.shape[-1]
    n = size // LANES
    rows = NV * n

    def view(array):
        k = array.shape[0]
        return array.reshape(k, CAX, n, LANES).transpose(0, 2, 1, 3).reshape(k, CAX * n, LANES)

    def number(i, j, p):
        return (i * n_ax + j) * 2 + p

    every = [(i, j) for i in range(n_az) for j in range(n_ax)]

    def send(x, route):
        return lax.ppermute(x, AXES, [(number(*a), number(*b)) for a, b in route])

    def ring(step):
        return [((i, j, p), ((i + step) % n_az, j, p)) for i, j in every for p in (0, 1)]

    swap = [((i, j, p), (i, j, 1 - p)) for i, j in every for p in (0, 1)]
    n_out = n_az - 1

    def mate(k, j):
        return j ^ 1 if k == 0 else ((j + 1) ^ 1) - 1 if 0 < j < n_ax - 1 else n_ax - 1 - j

    def spread(k):
        out = [((i, j, 1), ((i + k + 1) % n_az, j, 1)) for i, j in every]
        if k < 2:
            out += [((i, j, 0), (i, mate(k, j), 0)) for i, j in every]
        return out

    q, vel = view(cells[0]), view(speeds[0])
    sup = supply.reshape(rows, LANES)
    col, slot, opened = inj_column.reshape(-1), inj_slot, inj_open
    react = (mix, prefactor, activation, heat)
    row, edge = shape(rows, LANES), shape(NV * CAX, LANES)
    plen = lax.axis_index("pl")
    ax = lax.axis_index("ax")

    got = call(functools.partial(first_kernel, n_az, n_out), (q, vel, col, slot, opened), "vvsss",
               [row] * (n_out + 2) + [shape((NV + 1) * CAX, LANES)] * 2)
    outs, (s0, own0, er, el) = got[:n_out], got[n_out:]
    ra = [send(x, spread(k)) for k, x in enumerate(outs)]
    s0r = send(s0, swap)
    hl0, hr0 = send(er, ring(1)), send(el, ring(-1))

    got = call(functools.partial(section_one_kernel, n_az, n_ax, n_out),
               (q, vel, hl0, hr0, s0r, sup, own0, col, slot, opened) + react + tuple(ra),
               "v" * 7 + "s" * 7 + "v" * n_out,
               [row] * n_out + [shape(*q.shape)] + [row] * 3 + [edge] * 2,
               [pltpu.VMEM((rows, LANES), f32)] * 2)
    outs, (q1, tile0, s1, own1, er, el) = got[:n_out], got[n_out:]
    down = [((i, j, 1), (i, j - 1, 1)) for i, j in every if j % 2 == 1]
    across = [((i, 2, 1), (i, 0, 0)) for i in range(n_az)]
    rb = [send(x, spread(k)) for k, x in enumerate(outs)]
    s1r = send(s1, swap)
    hl1, hr1 = send(er, ring(1)), send(el, ring(-1))
    pair0 = tile0 + send(tile0, down)

    tile1 = own1
    for x in rb:
        tile1 = tile1 + x
    pair1_in = send(tile1, down)
    far0 = send(pair0, across)
    near0 = send(pair0, swap)

    u_l, u_r = hl0[NV * CAX:], hr0[NV * CAX:]
    part, base, vrow = call(functools.partial(section_two_kernel, n_ax),
                            (q, q1, vel, hl1, hr1, u_l, u_r, rb[0], rb[1], s1r, sup) + react,
                            "v" * 11 + "s" * 4,
                            [shape(*q.shape), row, shape(2 * n, LANES)],
                            [pltpu.VMEM((rows, LANES), f32)] * 2)
    inlet_side = jnp.logical_and(ax == 0, plen == 0)
    dq = jnp.where(inlet_side, 0.1 * (far0 + near0), 0.0)
    pair1 = tile1 + pair1_in
    dq3 = dq.reshape(NV, n, LANES)
    far1 = send(pair1, across)
    near1 = send(jnp.where(plen == 0, dq, pair1), swap)
    dl, dr = send(dq3[:, n - 1], ring(1)), send(dq3[:, 0], ring(-1))
    out, = call(last_kernel,
                (part, base, vrow, s1, dq, near1, far1, dl, dr, hl1, hr1, u_l, u_r) + react,
                "v" * 13 + "s" * 4, [shape(*q.shape)])
    return out.reshape(NV, n, CAX, LANES).transpose(0, 2, 1, 3).reshape(1, NV, CAX, size)


def solution(mesh):
    return jax.shard_map(
        functools.partial(local, mesh.shape["az"], mesh.shape["ax"]),
        mesh=mesh,
        in_specs=(
            P("pl", None, "ax", "az"),
            P("pl", None, "ax", "az"),
            P(None, "ax", "az"),
            P(),
            P(),
            P(),
            P(),
            P(("az", "ax"), None),
            P(("az", "ax")),
            P(("az", "ax")),
        ),
        out_specs=P("pl", None, "ax", "az"),
        check_vma=False,
    )
```

```python
import functools

import jax
import jax.numpy as jnp
from jax import lax
from jax.experimental import pallas as pl
from jax.experimental.pallas import tpu as pltpu
from jax.sharding import PartitionSpec as P

NV = 10
NS = 9
LANES = 128
CAX = 8
HALF = 64
AXES = ("az", "ax", "pl")
NJ = 4
LIMIT = 16 * 1024 * 1024

f32 = jnp.float32


def roles():
    return lax.axis_index("az"), lax.axis_index("ax"), lax.axis_index("pl")


def low_half():
    return lax.broadcasted_iota(jnp.int32, (CAX, LANES), 1) < HALF


def extract(q_ref, vel_ref, col_ref, slot_ref, open_ref, out_refs, s_ref, own_ref, n_az):
    az, ax, plen = roles()
    n = q_ref.shape[1] // CAX
    for v in range(NV):
        s_ref[pl.ds(v * n, n), :] = q_ref[v, pl.ds(0, n, stride=CAX), :]

    @pl.when(plen == 0)
    def _():
        w_low = vel_ref[1, pl.ds(0, n, stride=CAX), :]
        w_top = vel_ref[1, pl.ds(CAX - 1, n, stride=CAX), :]
        even = ax % 2 == 0

        def put(up_ref, down_ref):
            for v in range(NV):
                up_ref[pl.ds(v * n, n), :] = (1.0 + w_top) * q_ref[v, pl.ds(CAX - 1, n, stride=CAX), :]
                down_ref[pl.ds(v * n, n), :] = (1.0 - w_low) * q_ref[v, pl.ds(0, n, stride=CAX), :]

        @pl.when(even)
        def _():
            put(out_refs[0], out_refs[1])

        @pl.when(jnp.logical_not(even))
        def _():
            put(out_refs[1], out_refs[0])

    @pl.when(plen == 1)
    def _():
        refs = (own_ref,) + tuple(out_refs)
        for ref in refs:
            ref[...] = jnp.zeros_like(ref)
        blocks = n // CAX
        for b in range(blocks):
            tile = slot_ref[b]
            for shift, ref in enumerate(refs):
                here = jnp.logical_and(col_ref[b] == (az + shift) % n_az, open_ref[b] != 0)

                @pl.when(here)
                def _(ref=ref, b=b, tile=tile):
                    for v in range(NV):
                        row = pl.multiple_of(v * n + tile * CAX, CAX)
                        ref[pl.ds(row, CAX), :] += q_ref[v, pl.ds(CAX * CAX * b + CAX - 1, CAX, stride=CAX), :]


def first_kernel(n_az, n_out, q_any, vel_any, col_ref, slot_ref, open_ref, *outs):
    out_refs, (q_ref, vel_ref, s_ref, own_ref, er_ref, el_ref, sems) = outs[:n_out], outs[n_out:]
    copies = [pltpu.make_async_copy(q_any, q_ref, sems.at[0]), pltpu.make_async_copy(vel_any, vel_ref, sems.at[1])]
    for copy in copies:
        copy.start()
    for copy in copies:
        copy.wait()
    n = q_ref.shape[1] // CAX
    for v in range(NV):
        el_ref[pl.ds(v * CAX, CAX), :] = q_ref[v, pl.ds(0, CAX), :]
        er_ref[pl.ds(v * CAX, CAX), :] = q_ref[v, pl.ds((n - 1) * CAX, CAX), :]
    el_ref[pl.ds(NV * CAX, CAX), :] = vel_ref[0, pl.ds(0, CAX), :]
    er_ref[pl.ds(NV * CAX, CAX), :] = vel_ref[0, pl.ds((n - 1) * CAX, CAX), :]
    extract(q_ref, vel_ref, col_ref, slot_ref, open_ref, out_refs, s_ref, own_ref, n_az)


def source(state, mix_ref, pre_ref, act_ref, heat_ref):
    inv = 1.0 / jnp.maximum(state[NS], 0.5)
    rates = [pre_ref[k] * jnp.exp(-act_ref[k] * inv) * jnp.maximum(state[k], 0.0) for k in range(NS)]
    out = []
    for v in range(NV):
        acc = None
        for k in range(NS):
            term = (mix_ref[v, k] if v < NS else heat_ref[k]) * rates[k]
            acc = term if acc is None else acc + term
        out.append(0.2 * acc)
    return out


def boundary(state_ref, dst_ref, scale, ra_ref, rb_ref, high_refs, supply_ref, hl_ref, hr_ref, ul_ref, ur_ref, n_ax):
    _, ax, plen = roles()
    n = dst_ref.shape[1] // CAX
    even = ax % 2 == 0
    odd = jnp.logical_not(even)
    cham = plen == 0

    def add(row, rows_of):
        for v in range(NV):
            dst_ref[v, pl.ds(row, n, stride=CAX), :] += scale * rows_of(v)

    def rows(*refs):
        return lambda v: sum(ref[pl.ds(v * n, n), :] for ref in refs)

    @pl.when(plen == 1)
    def _():
        add(0, rows(supply_ref))
        add(CAX - 1, rows(*high_refs))

    @pl.when(jnp.logical_and(cham, even))
    def _():
        add(CAX - 1, rows(ra_ref))

    @pl.when(jnp.logical_and(cham, odd))
    def _():
        add(0, rows(ra_ref))

    @pl.when(jnp.logical_and(cham, jnp.logical_and(even, ax > 0)))
    def _():
        add(0, rows(rb_ref))

    @pl.when(jnp.logical_and(cham, jnp.logical_and(odd, ax < n_ax - 1)))
    def _():
        add(CAX - 1, rows(rb_ref))

    @pl.when(jnp.logical_and(cham, ax == n_ax - 1))
    def _():
        add(CAX - 1, lambda v: state_ref[v, pl.ds(CAX - 1, n, stride=CAX), :])

    left = low_half()
    al = scale + scale * pltpu.roll(ul_ref[...], HALF, 1)
    ar = scale - scale * pltpu.roll(ur_ref[...], HALF, 1)
    for v in range(NV):
        head = pltpu.roll(hl_ref[pl.ds(v * CAX, CAX), :], HALF, 1)
        tail = pltpu.roll(hr_ref[pl.ds(v * CAX, CAX), :], HALF, 1)
        dst_ref[v, pl.ds(0, CAX), :] += jnp.where(left, al * head, 0.0)
        dst_ref[v, pl.ds((n - 1) * CAX, CAX), :] += jnp.where(left, 0.0, ar * tail)


def interior(q_ref, vel_ref, mix_ref, pre_ref, act_ref, heat_ref, finish):
    n = q_ref.shape[1] // CAX
    left = low_half()
    sub = lax.broadcasted_iota(jnp.int32, (CAX, LANES), 0)
    bottom, top = sub == 0, sub == CAX - 1

    def column(ref, v, j0):
        regs = [ref[v, pl.ds(pl.multiple_of((j0 + d) * CAX, CAX), CAX), :] for d in range(NJ)]
        before = ref[v, pl.ds(pl.multiple_of(jnp.maximum(j0 - 1, 0) * CAX, CAX), CAX), :]
        after = ref[v, pl.ds(pl.multiple_of(jnp.minimum(j0 + NJ, n - 1) * CAX, CAX), CAX), :]
        before = jnp.where(j0 == 0, 0.0, before)
        after = jnp.where(j0 + NJ == n, 0.0, after)
        turned = [pltpu.roll(x, HALF, 1) for x in [before] + regs + [after]]
        lefts = [jnp.where(left, turned[d], turned[d + 1]) for d in range(NJ)]
        rights = [jnp.where(left, turned[d + 1], turned[d + 2]) for d in range(NJ)]
        return regs, lefts, rights

    def body(c, carry):
        j0 = c * NJ
        _, u_left, u_right = column(vel_ref, 0, j0)
        w = [vel_ref[1, pl.ds(pl.multiple_of((j0 + d) * CAX, CAX), CAX), :] for d in range(NJ)]
        al = [0.1 + 0.1 * x for x in u_left]
        ar = [0.1 - 0.1 * x for x in u_right]
        wu = [0.1 + 0.1 * x for x in w]
        wd = [0.1 - 0.1 * x for x in w]
        src = []
        for d in range(NJ):
            state = [q_ref[v, pl.ds(pl.multiple_of((j0 + d) * CAX, CAX), CAX), :] for v in range(NV)]
            src.append(source(state, mix_ref, pre_ref, act_ref, heat_ref))
        for v in range(NV):
            regs, lefts, rights = column(q_ref, v, j0)
            for d in range(NJ):
                below = jnp.where(bottom, 0.0, pltpu.roll(wu[d] * regs[d], 1, 0))
                above = jnp.where(top, 0.0, pltpu.roll(wd[d] * regs[d], CAX - 1, 0))
                new = (0.6 * regs[d] + src[d][v]) + (al[d] * lefts[d] + ar[d] * rights[d]) + (below + above)
                finish(j0 + d, v, new)
        return carry

    lax.fori_loop(0, n // NJ, body, 0)


def inside_one_kernel(q_ref, vel_ref, mix_ref, pre_ref, act_ref, heat_ref, out_ref):
    def finish(j, v, new):
        out_ref[v, pl.ds(pl.multiple_of(j * CAX, CAX), CAX), :] = new

    interior(q_ref, vel_ref, mix_ref, pre_ref, act_ref, heat_ref, finish)


def inside_two_kernel(q_ref, q1_ref, vel_ref, mix_ref, pre_ref, act_ref, heat_ref, out_ref):
    def finish(j, v, new):
        at = pl.ds(pl.multiple_of(j * CAX, CAX), CAX)
        out_ref[v, at, :] = 0.5 * q_ref[v, at, :] + 0.5 * new

    interior(q1_ref, vel_ref, mix_ref, pre_ref, act_ref, heat_ref, finish)


def border_one_kernel(n_az, n_ax, n_out, part_ref, q_ref, vel_ref, hl_ref, hr_ref, s_in_ref, supply_ref, own_in_ref,
                      col_ref, slot_ref, open_ref, *rest):
    got, rest = rest[:n_out], rest[n_out:]
    out_refs, (q1_ref, tile_ref, s_ref, own_ref) = rest[:n_out], rest[n_out:]
    _, _, plen = roles()
    q1_ref[...] = part_ref[...]
    boundary(q_ref, q1_ref, 0.1, got[0], got[1], (s_in_ref,), supply_ref, hl_ref, hr_ref,
             hl_ref.at[pl.ds(NV * CAX, CAX)], hr_ref.at[pl.ds(NV * CAX, CAX)], n_ax)

    @pl.when(plen == 1)
    def _():
        total = own_in_ref[...]
        for ref in got:
            total = total + ref[...]
        tile_ref[...] = total

    @pl.when(plen == 0)
    def _():
        tile_ref[...] = jnp.zeros_like(tile_ref)

    extract(q1_ref, vel_ref, col_ref, slot_ref, open_ref, out_refs, s_ref, own_ref, n_az)


def tree_kernel(n_out, tile0_ref, down0_ref, own_ref, s1_ref, *rest):
    got, (tile_ref, step_ref, core_ref) = rest[:n_out], rest[n_out:]
    _, ax, plen = roles()

    @pl.when(plen == 0)
    def _():
        core_ref[...] = s1_ref[...]
        tile_ref[...] = jnp.zeros_like(tile_ref)
        step_ref[...] = jnp.zeros_like(step_ref)

    @pl.when(plen == 1)
    def _():
        total = own_ref[...]
        for ref in got:
            total = total + ref[...]
        tile_ref[...] = total
        pair = tile0_ref[...] + down0_ref[...]
        core_ref[...] = pair
        step_ref[...] = jnp.where(ax % 2 == 1, total, pair)


def inlet_kernel(q1_ref, tile_ref, step_ref, core_ref, dq_ref, pair_ref, core_out_ref, er_ref, el_ref):
    _, ax, plen = roles()
    n = q1_ref.shape[1] // CAX
    for v in range(NV):
        el_ref[pl.ds(v * CAX, CAX), :] = q1_ref[v, pl.ds(0, CAX), :]
        er_ref[pl.ds(v * CAX, CAX), :] = q1_ref[v, pl.ds((n - 1) * CAX, CAX), :]

    @pl.when(plen == 1)
    def _():
        pair = tile_ref[...] + step_ref[...]
        pair_ref[...] = pair
        core_out_ref[...] = pair
        dq_ref[...] = jnp.zeros_like(dq_ref)

    @pl.when(jnp.logical_and(plen == 0, ax > 0))
    def _():
        pair_ref[...] = jnp.zeros_like(pair_ref)
        core_out_ref[...] = jnp.zeros_like(core_out_ref)
        dq_ref[...] = jnp.zeros_like(dq_ref)

    @pl.when(jnp.logical_and(plen == 0, ax == 0))
    def _():
        pair_ref[...] = jnp.zeros_like(pair_ref)
        dq = 0.1 * (step_ref[...] + core_ref[...])
        dq_ref[...] = dq
        core_out_ref[...] = dq
        for v in range(NV):
            el_ref[pl.ds(v * CAX, 1), :] += dq_ref[pl.ds(v * n, 1), :]
            er_ref[pl.ds(v * CAX, 1), :] += dq_ref[pl.ds(v * n + n - 1, 1), :]


def last_kernel(n_ax, part_ref, q_ref, q1_ref, vel_ref, s1_in_ref, supply_ref, ra_ref, rb_ref, dq_ref, core_ref, far_ref,
                hl_ref, hr_ref, hl0_ref, hr0_ref, mix_ref, pre_ref, act_ref, heat_ref, out_ref):
    n = out_ref.shape[1] // CAX
    _, ax, plen = roles()
    out_ref[...] = part_ref[...]
    ul_ref, ur_ref = hl0_ref.at[pl.ds(NV * CAX, CAX)], hr0_ref.at[pl.ds(NV * CAX, CAX)]
    boundary(q1_ref, out_ref, 0.05, ra_ref, rb_ref, (s1_in_ref, core_ref), supply_ref, hl_ref, hr_ref, ul_ref, ur_ref, n_ax)

    @pl.when(jnp.logical_and(ax == 0, plen == 0))
    def _():
        first = lax.broadcasted_iota(jnp.int32, (n, LANES), 0) == 0
        last = lax.broadcasted_iota(jnp.int32, (n, LANES), 0) == n - 1
        left = lax.broadcasted_iota(jnp.int32, (n, LANES), 1) < HALF

        def neighbours(x, head, tail):
            before = jnp.where(first, head, pltpu.roll(x, 1, 0))
            after = jnp.where(last, tail, pltpu.roll(x, n - 1, 0))
            mid = pltpu.roll(x, HALF, 1)
            return (jnp.where(left, pltpu.roll(before, HALF, 1), mid),
                    jnp.where(left, mid, pltpu.roll(after, HALF, 1)))

        u = vel_ref[0, pl.ds(0, n, stride=CAX), :]
        w = vel_ref[1, pl.ds(0, n, stride=CAX), :]
        w_next = vel_ref[1, pl.ds(1, n, stride=CAX), :]
        u_left, u_right = neighbours(u, ul_ref[pl.ds(0, 1), :], ur_ref[pl.ds(0, 1), :])
        state = [q1_ref[v, pl.ds(0, n, stride=CAX), :] + dq_ref[pl.ds(v * n, n), :] for v in range(NV)]
        src = source(state, mix_ref, pre_ref, act_ref, heat_ref)
        for v in range(NV):
            q_left, q_right = neighbours(state[v], hl_ref[pl.ds(v * CAX, 1), :], hr_ref[pl.ds(v * CAX, 1), :])
            inlet = core_ref[pl.ds(v * n, n), :] + far_ref[pl.ds(v * n, n), :]
            above = (1.0 - w_next) * q1_ref[v, pl.ds(1, n, stride=CAX), :]
            new = 0.6 * state[v] + 0.1 * ((1.0 + u_left) * q_left + (1.0 - u_right) * q_right + inlet + above) + src[v]
            out_ref[v, pl.ds(0, n, stride=CAX), :] = 0.5 * q_ref[v, pl.ds(0, n, stride=CAX), :] + 0.5 * new
            out_ref[v, pl.ds(1, n, stride=CAX), :] += 0.05 * ((1.0 + w) * dq_ref[pl.ds(v * n, n), :])


def shape(*dims):
    return jax.ShapeDtypeStruct(dims, f32)


def call(kernel, inputs, kinds, outs, scratch=(), cost=None):
    spaces = {"s": pltpu.SMEM, "v": pltpu.VMEM, "a": pl.ANY}
    return pl.pallas_call(
        kernel,
        in_specs=[pl.BlockSpec(memory_space=spaces[k]) for k in kinds],
        out_specs=[pl.BlockSpec(memory_space=pltpu.VMEM)] * len(outs),
        out_shape=outs,
        scratch_shapes=list(scratch),
        cost_estimate=cost,
        compiler_params=pltpu.CompilerParams(vmem_limit_bytes=LIMIT),
    )(*inputs)


def local(n_az, n_ax, cells, speeds, supply, mix, prefactor, activation, heat, inj_column, inj_slot, inj_open):
    size = cells.shape[-1]
    n = size // LANES
    rows = NV * n

    def view(array):
        k = array.shape[0]
        return array.reshape(k, CAX, n, LANES).transpose(0, 2, 1, 3).reshape(k, CAX * n, LANES)

    def number(i, j, p):
        return (i * n_ax + j) * 2 + p

    every = [(i, j) for i in range(n_az) for j in range(n_ax)]

    def send(x, route):
        return lax.ppermute(x, AXES, [(number(*a), number(*b)) for a, b in route])

    def ring(step):
        return [((i, j, p), ((i + step) % n_az, j, p)) for i, j in every for p in (0, 1)]

    swap = [((i, j, p), (i, j, 1 - p)) for i, j in every for p in (0, 1)]
    n_out = n_az - 1

    def mate(k, j):
        return j ^ 1 if k == 0 else ((j + 1) ^ 1) - 1 if 0 < j < n_ax - 1 else n_ax - 1 - j

    def spread(k):
        out = [((i, j, 1), ((i + k + 1) % n_az, j, 1)) for i, j in every]
        if k < 2:
            out += [((i, j, 0), (i, mate(k, j), 0)) for i, j in every]
        return out

    q, vel = view(cells[0]), view(speeds[0])
    sup = supply.reshape(rows, LANES)
    col, slot, opened = inj_column.reshape(-1), inj_slot, inj_open
    react = (mix, prefactor, activation, heat)
    row, edge = shape(rows, LANES), shape(NV * CAX, LANES)

    whole = shape(*q.shape)
    work = pl.CostEstimate(flops=300 * q.shape[1] * LANES, transcendentals=20 * q.shape[1] * LANES,
                           bytes_accessed=12_000_000)

    got = call(functools.partial(first_kernel, n_az, n_out), (q, vel, col, slot, opened), "aasss",
               [row] * n_out + [whole, shape(*vel.shape), row, row] + [shape((NV + 1) * CAX, LANES)] * 2,
               [pltpu.SemaphoreType.DMA((2,))])
    outs, (qv, velv, s0, own0, er, el) = got[:n_out], got[n_out:]
    hl0, hr0 = send(er, ring(1)), send(el, ring(-1))
    s0r = send(s0, swap)
    ra = [send(x, spread(k)) for k, x in enumerate(outs)]
    part, = call(inside_one_kernel, (qv, velv) + react, "vvssss", [whole], cost=work)

    got = call(functools.partial(border_one_kernel, n_az, n_ax, n_out),
               (part, qv, velv, hl0, hr0, s0r, sup, own0, col, slot, opened) + tuple(ra),
               "v" * 8 + "s" * 3 + "v" * n_out, [row] * n_out + [whole, row, row, row])
    outs, (q1, tile0, s1, own1) = got[:n_out], got[n_out:]
    down = [((i, j, 1), (i, j - 1, 1)) for i, j in every if j % 2 == 1]
    across = [((i, 2, 1), (i, 0, 0)) for i in range(n_az)]
    rb = [send(x, spread(k)) for k, x in enumerate(outs)]
    down0 = send(tile0, down)

    tile1, step, core = call(functools.partial(tree_kernel, n_out), (tile0, down0, own1, s1) + tuple(rb),
                             "v" * (4 + n_out), [row] * 3)
    step_in = send(step, down + across)
    core_in = send(core, swap)
    part, = call(inside_two_kernel, (qv, q1, velv) + react, "vvvssss", [whole], cost=work)

    dq, pair1, core2, er, el = call(inlet_kernel, (q1, tile1, step_in, core_in), "vvvv", [row] * 3 + [edge] * 2)
    core2_in = send(core2, swap)
    far1 = send(pair1, across)
    hl1, hr1 = send(er, ring(1)), send(el, ring(-1))
    out, = call(functools.partial(last_kernel, n_ax),
                (part, qv, q1, velv, core_in, sup, rb[0], rb[1], dq, core2_in, far1, hl1, hr1, hl0, hr0) + react,
                "v" * 15 + "s" * 4, [whole])
    return out.reshape(NV, n, CAX, LANES).transpose(0, 2, 1, 3).reshape(1, NV, CAX, size)


def solution(mesh):
    return jax.shard_map(
        functools.partial(local, mesh.shape["az"], mesh.shape["ax"]),
        mesh=mesh,
        in_specs=(
            P("pl", None, "ax", "az"),
            P("pl", None, "ax", "az"),
            P(None, "ax", "az"),
            P(),
            P(),
            P(),
            P(),
            P(("az", "ax"), None),
            P(("az", "ax")),
            P(("az", "ax")),
        ),
        out_specs=P("pl", None, "ax", "az"),
        check_vma=False,
    )
```

```python
import functools

import jax
import jax.numpy as jnp
from jax import lax
from jax.experimental import pallas as pl
from jax.experimental.pallas import tpu as pltpu
from jax.sharding import PartitionSpec as P

NV = 10
NS = 9
LANES = 128
CAX = 8
HALF = 64
AXES = ("az", "ax", "pl")
NJ = 4
LOG2E = 1.4426950408889634
LIMIT = 16 * 1024 * 1024

f32 = jnp.float32


def roles():
    return lax.axis_index("az"), lax.axis_index("ax"), lax.axis_index("pl")


def low_half():
    return lax.broadcasted_iota(jnp.int32, (CAX, LANES), 1) < HALF


def extract(q_ref, vel_ref, col_ref, slot_ref, open_ref, out_refs, s_ref, own_ref, n_az):
    az, ax, plen = roles()
    n = q_ref.shape[1] // CAX
    for v in range(NV):
        s_ref[pl.ds(v * n, n), :] = q_ref[v, pl.ds(0, n, stride=CAX), :]

    @pl.when(plen == 0)
    def _():
        w_low = vel_ref[1, pl.ds(0, n, stride=CAX), :]
        w_top = vel_ref[1, pl.ds(CAX - 1, n, stride=CAX), :]
        even = ax % 2 == 0

        def put(up_ref, down_ref):
            for v in range(NV):
                up_ref[pl.ds(v * n, n), :] = (1.0 + w_top) * q_ref[v, pl.ds(CAX - 1, n, stride=CAX), :]
                down_ref[pl.ds(v * n, n), :] = (1.0 - w_low) * q_ref[v, pl.ds(0, n, stride=CAX), :]

        @pl.when(even)
        def _():
            put(out_refs[0], out_refs[1])

        @pl.when(jnp.logical_not(even))
        def _():
            put(out_refs[1], out_refs[0])

    @pl.when(plen == 1)
    def _():
        refs = (own_ref,) + tuple(out_refs)
        for ref in refs:
            ref[...] = jnp.zeros_like(ref)
        blocks = n // CAX
        for b in range(blocks):
            tile = slot_ref[b]
            for shift, ref in enumerate(refs):
                here = jnp.logical_and(col_ref[b] == (az + shift) % n_az, open_ref[b] != 0)

                @pl.when(here)
                def _(ref=ref, b=b, tile=tile):
                    for v in range(NV):
                        row = pl.multiple_of(v * n + tile * CAX, CAX)
                        ref[pl.ds(row, CAX), :] += q_ref[v, pl.ds(CAX * CAX * b + CAX - 1, CAX, stride=CAX), :]


def edge_kernel(q_any, vel_any, er_ref, el_ref, q_l, q_r, sems):
    n = q_any.shape[1] // CAX
    ends = [(q_l, el_ref, 0), (q_r, er_ref, (n - 1) * CAX)]
    copies = []
    for k, (q_ref, e_ref, at) in enumerate(ends):
        copies.append(pltpu.make_async_copy(q_any.at[:, pl.ds(at, CAX)], q_ref, sems.at[2 * k]))
        copies.append(pltpu.make_async_copy(vel_any.at[0, pl.ds(at, CAX)], e_ref.at[pl.ds(NV * CAX, CAX)], sems.at[2 * k + 1]))
    for copy in copies:
        copy.start()
    for copy in copies:
        copy.wait()
    for q_ref, e_ref, _ in ends:
        for v in range(NV):
            e_ref[pl.ds(v * CAX, CAX), :] = q_ref[v]


def first_kernel(n_az, n_out, q_any, vel_any, col_any, slot_any, open_any, *outs):
    out_refs, rest = outs[:n_out], outs[n_out:]
    q_ref, vel_ref, s_ref, own_ref, col_ref, slot_ref, open_ref, sems = rest
    pairs = [(vel_any, vel_ref), (col_any, col_ref), (slot_any, slot_ref), (open_any, open_ref)]
    pairs += [(q_any.at[pl.ds(v, 2)], q_ref.at[pl.ds(v, 2)]) for v in range(0, NV, 2)]
    copies = [pltpu.make_async_copy(x, y, sems.at[k]) for k, (x, y) in enumerate(pairs)]
    for copy in copies:
        copy.start()
    for copy in copies:
        copy.wait()
    extract(q_ref, vel_ref, col_ref, slot_ref, open_ref, out_refs, s_ref, own_ref, n_az)


def source(state, mix_ref, pre_ref, act_ref, heat_ref):
    inv = 1.0 / jnp.maximum(state[NS], 0.5)
    rates = [pre_ref[k] * jnp.exp(-act_ref[k] * inv) * jnp.maximum(state[k], 0.0) for k in range(NS)]
    out = []
    for v in range(NV):
        acc = None
        for k in range(NS):
            term = (mix_ref[v, k] if v < NS else heat_ref[k]) * rates[k]
            acc = term if acc is None else acc + term
        out.append(0.2 * acc)
    return out


def fill_ghosts(state_ref, lo_ref, hi_ref, ra_ref, rb_ref, high_refs, supply_ref, n_ax):
    _, ax, plen = roles()
    n = state_ref.shape[1] // CAX
    even = ax % 2 == 0
    odd = jnp.logical_not(even)
    cham = plen == 0

    @pl.when(plen == 1)
    def _():
        lo_ref[...] = supply_ref[...]
        hi_ref[...] = sum(ref[...] for ref in high_refs)

    @pl.when(jnp.logical_and(cham, even))
    def _():
        hi_ref[...] = ra_ref[...]

    @pl.when(jnp.logical_and(cham, odd))
    def _():
        lo_ref[...] = ra_ref[...]

    @pl.when(jnp.logical_and(cham, ax == 0))
    def _():
        lo_ref[...] = jnp.zeros_like(lo_ref)

    @pl.when(jnp.logical_and(cham, jnp.logical_and(even, ax > 0)))
    def _():
        lo_ref[...] = rb_ref[...]

    @pl.when(jnp.logical_and(cham, jnp.logical_and(odd, ax < n_ax - 1)))
    def _():
        hi_ref[...] = rb_ref[...]

    @pl.when(jnp.logical_and(cham, ax == n_ax - 1))
    def _():
        for v in range(NV):
            hi_ref[pl.ds(v * n, n), :] = state_ref[v, pl.ds(CAX - 1, n, stride=CAX), :]


def add_border(v, dst_ref, scale, lo_ref, hi_ref, hl_ref, hr_ref, ul_ref, ur_ref):
    n = dst_ref.shape[1] // CAX
    left = low_half()
    dst_ref[v, pl.ds(0, n, stride=CAX), :] += scale * lo_ref[pl.ds(v * n, n), :]
    dst_ref[v, pl.ds(CAX - 1, n, stride=CAX), :] += scale * hi_ref[pl.ds(v * n, n), :]
    al = scale + scale * pltpu.roll(ul_ref[...], HALF, 1)
    ar = scale - scale * pltpu.roll(ur_ref[...], HALF, 1)
    head = pltpu.roll(hl_ref[pl.ds(v * CAX, CAX), :], HALF, 1)
    tail = pltpu.roll(hr_ref[pl.ds(v * CAX, CAX), :], HALF, 1)
    dst_ref[v, pl.ds(0, CAX), :] += jnp.where(left, al * head, 0.0)
    dst_ref[v, pl.ds((n - 1) * CAX, CAX), :] += jnp.where(left, 0.0, ar * tail)


def mixing(a_ref, scale, mix_ref, pre_ref, heat_ref):
    width = NV * CAX
    col = lax.broadcasted_iota(jnp.int32, (CAX, 3 * width), 1)
    row = lax.broadcasted_iota(jnp.int32, (CAX, 3 * width), 0)
    inner = col % width
    species, lane = inner // CAX, inner % CAX
    for v in range(NV):
        block = jnp.zeros((CAX, 3 * width), f32)
        for k in range(NS):
            value = (0.2 * scale) * pre_ref[k] * (mix_ref[v, k] if v < NS else heat_ref[k])
            block = jnp.where(species == k, value, block)
        block = jnp.where(lane == row, block, 0.0)
        high = block.astype(jnp.bfloat16).astype(f32)
        a_ref[pl.ds(v * CAX, CAX), :] = jnp.where(col // width == 1, block - high, high)


def interior(q_ref, vel_ref, a_ref, scale, mix_ref, pre_ref, act_ref, heat_ref, finish):
    n = q_ref.shape[1] // CAX
    left = low_half()
    sub = lax.broadcasted_iota(jnp.int32, (CAX, LANES), 0)
    bottom, top = sub == 0, sub == CAX - 1
    mixing(a_ref, scale, mix_ref, pre_ref, heat_ref)
    a = a_ref[...].astype(jnp.bfloat16)
    power = [act_ref[k] * (-LOG2E) for k in range(NS)]
    c = 0.1 * scale

    def reg(ref, v, j):
        return ref[v, pl.ds(pl.multiple_of(j * CAX, CAX), CAX), :]

    def column(ref, v, j0):
        regs = [reg(ref, v, j0 + d) for d in range(NJ)]
        before = jnp.where(j0 == 0, 0.0, reg(ref, v, jnp.maximum(j0 - 1, 0)))
        after = jnp.where(j0 + NJ == n, 0.0, reg(ref, v, jnp.minimum(j0 + NJ, n - 1)))
        turned = [pltpu.roll(x, HALF, 1) for x in [before] + regs + [after]]
        lefts = [jnp.where(left, turned[d], turned[d + 1]) for d in range(NJ)]
        rights = [jnp.where(left, turned[d + 1], turned[d + 2]) for d in range(NJ)]
        return regs, lefts, rights

    def body(step, carry):
        j0 = step * NJ
        rates = []
        for d in range(NJ):
            inv = 1.0 / jnp.maximum(reg(q_ref, NS, j0 + d), 0.5)
            some = [jnp.exp2(power[k] * inv) * jnp.maximum(reg(q_ref, k, j0 + d), 0.0) for k in range(NS)]
            rates.append(jnp.concatenate(some + [jnp.zeros((CAX, LANES), f32)], axis=0))
        rate = jnp.concatenate(rates, axis=1)
        high = rate.astype(jnp.bfloat16)
        low = (rate - high.astype(f32)).astype(jnp.bfloat16)
        src = jnp.dot(a, jnp.concatenate([high, high, low], axis=0), preferred_element_type=f32)
        _, u_left, u_right = column(vel_ref, 0, j0)
        w = [reg(vel_ref, 1, j0 + d) for d in range(NJ)]
        al = [c + c * x for x in u_left]
        ar = [c - c * x for x in u_right]
        wu = [jnp.where(bottom, 0.0, c + c * pltpu.roll(x, 1, 0)) for x in w]
        wd = [jnp.where(top, 0.0, c - c * pltpu.roll(x, CAX - 1, 0)) for x in w]
        for v in range(NV):
            regs, lefts, rights = column(q_ref, v, j0)
            for d in range(NJ):
                vertical = wu[d] * pltpu.roll(regs[d], 1, 0) + wd[d] * pltpu.roll(regs[d], CAX - 1, 0)
                new = (0.6 * scale) * regs[d] + src[v * CAX:(v + 1) * CAX, d * LANES:(d + 1) * LANES]
                finish(j0 + d, v, new + (al[d] * lefts[d] + ar[d] * rights[d]) + vertical)
        return carry

    lax.fori_loop(0, n // NJ, body, 0)


def inside_one_kernel(q_ref, vel_ref, mix_ref, pre_ref, act_ref, heat_ref, out_ref, a_ref):
    def finish(j, v, new):
        out_ref[v, pl.ds(pl.multiple_of(j * CAX, CAX), CAX), :] = new

    interior(q_ref, vel_ref, a_ref, 1.0, mix_ref, pre_ref, act_ref, heat_ref, finish)


def inside_two_kernel(q_ref, q1_ref, vel_ref, mix_ref, pre_ref, act_ref, heat_ref, out_ref, er_ref, el_ref, a_ref):
    n = q_ref.shape[1] // CAX
    for v in range(NV):
        el_ref[pl.ds(v * CAX, CAX), :] = q1_ref[v, pl.ds(0, CAX), :]
        er_ref[pl.ds(v * CAX, CAX), :] = q1_ref[v, pl.ds((n - 1) * CAX, CAX), :]

    def finish(j, v, new):
        at = pl.ds(pl.multiple_of(j * CAX, CAX), CAX)
        out_ref[v, at, :] = 0.5 * q_ref[v, at, :] + new

    interior(q1_ref, vel_ref, a_ref, 0.5, mix_ref, pre_ref, act_ref, heat_ref, finish)


def border_one_kernel(n_az, n_ax, n_out, s_in_ref, *rest):
    late, rest = rest[:n_out - 2], rest[n_out - 2:]
    hl_ref, hr_ref, part_ref, q_ref, vel_ref, supply_ref, own_in_ref, col_ref, slot_ref, open_ref = rest[2:12]
    got, rest = rest[:2] + late, rest[12:]
    out_refs, (q1_ref, tile_ref, s_ref, own_ref, lo_ref, hi_ref) = rest[:n_out], rest[n_out:]
    _, _, plen = roles()
    fill_ghosts(q_ref, lo_ref, hi_ref, got[0], got[1], (s_in_ref,), supply_ref, n_ax)
    for v in range(NV):
        q1_ref[v] = part_ref[v]
        add_border(v, q1_ref, 0.1, lo_ref, hi_ref, hl_ref, hr_ref,
                   hl_ref.at[pl.ds(NV * CAX, CAX)], hr_ref.at[pl.ds(NV * CAX, CAX)])

    @pl.when(plen == 1)
    def _():
        total = own_in_ref[...]
        for ref in got:
            total = total + ref[...]
        tile_ref[...] = total

    @pl.when(plen == 0)
    def _():
        tile_ref[...] = jnp.zeros_like(tile_ref)

    extract(q1_ref, vel_ref, col_ref, slot_ref, open_ref, out_refs, s_ref, own_ref, n_az)


def tree_kernel(n_out, tile0_ref, down0_ref, own_ref, s1_ref, row_ref, *rest):
    got, (tile_ref, step_ref, core_ref) = rest[:n_out], rest[n_out:]
    _, ax, plen = roles()

    @pl.when(plen == 0)
    def _():
        core_ref[...] = s1_ref[...]
        tile_ref[...] = jnp.zeros_like(tile_ref)
        step_ref[...] = row_ref[...]

    @pl.when(plen == 1)
    def _():
        total = own_ref[...]
        for ref in got:
            total = total + ref[...]
        tile_ref[...] = total
        pair = tile0_ref[...] + down0_ref[...]
        core_ref[...] = pair
        step_ref[...] = jnp.where(ax % 2 == 1, total, pair)


def inlet_kernel(er_in_ref, el_in_ref, tile_ref, step_ref, core_ref, dq_ref, pair_ref, core_out_ref, er_ref, el_ref):
    _, ax, plen = roles()
    n = dq_ref.shape[0] // NV
    er_ref[...] = er_in_ref[...]
    el_ref[...] = el_in_ref[...]

    @pl.when(plen == 1)
    def _():
        pair = tile_ref[...] + step_ref[...]
        pair_ref[...] = pair
        core_out_ref[...] = pair
        dq_ref[...] = jnp.zeros_like(dq_ref)

    @pl.when(jnp.logical_and(plen == 0, ax > 0))
    def _():
        pair_ref[...] = jnp.zeros_like(pair_ref)
        core_out_ref[...] = jnp.zeros_like(core_out_ref)
        dq_ref[...] = jnp.zeros_like(dq_ref)

    @pl.when(jnp.logical_and(plen == 0, ax == 0))
    def _():
        pair_ref[...] = jnp.zeros_like(pair_ref)
        dq = 0.1 * (step_ref[...] + core_ref[...])
        dq_ref[...] = dq
        core_out_ref[...] = dq
        for v in range(NV):
            el_ref[pl.ds(v * CAX, 1), :] += dq_ref[pl.ds(v * n, 1), :]
            er_ref[pl.ds(v * CAX, 1), :] += dq_ref[pl.ds(v * n + n - 1, 1), :]


def last_kernel(n_ax, part_ref, q_ref, q1_ref, vel_ref, s1_in_ref, supply_ref, ra_ref, rb_ref, dq_ref, core_ref, far_ref,
                hl_ref, hr_ref, hl0_ref, hr0_ref, mix_ref, pre_ref, act_ref, heat_ref, out_any,
                out_ref, row_ref, lo_ref, hi_ref, sems):
    n = out_ref.shape[1] // CAX
    _, ax, plen = roles()
    inlet_side = jnp.logical_and(ax == 0, plen == 0)
    ul_ref, ur_ref = hl0_ref.at[pl.ds(NV * CAX, CAX)], hr0_ref.at[pl.ds(NV * CAX, CAX)]
    fill_ghosts(q1_ref, lo_ref, hi_ref, ra_ref, rb_ref, (s1_in_ref, core_ref), supply_ref, n_ax)

    @pl.when(inlet_side)
    def _():
        first = lax.broadcasted_iota(jnp.int32, (n, LANES), 0) == 0
        last = lax.broadcasted_iota(jnp.int32, (n, LANES), 0) == n - 1
        left = lax.broadcasted_iota(jnp.int32, (n, LANES), 1) < HALF

        def neighbours(x, head, tail):
            before = jnp.where(first, head, pltpu.roll(x, 1, 0))
            after = jnp.where(last, tail, pltpu.roll(x, n - 1, 0))
            mid = pltpu.roll(x, HALF, 1)
            return (jnp.where(left, pltpu.roll(before, HALF, 1), mid),
                    jnp.where(left, mid, pltpu.roll(after, HALF, 1)))

        u = vel_ref[0, pl.ds(0, n, stride=CAX), :]
        w_next = vel_ref[1, pl.ds(1, n, stride=CAX), :]
        u_left, u_right = neighbours(u, ul_ref[pl.ds(0, 1), :], ur_ref[pl.ds(0, 1), :])
        state = [q1_ref[v, pl.ds(0, n, stride=CAX), :] + dq_ref[pl.ds(v * n, n), :] for v in range(NV)]
        src = source(state, mix_ref, pre_ref, act_ref, heat_ref)
        for v in range(NV):
            q_left, q_right = neighbours(state[v], hl_ref[pl.ds(v * CAX, 1), :], hr_ref[pl.ds(v * CAX, 1), :])
            inlet = core_ref[pl.ds(v * n, n), :] + far_ref[pl.ds(v * n, n), :]
            above = (1.0 - w_next) * q1_ref[v, pl.ds(1, n, stride=CAX), :]
            new = 0.6 * state[v] + 0.1 * ((1.0 + u_left) * q_left + (1.0 - u_right) * q_right + inlet + above) + src[v]
            row_ref[pl.ds(v * n, n), :] = 0.5 * q_ref[v, pl.ds(0, n, stride=CAX), :] + 0.5 * new

    copies = []
    for v in range(NV):
        out_ref[v] = part_ref[v]
        add_border(v, out_ref, 0.05, lo_ref, hi_ref, hl_ref, hr_ref, ul_ref, ur_ref)

        @pl.when(inlet_side)
        def _(v=v):
            w = vel_ref[1, pl.ds(0, n, stride=CAX), :]
            out_ref[v, pl.ds(0, n, stride=CAX), :] = row_ref[pl.ds(v * n, n), :]
            out_ref[v, pl.ds(1, n, stride=CAX), :] += 0.05 * ((1.0 + w) * dq_ref[pl.ds(v * n, n), :])

        copies.append(pltpu.make_async_copy(out_ref.at[v], out_any.at[v], sems.at[v]))
        copies[-1].start()
    for copy in copies:
        copy.wait()


def shape(*dims):
    return jax.ShapeDtypeStruct(dims, f32)


def call(kernel, inputs, kinds, outs, scratch=(), cost=None, to=pltpu.VMEM):
    spaces = {"s": pltpu.SMEM, "v": pltpu.VMEM, "h": pltpu.HBM}
    return pl.pallas_call(
        kernel,
        in_specs=[pl.BlockSpec(memory_space=spaces[k]) for k in kinds],
        out_specs=[pl.BlockSpec(memory_space=to)] * len(outs),
        out_shape=outs,
        scratch_shapes=list(scratch),
        cost_estimate=cost,
        compiler_params=pltpu.CompilerParams(vmem_limit_bytes=LIMIT),
    )(*inputs)


def local(n_az, n_ax, cells, speeds, supply, mix, prefactor, activation, heat, inj_column, inj_slot, inj_open):
    size = cells.shape[-1]
    n = size // LANES
    rows = NV * n

    def view(array):
        k = array.shape[0]
        return array.reshape(k, CAX, n, LANES).transpose(0, 2, 1, 3).reshape(k, CAX * n, LANES)

    def number(i, j, p):
        return (i * n_ax + j) * 2 + p

    every = [(i, j) for i in range(n_az) for j in range(n_ax)]

    def send(x, route):
        return lax.ppermute(x, AXES, [(number(*a), number(*b)) for a, b in route])

    def ring(step):
        return [((i, j, p), ((i + step) % n_az, j, p)) for i, j in every for p in (0, 1)]

    swap = [((i, j, p), (i, j, 1 - p)) for i, j in every for p in (0, 1)]
    n_out = n_az - 1

    def mate(k, j):
        return j ^ 1 if k == 0 else ((j + 1) ^ 1) - 1 if 0 < j < n_ax - 1 else n_ax - 1 - j

    def spread(k):
        out = [((i, j, 1), ((i + k + 1) % n_az, j, 1)) for i, j in every]
        if k < 2:
            out += [((i, j, 0), (i, mate(k, j), 0)) for i, j in every]
        return out

    q, vel = view(cells[0]), view(speeds[0])
    sup = supply.reshape(rows, LANES)
    col, slot, opened = inj_column.reshape(-1), inj_slot, inj_open
    react = (mix, prefactor, activation, heat)
    row, edge = shape(rows, LANES), shape(NV * CAX, LANES)

    whole = shape(*q.shape)
    work = pl.CostEstimate(flops=300 * q.shape[1] * LANES, transcendentals=20 * q.shape[1] * LANES,
                           bytes_accessed=12_000_000)

    raw = tuple(pltpu.with_memory_space_constraint(x, pltpu.HBM) for x in (q, vel, col, slot, opened))
    er, el = call(edge_kernel, raw[:2], "hh", [shape((NV + 1) * CAX, LANES)] * 2,
                  [pltpu.VMEM((NV, CAX, LANES), f32)] * 2 + [pltpu.SemaphoreType.DMA((4,))])
    hl0, hr0 = send(er, ring(1)), send(el, ring(-1))
    got = call(functools.partial(first_kernel, n_az, n_out), raw, "hhhhh",
               [row] * n_out + [whole, shape(*vel.shape), row, row],
               [pltpu.SMEM(col.shape, jnp.int32)] * 3 + [pltpu.SemaphoreType.DMA((4 + NV // 2,))])
    outs, (qv, velv, s0, own0) = got[:n_out], got[n_out:]
    s0r = send(s0, swap)
    late = [send(outs[k], spread(k)) for k in range(2, n_out)]
    ra = [send(outs[0], spread(0))]
    after, hl0, hr0 = lax.optimization_barrier((outs[1], hl0, hr0))
    ra.append(send(after, spread(1)))
    matrix = pltpu.VMEM((NV * CAX, 3 * NV * CAX), f32)
    part, = call(inside_one_kernel, (qv, velv) + react, "vvssss", [whole], [matrix], cost=work)

    got = call(functools.partial(border_one_kernel, n_az, n_ax, n_out),
               (s0r, *late, *ra, hl0, hr0, part, qv, velv, sup, own0, col, slot, opened),
               "v" * (n_out + 8) + "s" * 3, [row] * n_out + [whole, row, row, row],
               [pltpu.VMEM((rows, LANES), f32)] * 2)
    outs, (q1, tile0, s1, own1) = got[:n_out], got[n_out:]
    down = [((i, j, 1), (i, j - 1, 1)) for i, j in every if j % 2 == 1]
    across = [((i, 2, 1), (i, 0, 0)) for i in range(n_az)]
    inner = [((i, j, 0), (i, mate(1, j), 0)) for i, j in every if 0 < j < n_ax - 1]
    rb = [send(outs[k], [(x, y) for x, y in spread(k) if k == 0 or x[2] == 1]) for k in range(n_out)]
    down0 = send(tile0, down)

    tile1, step, core = call(functools.partial(tree_kernel, n_out), (tile0, down0, own1, s1, outs[1]) + tuple(rb),
                             "v" * (5 + n_out), [row] * 3)
    step_in = send(step, down + across + inner)
    core_in = send(core, swap)
    part, er, el = call(inside_two_kernel, (qv, q1, velv) + react, "vvvssss", [whole, edge, edge], [matrix], cost=work)

    dq, pair1, core2, er, el = call(inlet_kernel, (er, el, tile1, step_in, core_in), "vvvvv", [row] * 3 + [edge] * 2)
    far1 = send(pair1, across)
    core2_in = send(core2, swap)
    hl1, hr1 = send(er, ring(1)), send(el, ring(-1))
    out, = call(functools.partial(last_kernel, n_ax),
                (part, qv, q1, velv, core_in, sup, rb[0], step_in, dq, core2_in, far1, hl1, hr1, hl0, hr0) + react,
                "v" * 15 + "s" * 4, [whole],
                [pltpu.VMEM(q.shape, f32)] + [pltpu.VMEM((rows, LANES), f32)] * 3 + [pltpu.SemaphoreType.DMA((NV,))],
                to=pltpu.HBM)
    return out.reshape(NV, n, CAX, LANES).transpose(0, 2, 1, 3).reshape(1, NV, CAX, size)


def solution(mesh):
    return jax.shard_map(
        functools.partial(local, mesh.shape["az"], mesh.shape["ax"]),
        mesh=mesh,
        in_specs=(
            P("pl", None, "ax", "az"),
            P("pl", None, "ax", "az"),
            P(None, "ax", "az"),
            P(),
            P(),
            P(),
            P(),
            P(("az", "ax"), None),
            P(("az", "ax")),
            P(("az", "ax")),
        ),
        out_specs=P("pl", None, "ax", "az"),
        check_vma=False,
    )
```

```python
import functools

import jax
import jax.numpy as jnp
from jax import lax
from jax.experimental import pallas as pl
from jax.experimental.pallas import tpu as pltpu
from jax.sharding import PartitionSpec as P

NV = 10
NS = 9
LANES = 128
CAX = 8
HALF = 64
AXES = ("az", "ax", "pl")
NJ = 4
EXT = 16
LOG2E = 1.4426950408889634
LIMIT = 16 * 1024 * 1024

f32 = jnp.float32


def roles():
    return lax.axis_index("az"), lax.axis_index("ax"), lax.axis_index("pl")


def low_half():
    return lax.broadcasted_iota(jnp.int32, (CAX, LANES), 1) < HALF


def block(q_ref, v, b):
    return q_ref[v, pl.ds(CAX * CAX * b + CAX - 1, CAX, stride=CAX), :]


def axial_rows(q_ref, vel_ref, first_mate, second_mate):
    _, ax, _ = roles()
    n = q_ref.shape[1] // CAX

    def up(v, at, size):
        rows = pl.ds(CAX * at + CAX - 1, size, stride=CAX)
        return (1.0 + vel_ref[1, rows, :]) * q_ref[v, rows, :]

    def down(v, at, size):
        rows = pl.ds(CAX * at, size, stride=CAX)
        return (1.0 - vel_ref[1, rows, :]) * q_ref[v, rows, :]

    def put(refs, value):
        size = NV * n // len(refs)
        step = min(n, size) if size % n == 0 or n % size == 0 else n // 2
        for k in range(NV * n // step):
            at = k * step
            refs[at // size][pl.ds(at % size, step), :] = value(at // n, at % n, step)

    @pl.when(ax % 2 == 0)
    def _():
        put(first_mate, up)
        put(second_mate, down)

    @pl.when(ax % 2 == 1)
    def _():
        put(first_mate, down)
        put(second_mate, up)


def edges(q_ref, er_ref, el_ref):
    n = q_ref.shape[1] // CAX
    for v in range(NV):
        el_ref[pl.ds(v * CAX, CAX), :] = q_ref[v, pl.ds(0, CAX), :]
        er_ref[pl.ds(v * CAX, CAX), :] = q_ref[v, pl.ds((n - 1) * CAX, CAX), :]


def first_kernel(n_az, n_out, q_any, vel_any, col_any, slot_any, open_any, *outs):
    out_refs, rest = outs[:n_out], outs[n_out:]
    q_ref, vel_ref, s_ref, own_ref, er_ref, el_ref, col_ref, slot_ref, open_ref, sems = rest
    pairs = [(vel_any, vel_ref), (col_any, col_ref), (slot_any, slot_ref), (open_any, open_ref)]
    pairs += [(q_any.at[pl.ds(v, 2)], q_ref.at[pl.ds(v, 2)]) for v in range(0, NV, 2)]
    copies = [pltpu.make_async_copy(x, y, sems.at[k]) for k, (x, y) in enumerate(pairs)]
    for copy in copies:
        copy.start()
    for copy in copies:
        copy.wait()
    az, _, plen = roles()
    n = q_ref.shape[1] // CAX
    rows = NV * n
    edges(q_ref, er_ref, el_ref)
    el_ref[pl.ds(NV * CAX, CAX), :] = vel_ref[0, pl.ds(0, CAX), :]
    er_ref[pl.ds(NV * CAX, CAX), :] = vel_ref[0, pl.ds((n - 1) * CAX, CAX), :]
    for v in range(NV):
        s_ref[pl.ds(v * n, n), :] = q_ref[v, pl.ds(0, n, stride=CAX), :]

    @pl.when(plen == 0)
    def _():
        axial_rows(q_ref, vel_ref, out_refs[:1], out_refs[1:2])

    @pl.when(plen == 1)
    def _():
        sub = lax.broadcasted_iota(jnp.int32, (CAX, LANES), 0)
        left = lax.broadcasted_iota(jnp.int32, (1, LANES), 1) < HALF
        blocks = n // CAX
        for shift, ref in enumerate((own_ref,) + tuple(out_refs)):
            ref[pl.ds(0, rows + EXT), :] = jnp.zeros((rows + EXT, LANES), f32)
            table = jnp.full((CAX, LANES), -1.0, f32)
            used = jnp.int32(0)
            for b in range(blocks):
                tile, opened = slot_ref[b], open_ref[b] != 0
                ahead = (col_ref[b] - az - shift + 2 * n_az) % n_az
                here = jnp.logical_and(ahead == 0, opened)
                table = jnp.where(sub == jnp.where(here, used, CAX), tile.astype(f32), table)
                used = used + here.astype(jnp.int32)

                @pl.when(here)
                def _(ref=ref, b=b, tile=tile):
                    for v in range(NV):
                        at = pl.ds(pl.multiple_of(v * n + tile * CAX, CAX), CAX)
                        ref[at, :] += block(q_ref, v, b)

                @pl.when(jnp.logical_and(opened, jnp.logical_and(ahead == 1, tile == 0)))
                def _(ref=ref, b=b):
                    for v in range(NV):
                        cell = q_ref[v, pl.ds(CAX * CAX * b + CAX - 1, 1), :]
                        ref[pl.ds(rows + v, 1), :] += jnp.where(left, cell, 0.0)

                @pl.when(jnp.logical_and(opened, jnp.logical_and(ahead == n_az - 1, tile == blocks - 1)))
                def _(ref=ref, b=b):
                    for v in range(NV):
                        cell = q_ref[v, pl.ds(CAX * CAX * (b + 1) - 1, 1), :]
                        ref[pl.ds(rows + v, 1), :] += jnp.where(left, 0.0, cell)

            if shift > 0:
                ref[pl.ds(rows + EXT, CAX), :] = table


def source(state, mix_ref, pre_ref, act_ref, heat_ref):
    inv = 1.0 / jnp.maximum(state[NS], 0.5)
    rates = [pre_ref[k] * jnp.exp(-act_ref[k] * inv) * jnp.maximum(state[k], 0.0) for k in range(NS)]
    out = []
    for v in range(NV):
        acc = None
        for k in range(NS):
            term = (mix_ref[v, k] if v < NS else heat_ref[k]) * rates[k]
            acc = term if acc is None else acc + term
        out.append(0.2 * acc)
    return out


def fill_ghosts(state_ref, lo_ref, hi_ref, ra_refs, rb_ref, high_ref, supply_ref, n_ax):
    _, ax, plen = roles()
    n = state_ref.shape[1] // CAX
    even = ax % 2 == 0
    odd = jnp.logical_not(even)
    cham = plen == 0

    def put(ref):
        size = ref.shape[0] // len(ra_refs)
        for k, part in enumerate(ra_refs):
            ref[pl.ds(k * size, size), :] = part[pl.ds(0, size), :]

    @pl.when(plen == 1)
    def _():
        lo_ref[...] = supply_ref[...]
        hi_ref[...] = high_ref[pl.ds(0, hi_ref.shape[0]), :]

    @pl.when(jnp.logical_and(cham, even))
    def _():
        put(hi_ref)

    @pl.when(jnp.logical_and(cham, odd))
    def _():
        put(lo_ref)

    @pl.when(jnp.logical_and(cham, ax == 0))
    def _():
        lo_ref[...] = jnp.zeros_like(lo_ref)

    @pl.when(jnp.logical_and(cham, jnp.logical_and(even, ax > 0)))
    def _():
        lo_ref[...] = rb_ref[pl.ds(0, lo_ref.shape[0]), :]

    @pl.when(jnp.logical_and(cham, jnp.logical_and(odd, ax < n_ax - 1)))
    def _():
        hi_ref[...] = rb_ref[pl.ds(0, hi_ref.shape[0]), :]

    @pl.when(jnp.logical_and(cham, ax == n_ax - 1))
    def _():
        for v in range(NV):
            hi_ref[pl.ds(v * n, n), :] = state_ref[v, pl.ds(CAX - 1, n, stride=CAX), :]


def add_border(v, dst_ref, scale, lo_ref, hi_ref, hl_ref, hr_ref, ul_ref, ur_ref):
    n = dst_ref.shape[1] // CAX
    left = low_half()
    dst_ref[v, pl.ds(0, n, stride=CAX), :] += scale * lo_ref[pl.ds(v * n, n), :]
    dst_ref[v, pl.ds(CAX - 1, n, stride=CAX), :] += scale * hi_ref[pl.ds(v * n, n), :]
    al = scale + scale * pltpu.roll(ul_ref[...], HALF, 1)
    ar = scale - scale * pltpu.roll(ur_ref[...], HALF, 1)
    head = pltpu.roll(hl_ref[pl.ds(v * CAX, CAX), :], HALF, 1)
    tail = pltpu.roll(hr_ref[pl.ds(v * CAX, CAX), :], HALF, 1)
    dst_ref[v, pl.ds(0, CAX), :] += jnp.where(left, al * head, 0.0)
    dst_ref[v, pl.ds((n - 1) * CAX, CAX), :] += jnp.where(left, 0.0, ar * tail)


def mixing(a_ref, scale, mix_ref, pre_ref, heat_ref):
    width = NV * CAX
    col = lax.broadcasted_iota(jnp.int32, (CAX, 3 * width), 1)
    row = lax.broadcasted_iota(jnp.int32, (CAX, 3 * width), 0)
    inner = col % width
    species, lane = inner // CAX, inner % CAX
    for v in range(NV):
        block = jnp.zeros((CAX, 3 * width), f32)
        for k in range(NS):
            value = (0.2 * scale) * pre_ref[k] * (mix_ref[v, k] if v < NS else heat_ref[k])
            block = jnp.where(species == k, value, block)
        block = jnp.where(lane == row, block, 0.0)
        high = block.astype(jnp.bfloat16).astype(f32)
        a_ref[pl.ds(v * CAX, CAX), :] = jnp.where(col // width == 1, block - high, high)


def interior(q_ref, vel_ref, a_ref, scale, mix_ref, pre_ref, act_ref, heat_ref, finish):
    n = q_ref.shape[1] // CAX
    left = low_half()
    sub = lax.broadcasted_iota(jnp.int32, (CAX, LANES), 0)
    bottom, top = sub == 0, sub == CAX - 1
    mixing(a_ref, scale, mix_ref, pre_ref, heat_ref)
    a = a_ref[...].astype(jnp.bfloat16)
    power = [act_ref[k] * (-LOG2E) for k in range(NS)]
    c = 0.1 * scale

    def reg(ref, v, j):
        return ref[v, pl.ds(pl.multiple_of(j * CAX, CAX), CAX), :]

    def column(ref, v, j0):
        regs = [reg(ref, v, j0 + d) for d in range(NJ)]
        before = jnp.where(j0 == 0, 0.0, reg(ref, v, jnp.maximum(j0 - 1, 0)))
        after = jnp.where(j0 + NJ == n, 0.0, reg(ref, v, jnp.minimum(j0 + NJ, n - 1)))
        turned = [pltpu.roll(x, HALF, 1) for x in [before] + regs + [after]]
        lefts = [jnp.where(left, turned[d], turned[d + 1]) for d in range(NJ)]
        rights = [jnp.where(left, turned[d + 1], turned[d + 2]) for d in range(NJ)]
        return regs, lefts, rights

    def body(step, carry):
        j0 = step * NJ
        rates = []
        for d in range(NJ):
            inv = 1.0 / jnp.maximum(reg(q_ref, NS, j0 + d), 0.5)
            some = [jnp.exp2(power[k] * inv) * jnp.maximum(reg(q_ref, k, j0 + d), 0.0) for k in range(NS)]
            rates.append(jnp.concatenate(some + [jnp.zeros((CAX, LANES), f32)], axis=0))
        rate = jnp.concatenate(rates, axis=1)
        high = rate.astype(jnp.bfloat16)
        low = (rate - high.astype(f32)).astype(jnp.bfloat16)
        src = jnp.dot(a, jnp.concatenate([high, high, low], axis=0), preferred_element_type=f32)
        _, u_left, u_right = column(vel_ref, 0, j0)
        w = [reg(vel_ref, 1, j0 + d) for d in range(NJ)]
        al = [c + c * x for x in u_left]
        ar = [c - c * x for x in u_right]
        wu = [jnp.where(bottom, 0.0, c + c * pltpu.roll(x, 1, 0)) for x in w]
        wd = [jnp.where(top, 0.0, c - c * pltpu.roll(x, CAX - 1, 0)) for x in w]
        for v in range(NV):
            regs, lefts, rights = column(q_ref, v, j0)
            for d in range(NJ):
                vertical = wu[d] * pltpu.roll(regs[d], 1, 0) + wd[d] * pltpu.roll(regs[d], CAX - 1, 0)
                new = (0.6 * scale) * regs[d] + src[v * CAX:(v + 1) * CAX, d * LANES:(d + 1) * LANES]
                finish(j0 + d, v, new + (al[d] * lefts[d] + ar[d] * rights[d]) + vertical)
        return carry

    lax.fori_loop(0, n // NJ, body, 0)


def inside_one_kernel(q_ref, vel_ref, mix_ref, pre_ref, act_ref, heat_ref, out_ref, a_ref):
    def finish(j, v, new):
        out_ref[v, pl.ds(pl.multiple_of(j * CAX, CAX), CAX), :] = new

    interior(q_ref, vel_ref, a_ref, 1.0, mix_ref, pre_ref, act_ref, heat_ref, finish)


def inside_two_kernel(q_ref, q1_ref, vel_ref, mix_ref, pre_ref, act_ref, heat_ref, out_ref, a_ref):
    def finish(j, v, new):
        at = pl.ds(pl.multiple_of(j * CAX, CAX), CAX)
        out_ref[v, at, :] = 0.5 * q_ref[v, at, :] + new

    interior(q1_ref, vel_ref, a_ref, 0.5, mix_ref, pre_ref, act_ref, heat_ref, finish)


def border_one_kernel(n_az, n_ax, n_out, cap, s_in_ref, *rest):
    got, rest = rest[:n_out], rest[n_out:]
    hl_ref, hr_ref, part_ref, q_ref, vel_ref, supply_ref, own_in_ref, col_ref, slot_ref, open_ref = rest[:10]
    out_refs, rest = rest[10:10 + n_out], rest[10 + n_out:]
    q1_ref, tile_ref, s_ref, z_ref, own_ref, er_ref, el_ref, lo_ref, hi_ref = rest
    az, _, plen = roles()
    n = q_ref.shape[1] // CAX
    rows = NV * n
    fill_ghosts(q_ref, lo_ref, hi_ref, got[:1], got[1], s_in_ref, supply_ref, n_ax)
    for v in range(NV):
        q1_ref[v] = part_ref[v]
        add_border(v, q1_ref, 0.1, lo_ref, hi_ref, hl_ref, hr_ref,
                   hl_ref.at[pl.ds(NV * CAX, CAX)], hr_ref.at[pl.ds(NV * CAX, CAX)])
    edges(q1_ref, er_ref, el_ref)

    @pl.when(plen == 0)
    def _():
        tile_ref[...] = jnp.zeros_like(tile_ref)
        for v in range(NV):
            s_ref[pl.ds(v * n, n), :] = q1_ref[v, pl.ds(0, n, stride=CAX), :]
        axial_rows(q1_ref, vel_ref, out_refs[:CAX // cap], (z_ref,))

    @pl.when(plen == 1)
    def _():
        total = own_in_ref[...]
        for ref in got:
            total = total + ref[pl.ds(0, rows + EXT), :]
        tile_ref[...] = total
        own_ref[...] = jnp.zeros_like(own_ref)
        used = [jnp.int32(0)] * n_out
        for b in range(n // CAX):
            tile = slot_ref[b]
            ahead = (col_ref[b] - az + n_az) % n_az
            opened = open_ref[b] != 0

            @pl.when(jnp.logical_and(opened, ahead == 0))
            def _(b=b, tile=tile):
                for v in range(NV):
                    at = pl.ds(pl.multiple_of(v * n + tile * CAX, CAX), CAX)
                    own_ref[at, :] += block(q1_ref, v, b)

            for k, ref in enumerate(out_refs):
                here = jnp.logical_and(opened, ahead == k + 1)

                @pl.when(here)
                def _(ref=ref, b=b, slot=used[k]):
                    for v in range(NV):
                        at = pl.ds(pl.multiple_of((slot * NV + v) * CAX, CAX), CAX)
                        ref[at, :] = block(q1_ref, v, b)

                used[k] = used[k] + here.astype(jnp.int32)


def tree_kernel(n_out, cap, tile0_ref, down0_ref, own_ref, s1_ref, z_ref, *rest):
    got, tables, (tile_ref, step_ref, core_ref) = rest[:n_out], rest[n_out:2 * n_out], rest[2 * n_out:]
    _, ax, plen = roles()
    rows = own_ref.shape[0]
    n = rows // NV

    @pl.when(plen == 0)
    def _():
        core_ref[pl.ds(0, rows), :] = s1_ref[...]
        step_ref[pl.ds(0, rows), :] = z_ref[...]
        core_ref[pl.ds(rows, EXT), :] = jnp.zeros((EXT, LANES), f32)
        step_ref[pl.ds(rows, EXT), :] = jnp.zeros((EXT, LANES), f32)
        tile_ref[...] = jnp.zeros_like(tile_ref)

    @pl.when(plen == 1)
    def _():
        core_ref[...] = tile0_ref[...] + down0_ref[...]
        slots = [(k, m) for k in range(n_out) for m in range(cap)]
        named = [jnp.broadcast_to(tables[k][pl.ds(rows + EXT + m, 1), :], (CAX, LANES)) for k, m in slots]
        for v in range(NV):
            blocks = [got[k][pl.ds((m * NV + v) * CAX, CAX), :] for k, m in slots]
            for t in range(n // CAX):
                at = pl.ds(v * n + t * CAX, CAX)
                total = own_ref[at, :]
                for name, value in zip(named, blocks):
                    total = total + jnp.where(name == t, value, 0.0)
                tile_ref[at, :] = total

        @pl.when(ax % 2 == 1)
        def _():
            step_ref[pl.ds(0, rows), :] = tile_ref[...]
            step_ref[pl.ds(rows, EXT), :] = jnp.zeros((EXT, LANES), f32)

        @pl.when(ax % 2 == 0)
        def _():
            step_ref[...] = core_ref[...]


def inlet_kernel(tile_ref, step_ref, core_ref, dq_ref, pair_ref, core_out_ref):
    _, ax, plen = roles()
    rows = tile_ref.shape[0]

    @pl.when(plen == 1)
    def _():
        pair = tile_ref[...] + step_ref[pl.ds(0, rows), :]
        pair_ref[...] = pair
        core_out_ref[...] = pair
        dq_ref[...] = jnp.zeros_like(dq_ref)

    @pl.when(jnp.logical_and(plen == 0, ax > 0))
    def _():
        pair_ref[...] = jnp.zeros_like(pair_ref)
        core_out_ref[...] = jnp.zeros_like(core_out_ref)
        dq_ref[...] = jnp.zeros_like(dq_ref)

    @pl.when(jnp.logical_and(plen == 0, ax == 0))
    def _():
        pair_ref[...] = jnp.zeros_like(pair_ref)
        dq_ref[...] = 0.1 * (step_ref[...] + core_ref[...])
        core_out_ref[...] = dq_ref[pl.ds(0, rows), :]


def border_two_kernel(n_ax, n_z, part_ref, q_ref, q1_ref, vel_ref, core_ref, supply_ref, step_ref, dq_ref, hl_ref, hr_ref,
                      hl0_ref, hr0_ref, *rest):
    ra_refs, rest = rest[:n_z], rest[n_z:]
    mix_ref, pre_ref, act_ref, heat_ref, out_any, keep_ref, out_ref, lo_ref, hi_ref, sems = rest
    n = out_ref.shape[1] // CAX
    rows = NV * n
    _, ax, plen = roles()
    inlet_side = jnp.logical_and(ax == 0, plen == 0)
    ul_ref, ur_ref = hl0_ref.at[pl.ds(NV * CAX, CAX)], hr0_ref.at[pl.ds(NV * CAX, CAX)]
    fill_ghosts(q1_ref, lo_ref, hi_ref, ra_refs, step_ref, core_ref, supply_ref, n_ax)

    @pl.when(inlet_side)
    def _():
        first = lax.broadcasted_iota(jnp.int32, (n, LANES), 0) == 0
        last = lax.broadcasted_iota(jnp.int32, (n, LANES), 0) == n - 1
        left = lax.broadcasted_iota(jnp.int32, (n, LANES), 1) < HALF

        def neighbours(x, head, tail):
            before = jnp.where(first, head, pltpu.roll(x, 1, 0))
            after = jnp.where(last, tail, pltpu.roll(x, n - 1, 0))
            mid = pltpu.roll(x, HALF, 1)
            return (jnp.where(left, pltpu.roll(before, HALF, 1), mid),
                    jnp.where(left, mid, pltpu.roll(after, HALF, 1)))

        u = vel_ref[0, pl.ds(0, n, stride=CAX), :]
        w_next = vel_ref[1, pl.ds(1, n, stride=CAX), :]
        u_left, u_right = neighbours(u, ul_ref[pl.ds(0, 1), :], ur_ref[pl.ds(0, 1), :])
        state = [q1_ref[v, pl.ds(0, n, stride=CAX), :] + dq_ref[pl.ds(v * n, n), :] for v in range(NV)]
        src = source(state, mix_ref, pre_ref, act_ref, heat_ref)
        for v in range(NV):
            beside = dq_ref[pl.ds(rows + v, 1), :]
            q_left, q_right = neighbours(state[v], hl_ref[pl.ds(v * CAX, 1), :] + beside, hr_ref[pl.ds(v * CAX, 1), :] + beside)
            above = (1.0 - w_next) * q1_ref[v, pl.ds(1, n, stride=CAX), :]
            new = 0.6 * state[v] + 0.1 * ((1.0 + u_left) * q_left + (1.0 - u_right) * q_right + above) + src[v]
            keep_ref[pl.ds(v * n, n), :] = 0.5 * q_ref[v, pl.ds(0, n, stride=CAX), :] + 0.5 * new

    copies = []
    for v in range(NV):
        out_ref[v] = part_ref[v]
        add_border(v, out_ref, 0.05, lo_ref, hi_ref, hl_ref, hr_ref, ul_ref, ur_ref)

        @pl.when(inlet_side)
        def _(v=v):
            w = vel_ref[1, pl.ds(0, n, stride=CAX), :]
            out_ref[v, pl.ds(1, n, stride=CAX), :] += 0.05 * ((1.0 + w) * dq_ref[pl.ds(v * n, n), :])

        @pl.when(plen == 1)
        def _(v=v):
            keep_ref[pl.ds(v * n, n), :] = out_ref[v, pl.ds(CAX - 1, n, stride=CAX), :]

        copies.append(pltpu.make_async_copy(out_ref.at[v], out_any.at[v], sems.at[v]))
        copies[-1].start()
    for copy in copies:
        copy.wait()


def last_kernel(in_any, keep_ref, core_ref, far_ref, out_any, row_ref, sem):
    _, ax, plen = roles()
    n = keep_ref.shape[0] // NV

    def patch(at, value):
        for v in range(NV):
            row_ref[v, :, 0, :] = value(pl.ds(v * n, n))
        copy = pltpu.make_async_copy(row_ref, out_any.at[:, :, pl.ds(at, 1), :], sem)
        copy.start()
        copy.wait()

    @pl.when(jnp.logical_and(ax == 0, plen == 0))
    def _():
        patch(0, lambda at: keep_ref[at, :] + 0.05 * (core_ref[at, :] + far_ref[at, :]))

    @pl.when(jnp.logical_and(ax == 0, plen == 1))
    def _():
        patch(CAX - 1, lambda at: keep_ref[at, :] + 0.05 * core_ref[at, :])


def shape(*dims):
    return jax.ShapeDtypeStruct(dims, f32)


SPACES = {"s": pltpu.SMEM, "v": pltpu.VMEM, "h": pltpu.HBM}


def call(kernel, inputs, kinds, outs, scratch=(), cost=None, to=None, aliases=None):
    return pl.pallas_call(
        kernel,
        in_specs=[pl.BlockSpec(memory_space=SPACES[k]) for k in kinds],
        out_specs=[pl.BlockSpec(memory_space=SPACES[k]) for k in (to or "v" * len(outs))],
        out_shape=outs,
        scratch_shapes=list(scratch),
        cost_estimate=cost,
        input_output_aliases=aliases or {},
        compiler_params=pltpu.CompilerParams(vmem_limit_bytes=LIMIT),
    )(*inputs)


def local(n_az, n_ax, cells, speeds, supply, mix, prefactor, activation, heat, inj_column, inj_slot, inj_open):
    size = cells.shape[-1]
    n = size // LANES
    rows = NV * n

    def view(array):
        k = array.shape[0]
        return array.reshape(k, CAX, n, LANES).transpose(0, 2, 1, 3).reshape(k, CAX * n, LANES)

    def number(i, j, p):
        return (i * n_ax + j) * 2 + p

    every = [(i, j) for i in range(n_az) for j in range(n_ax)]

    def send(x, route):
        return lax.ppermute(x, AXES, [(number(*a), number(*b)) for a, b in route])

    def ring(step):
        return [((i, j, p), ((i + step) % n_az, j, p)) for i, j in every for p in (0, 1)]

    swap = [((i, j, p), (i, j, 1 - p)) for i, j in every for p in (0, 1)]
    n_out = n_az - 1

    def mate(k, j):
        return j ^ 1 if k == 0 else ((j + 1) ^ 1) - 1 if 0 < j < n_ax - 1 else n_ax - 1 - j

    cap = CAX // 4 if n_az > 4 else CAX // 2
    pieces = CAX // cap

    def dense(k):
        out = [((i, j, 1), ((i + k + 1) % n_az, j, 1)) for i, j in every]
        if k < 2:
            out += [((i, j, 0), (i, mate(k, j), 0)) for i, j in every]
        return out

    def compact(k):
        out = [((i, j, 1), ((i + k + 1) % n_az, j, 1)) for i, j in every]
        if k < pieces:
            return out + [((i, j, 0), (i, mate(0, j), 0)) for i, j in every]
        return out + [((i, j, 0), ((i + k + 1) % n_az, j, 0)) for i, j in every]

    q, vel = view(cells[0]), view(speeds[0])
    sup = supply.reshape(rows, LANES)
    col, slot, opened = inj_column.reshape(-1), inj_slot, inj_open
    react = (mix, prefactor, activation, heat)
    row, edge = shape(rows, LANES), shape(NV * CAX, LANES)

    whole = shape(*q.shape)
    work = pl.CostEstimate(flops=300 * q.shape[1] * LANES, transcendentals=20 * q.shape[1] * LANES,
                           bytes_accessed=12_000_000)

    raw = tuple(pltpu.with_memory_space_constraint(x, pltpu.HBM) for x in (q, vel, col, slot, opened))
    wide, edge0 = shape(rows + EXT, LANES), shape((NV + 1) * CAX, LANES)
    got = call(functools.partial(first_kernel, n_az, n_out), raw, "hhhhh",
               [shape(rows + EXT + CAX, LANES)] * n_out + [whole, shape(*vel.shape), row, wide, edge0, edge0],
               [pltpu.SMEM(col.shape, jnp.int32)] * 3 + [pltpu.SemaphoreType.DMA((4 + NV // 2,))])
    outs, (qv, velv, s0, own0, er, el) = got[:n_out], got[n_out:]
    ra = [send(x, dense(k)) for k, x in enumerate(outs)]
    s0r = send(s0, swap)
    hl0 = send(er, ring(1))
    el, s0r = lax.optimization_barrier((el, s0r))
    hr0 = send(el, ring(-1))
    matrix = pltpu.VMEM((NV * CAX, 3 * NV * CAX), f32)
    part, = call(inside_one_kernel, (qv, velv) + react, "vvssss", [whole], [matrix], cost=work)

    got = call(functools.partial(border_one_kernel, n_az, n_ax, n_out, cap),
               (s0r, *ra, hl0, hr0, part, qv, velv, sup, own0, col, slot, opened),
               "v" * (n_out + 8) + "s" * 3,
               [shape(cap * NV * CAX, LANES)] * n_out + [whole, wide, row, row, row, edge, edge],
               [pltpu.VMEM((rows, LANES), f32)] * 2)
    outs, (q1, tile0, s1, z1, own1, er, el) = got[:n_out], got[n_out:]
    down = [((i, j, 1), (i, j - 1, 1)) for i, j in every if j % 2 == 1]
    across = [((i, 2, 1), (i, 0, 0)) for i in range(n_az)]
    inner = [((i, j, 0), (i, mate(1, j), 0)) for i, j in every if 0 < j < n_ax - 1]
    rb = [send(x, compact(k)) for k, x in enumerate(outs)]
    down0 = send(tile0, down)

    tile1, step, core = call(functools.partial(tree_kernel, n_out, cap), (tile0, down0, own1, s1, z1, *rb, *ra),
                             "v" * (5 + 2 * n_out), [row, wide, wide])
    step_in = send(step, down + across + inner)
    core_in = send(core, swap)
    hl1, hr1 = send(er, ring(1)), send(el, ring(-1))
    part, = call(inside_two_kernel, (qv, q1, velv) + react, "vvvssss", [whole], [matrix], cost=work)
    part, tile1, hl1, hr1 = lax.optimization_barrier((part, tile1, hl1, hr1))

    dq, pair1, core2 = call(inlet_kernel, (tile1, step_in, core_in), "vvv", [wide, row, row])
    far1 = send(pair1, across)
    core2_in = send(core2, swap)
    out, keep = call(functools.partial(border_two_kernel, n_ax, pieces),
                     (part, qv, q1, velv, core_in, sup, step_in, dq, hl1, hr1, hl0, hr0, *rb[:pieces]) + react,
                     "v" * (12 + pieces) + "s" * 4, [whole, row],
                     [pltpu.VMEM(q.shape, f32)] + [pltpu.VMEM((rows, LANES), f32)] * 2 + [pltpu.SemaphoreType.DMA((NV,))],
                     cost=work, to="hv")
    out, = call(last_kernel, (out.reshape(NV, n, CAX, LANES), keep, core2_in, far1), "hvvv", [shape(NV, n, CAX, LANES)],
                [pltpu.VMEM((NV, n, 1, LANES), f32), pltpu.SemaphoreType.DMA(())], to="h", aliases={0: 0})
    return out.transpose(0, 2, 1, 3).reshape(1, NV, CAX, size)


def solution(mesh):
    return jax.shard_map(
        functools.partial(local, mesh.shape["az"], mesh.shape["ax"]),
        mesh=mesh,
        in_specs=(
            P("pl", None, "ax", "az"),
            P("pl", None, "ax", "az"),
            P(None, "ax", "az"),
            P(),
            P(),
            P(),
            P(),
            P(("az", "ax"), None),
            P(("az", "ax")),
            P(("az", "ax")),
        ),
        out_specs=P("pl", None, "ax", "az"),
        check_vma=False,
    )
```

```python
import functools

import jax
import jax.numpy as jnp
from jax import lax
from jax.experimental import pallas as pl
from jax.experimental.pallas import tpu as pltpu
from jax.sharding import PartitionSpec as P

NV = 10
NS = 9
LANES = 128
CAX = 8
HALF = 64
AXES = ("az", "ax", "pl")
NJ = 4
EXT = 16
LOG2E = 1.4426950408889634
LIMIT = 16 * 1024 * 1024

f32 = jnp.float32


def roles():
    return lax.axis_index("az"), lax.axis_index("ax"), lax.axis_index("pl")


def low_half():
    return lax.broadcasted_iota(jnp.int32, (CAX, LANES), 1) < HALF


def block(q_ref, v, b):
    return q_ref[v, pl.ds(CAX * CAX * b + CAX - 1, CAX, stride=CAX), :]


def axial_rows(q_ref, vel_ref, first_mate, second_mate):
    _, ax, _ = roles()
    n = q_ref.shape[1] // CAX

    def up(v, at, size):
        rows = pl.ds(CAX * at + CAX - 1, size, stride=CAX)
        return (1.0 + vel_ref[1, rows, :]) * q_ref[v, rows, :]

    def down(v, at, size):
        rows = pl.ds(CAX * at, size, stride=CAX)
        return (1.0 - vel_ref[1, rows, :]) * q_ref[v, rows, :]

    def put(refs, value):
        size = NV * n // len(refs)
        step = min(n, size) if size % n == 0 or n % size == 0 else n // 2
        for k in range(NV * n // step):
            at = k * step
            refs[at // size][pl.ds(at % size, step), :] = value(at // n, at % n, step)

    @pl.when(ax % 2 == 0)
    def _():
        put(first_mate, up)
        put(second_mate, down)

    @pl.when(ax % 2 == 1)
    def _():
        put(first_mate, down)
        put(second_mate, up)


def edges(q_ref, er_ref, el_ref):
    n = q_ref.shape[1] // CAX
    for v in range(NV):
        el_ref[pl.ds(v * CAX, CAX), :] = q_ref[v, pl.ds(0, CAX), :]
        er_ref[pl.ds(v * CAX, CAX), :] = q_ref[v, pl.ds((n - 1) * CAX, CAX), :]


def first_kernel(n_az, n_out, q_any, vel_any, col_any, slot_any, open_any, *outs):
    out_refs, rest = outs[:n_out], outs[n_out:]
    q_ref, vel_ref, s_ref, own_ref, er_ref, el_ref, col_ref, slot_ref, open_ref, sems = rest
    pairs = [(vel_any, vel_ref), (col_any, col_ref), (slot_any, slot_ref), (open_any, open_ref)]
    pairs += [(q_any.at[pl.ds(v, 2)], q_ref.at[pl.ds(v, 2)]) for v in range(0, NV, 2)]
    copies = [pltpu.make_async_copy(x, y, sems.at[k]) for k, (x, y) in enumerate(pairs)]
    for copy in copies:
        copy.start()
    for copy in copies:
        copy.wait()
    az, _, plen = roles()
    n = q_ref.shape[1] // CAX
    rows = NV * n
    edges(q_ref, er_ref, el_ref)
    el_ref[pl.ds(NV * CAX, CAX), :] = vel_ref[0, pl.ds(0, CAX), :]
    er_ref[pl.ds(NV * CAX, CAX), :] = vel_ref[0, pl.ds((n - 1) * CAX, CAX), :]
    for v in range(NV):
        s_ref[pl.ds(v * n, n), :] = q_ref[v, pl.ds(0, n, stride=CAX), :]

    @pl.when(plen == 0)
    def _():
        axial_rows(q_ref, vel_ref, out_refs[:1], out_refs[1:2])

    @pl.when(plen == 1)
    def _():
        sub = lax.broadcasted_iota(jnp.int32, (CAX, LANES), 0)
        left = lax.broadcasted_iota(jnp.int32, (1, LANES), 1) < HALF
        blocks = n // CAX
        for shift, ref in enumerate((own_ref,) + tuple(out_refs)):
            ref[pl.ds(0, rows + EXT), :] = jnp.zeros((rows + EXT, LANES), f32)
            table = jnp.full((CAX, LANES), -1.0, f32)
            used = jnp.int32(0)
            for b in range(blocks):
                tile, opened = slot_ref[b], open_ref[b] != 0
                ahead = (col_ref[b] - az - shift + 2 * n_az) % n_az
                here = jnp.logical_and(ahead == 0, opened)
                table = jnp.where(sub == jnp.where(here, used, CAX), tile.astype(f32), table)
                used = used + here.astype(jnp.int32)

                @pl.when(here)
                def _(ref=ref, b=b, tile=tile):
                    for v in range(NV):
                        at = pl.ds(pl.multiple_of(v * n + tile * CAX, CAX), CAX)
                        ref[at, :] += block(q_ref, v, b)

                @pl.when(jnp.logical_and(opened, jnp.logical_and(ahead == 1, tile == 0)))
                def _(ref=ref, b=b):
                    for v in range(NV):
                        cell = q_ref[v, pl.ds(CAX * CAX * b + CAX - 1, 1), :]
                        ref[pl.ds(rows + v, 1), :] += jnp.where(left, cell, 0.0)

                @pl.when(jnp.logical_and(opened, jnp.logical_and(ahead == n_az - 1, tile == blocks - 1)))
                def _(ref=ref, b=b):
                    for v in range(NV):
                        cell = q_ref[v, pl.ds(CAX * CAX * (b + 1) - 1, 1), :]
                        ref[pl.ds(rows + v, 1), :] += jnp.where(left, 0.0, cell)

            if shift > 0:
                ref[pl.ds(rows + EXT, CAX), :] = table


def source(state, mix_ref, pre_ref, act_ref, heat_ref):
    inv = 1.0 / jnp.maximum(state[NS], 0.5)
    rates = [pre_ref[k] * jnp.exp(-act_ref[k] * inv) * jnp.maximum(state[k], 0.0) for k in range(NS)]
    out = []
    for v in range(NV):
        acc = None
        for k in range(NS):
            term = (mix_ref[v, k] if v < NS else heat_ref[k]) * rates[k]
            acc = term if acc is None else acc + term
        out.append(0.2 * acc)
    return out


def fill_ghosts(state_ref, lo_ref, hi_ref, ra_refs, rb_ref, high_ref, supply_ref, n_ax):
    _, ax, plen = roles()
    n = state_ref.shape[1] // CAX
    even = ax % 2 == 0
    odd = jnp.logical_not(even)
    cham = plen == 0

    def put(ref):
        size = ref.shape[0] // len(ra_refs)
        for k, part in enumerate(ra_refs):
            ref[pl.ds(k * size, size), :] = part[pl.ds(0, size), :]

    @pl.when(plen == 1)
    def _():
        lo_ref[...] = supply_ref[...]
        hi_ref[...] = high_ref[pl.ds(0, hi_ref.shape[0]), :]

    @pl.when(jnp.logical_and(cham, even))
    def _():
        put(hi_ref)

    @pl.when(jnp.logical_and(cham, odd))
    def _():
        put(lo_ref)

    @pl.when(jnp.logical_and(cham, ax == 0))
    def _():
        lo_ref[...] = jnp.zeros_like(lo_ref)

    @pl.when(jnp.logical_and(cham, jnp.logical_and(even, ax > 0)))
    def _():
        lo_ref[...] = rb_ref[pl.ds(0, lo_ref.shape[0]), :]

    @pl.when(jnp.logical_and(cham, jnp.logical_and(odd, ax < n_ax - 1)))
    def _():
        hi_ref[...] = rb_ref[pl.ds(0, hi_ref.shape[0]), :]

    @pl.when(jnp.logical_and(cham, ax == n_ax - 1))
    def _():
        for v in range(NV):
            hi_ref[pl.ds(v * n, n), :] = state_ref[v, pl.ds(CAX - 1, n, stride=CAX), :]


def add_border(v, dst_ref, scale, lo_ref, hi_ref, hl_ref, hr_ref, ul_ref, ur_ref):
    n = dst_ref.shape[1] // CAX
    left = low_half()
    dst_ref[v, pl.ds(0, n, stride=CAX), :] += scale * lo_ref[pl.ds(v * n, n), :]
    dst_ref[v, pl.ds(CAX - 1, n, stride=CAX), :] += scale * hi_ref[pl.ds(v * n, n), :]
    al = scale + scale * pltpu.roll(ul_ref[...], HALF, 1)
    ar = scale - scale * pltpu.roll(ur_ref[...], HALF, 1)
    head = pltpu.roll(hl_ref[pl.ds(v * CAX, CAX), :], HALF, 1)
    tail = pltpu.roll(hr_ref[pl.ds(v * CAX, CAX), :], HALF, 1)
    dst_ref[v, pl.ds(0, CAX), :] += jnp.where(left, al * head, 0.0)
    dst_ref[v, pl.ds((n - 1) * CAX, CAX), :] += jnp.where(left, 0.0, ar * tail)


def mixing(a_ref, scale, mix_ref, pre_ref, heat_ref):
    width = NV * CAX
    col = lax.broadcasted_iota(jnp.int32, (CAX, 3 * width), 1)
    row = lax.broadcasted_iota(jnp.int32, (CAX, 3 * width), 0)
    inner = col % width
    species, lane = inner // CAX, inner % CAX
    for v in range(NV):
        block = jnp.zeros((CAX, 3 * width), f32)
        for k in range(NS):
            value = (0.2 * scale) * pre_ref[k] * (mix_ref[v, k] if v < NS else heat_ref[k])
            block = jnp.where(species == k, value, block)
        block = jnp.where(lane == row, block, 0.0)
        high = block.astype(jnp.bfloat16).astype(f32)
        a_ref[pl.ds(v * CAX, CAX), :] = jnp.where(col // width == 1, block - high, high)


def interior(q_ref, vel_ref, a_ref, scale, mix_ref, pre_ref, act_ref, heat_ref, finish):
    n = q_ref.shape[1] // CAX
    left = low_half()
    sub = lax.broadcasted_iota(jnp.int32, (CAX, LANES), 0)
    bottom, top = sub == 0, sub == CAX - 1
    mixing(a_ref, scale, mix_ref, pre_ref, heat_ref)
    a = a_ref[...].astype(jnp.bfloat16)
    power = [act_ref[k] * (-LOG2E) for k in range(NS)]
    c = 0.1 * scale

    def reg(ref, v, j):
        return ref[v, pl.ds(pl.multiple_of(j * CAX, CAX), CAX), :]

    def column(ref, v, j0):
        regs = [reg(ref, v, j0 + d) for d in range(NJ)]
        before = jnp.where(j0 == 0, 0.0, reg(ref, v, jnp.maximum(j0 - 1, 0)))
        after = jnp.where(j0 + NJ == n, 0.0, reg(ref, v, jnp.minimum(j0 + NJ, n - 1)))
        turned = [pltpu.roll(x, HALF, 1) for x in [before] + regs + [after]]
        lefts = [jnp.where(left, turned[d], turned[d + 1]) for d in range(NJ)]
        rights = [jnp.where(left, turned[d + 1], turned[d + 2]) for d in range(NJ)]
        return regs, lefts, rights

    def body(step, carry):
        j0 = step * NJ
        rates = []
        for d in range(NJ):
            inv = 1.0 / jnp.maximum(reg(q_ref, NS, j0 + d), 0.5)
            some = [jnp.exp2(power[k] * inv) * jnp.maximum(reg(q_ref, k, j0 + d), 0.0) for k in range(NS)]
            rates.append(jnp.concatenate(some + [jnp.zeros((CAX, LANES), f32)], axis=0))
        rate = jnp.concatenate(rates, axis=1)
        high = rate.astype(jnp.bfloat16)
        low = (rate - high.astype(f32)).astype(jnp.bfloat16)
        src = jnp.dot(a, jnp.concatenate([high, high, low], axis=0), preferred_element_type=f32)
        _, u_left, u_right = column(vel_ref, 0, j0)
        w = [reg(vel_ref, 1, j0 + d) for d in range(NJ)]
        al = [c + c * x for x in u_left]
        ar = [c - c * x for x in u_right]
        wu = [jnp.where(bottom, 0.0, c + c * pltpu.roll(x, 1, 0)) for x in w]
        wd = [jnp.where(top, 0.0, c - c * pltpu.roll(x, CAX - 1, 0)) for x in w]
        for v in range(NV):
            regs, lefts, rights = column(q_ref, v, j0)
            for d in range(NJ):
                vertical = wu[d] * pltpu.roll(regs[d], 1, 0) + wd[d] * pltpu.roll(regs[d], CAX - 1, 0)
                new = (0.6 * scale) * regs[d] + src[v * CAX:(v + 1) * CAX, d * LANES:(d + 1) * LANES]
                finish(j0 + d, v, new + (al[d] * lefts[d] + ar[d] * rights[d]) + vertical)
        return carry

    lax.fori_loop(0, n // NJ, body, 0)


def inside_one_kernel(q_ref, vel_ref, mix_ref, pre_ref, act_ref, heat_ref, out_ref, a_ref):
    def finish(j, v, new):
        out_ref[v, pl.ds(pl.multiple_of(j * CAX, CAX), CAX), :] = new

    interior(q_ref, vel_ref, a_ref, 1.0, mix_ref, pre_ref, act_ref, heat_ref, finish)


def inside_two_kernel(q_ref, q1_ref, vel_ref, mix_ref, pre_ref, act_ref, heat_ref, out_ref, a_ref):
    def finish(j, v, new):
        at = pl.ds(pl.multiple_of(j * CAX, CAX), CAX)
        out_ref[v, at, :] = 0.5 * q_ref[v, at, :] + new

    interior(q1_ref, vel_ref, a_ref, 0.5, mix_ref, pre_ref, act_ref, heat_ref, finish)


def border_one_kernel(n_az, n_ax, n_out, cap, s_in_ref, *rest):
    got, rest = rest[:n_out], rest[n_out:]
    hl_ref, hr_ref, part_ref, q_ref, vel_ref, supply_ref, own_in_ref, col_ref, slot_ref, open_ref = rest[:10]
    out_refs, rest = rest[10:10 + n_out], rest[10 + n_out:]
    q1_ref, tile_ref, s_ref, z_ref, own_ref, er_ref, el_ref, lo_ref, hi_ref = rest
    az, _, plen = roles()
    n = q_ref.shape[1] // CAX
    rows = NV * n
    fill_ghosts(q_ref, lo_ref, hi_ref, got[:1], got[1], s_in_ref, supply_ref, n_ax)
    for v in range(NV):
        q1_ref[v] = part_ref[v]
        add_border(v, q1_ref, 0.1, lo_ref, hi_ref, hl_ref, hr_ref,
                   hl_ref.at[pl.ds(NV * CAX, CAX)], hr_ref.at[pl.ds(NV * CAX, CAX)])
    edges(q1_ref, er_ref, el_ref)

    @pl.when(plen == 0)
    def _():
        tile_ref[...] = jnp.zeros_like(tile_ref)
        for v in range(NV):
            s_ref[pl.ds(v * n, n), :] = q1_ref[v, pl.ds(0, n, stride=CAX), :]
        axial_rows(q1_ref, vel_ref, out_refs[:CAX // cap], (z_ref,))

    @pl.when(plen == 1)
    def _():
        total = own_in_ref[...]
        for ref in got:
            total = total + ref[pl.ds(0, rows + EXT), :]
        tile_ref[...] = total
        own_ref[...] = jnp.zeros_like(own_ref)
        used = [jnp.int32(0)] * n_out
        for b in range(n // CAX):
            tile = slot_ref[b]
            ahead = (col_ref[b] - az + n_az) % n_az
            opened = open_ref[b] != 0

            @pl.when(jnp.logical_and(opened, ahead == 0))
            def _(b=b, tile=tile):
                for v in range(NV):
                    at = pl.ds(pl.multiple_of(v * n + tile * CAX, CAX), CAX)
                    own_ref[at, :] += block(q1_ref, v, b)

            for k, ref in enumerate(out_refs):
                here = jnp.logical_and(opened, ahead == k + 1)

                @pl.when(here)
                def _(ref=ref, b=b, slot=used[k]):
                    for v in range(NV):
                        at = pl.ds(pl.multiple_of((slot * NV + v) * CAX, CAX), CAX)
                        ref[at, :] = block(q1_ref, v, b)

                used[k] = used[k] + here.astype(jnp.int32)


def tile_kernel(n_out, cap, own_ref, z_ref, *rest):
    got, tables, (step_ref,) = rest[:n_out], rest[n_out:2 * n_out], rest[2 * n_out:]
    _, _, plen = roles()
    rows = own_ref.shape[0]
    n = rows // NV

    @pl.when(plen == 0)
    def _():
        step_ref[...] = z_ref[...]

    @pl.when(plen == 1)
    def _():
        slots = [(k, m) for k in range(n_out) for m in range(cap)]
        named = [jnp.broadcast_to(tables[k][pl.ds(rows + EXT + m, 1), :], (CAX, LANES)) for k, m in slots]
        for v in range(NV):
            blocks = [got[k][pl.ds((m * NV + v) * CAX, CAX), :] for k, m in slots]
            for t in range(n // CAX):
                at = pl.ds(v * n + t * CAX, CAX)
                total = own_ref[at, :]
                for name, value in zip(named, blocks):
                    total = total + jnp.where(name == t, value, 0.0)
                step_ref[at, :] = total


def pair_kernel(tile_ref, down_ref, s1_ref, core_ref):
    _, _, plen = roles()
    rows = s1_ref.shape[0]

    @pl.when(plen == 0)
    def _():
        core_ref[pl.ds(0, rows), :] = s1_ref[...]
        core_ref[pl.ds(rows, EXT), :] = jnp.zeros((EXT, LANES), f32)

    @pl.when(plen == 1)
    def _():
        core_ref[...] = tile_ref[...] + down_ref[...]


def add_kernel(x_ref, y_ref, out_ref):
    out_ref[...] = x_ref[...] + y_ref[...]


def inlet_kernel(pair_ref, far_ref, core_ref, dq_ref, out_ref):
    _, ax, plen = roles()
    rows = out_ref.shape[0]
    inlet_side = jnp.logical_and(plen == 0, ax == 0)

    @pl.when(inlet_side)
    def _():
        dq_ref[...] = 0.1 * (far_ref[...] + core_ref[...])
        out_ref[...] = dq_ref[pl.ds(0, rows), :]

    @pl.when(jnp.logical_not(inlet_side))
    def _():
        dq_ref[...] = jnp.zeros_like(dq_ref)
        out_ref[...] = pair_ref[...]


def border_two_kernel(n_ax, n_z, part_ref, q_ref, q1_ref, vel_ref, core_ref, supply_ref, step_ref, dq_ref, hl_ref, hr_ref,
                      hl0_ref, hr0_ref, *rest):
    ra_refs, rest = rest[:n_z], rest[n_z:]
    mix_ref, pre_ref, act_ref, heat_ref, out_any, keep_ref, out_ref, lo_ref, hi_ref, sems = rest
    n = out_ref.shape[1] // CAX
    rows = NV * n
    _, ax, plen = roles()
    inlet_side = jnp.logical_and(ax == 0, plen == 0)
    ul_ref, ur_ref = hl0_ref.at[pl.ds(NV * CAX, CAX)], hr0_ref.at[pl.ds(NV * CAX, CAX)]
    fill_ghosts(q1_ref, lo_ref, hi_ref, ra_refs, step_ref, core_ref, supply_ref, n_ax)

    @pl.when(inlet_side)
    def _():
        first = lax.broadcasted_iota(jnp.int32, (n, LANES), 0) == 0
        last = lax.broadcasted_iota(jnp.int32, (n, LANES), 0) == n - 1
        left = lax.broadcasted_iota(jnp.int32, (n, LANES), 1) < HALF

        def neighbours(x, head, tail):
            before = jnp.where(first, head, pltpu.roll(x, 1, 0))
            after = jnp.where(last, tail, pltpu.roll(x, n - 1, 0))
            mid = pltpu.roll(x, HALF, 1)
            return (jnp.where(left, pltpu.roll(before, HALF, 1), mid),
                    jnp.where(left, mid, pltpu.roll(after, HALF, 1)))

        u = vel_ref[0, pl.ds(0, n, stride=CAX), :]
        w_next = vel_ref[1, pl.ds(1, n, stride=CAX), :]
        u_left, u_right = neighbours(u, ul_ref[pl.ds(0, 1), :], ur_ref[pl.ds(0, 1), :])
        state = [q1_ref[v, pl.ds(0, n, stride=CAX), :] + dq_ref[pl.ds(v * n, n), :] for v in range(NV)]
        src = source(state, mix_ref, pre_ref, act_ref, heat_ref)
        for v in range(NV):
            beside = dq_ref[pl.ds(rows + v, 1), :]
            q_left, q_right = neighbours(state[v], hl_ref[pl.ds(v * CAX, 1), :] + beside, hr_ref[pl.ds(v * CAX, 1), :] + beside)
            above = (1.0 - w_next) * q1_ref[v, pl.ds(1, n, stride=CAX), :]
            new = 0.6 * state[v] + 0.1 * ((1.0 + u_left) * q_left + (1.0 - u_right) * q_right + above) + src[v]
            keep_ref[pl.ds(v * n, n), :] = 0.5 * q_ref[v, pl.ds(0, n, stride=CAX), :] + 0.5 * new

    copies = []
    for v in range(NV):
        out_ref[v] = part_ref[v]
        add_border(v, out_ref, 0.05, lo_ref, hi_ref, hl_ref, hr_ref, ul_ref, ur_ref)

        @pl.when(inlet_side)
        def _(v=v):
            w = vel_ref[1, pl.ds(0, n, stride=CAX), :]
            out_ref[v, pl.ds(1, n, stride=CAX), :] += 0.05 * ((1.0 + w) * dq_ref[pl.ds(v * n, n), :])

        @pl.when(plen == 1)
        def _(v=v):
            keep_ref[pl.ds(v * n, n), :] = out_ref[v, pl.ds(CAX - 1, n, stride=CAX), :]

        copies.append(pltpu.make_async_copy(out_ref.at[v], out_any.at[v], sems.at[v]))
        copies[-1].start()
    for copy in copies:
        copy.wait()


def last_kernel(in_any, keep_ref, core_ref, far_ref, out_any, row_ref, sem):
    _, ax, plen = roles()
    n = keep_ref.shape[0] // NV

    def patch(at, value):
        for v in range(NV):
            row_ref[v, :, 0, :] = value(pl.ds(v * n, n))
        copy = pltpu.make_async_copy(row_ref, out_any.at[:, :, pl.ds(at, 1), :], sem)
        copy.start()
        copy.wait()

    @pl.when(jnp.logical_and(ax == 0, plen == 0))
    def _():
        patch(0, lambda at: keep_ref[at, :] + 0.05 * (core_ref[at, :] + far_ref[at, :]))

    @pl.when(jnp.logical_and(ax == 0, plen == 1))
    def _():
        patch(CAX - 1, lambda at: keep_ref[at, :] + 0.05 * core_ref[at, :])


def shape(*dims):
    return jax.ShapeDtypeStruct(dims, f32)


SPACES = {"s": pltpu.SMEM, "v": pltpu.VMEM, "h": pltpu.HBM}


def call(kernel, inputs, kinds, outs, scratch=(), cost=None, to=None, aliases=None):
    return pl.pallas_call(
        kernel,
        in_specs=[pl.BlockSpec(memory_space=SPACES[k]) for k in kinds],
        out_specs=[pl.BlockSpec(memory_space=SPACES[k]) for k in (to or "v" * len(outs))],
        out_shape=outs,
        scratch_shapes=list(scratch),
        cost_estimate=cost,
        input_output_aliases=aliases or {},
        compiler_params=pltpu.CompilerParams(vmem_limit_bytes=LIMIT),
    )(*inputs)


def local(n_az, n_ax, cells, speeds, supply, mix, prefactor, activation, heat, inj_column, inj_slot, inj_open):
    size = cells.shape[-1]
    n = size // LANES
    rows = NV * n

    def view(array):
        k = array.shape[0]
        return array.reshape(k, CAX, n, LANES).transpose(0, 2, 1, 3).reshape(k, CAX * n, LANES)

    def number(i, j, p):
        return (i * n_ax + j) * 2 + p

    every = [(i, j) for i in range(n_az) for j in range(n_ax)]

    def send(x, route):
        return lax.ppermute(x, AXES, [(number(*a), number(*b)) for a, b in route])

    def ring(step):
        return [((i, j, p), ((i + step) % n_az, j, p)) for i, j in every for p in (0, 1)]

    swap = [((i, j, p), (i, j, 1 - p)) for i, j in every for p in (0, 1)]
    n_out = n_az - 1

    def mate(k, j):
        return j ^ 1 if k == 0 else ((j + 1) ^ 1) - 1 if 0 < j < n_ax - 1 else n_ax - 1 - j

    cap = CAX // 4 if n_az > 4 else CAX // 2
    pieces = CAX // cap

    def dense(k):
        out = [((i, j, 1), ((i + k + 1) % n_az, j, 1)) for i, j in every]
        if k < 2:
            out += [((i, j, 0), (i, mate(k, j), 0)) for i, j in every]
        return out

    def compact(k):
        out = [((i, j, 1), ((i + k + 1) % n_az, j, 1)) for i, j in every]
        if k < pieces:
            return out + [((i, j, 0), (i, mate(0, j), 0)) for i, j in every]
        return out + [((i, j, 0), ((i + k + 1) % n_az, j, 0)) for i, j in every]

    q, vel = view(cells[0]), view(speeds[0])
    sup = supply.reshape(rows, LANES)
    col, slot, opened = inj_column.reshape(-1), inj_slot, inj_open
    react = (mix, prefactor, activation, heat)
    row, edge = shape(rows, LANES), shape(NV * CAX, LANES)

    whole = shape(*q.shape)
    work = pl.CostEstimate(flops=300 * q.shape[1] * LANES, transcendentals=20 * q.shape[1] * LANES,
                           bytes_accessed=12_000_000)

    raw = tuple(pltpu.with_memory_space_constraint(x, pltpu.HBM) for x in (q, vel, col, slot, opened))
    wide, edge0 = shape(rows + EXT, LANES), shape((NV + 1) * CAX, LANES)
    got = call(functools.partial(first_kernel, n_az, n_out), raw, "hhhhh",
               [shape(rows + EXT + CAX, LANES)] * n_out + [whole, shape(*vel.shape), row, wide, edge0, edge0],
               [pltpu.SMEM(col.shape, jnp.int32)] * 3 + [pltpu.SemaphoreType.DMA((4 + NV // 2,))])
    outs, (qv, velv, s0, own0, er, el) = got[:n_out], got[n_out:]
    ra = [send(x, dense(k)) for k, x in enumerate(outs)]
    s0r = send(s0, swap)
    hl0 = send(er, ring(1))
    el, s0r = lax.optimization_barrier((el, s0r))
    hr0 = send(el, ring(-1))
    matrix = pltpu.VMEM((NV * CAX, 3 * NV * CAX), f32)
    part, = call(inside_one_kernel, (qv, velv) + react, "vvssss", [whole], [matrix], cost=work)

    got = call(functools.partial(border_one_kernel, n_az, n_ax, n_out, cap),
               (s0r, *ra, hl0, hr0, part, qv, velv, sup, own0, col, slot, opened),
               "v" * (n_out + 8) + "s" * 3,
               [shape(cap * NV * CAX, LANES)] * n_out + [whole, wide, row, row, row, edge, edge],
               [pltpu.VMEM((rows, LANES), f32)] * 2)
    outs, (q1, tile0, s1, z1, own1, er, el) = got[:n_out], got[n_out:]
    down = [((i, j, 1), (i, j - 1, 1)) for i, j in every if j % 2 == 1]
    across = [((i, 2, 1), (i, 0, 0)) for i in range(n_az)]
    inner = [((i, j, 0), (i, mate(1, j), 0)) for i, j in every if 0 < j < n_ax - 1]
    rb = [send(x, compact(k)) for k, x in enumerate(outs)]
    down0 = send(tile0, down)

    step, = call(functools.partial(tile_kernel, n_out, cap), (own1, z1, *rb, *ra), "v" * (2 + 2 * n_out), [row])
    step_in = send(step, down + inner)
    er, el, step = lax.optimization_barrier((er, el, step))
    hl1, hr1 = send(er, ring(1)), send(el, ring(-1))
    core, = call(pair_kernel, (tile0, down0, s1), "vvv", [wide])
    far0 = send(core, across)
    core_in = send(core, swap)
    pair1, = call(add_kernel, (step, step_in), "vv", [row])
    far1 = send(pair1, across)
    q1, pair1 = lax.optimization_barrier((q1, pair1))
    part, = call(inside_two_kernel, (qv, q1, velv) + react, "vvvssss", [whole], [matrix], cost=work)
    part, pair1, hl1, hr1 = lax.optimization_barrier((part, pair1, hl1, hr1))

    dq, core2 = call(inlet_kernel, (pair1, far0, core_in), "vvv", [wide, row])
    core2_in = send(core2, swap)
    out, keep = call(functools.partial(border_two_kernel, n_ax, pieces),
                     (part, qv, q1, velv, core_in, sup, step_in, dq, hl1, hr1, hl0, hr0, *rb[:pieces]) + react,
                     "v" * (12 + pieces) + "s" * 4, [whole, row],
                     [pltpu.VMEM(q.shape, f32)] + [pltpu.VMEM((rows, LANES), f32)] * 2 + [pltpu.SemaphoreType.DMA((NV,))],
                     cost=work, to="hv")
    out, = call(last_kernel, (out.reshape(NV, n, CAX, LANES), keep, core2_in, far1), "hvvv", [shape(NV, n, CAX, LANES)],
                [pltpu.VMEM((NV, n, 1, LANES), f32), pltpu.SemaphoreType.DMA(())], to="h", aliases={0: 0})
    return out.transpose(0, 2, 1, 3).reshape(1, NV, CAX, size)


def solution(mesh):
    return jax.shard_map(
        functools.partial(local, mesh.shape["az"], mesh.shape["ax"]),
        mesh=mesh,
        in_specs=(
            P("pl", None, "ax", "az"),
            P("pl", None, "ax", "az"),
            P(None, "ax", "az"),
            P(),
            P(),
            P(),
            P(),
            P(("az", "ax"), None),
            P(("az", "ax")),
            P(("az", "ax")),
        ),
        out_specs=P("pl", None, "ax", "az"),
        check_vma=False,
    )
```

```python
import functools

import jax
import jax.numpy as jnp
from jax import lax
from jax.experimental import pallas as pl
from jax.experimental.pallas import tpu as pltpu
from jax.sharding import PartitionSpec as P

NV = 10
NS = 9
LANES = 128
CAX = 8
HALF = 64
AXES = ("az", "ax", "pl")
NJ = 8
EXT = 16
LOG2E = 1.4426950408889634
LIMIT = 16 * 1024 * 1024

f32 = jnp.float32


def roles():
    return lax.axis_index("az"), lax.axis_index("ax"), lax.axis_index("pl")


def low_half():
    return lax.broadcasted_iota(jnp.int32, (CAX, LANES), 1) < HALF


def block(q_ref, v, b):
    return q_ref[v, pl.ds(CAX * CAX * b + CAX - 1, CAX, stride=CAX), :]


def axial_rows(q_ref, vel_ref, first_mate, second_mate):
    _, ax, _ = roles()
    n = q_ref.shape[1] // CAX

    def up(v, at, size):
        rows = pl.ds(CAX * at + CAX - 1, size, stride=CAX)
        return (1.0 + vel_ref[1, rows, :]) * q_ref[v, rows, :]

    def down(v, at, size):
        rows = pl.ds(CAX * at, size, stride=CAX)
        return (1.0 - vel_ref[1, rows, :]) * q_ref[v, rows, :]

    def put(refs, value):
        size = NV * n // len(refs)
        step = min(n, size) if size % n == 0 or n % size == 0 else n // 2
        for k in range(NV * n // step):
            at = k * step
            refs[at // size][pl.ds(at % size, step), :] = value(at // n, at % n, step)

    @pl.when(ax % 2 == 0)
    def _():
        put(first_mate, up)
        put(second_mate, down)

    @pl.when(ax % 2 == 1)
    def _():
        put(first_mate, down)
        put(second_mate, up)


def edges(q_ref, er_ref, el_ref):
    n = q_ref.shape[1] // CAX
    for v in range(NV):
        el_ref[pl.ds(v * CAX, CAX), :] = q_ref[v, pl.ds(0, CAX), :]
        er_ref[pl.ds(v * CAX, CAX), :] = q_ref[v, pl.ds((n - 1) * CAX, CAX), :]


def first_kernel(n_az, n_out, q_any, vel_any, col_any, slot_any, open_any, mix_any, pre_any, act_any, heat_any, *outs):
    out_refs, rest = outs[:n_out], outs[n_out:]
    (q_ref, vel_ref, s_ref, own_ref, er_ref, el_ref, a_ref, power_ref,
     col_ref, slot_ref, open_ref, mix_ref, pre_ref, act_ref, heat_ref, sems) = rest
    pairs = [(mix_any, mix_ref), (pre_any, pre_ref), (act_any, act_ref), (heat_any, heat_ref),
             (col_any, col_ref), (slot_any, slot_ref), (open_any, open_ref), (vel_any, vel_ref)]
    small = len(pairs) - 1
    pairs += [(q_any.at[pl.ds(v, 2)], q_ref.at[pl.ds(v, 2)]) for v in range(0, NV, 2)]
    copies = [pltpu.make_async_copy(x, y, sems.at[k]) for k, (x, y) in enumerate(pairs)]
    for copy in copies[small:] + copies[:small]:
        copy.start()
    az, _, plen = roles()
    n = q_ref.shape[1] // CAX
    rows = NV * n

    @pl.when(plen == 1)
    def _():
        for ref in (own_ref,) + tuple(out_refs):
            ref[pl.ds(0, rows + EXT), :] = jnp.zeros((rows + EXT, LANES), f32)

    for copy in copies[:small]:
        copy.wait()
    mixing(a_ref, mix_ref, pre_ref, heat_ref)
    for k in range(NS):
        power_ref[pl.ds(k * CAX, CAX), :] = jnp.full((CAX, LANES), act_ref[k] * (-LOG2E), f32)
    for copy in copies[small:]:
        copy.wait()
    edges(q_ref, er_ref, el_ref)
    el_ref[pl.ds(NV * CAX, CAX), :] = vel_ref[0, pl.ds(0, CAX), :]
    er_ref[pl.ds(NV * CAX, CAX), :] = vel_ref[0, pl.ds((n - 1) * CAX, CAX), :]

    @pl.when(plen == 0)
    def _():
        for v in range(NV):
            s_ref[pl.ds(v * n, n), :] = q_ref[v, pl.ds(0, n, stride=CAX), :]
        axial_rows(q_ref, vel_ref, out_refs[:1], out_refs[1:2])

    @pl.when(plen == 1)
    def _():
        sub = lax.broadcasted_iota(jnp.int32, (CAX, LANES), 0)
        left = lax.broadcasted_iota(jnp.int32, (1, LANES), 1) < HALF
        blocks = n // CAX
        refs = (own_ref,) + tuple(out_refs)
        tables = [jnp.full((CAX, LANES), -1.0, f32)] * n_az
        used = [jnp.int32(0)] * n_az
        for b in range(blocks):
            tile, opened = slot_ref[b], open_ref[b] != 0
            ahead = (col_ref[b] - az + n_az) % n_az
            for shift, ref in enumerate(refs):
                here = jnp.logical_and(ahead == shift, opened)
                tables[shift] = jnp.where(sub == jnp.where(here, used[shift], CAX), tile.astype(f32), tables[shift])
                used[shift] = used[shift] + here.astype(jnp.int32)

                @pl.when(here)
                def _(ref=ref, b=b, tile=tile):
                    for v in range(NV):
                        at = pl.ds(pl.multiple_of(v * n + tile * CAX, CAX), CAX)
                        ref[at, :] += block(q_ref, v, b)

            def beside(end, step, row, keep_left, b=b, tile=tile, opened=opened, ahead=ahead):
                @pl.when(jnp.logical_and(opened, tile == end))
                def _():
                    for shift, ref in enumerate(refs):
                        @pl.when(ahead == (shift + step) % n_az)
                        def _(ref=ref):
                            for v in range(NV):
                                cell = q_ref[v, pl.ds(row, 1), :]
                                cell = jnp.where(left, cell, 0.0) if keep_left else jnp.where(left, 0.0, cell)
                                ref[pl.ds(rows + v, 1), :] += cell

            beside(0, 1, CAX * CAX * b + CAX - 1, True)
            beside(blocks - 1, n_az - 1, CAX * CAX * (b + 1) - 1, False)
        for ref, table in zip(out_refs, tables[1:]):
            ref[pl.ds(rows + EXT, CAX), :] = table


def fill_ghosts(state_ref, lo_ref, hi_ref, ra_refs, rb_ref, high_ref, supply_ref, n_ax):
    _, ax, plen = roles()
    n = state_ref.shape[1] // CAX
    even = ax % 2 == 0
    odd = jnp.logical_not(even)
    cham = plen == 0

    def put(ref):
        size = ref.shape[0] // len(ra_refs)
        for k, part in enumerate(ra_refs):
            ref[pl.ds(k * size, size), :] = part[pl.ds(0, size), :]

    @pl.when(plen == 1)
    def _():
        lo_ref[...] = supply_ref[...]
        hi_ref[...] = high_ref[pl.ds(0, hi_ref.shape[0]), :]

    @pl.when(jnp.logical_and(cham, even))
    def _():
        put(hi_ref)

    @pl.when(jnp.logical_and(cham, odd))
    def _():
        put(lo_ref)

    @pl.when(jnp.logical_and(cham, ax == 0))
    def _():
        lo_ref[...] = jnp.zeros_like(lo_ref)

    @pl.when(jnp.logical_and(cham, jnp.logical_and(even, ax > 0)))
    def _():
        lo_ref[...] = rb_ref[pl.ds(0, lo_ref.shape[0]), :]

    @pl.when(jnp.logical_and(cham, jnp.logical_and(odd, ax < n_ax - 1)))
    def _():
        hi_ref[...] = rb_ref[pl.ds(0, hi_ref.shape[0]), :]

    @pl.when(jnp.logical_and(cham, ax == n_ax - 1))
    def _():
        for v in range(NV):
            hi_ref[pl.ds(v * n, n), :] = state_ref[v, pl.ds(CAX - 1, n, stride=CAX), :]


def add_border(v, dst_ref, scale, lo_ref, hi_ref, hl_ref, hr_ref, ul_ref, ur_ref):
    n = dst_ref.shape[1] // CAX
    left = low_half()
    dst_ref[v, pl.ds(0, n, stride=CAX), :] += scale * lo_ref[pl.ds(v * n, n), :]
    dst_ref[v, pl.ds(CAX - 1, n, stride=CAX), :] += scale * hi_ref[pl.ds(v * n, n), :]
    al = scale + scale * pltpu.roll(ul_ref[...], HALF, 1)
    ar = scale - scale * pltpu.roll(ur_ref[...], HALF, 1)
    head = pltpu.roll(hl_ref[pl.ds(v * CAX, CAX), :], HALF, 1)
    tail = pltpu.roll(hr_ref[pl.ds(v * CAX, CAX), :], HALF, 1)
    dst_ref[v, pl.ds(0, CAX), :] += jnp.where(left, al * head, 0.0)
    dst_ref[v, pl.ds((n - 1) * CAX, CAX), :] += jnp.where(left, 0.0, ar * tail)


def mixing(a_ref, mix_ref, pre_ref, heat_ref):
    width = NV * CAX
    col = lax.broadcasted_iota(jnp.int32, (CAX, 3 * width), 1)
    row = lax.broadcasted_iota(jnp.int32, (CAX, 3 * width), 0)
    inner = col % width
    species, lane = inner // CAX, inner % CAX
    for v in range(NV):
        block = jnp.zeros((CAX, 3 * width), f32)
        for k in range(NS):
            value = 0.2 * pre_ref[k] * (mix_ref[v, k] if v < NS else heat_ref[k])
            block = jnp.where(species == k, value, block)
        block = jnp.where(lane == row, block, 0.0)
        high = block.astype(jnp.bfloat16).astype(f32)
        a_ref[pl.ds(v * CAX, CAX), :] = jnp.where(col // width == 1, block - high, high)


def reactions(states, a, power_ref):
    rates = []
    for state in states:
        inv = 1.0 / jnp.maximum(state[NS], 0.5)
        some = [jnp.exp2(power_ref[pl.ds(k * CAX, CAX), :] * inv) * jnp.maximum(state[k], 0.0) for k in range(NS)]
        rates.append(jnp.concatenate(some + [jnp.zeros((CAX, LANES), f32)], axis=0))
    rate = jnp.concatenate(rates, axis=1)
    high = rate.astype(jnp.bfloat16)
    low = (rate - high.astype(f32)).astype(jnp.bfloat16)
    return jnp.dot(a, jnp.concatenate([high, high, low], axis=0), preferred_element_type=f32)


def interior(q_ref, vel_ref, a_ref, power_ref, scale, finish):
    n = q_ref.shape[1] // CAX
    left = low_half()
    sub = lax.broadcasted_iota(jnp.int32, (CAX, LANES), 0)
    bottom, top = sub == 0, sub == CAX - 1
    a = (scale * a_ref[...]).astype(jnp.bfloat16)
    c = 0.1 * scale

    def reg(ref, v, j):
        return ref[v, pl.ds(pl.multiple_of(j * CAX, CAX), CAX), :]

    def column(ref, v, j0):
        regs = [reg(ref, v, j0 + d) for d in range(NJ)]
        before = jnp.where(j0 == 0, 0.0, reg(ref, v, jnp.maximum(j0 - 1, 0)))
        after = jnp.where(j0 + NJ == n, 0.0, reg(ref, v, jnp.minimum(j0 + NJ, n - 1)))
        turned = [pltpu.roll(x, HALF, 1) for x in [before] + regs + [after]]
        lefts = [jnp.where(left, turned[d], turned[d + 1]) for d in range(NJ)]
        rights = [jnp.where(left, turned[d + 1], turned[d + 2]) for d in range(NJ)]
        return regs, lefts, rights

    def body(step, carry):
        j0 = step * NJ
        src = reactions([[reg(q_ref, v, j0 + d) for v in range(NV)] for d in range(NJ)], a, power_ref)
        _, u_left, u_right = column(vel_ref, 0, j0)
        w = [reg(vel_ref, 1, j0 + d) for d in range(NJ)]
        al = [c + c * x for x in u_left]
        ar = [c - c * x for x in u_right]
        wu = [jnp.where(bottom, 0.0, c + c * pltpu.roll(x, 1, 0)) for x in w]
        wd = [jnp.where(top, 0.0, c - c * pltpu.roll(x, CAX - 1, 0)) for x in w]
        for v in range(NV):
            regs, lefts, rights = column(q_ref, v, j0)
            for d in range(NJ):
                vertical = wu[d] * pltpu.roll(regs[d], 1, 0) + wd[d] * pltpu.roll(regs[d], CAX - 1, 0)
                new = (0.6 * scale) * regs[d] + src[v * CAX:(v + 1) * CAX, d * LANES:(d + 1) * LANES]
                finish(j0 + d, v, new + (al[d] * lefts[d] + ar[d] * rights[d]) + vertical)
        return carry

    lax.fori_loop(0, n // NJ, body, 0)


def inside_one_kernel(q_ref, vel_ref, a_ref, power_ref, out_ref):
    def finish(j, v, new):
        out_ref[v, pl.ds(pl.multiple_of(j * CAX, CAX), CAX), :] = new

    interior(q_ref, vel_ref, a_ref, power_ref, 1.0, finish)


def inside_two_kernel(q_ref, q1_ref, vel_ref, a_ref, power_ref, out_ref):
    def finish(j, v, new):
        at = pl.ds(pl.multiple_of(j * CAX, CAX), CAX)
        out_ref[v, at, :] = 0.5 * q_ref[v, at, :] + new

    interior(q1_ref, vel_ref, a_ref, power_ref, 0.5, finish)


def border_one_kernel(n_az, n_ax, n_out, cap, s_in_ref, *rest):
    got, rest = rest[:n_out], rest[n_out:]
    hl_ref, hr_ref, part_ref, q_ref, vel_ref, supply_ref, own_in_ref, col_any, slot_any, open_any = rest[:10]
    out_refs, rest = rest[10:10 + n_out], rest[10 + n_out:]
    (q1_ref, tile_ref, s_ref, z_ref, own_ref, er_ref, el_ref, lo_ref, hi_ref,
     col_ref, slot_ref, open_ref, sems) = rest
    pairs = [(col_any, col_ref), (slot_any, slot_ref), (open_any, open_ref)]
    copies = [pltpu.make_async_copy(x, y, sems.at[k]) for k, (x, y) in enumerate(pairs)]
    for copy in copies:
        copy.start()
    az, _, plen = roles()
    n = q_ref.shape[1] // CAX
    rows = NV * n
    fill_ghosts(q_ref, lo_ref, hi_ref, got[:1], got[1], s_in_ref, supply_ref, n_ax)
    for v in range(NV):
        q1_ref[v] = part_ref[v]
        add_border(v, q1_ref, 0.1, lo_ref, hi_ref, hl_ref, hr_ref,
                   hl_ref.at[pl.ds(NV * CAX, CAX)], hr_ref.at[pl.ds(NV * CAX, CAX)])
    edges(q1_ref, er_ref, el_ref)
    for copy in copies:
        copy.wait()

    @pl.when(plen == 0)
    def _():
        tile_ref[...] = jnp.zeros_like(tile_ref)
        for v in range(NV):
            s_ref[pl.ds(v * n, n), :] = q1_ref[v, pl.ds(0, n, stride=CAX), :]
        axial_rows(q1_ref, vel_ref, out_refs[:CAX // cap], (z_ref,))

    @pl.when(plen == 1)
    def _():
        total = own_in_ref[...]
        for ref in got:
            total = total + ref[pl.ds(0, rows + EXT), :]
        tile_ref[...] = total
        own_ref[...] = jnp.zeros_like(own_ref)
        used = [jnp.int32(0)] * n_out
        for b in range(n // CAX):
            tile = slot_ref[b]
            ahead = (col_ref[b] - az + n_az) % n_az
            opened = open_ref[b] != 0

            @pl.when(jnp.logical_and(opened, ahead == 0))
            def _(b=b, tile=tile):
                for v in range(NV):
                    at = pl.ds(pl.multiple_of(v * n + tile * CAX, CAX), CAX)
                    own_ref[at, :] += block(q1_ref, v, b)

            for k, ref in enumerate(out_refs):
                here = jnp.logical_and(opened, ahead == k + 1)

                @pl.when(here)
                def _(ref=ref, b=b, slot=used[k]):
                    for v in range(NV):
                        at = pl.ds(pl.multiple_of((slot * NV + v) * CAX, CAX), CAX)
                        ref[at, :] = block(q1_ref, v, b)

                used[k] = used[k] + here.astype(jnp.int32)


def tile_kernel(n_out, cap, own_ref, z_ref, *rest):
    got, tables, (step_ref,) = rest[:n_out], rest[n_out:2 * n_out], rest[2 * n_out:]
    _, _, plen = roles()
    rows = own_ref.shape[0]
    n = rows // NV

    @pl.when(plen == 0)
    def _():
        step_ref[...] = z_ref[...]

    @pl.when(plen == 1)
    def _():
        slots = [(k, m) for k in range(n_out) for m in range(cap)]
        named = [jnp.broadcast_to(tables[k][pl.ds(rows + EXT + m, 1), :], (CAX, LANES)) for k, m in slots]
        for v in range(NV):
            blocks = [got[k][pl.ds((m * NV + v) * CAX, CAX), :] for k, m in slots]
            for t in range(n // CAX):
                at = pl.ds(v * n + t * CAX, CAX)
                total = own_ref[at, :]
                for name, value in zip(named, blocks):
                    total = total + jnp.where(name == t, value, 0.0)
                step_ref[at, :] = total


def pair_kernel(tile_ref, down_ref, s1_ref, core_ref):
    _, _, plen = roles()
    rows = s1_ref.shape[0]

    @pl.when(plen == 0)
    def _():
        core_ref[pl.ds(0, rows), :] = s1_ref[...]
        core_ref[pl.ds(rows, EXT), :] = jnp.zeros((EXT, LANES), f32)

    @pl.when(plen == 1)
    def _():
        core_ref[...] = tile_ref[...] + down_ref[...]


def add_kernel(x_ref, y_ref, out_ref):
    out_ref[...] = x_ref[...] + y_ref[...]


def inlet_kernel(pair_ref, far_ref, core_ref, dq_ref, out_ref):
    _, ax, plen = roles()
    rows = out_ref.shape[0]
    inlet_side = jnp.logical_and(plen == 0, ax == 0)

    @pl.when(inlet_side)
    def _():
        dq_ref[...] = 0.1 * (far_ref[...] + core_ref[...])
        out_ref[...] = dq_ref[pl.ds(0, rows), :]

    @pl.when(jnp.logical_not(inlet_side))
    def _():
        dq_ref[...] = jnp.zeros_like(dq_ref)
        out_ref[...] = pair_ref[...]


def border_two_kernel(n_ax, n_z, part_ref, q_ref, q1_ref, vel_ref, core_ref, supply_ref, step_ref, dq_ref, hl_ref, hr_ref,
                      hl0_ref, hr0_ref, *rest):
    ra_refs, rest = rest[:n_z], rest[n_z:]
    a_ref, power_ref, out_any, keep_ref, out_ref, lo_ref, hi_ref, sems = rest
    n = out_ref.shape[1] // CAX
    rows = NV * n
    _, ax, plen = roles()
    inlet_side = jnp.logical_and(ax == 0, plen == 0)
    ul_ref, ur_ref = hl0_ref.at[pl.ds(NV * CAX, CAX)], hr0_ref.at[pl.ds(NV * CAX, CAX)]
    fill_ghosts(q1_ref, lo_ref, hi_ref, ra_refs, step_ref, core_ref, supply_ref, n_ax)

    @pl.when(inlet_side)
    def _():
        first = lax.broadcasted_iota(jnp.int32, (n, LANES), 0) == 0
        last = lax.broadcasted_iota(jnp.int32, (n, LANES), 0) == n - 1
        left = lax.broadcasted_iota(jnp.int32, (n, LANES), 1) < HALF

        def neighbours(x, head, tail):
            before = jnp.where(first, head, pltpu.roll(x, 1, 0))
            after = jnp.where(last, tail, pltpu.roll(x, n - 1, 0))
            mid = pltpu.roll(x, HALF, 1)
            return (jnp.where(left, pltpu.roll(before, HALF, 1), mid),
                    jnp.where(left, mid, pltpu.roll(after, HALF, 1)))

        u = vel_ref[0, pl.ds(0, n, stride=CAX), :]
        w_next = vel_ref[1, pl.ds(1, n, stride=CAX), :]
        u_left, u_right = neighbours(u, ul_ref[pl.ds(0, 1), :], ur_ref[pl.ds(0, 1), :])
        state = [q1_ref[v, pl.ds(0, n, stride=CAX), :] + dq_ref[pl.ds(v * n, n), :] for v in range(NV)]
        parts = [[x[d * CAX:(d + 1) * CAX] for x in state] for d in range(n // CAX)]
        src = reactions(parts, a_ref[...].astype(jnp.bfloat16), power_ref)
        for v in range(NV):
            beside = dq_ref[pl.ds(rows + v, 1), :]
            q_left, q_right = neighbours(state[v], hl_ref[pl.ds(v * CAX, 1), :] + beside, hr_ref[pl.ds(v * CAX, 1), :] + beside)
            above = (1.0 - w_next) * q1_ref[v, pl.ds(1, n, stride=CAX), :]
            mixed = src[v * CAX:(v + 1) * CAX]
            mixed = jnp.concatenate([mixed[:, d * LANES:(d + 1) * LANES] for d in range(n // CAX)], axis=0)
            new = 0.6 * state[v] + 0.1 * ((1.0 + u_left) * q_left + (1.0 - u_right) * q_right + above) + mixed
            keep_ref[pl.ds(v * n, n), :] = 0.5 * q_ref[v, pl.ds(0, n, stride=CAX), :] + 0.5 * new

    copies = []
    for v in range(NV):
        out_ref[v] = part_ref[v]
        add_border(v, out_ref, 0.05, lo_ref, hi_ref, hl_ref, hr_ref, ul_ref, ur_ref)

        @pl.when(inlet_side)
        def _(v=v):
            w = vel_ref[1, pl.ds(0, n, stride=CAX), :]
            out_ref[v, pl.ds(1, n, stride=CAX), :] += 0.05 * ((1.0 + w) * dq_ref[pl.ds(v * n, n), :])

        @pl.when(plen == 1)
        def _(v=v):
            keep_ref[pl.ds(v * n, n), :] = out_ref[v, pl.ds(CAX - 1, n, stride=CAX), :]

        copies.append(pltpu.make_async_copy(out_ref.at[v], out_any.at[v], sems.at[v]))
        copies[-1].start()
    for copy in copies:
        copy.wait()


def last_kernel(in_any, keep_ref, core_ref, far_ref, out_any, row_ref, sem):
    _, ax, plen = roles()
    n = keep_ref.shape[0] // NV

    def patch(at, value):
        for v in range(NV):
            row_ref[v, :, 0, :] = value(pl.ds(v * n, n))
        copy = pltpu.make_async_copy(row_ref, out_any.at[:, :, pl.ds(at, 1), :], sem)
        copy.start()
        copy.wait()

    @pl.when(jnp.logical_and(ax == 0, plen == 0))
    def _():
        patch(0, lambda at: keep_ref[at, :] + 0.05 * (core_ref[at, :] + far_ref[at, :]))

    @pl.when(jnp.logical_and(ax == 0, plen == 1))
    def _():
        patch(CAX - 1, lambda at: keep_ref[at, :] + 0.05 * core_ref[at, :])


def shape(*dims):
    return jax.ShapeDtypeStruct(dims, f32)


SPACES = {"s": pltpu.SMEM, "v": pltpu.VMEM, "h": pltpu.HBM}


def call(kernel, inputs, kinds, outs, scratch=(), cost=None, to=None, aliases=None):
    return pl.pallas_call(
        kernel,
        in_specs=[pl.BlockSpec(memory_space=SPACES[k]) for k in kinds],
        out_specs=[pl.BlockSpec(memory_space=SPACES[k]) for k in (to or "v" * len(outs))],
        out_shape=outs,
        scratch_shapes=list(scratch),
        cost_estimate=cost,
        input_output_aliases=aliases or {},
        compiler_params=pltpu.CompilerParams(vmem_limit_bytes=LIMIT),
    )(*inputs)


def local(n_az, n_ax, cells, speeds, supply, mix, prefactor, activation, heat, inj_column, inj_slot, inj_open):
    size = cells.shape[-1]
    n = size // LANES
    rows = NV * n

    def view(array):
        k = array.shape[0]
        return array.reshape(k, CAX, n, LANES).transpose(0, 2, 1, 3).reshape(k, CAX * n, LANES)

    def number(i, j, p):
        return (i * n_ax + j) * 2 + p

    every = [(i, j) for i in range(n_az) for j in range(n_ax)]

    def send(x, route):
        return lax.ppermute(x, AXES, [(number(*a), number(*b)) for a, b in route])

    def ring(step):
        return [((i, j, p), ((i + step) % n_az, j, p)) for i, j in every for p in (0, 1)]

    swap = [((i, j, p), (i, j, 1 - p)) for i, j in every for p in (0, 1)]
    n_out = n_az - 1

    def mate(k, j):
        return j ^ 1 if k == 0 else ((j + 1) ^ 1) - 1 if 0 < j < n_ax - 1 else n_ax - 1 - j

    cap = CAX // 4 if n_az > 4 else CAX // 2
    pieces = CAX // cap

    def dense(k):
        out = [((i, j, 1), ((i + k + 1) % n_az, j, 1)) for i, j in every]
        if k < 2:
            out += [((i, j, 0), (i, mate(k, j), 0)) for i, j in every]
        return out

    def compact(k):
        out = [((i, j, 1), ((i + k + 1) % n_az, j, 1)) for i, j in every]
        if k < pieces:
            return out + [((i, j, 0), (i, mate(0, j), 0)) for i, j in every]
        return out + [((i, j, 0), ((i + k + 1) % n_az, j, 0)) for i, j in every]

    q, vel = view(cells[0]), view(speeds[0])
    sup = supply.reshape(rows, LANES)
    col, slot, opened = inj_column.reshape(-1), inj_slot, inj_open
    react = (mix, prefactor, activation, heat)
    row, edge = shape(rows, LANES), shape(NV * CAX, LANES)

    whole = shape(*q.shape)
    work = pl.CostEstimate(flops=300 * q.shape[1] * LANES, transcendentals=20 * q.shape[1] * LANES,
                           bytes_accessed=12_000_000)

    raw = tuple(pltpu.with_memory_space_constraint(x, pltpu.HBM) for x in (q, vel, col, slot, opened) + react)
    wide, edge0 = shape(rows + EXT, LANES), shape((NV + 1) * CAX, LANES)
    got = call(functools.partial(first_kernel, n_az, n_out), raw, "h" * 9,
               [shape(rows + EXT + CAX, LANES)] * n_out + [whole, shape(*vel.shape), row, wide, edge0, edge0,
                                                         shape(NV * CAX, 3 * NV * CAX), shape(NS * CAX, LANES)],
               [pltpu.SMEM(col.shape, jnp.int32)] * 3 + [pltpu.SMEM(x.shape, f32) for x in react]
               + [pltpu.SemaphoreType.DMA((8 + NV // 2,))])
    outs, (qv, velv, s0, own0, er, el, matrix, power) = got[:n_out], got[n_out:]
    ra = [send(x, dense(k)) for k, x in enumerate(outs)]
    s0r = send(s0, swap)
    hl0 = send(er, ring(1))
    el, s0r = lax.optimization_barrier((el, s0r))
    hr0 = send(el, ring(-1))
    part, = call(inside_one_kernel, (qv, velv, matrix, power), "vvvv", [whole], cost=work)

    got = call(functools.partial(border_one_kernel, n_az, n_ax, n_out, cap),
               (s0r, *ra, hl0, hr0, part, qv, velv, sup, own0, col, slot, opened),
               "v" * (n_out + 11),
               [shape(cap * NV * CAX, LANES)] * n_out + [whole, wide, row, row, row, edge, edge],
               [pltpu.VMEM((rows, LANES), f32)] * 2 + [pltpu.SMEM(col.shape, jnp.int32)] * 3
               + [pltpu.SemaphoreType.DMA((3,))])
    outs, (q1, tile0, s1, z1, own1, er, el) = got[:n_out], got[n_out:]
    down = [((i, j, 1), (i, j - 1, 1)) for i, j in every if j % 2 == 1]
    across = [((i, 2, 1), (i, 0, 0)) for i in range(n_az)]
    inner = [((i, j, 0), (i, mate(1, j), 0)) for i, j in every if 0 < j < n_ax - 1]
    rb = [send(x, compact(k)) for k, x in enumerate(outs)]
    down0 = send(tile0, down)

    part, = call(inside_two_kernel, (qv, q1, velv, matrix, power), "vvvvv", [whole], cost=work)
    part, own1, s1 = lax.optimization_barrier((part, own1, s1))
    step, = call(functools.partial(tile_kernel, n_out, cap), (own1, z1, *rb, *ra), "v" * (2 + 2 * n_out), [row])
    step_in = send(step, down + inner)
    er, el, step = lax.optimization_barrier((er, el, step))
    hl1, hr1 = send(er, ring(1)), send(el, ring(-1))
    core, = call(pair_kernel, (tile0, down0, s1), "vvv", [wide])
    far0 = send(core, across)
    core_in = send(core, swap)
    pair1, = call(add_kernel, (step, step_in), "vv", [row])
    far1 = send(pair1, across)
    pair1, hl1, hr1 = lax.optimization_barrier((pair1, hl1, hr1))

    dq, core2 = call(inlet_kernel, (pair1, far0, core_in), "vvv", [wide, row])
    core2_in = send(core2, swap)
    out, keep = call(functools.partial(border_two_kernel, n_ax, pieces),
                     (part, qv, q1, velv, core_in, sup, step_in, dq, hl1, hr1, hl0, hr0, *rb[:pieces], matrix, power),
                     "v" * (14 + pieces), [whole, row],
                     [pltpu.VMEM(q.shape, f32)] + [pltpu.VMEM((rows, LANES), f32)] * 2 + [pltpu.SemaphoreType.DMA((NV,))],
                     cost=work, to="hv")
    out, = call(last_kernel, (out.reshape(NV, n, CAX, LANES), keep, core2_in, far1), "hvvv", [shape(NV, n, CAX, LANES)],
                [pltpu.VMEM((NV, n, 1, LANES), f32), pltpu.SemaphoreType.DMA(())], to="h", aliases={0: 0})
    return out.transpose(0, 2, 1, 3).reshape(1, NV, CAX, size)


def solution(mesh):
    return jax.shard_map(
        functools.partial(local, mesh.shape["az"], mesh.shape["ax"]),
        mesh=mesh,
        in_specs=(
            P("pl", None, "ax", "az"),
            P("pl", None, "ax", "az"),
            P(None, "ax", "az"),
            P(),
            P(),
            P(),
            P(),
            P(("az", "ax"), None),
            P(("az", "ax")),
            P(("az", "ax")),
        ),
        out_specs=P("pl", None, "ax", "az"),
        check_vma=False,
    )
```

```python
import functools

import jax
import jax.numpy as jnp
from jax import lax
from jax.experimental import pallas as pl
from jax.experimental.pallas import tpu as pltpu
from jax.sharding import PartitionSpec as P

NV = 10
NS = 9
LANES = 128
CAX = 8
HALF = 64
AXES = ("az", "ax", "pl")
NJ = 8
EXT = 16
LOG2E = 1.4426950408889634
LIMIT = 16 * 1024 * 1024

f32 = jnp.float32


def roles():
    return lax.axis_index("az"), lax.axis_index("ax"), lax.axis_index("pl")


def low_half():
    return lax.broadcasted_iota(jnp.int32, (CAX, LANES), 1) < HALF


def block(q_ref, v, b):
    return q_ref[v, pl.ds(CAX * CAX * b + CAX - 1, CAX, stride=CAX), :]


def axial_rows(q_ref, vel_ref, first_mate, second_mate):
    _, ax, _ = roles()
    n = q_ref.shape[1] // CAX

    def up(v, at, size):
        rows = pl.ds(CAX * at + CAX - 1, size, stride=CAX)
        return (1.0 + vel_ref[1, rows, :]) * q_ref[v, rows, :]

    def down(v, at, size):
        rows = pl.ds(CAX * at, size, stride=CAX)
        return (1.0 - vel_ref[1, rows, :]) * q_ref[v, rows, :]

    def put(refs, value):
        size = NV * n // len(refs)
        step = min(n, size) if size % n == 0 or n % size == 0 else n // 2
        for k in range(NV * n // step):
            at = k * step
            refs[at // size][pl.ds(at % size, step), :] = value(at // n, at % n, step)

    @pl.when(ax % 2 == 0)
    def _():
        put(first_mate, up)
        put(second_mate, down)

    @pl.when(ax % 2 == 1)
    def _():
        put(first_mate, down)
        put(second_mate, up)


def edges(q_ref, er_ref, el_ref):
    n = q_ref.shape[1] // CAX
    for v in range(NV):
        el_ref[pl.ds(v * CAX, CAX), :] = q_ref[v, pl.ds(0, CAX), :]
        er_ref[pl.ds(v * CAX, CAX), :] = q_ref[v, pl.ds((n - 1) * CAX, CAX), :]


def first_kernel(n_az, n_out, pieces, q_any, vel_any, col_any, slot_any, open_any, mix_any, pre_any, act_any, heat_any, *outs):
    out_refs, rest = outs[:n_out], outs[n_out:]
    (q_ref, vel_ref, s_ref, own_ref, er_ref, el_ref, a_ref, power_ref,
     col_ref, slot_ref, open_ref, mix_ref, pre_ref, act_ref, heat_ref, sems) = rest
    pairs = [(mix_any, mix_ref), (pre_any, pre_ref), (act_any, act_ref), (heat_any, heat_ref),
             (col_any, col_ref), (slot_any, slot_ref), (open_any, open_ref), (vel_any, vel_ref)]
    small = len(pairs) - 1
    pairs += [(q_any.at[pl.ds(v, 2)], q_ref.at[pl.ds(v, 2)]) for v in range(0, NV, 2)]
    copies = [pltpu.make_async_copy(x, y, sems.at[k]) for k, (x, y) in enumerate(pairs)]
    for copy in copies[small:] + copies[:small]:
        copy.start()
    az, _, plen = roles()
    n = q_ref.shape[1] // CAX
    rows = NV * n
    refs = (own_ref,) + tuple(out_refs)
    beside_at = [rows] + [ref.shape[0] - CAX - EXT for ref in out_refs]

    @pl.when(plen == 1)
    def _():
        for ref in (own_ref, out_refs[0]):
            ref[pl.ds(0, rows), :] = jnp.zeros((rows, LANES), f32)
        for ref, at in zip(refs, beside_at):
            ref[pl.ds(at, EXT), :] = jnp.zeros((EXT, LANES), f32)

    for copy in copies[:small]:
        copy.wait()
    mixing(a_ref, mix_ref, pre_ref, heat_ref)
    for k in range(NS):
        power_ref[pl.ds(k * CAX, CAX), :] = jnp.full((CAX, LANES), act_ref[k] * (-LOG2E), f32)
    for copy in copies[small:]:
        copy.wait()
    edges(q_ref, er_ref, el_ref)
    el_ref[pl.ds(NV * CAX, CAX), :] = vel_ref[0, pl.ds(0, CAX), :]
    er_ref[pl.ds(NV * CAX, CAX), :] = vel_ref[0, pl.ds((n - 1) * CAX, CAX), :]

    @pl.when(plen == 0)
    def _():
        for v in range(NV):
            s_ref[pl.ds(v * n, n), :] = q_ref[v, pl.ds(0, n, stride=CAX), :]
        axial_rows(q_ref, vel_ref, out_refs[:1], out_refs[1:1 + pieces])

    @pl.when(plen == 1)
    def _():
        sub = lax.broadcasted_iota(jnp.int32, (CAX, LANES), 0)
        left = lax.broadcasted_iota(jnp.int32, (1, LANES), 1) < HALF
        blocks = n // CAX
        tables = [jnp.full((CAX, LANES), -1.0, f32)] * n_az
        used = [jnp.int32(0)] * n_az
        for b in range(blocks):
            tile, opened = slot_ref[b], open_ref[b] != 0
            ahead = (col_ref[b] - az + n_az) % n_az
            for shift, ref in enumerate(refs):
                here = jnp.logical_and(ahead == shift, opened)
                tables[shift] = jnp.where(sub == jnp.where(here, used[shift], CAX), tile.astype(f32), tables[shift])

                @pl.when(here)
                def _(ref=ref, b=b, tile=tile, shift=shift, slot=used[shift]):
                    for v in range(NV):
                        if shift < 2:
                            at = pl.ds(pl.multiple_of(v * n + tile * CAX, CAX), CAX)
                            ref[at, :] += block(q_ref, v, b)
                        else:
                            at = pl.ds(pl.multiple_of((slot * NV + v) * CAX, CAX), CAX)
                            ref[at, :] = block(q_ref, v, b)

                used[shift] = used[shift] + here.astype(jnp.int32)

            def beside(end, step, row, keep_left, b=b, tile=tile, opened=opened, ahead=ahead):
                @pl.when(jnp.logical_and(opened, tile == end))
                def _():
                    for shift, ref in enumerate(refs):
                        @pl.when(ahead == (shift + step) % n_az)
                        def _(ref=ref, at=beside_at[shift]):
                            for v in range(NV):
                                cell = q_ref[v, pl.ds(row, 1), :]
                                cell = jnp.where(left, cell, 0.0) if keep_left else jnp.where(left, 0.0, cell)
                                ref[pl.ds(at + v, 1), :] += cell

            beside(0, 1, CAX * CAX * b + CAX - 1, True)
            beside(blocks - 1, n_az - 1, CAX * CAX * (b + 1) - 1, False)
        for ref, table in zip(out_refs, tables[1:]):
            ref[pl.ds(ref.shape[0] - CAX, CAX), :] = table


def fill_ghosts(state_ref, lo_ref, hi_ref, ra_refs, rb_refs, high_ref, supply_ref, n_ax):
    _, ax, plen = roles()
    n = state_ref.shape[1] // CAX
    even = ax % 2 == 0
    odd = jnp.logical_not(even)
    cham = plen == 0

    def put(ref, parts):
        size = ref.shape[0] // len(parts)
        for k, part in enumerate(parts):
            ref[pl.ds(k * size, size), :] = part[pl.ds(0, size), :]

    @pl.when(plen == 1)
    def _():
        lo_ref[...] = supply_ref[...]
        hi_ref[...] = high_ref[pl.ds(0, hi_ref.shape[0]), :]

    @pl.when(jnp.logical_and(cham, even))
    def _():
        put(hi_ref, ra_refs)

    @pl.when(jnp.logical_and(cham, odd))
    def _():
        put(lo_ref, ra_refs)

    @pl.when(jnp.logical_and(cham, ax == 0))
    def _():
        lo_ref[...] = jnp.zeros_like(lo_ref)

    @pl.when(jnp.logical_and(cham, jnp.logical_and(even, ax > 0)))
    def _():
        put(lo_ref, rb_refs)

    @pl.when(jnp.logical_and(cham, jnp.logical_and(odd, ax < n_ax - 1)))
    def _():
        put(hi_ref, rb_refs)

    @pl.when(jnp.logical_and(cham, ax == n_ax - 1))
    def _():
        for v in range(NV):
            hi_ref[pl.ds(v * n, n), :] = state_ref[v, pl.ds(CAX - 1, n, stride=CAX), :]


def add_border(v, dst_ref, scale, lo_ref, hi_ref, hl_ref, hr_ref, ul_ref, ur_ref):
    n = dst_ref.shape[1] // CAX
    left = low_half()
    dst_ref[v, pl.ds(0, n, stride=CAX), :] += scale * lo_ref[pl.ds(v * n, n), :]
    dst_ref[v, pl.ds(CAX - 1, n, stride=CAX), :] += scale * hi_ref[pl.ds(v * n, n), :]
    al = scale + scale * pltpu.roll(ul_ref[...], HALF, 1)
    ar = scale - scale * pltpu.roll(ur_ref[...], HALF, 1)
    head = pltpu.roll(hl_ref[pl.ds(v * CAX, CAX), :], HALF, 1)
    tail = pltpu.roll(hr_ref[pl.ds(v * CAX, CAX), :], HALF, 1)
    dst_ref[v, pl.ds(0, CAX), :] += jnp.where(left, al * head, 0.0)
    dst_ref[v, pl.ds((n - 1) * CAX, CAX), :] += jnp.where(left, 0.0, ar * tail)


def mixing(a_ref, mix_ref, pre_ref, heat_ref):
    width = NV * CAX
    col = lax.broadcasted_iota(jnp.int32, (CAX, 3 * width), 1)
    row = lax.broadcasted_iota(jnp.int32, (CAX, 3 * width), 0)
    inner = col % width
    species, lane = inner // CAX, inner % CAX
    for v in range(NV):
        block = jnp.zeros((CAX, 3 * width), f32)
        for k in range(NS):
            value = 0.2 * pre_ref[k] * (mix_ref[v, k] if v < NS else heat_ref[k])
            block = jnp.where(species == k, value, block)
        block = jnp.where(lane == row, block, 0.0)
        high = block.astype(jnp.bfloat16).astype(f32)
        a_ref[pl.ds(v * CAX, CAX), :] = jnp.where(col // width == 1, block - high, high)


def reactions(states, a, power_ref):
    rates = []
    for state in states:
        inv = 1.0 / jnp.maximum(state[NS], 0.5)
        some = [jnp.exp2(power_ref[pl.ds(k * CAX, CAX), :] * inv) * jnp.maximum(state[k], 0.0) for k in range(NS)]
        rates.append(jnp.concatenate(some + [jnp.zeros((CAX, LANES), f32)], axis=0))
    rate = jnp.concatenate(rates, axis=1)
    high = rate.astype(jnp.bfloat16)
    low = (rate - high.astype(f32)).astype(jnp.bfloat16)
    return jnp.dot(a, jnp.concatenate([high, high, low], axis=0), preferred_element_type=f32)


def interior(q_ref, vel_ref, a_ref, power_ref, scale, finish):
    n = q_ref.shape[1] // CAX
    left = low_half()
    sub = lax.broadcasted_iota(jnp.int32, (CAX, LANES), 0)
    bottom, top = sub == 0, sub == CAX - 1
    a = (scale * a_ref[...]).astype(jnp.bfloat16)
    c = 0.1 * scale

    def reg(ref, v, j):
        return ref[v, pl.ds(pl.multiple_of(j * CAX, CAX), CAX), :]

    def column(ref, v, j0):
        regs = [reg(ref, v, j0 + d) for d in range(NJ)]
        before = jnp.where(j0 == 0, 0.0, reg(ref, v, jnp.maximum(j0 - 1, 0)))
        after = jnp.where(j0 + NJ == n, 0.0, reg(ref, v, jnp.minimum(j0 + NJ, n - 1)))
        turned = [pltpu.roll(x, HALF, 1) for x in [before] + regs + [after]]
        lefts = [jnp.where(left, turned[d], turned[d + 1]) for d in range(NJ)]
        rights = [jnp.where(left, turned[d + 1], turned[d + 2]) for d in range(NJ)]
        return regs, lefts, rights

    def body(step, carry):
        j0 = step * NJ
        src = reactions([[reg(q_ref, v, j0 + d) for v in range(NV)] for d in range(NJ)], a, power_ref)
        _, u_left, u_right = column(vel_ref, 0, j0)
        w = [reg(vel_ref, 1, j0 + d) for d in range(NJ)]
        al = [c + c * x for x in u_left]
        ar = [c - c * x for x in u_right]
        wu = [jnp.where(bottom, 0.0, c + c * pltpu.roll(x, 1, 0)) for x in w]
        wd = [jnp.where(top, 0.0, c - c * pltpu.roll(x, CAX - 1, 0)) for x in w]
        for v in range(NV):
            regs, lefts, rights = column(q_ref, v, j0)
            for d in range(NJ):
                vertical = wu[d] * pltpu.roll(regs[d], 1, 0) + wd[d] * pltpu.roll(regs[d], CAX - 1, 0)
                new = (0.6 * scale) * regs[d] + src[v * CAX:(v + 1) * CAX, d * LANES:(d + 1) * LANES]
                finish(j0 + d, v, new + (al[d] * lefts[d] + ar[d] * rights[d]) + vertical)
        return carry

    lax.fori_loop(0, n // NJ, body, 0)


def inside_one_kernel(q_ref, vel_ref, a_ref, power_ref, out_ref):
    def finish(j, v, new):
        out_ref[v, pl.ds(pl.multiple_of(j * CAX, CAX), CAX), :] = new

    interior(q_ref, vel_ref, a_ref, power_ref, 1.0, finish)


def inside_two_kernel(q_ref, q1_ref, vel_ref, a_ref, power_ref, out_ref):
    def finish(j, v, new):
        at = pl.ds(pl.multiple_of(j * CAX, CAX), CAX)
        out_ref[v, at, :] = 0.5 * q_ref[v, at, :] + new

    interior(q1_ref, vel_ref, a_ref, power_ref, 0.5, finish)


def gather_slots(dst_ref, base, got, tables, cap):
    slots = [(k, m) for k in range(len(got)) for m in range(cap)]
    named = [jnp.broadcast_to(tables[k][pl.ds(tables[k].shape[0] - CAX + m, 1), :], (CAX, LANES)) for k, m in slots]
    for v in range(NV):
        blocks = [got[k][pl.ds((m * NV + v) * CAX, CAX), :] for k, m in slots]
        for t in range(CAX):
            at = pl.ds((v * CAX + t) * CAX, CAX)
            total = base(at)
            for name, value in zip(named, blocks):
                total = total + jnp.where(name == t, value, 0.0)
            dst_ref[at, :] = total


def border_one_kernel(n_az, n_ax, n_out, cap, s_in_ref, *rest):
    got, rest = rest[:n_out], rest[n_out:]
    hl_ref, hr_ref, part_ref, q_ref, vel_ref, supply_ref, own_in_ref, col_any, slot_any, open_any = rest[:10]
    out_refs, rest = rest[10:10 + n_out], rest[10 + n_out:]
    (q1_ref, core_ref, z_ref, own_ref, er_ref, el_ref, lo_ref, hi_ref,
     col_ref, slot_ref, open_ref, sems) = rest
    pairs = [(col_any, col_ref), (slot_any, slot_ref), (open_any, open_ref)]
    copies = [pltpu.make_async_copy(x, y, sems.at[k]) for k, (x, y) in enumerate(pairs)]
    for copy in copies:
        copy.start()
    az, _, plen = roles()
    n = q_ref.shape[1] // CAX
    rows = NV * n
    fill_ghosts(q_ref, lo_ref, hi_ref, got[:1], got[1:1 + CAX // cap], s_in_ref, supply_ref, n_ax)
    for v in range(NV):
        q1_ref[v] = part_ref[v]
        add_border(v, q1_ref, 0.1, lo_ref, hi_ref, hl_ref, hr_ref,
                   hl_ref.at[pl.ds(NV * CAX, CAX)], hr_ref.at[pl.ds(NV * CAX, CAX)])
    edges(q1_ref, er_ref, el_ref)
    for copy in copies:
        copy.wait()

    @pl.when(plen == 0)
    def _():
        core_ref[pl.ds(rows, EXT), :] = jnp.zeros((EXT, LANES), f32)
        for v in range(NV):
            core_ref[pl.ds(v * n, n), :] = q1_ref[v, pl.ds(0, n, stride=CAX), :]
        axial_rows(q1_ref, vel_ref, out_refs[:CAX // cap], (z_ref,))

    @pl.when(plen == 1)
    def _():
        gather_slots(core_ref, lambda at: own_in_ref[at, :] + got[0][at, :], got[1:], got[1:], cap)
        beside = own_in_ref[pl.ds(rows, EXT), :]
        for ref in got:
            beside = beside + ref[pl.ds(ref.shape[0] - CAX - EXT, EXT), :]
        core_ref[pl.ds(rows, EXT), :] = beside
        own_ref[...] = jnp.zeros_like(own_ref)
        used = [jnp.int32(0)] * n_out
        for b in range(n // CAX):
            tile = slot_ref[b]
            ahead = (col_ref[b] - az + n_az) % n_az
            opened = open_ref[b] != 0

            @pl.when(jnp.logical_and(opened, ahead == 0))
            def _(b=b, tile=tile):
                for v in range(NV):
                    at = pl.ds(pl.multiple_of(v * n + tile * CAX, CAX), CAX)
                    own_ref[at, :] += block(q1_ref, v, b)

            for k, ref in enumerate(out_refs):
                here = jnp.logical_and(opened, ahead == k + 1)

                @pl.when(here)
                def _(ref=ref, b=b, slot=used[k]):
                    for v in range(NV):
                        at = pl.ds(pl.multiple_of((slot * NV + v) * CAX, CAX), CAX)
                        ref[at, :] = block(q1_ref, v, b)

                used[k] = used[k] + here.astype(jnp.int32)


def tile_kernel(n_out, cap, own_ref, z_ref, *rest):
    got, tables, (step_ref,) = rest[:n_out], rest[n_out:2 * n_out], rest[2 * n_out:]
    _, _, plen = roles()

    @pl.when(plen == 0)
    def _():
        step_ref[...] = z_ref[...]

    @pl.when(plen == 1)
    def _():
        gather_slots(step_ref, lambda at: own_ref[at, :], got, tables, cap)


def add_kernel(x_ref, y_ref, out_ref):
    out_ref[...] = x_ref[...] + y_ref[...]


def inlet_kernel(pair_ref, far_ref, near_ref, dq_ref, out_ref):
    _, ax, plen = roles()
    rows = out_ref.shape[0]
    inlet_side = jnp.logical_and(plen == 0, ax == 0)

    @pl.when(inlet_side)
    def _():
        dq_ref[...] = 0.1 * (far_ref[...] + near_ref[...])
        out_ref[...] = dq_ref[pl.ds(0, rows), :]

    @pl.when(jnp.logical_not(inlet_side))
    def _():
        dq_ref[...] = jnp.zeros_like(dq_ref)
        out_ref[...] = pair_ref[...]


def border_two_kernel(n_ax, n_z, part_ref, q_ref, q1_ref, vel_ref, core_ref, supply_ref, step_ref, dq_ref, hl_ref, hr_ref,
                      hl0_ref, hr0_ref, *rest):
    ra_refs, rest = rest[:n_z], rest[n_z:]
    a_ref, power_ref, out_any, keep_ref, out_ref, lo_ref, hi_ref, sems = rest
    n = out_ref.shape[1] // CAX
    rows = NV * n
    _, ax, plen = roles()
    inlet_side = jnp.logical_and(ax == 0, plen == 0)
    ul_ref, ur_ref = hl0_ref.at[pl.ds(NV * CAX, CAX)], hr0_ref.at[pl.ds(NV * CAX, CAX)]
    fill_ghosts(q1_ref, lo_ref, hi_ref, ra_refs, (step_ref,), core_ref, supply_ref, n_ax)

    @pl.when(inlet_side)
    def _():
        first = lax.broadcasted_iota(jnp.int32, (n, LANES), 0) == 0
        last = lax.broadcasted_iota(jnp.int32, (n, LANES), 0) == n - 1
        left = lax.broadcasted_iota(jnp.int32, (n, LANES), 1) < HALF

        def neighbours(x, head, tail):
            before = jnp.where(first, head, pltpu.roll(x, 1, 0))
            after = jnp.where(last, tail, pltpu.roll(x, n - 1, 0))
            mid = pltpu.roll(x, HALF, 1)
            return (jnp.where(left, pltpu.roll(before, HALF, 1), mid),
                    jnp.where(left, mid, pltpu.roll(after, HALF, 1)))

        u = vel_ref[0, pl.ds(0, n, stride=CAX), :]
        w_next = vel_ref[1, pl.ds(1, n, stride=CAX), :]
        u_left, u_right = neighbours(u, ul_ref[pl.ds(0, 1), :], ur_ref[pl.ds(0, 1), :])
        state = [q1_ref[v, pl.ds(0, n, stride=CAX), :] + dq_ref[pl.ds(v * n, n), :] for v in range(NV)]
        parts = [[x[d * CAX:(d + 1) * CAX] for x in state] for d in range(n // CAX)]
        src = reactions(parts, a_ref[...].astype(jnp.bfloat16), power_ref)
        for v in range(NV):
            beside = dq_ref[pl.ds(rows + v, 1), :]
            q_left, q_right = neighbours(state[v], hl_ref[pl.ds(v * CAX, 1), :] + beside, hr_ref[pl.ds(v * CAX, 1), :] + beside)
            above = (1.0 - w_next) * q1_ref[v, pl.ds(1, n, stride=CAX), :]
            mixed = src[v * CAX:(v + 1) * CAX]
            mixed = jnp.concatenate([mixed[:, d * LANES:(d + 1) * LANES] for d in range(n // CAX)], axis=0)
            new = 0.6 * state[v] + 0.1 * ((1.0 + u_left) * q_left + (1.0 - u_right) * q_right + above) + mixed
            keep_ref[pl.ds(v * n, n), :] = 0.5 * q_ref[v, pl.ds(0, n, stride=CAX), :] + 0.5 * new

    copies = []
    for v in range(NV):
        out_ref[v] = part_ref[v]
        add_border(v, out_ref, 0.05, lo_ref, hi_ref, hl_ref, hr_ref, ul_ref, ur_ref)

        @pl.when(inlet_side)
        def _(v=v):
            w = vel_ref[1, pl.ds(0, n, stride=CAX), :]
            out_ref[v, pl.ds(1, n, stride=CAX), :] += 0.05 * ((1.0 + w) * dq_ref[pl.ds(v * n, n), :])

        @pl.when(plen == 1)
        def _(v=v):
            keep_ref[pl.ds(v * n, n), :] = out_ref[v, pl.ds(CAX - 1, n, stride=CAX), :]

        copies.append(pltpu.make_async_copy(out_ref.at[v], out_any.at[v], sems.at[v]))
        copies[-1].start()
    for copy in copies:
        copy.wait()


def last_kernel(in_any, keep_ref, core_ref, far_ref, out_any, row_ref, sem):
    _, ax, plen = roles()
    n = keep_ref.shape[0] // NV

    def patch(at, value):
        for v in range(NV):
            row_ref[v, :, 0, :] = value(pl.ds(v * n, n))
        copy = pltpu.make_async_copy(row_ref, out_any.at[:, :, pl.ds(at, 1), :], sem)
        copy.start()
        copy.wait()

    @pl.when(jnp.logical_and(ax == 0, plen == 0))
    def _():
        patch(0, lambda at: keep_ref[at, :] + 0.05 * (core_ref[at, :] + far_ref[at, :]))

    @pl.when(jnp.logical_and(ax == 0, plen == 1))
    def _():
        patch(CAX - 1, lambda at: keep_ref[at, :] + 0.05 * core_ref[at, :])


def shape(*dims):
    return jax.ShapeDtypeStruct(dims, f32)


SPACES = {"s": pltpu.SMEM, "v": pltpu.VMEM, "h": pltpu.HBM}


def call(kernel, inputs, kinds, outs, scratch=(), cost=None, to=None, aliases=None):
    return pl.pallas_call(
        kernel,
        in_specs=[pl.BlockSpec(memory_space=SPACES[k]) for k in kinds],
        out_specs=[pl.BlockSpec(memory_space=SPACES[k]) for k in (to or "v" * len(outs))],
        out_shape=outs,
        scratch_shapes=list(scratch),
        cost_estimate=cost,
        input_output_aliases=aliases or {},
        compiler_params=pltpu.CompilerParams(vmem_limit_bytes=LIMIT),
    )(*inputs)


def local(n_az, n_ax, cells, speeds, supply, mix, prefactor, activation, heat, inj_column, inj_slot, inj_open):
    size = cells.shape[-1]
    n = size // LANES
    rows = NV * n

    def view(array):
        k = array.shape[0]
        return array.reshape(k, CAX, n, LANES).transpose(0, 2, 1, 3).reshape(k, CAX * n, LANES)

    def number(i, j, p):
        return (i * n_ax + j) * 2 + p

    every = [(i, j) for i in range(n_az) for j in range(n_ax)]

    def send(x, route):
        return lax.ppermute(x, AXES, [(number(*a), number(*b)) for a, b in route])

    def ring(step):
        return [((i, j, p), ((i + step) % n_az, j, p)) for i, j in every for p in (0, 1)]

    swap = [((i, j, p), (i, j, 1 - p)) for i, j in every for p in (0, 1)]
    n_out = n_az - 1

    def mate(k, j):
        return j ^ 1 if k == 0 else ((j + 1) ^ 1) - 1 if 0 < j < n_ax - 1 else n_ax - 1 - j

    cap = CAX // 4 if n_az > 4 else CAX // 2
    pieces = CAX // cap

    def first(k):
        out = [((i, j, 1), ((i + k + 1) % n_az, j, 1)) for i, j in every]
        if k <= pieces:
            return out + [((i, j, 0), (i, mate(min(k, 1), j), 0)) for i, j in every]
        return out + [((i, j, 0), ((i + k + 1) % n_az, j, 0)) for i, j in every]

    def compact(k):
        out = [((i, j, 1), ((i + k + 1) % n_az, j, 1)) for i, j in every]
        if k < pieces:
            return out + [((i, j, 0), (i, mate(0, j), 0)) for i, j in every]
        return out + [((i, j, 0), ((i + k + 1) % n_az, j, 0)) for i, j in every]

    q, vel = view(cells[0]), view(speeds[0])
    sup = supply.reshape(rows, LANES)
    col, slot, opened = inj_column.reshape(-1), inj_slot, inj_open
    react = (mix, prefactor, activation, heat)
    row, edge = shape(rows, LANES), shape(NV * CAX, LANES)

    whole = shape(*q.shape)
    work = pl.CostEstimate(flops=300 * q.shape[1] * LANES, transcendentals=20 * q.shape[1] * LANES,
                           bytes_accessed=12_000_000)

    raw = tuple(pltpu.with_memory_space_constraint(x, pltpu.HBM) for x in (q, vel, col, slot, opened) + react)
    wide, edge0 = shape(rows + EXT, LANES), shape((NV + 1) * CAX, LANES)
    got = call(functools.partial(first_kernel, n_az, n_out, pieces), raw, "h" * 9,
               [shape(rows + EXT + CAX, LANES)] + [shape(cap * NV * CAX + EXT + CAX, LANES)] * (n_out - 1) + [whole, shape(*vel.shape), row, wide, edge0, edge0,
                                                         shape(NV * CAX, 3 * NV * CAX), shape(NS * CAX, LANES)],
               [pltpu.SMEM(col.shape, jnp.int32)] * 3 + [pltpu.SMEM(x.shape, f32) for x in react]
               + [pltpu.SemaphoreType.DMA((8 + NV // 2,))])
    outs, (qv, velv, s0, own0, er, el, matrix, power) = got[:n_out], got[n_out:]
    ra = [send(x, first(k)) for k, x in enumerate(outs)]
    s0r = send(s0, swap)
    hl0 = send(er, ring(1))
    el, s0r = lax.optimization_barrier((el, s0r))
    hr0 = send(el, ring(-1))
    part, = call(inside_one_kernel, (qv, velv, matrix, power), "vvvv", [whole], cost=work)

    got = call(functools.partial(border_one_kernel, n_az, n_ax, n_out, cap),
               (s0r, *ra, hl0, hr0, part, qv, velv, sup, own0, col, slot, opened),
               "v" * (n_out + 11),
               [shape(cap * NV * CAX, LANES)] * n_out + [whole, wide, row, row, edge, edge],
               [pltpu.VMEM((rows, LANES), f32)] * 2 + [pltpu.SMEM(col.shape, jnp.int32)] * 3
               + [pltpu.SemaphoreType.DMA((3,))])
    outs, (q1, core, z1, own1, er, el) = got[:n_out], got[n_out:]
    down = [((i, j, 1), (i, j - 1, 1)) for i, j in every if j % 2 == 1]
    across = [((i, 2, 1), (i, 0, 0)) for i in range(n_az)]
    inner = [((i, j, 0), (i, mate(1, j), 0)) for i, j in every if 0 < j < n_ax - 1]
    rb = [send(x, compact(k)) for k, x in enumerate(outs)]
    core_in = send(core, swap)
    down0 = send(core, [((i, j, 1), (i, j - 1, 0)) for i, j in every if j % 2 == 1])

    part, = call(inside_two_kernel, (qv, q1, velv, matrix, power), "vvvvv", [whole], cost=work)
    part, own1 = lax.optimization_barrier((part, own1))
    step, = call(functools.partial(tile_kernel, n_out, cap), (own1, z1, *rb, *ra), "v" * (2 + 2 * n_out), [row])
    step_in = send(step, down + inner)
    er, el, core_in, step = lax.optimization_barrier((er, el, core_in, step))
    hl1, hr1 = send(er, ring(1)), send(el, ring(-1))
    pair0, = call(add_kernel, (core_in, down0), "vv", [wide])
    far0 = send(pair0, [((i, 2, 0), (i, 0, 0)) for i in range(n_az)])
    pair1, = call(add_kernel, (step, step_in), "vv", [row])
    far1 = send(pair1, across)
    pair1, hl1, hr1 = lax.optimization_barrier((pair1, hl1, hr1))

    dq, core2 = call(inlet_kernel, (pair1, far0, pair0), "vvv", [wide, row])
    core2_in = send(core2, swap)
    out, keep = call(functools.partial(border_two_kernel, n_ax, pieces),
                     (part, qv, q1, velv, core_in, sup, step_in, dq, hl1, hr1, hl0, hr0, *rb[:pieces], matrix, power),
                     "v" * (14 + pieces), [whole, row],
                     [pltpu.VMEM(q.shape, f32)] + [pltpu.VMEM((rows, LANES), f32)] * 2 + [pltpu.SemaphoreType.DMA((NV,))],
                     cost=work, to="hv")
    out, = call(last_kernel, (out.reshape(NV, n, CAX, LANES), keep, core2_in, far1), "hvvv", [shape(NV, n, CAX, LANES)],
                [pltpu.VMEM((NV, n, 1, LANES), f32), pltpu.SemaphoreType.DMA(())], to="h", aliases={0: 0})
    return out.transpose(0, 2, 1, 3).reshape(1, NV, CAX, size)


def solution(mesh):
    return jax.shard_map(
        functools.partial(local, mesh.shape["az"], mesh.shape["ax"]),
        mesh=mesh,
        in_specs=(
            P("pl", None, "ax", "az"),
            P("pl", None, "ax", "az"),
            P(None, "ax", "az"),
            P(),
            P(),
            P(),
            P(),
            P(("az", "ax"), None),
            P(("az", "ax")),
            P(("az", "ax")),
        ),
        out_specs=P("pl", None, "ax", "az"),
        check_vma=False,
    )
```

```python
import functools

import jax
import jax.numpy as jnp
from jax import lax
from jax.experimental import pallas as pl
from jax.experimental.pallas import tpu as pltpu
from jax.sharding import PartitionSpec as P

NV = 10
NS = 9
LANES = 128
CAX = 8
HALF = 64
AXES = ("az", "ax", "pl")
NJ = 8
EXT = 16
LOG2E = 1.4426950408889634
LIMIT = 16 * 1024 * 1024

f32 = jnp.float32


def roles():
    return lax.axis_index("az"), lax.axis_index("ax"), lax.axis_index("pl")


def low_half():
    return lax.broadcasted_iota(jnp.int32, (CAX, LANES), 1) < HALF


def block(q_ref, v, b):
    return q_ref[v, pl.ds(CAX * CAX * b + CAX - 1, CAX, stride=CAX), :]


def axial_rows(q_ref, vel_ref, first_mate, second_mate):
    _, ax, _ = roles()
    n = q_ref.shape[1] // CAX

    def up(v, at, size):
        rows = pl.ds(CAX * at + CAX - 1, size, stride=CAX)
        return (1.0 + vel_ref[1, rows, :]) * q_ref[v, rows, :]

    def down(v, at, size):
        rows = pl.ds(CAX * at, size, stride=CAX)
        return (1.0 - vel_ref[1, rows, :]) * q_ref[v, rows, :]

    def put(refs, value):
        size = NV * n // len(refs)
        step = min(n, size) if size % n == 0 or n % size == 0 else n // 2
        for k in range(NV * n // step):
            at = k * step
            refs[at // size][pl.ds(at % size, step), :] = value(at // n, at % n, step)

    @pl.when(ax % 2 == 0)
    def _():
        put(first_mate, up)
        put(second_mate, down)

    @pl.when(ax % 2 == 1)
    def _():
        put(first_mate, down)
        put(second_mate, up)


def edges(q_ref, er_ref, el_ref):
    n = q_ref.shape[1] // CAX
    for v in range(NV):
        el_ref[pl.ds(v * CAX, CAX), :] = q_ref[v, pl.ds(0, CAX), :]
        er_ref[pl.ds(v * CAX, CAX), :] = q_ref[v, pl.ds((n - 1) * CAX, CAX), :]


def first_kernel(n_az, n_out, pieces, q_any, vel_any, col_any, slot_any, open_any, mix_any, pre_any, act_any, heat_any, *outs):
    out_refs, rest = outs[:n_out], outs[n_out:]
    (q_ref, vel_ref, s_ref, own_ref, er_ref, el_ref, a_ref, power_ref,
     col_ref, slot_ref, open_ref, mix_ref, pre_ref, act_ref, heat_ref, sems) = rest
    pairs = [(mix_any, mix_ref), (pre_any, pre_ref), (act_any, act_ref), (heat_any, heat_ref),
             (col_any, col_ref), (slot_any, slot_ref), (open_any, open_ref), (vel_any, vel_ref)]
    small = len(pairs) - 1
    pairs += [(q_any.at[pl.ds(v, 2)], q_ref.at[pl.ds(v, 2)]) for v in range(0, NV, 2)]
    copies = [pltpu.make_async_copy(x, y, sems.at[k]) for k, (x, y) in enumerate(pairs)]
    for copy in copies[small:] + copies[:small]:
        copy.start()
    az, _, plen = roles()
    n = q_ref.shape[1] // CAX
    rows = NV * n
    refs = (own_ref,) + tuple(out_refs)
    beside_at = [rows] + [ref.shape[0] - CAX - EXT for ref in out_refs]

    @pl.when(plen == 1)
    def _():
        for ref in (own_ref, out_refs[0]):
            ref[pl.ds(0, rows), :] = jnp.zeros((rows, LANES), f32)
        for ref, at in zip(refs, beside_at):
            ref[pl.ds(at, EXT), :] = jnp.zeros((EXT, LANES), f32)

    for copy in copies[:small]:
        copy.wait()
    mixing(a_ref, mix_ref, pre_ref, heat_ref)
    for k in range(NS):
        power_ref[pl.ds(k * CAX, CAX), :] = jnp.full((CAX, LANES), act_ref[k] * (-LOG2E), f32)
    for copy in copies[small:]:
        copy.wait()
    edges(q_ref, er_ref, el_ref)
    el_ref[pl.ds(NV * CAX, CAX), :] = vel_ref[0, pl.ds(0, CAX), :]
    er_ref[pl.ds(NV * CAX, CAX), :] = vel_ref[0, pl.ds((n - 1) * CAX, CAX), :]

    @pl.when(plen == 0)
    def _():
        for v in range(NV):
            s_ref[pl.ds(v * n, n), :] = q_ref[v, pl.ds(0, n, stride=CAX), :]
        axial_rows(q_ref, vel_ref, out_refs[:1], out_refs[1:1 + pieces])

    @pl.when(plen == 1)
    def _():
        sub = lax.broadcasted_iota(jnp.int32, (CAX, LANES), 0)
        left = lax.broadcasted_iota(jnp.int32, (1, LANES), 1) < HALF
        blocks = n // CAX
        tables = [jnp.full((CAX, LANES), -1.0, f32)] * n_az
        used = [jnp.int32(0)] * n_az
        for b in range(blocks):
            tile, opened = slot_ref[b], open_ref[b] != 0
            ahead = (col_ref[b] - az + n_az) % n_az
            for shift, ref in enumerate(refs):
                here = jnp.logical_and(ahead == shift, opened)
                tables[shift] = jnp.where(sub == jnp.where(here, used[shift], CAX), tile.astype(f32), tables[shift])

                @pl.when(here)
                def _(ref=ref, b=b, tile=tile, shift=shift, slot=used[shift]):
                    for v in range(NV):
                        if shift < 2:
                            at = pl.ds(pl.multiple_of(v * n + tile * CAX, CAX), CAX)
                            ref[at, :] += block(q_ref, v, b)
                        else:
                            at = pl.ds(pl.multiple_of((slot * NV + v) * CAX, CAX), CAX)
                            ref[at, :] = block(q_ref, v, b)

                used[shift] = used[shift] + here.astype(jnp.int32)

            def beside(end, step, row, keep_left, b=b, tile=tile, opened=opened, ahead=ahead):
                @pl.when(jnp.logical_and(opened, tile == end))
                def _():
                    for shift, ref in enumerate(refs):
                        @pl.when(ahead == (shift + step) % n_az)
                        def _(ref=ref, at=beside_at[shift]):
                            for v in range(NV):
                                cell = q_ref[v, pl.ds(row, 1), :]
                                cell = jnp.where(left, cell, 0.0) if keep_left else jnp.where(left, 0.0, cell)
                                ref[pl.ds(at + v, 1), :] += cell

            beside(0, 1, CAX * CAX * b + CAX - 1, True)
            beside(blocks - 1, n_az - 1, CAX * CAX * (b + 1) - 1, False)
        for ref, table in zip(out_refs, tables[1:]):
            ref[pl.ds(ref.shape[0] - CAX, CAX), :] = table


def fill_ghosts(state_ref, lo_ref, hi_ref, ra_refs, rb_refs, high_ref, supply_ref, n_ax):
    _, ax, plen = roles()
    n = state_ref.shape[1] // CAX
    even = ax % 2 == 0
    odd = jnp.logical_not(even)
    cham = plen == 0

    def put(ref, parts):
        size = ref.shape[0] // len(parts)
        for k, part in enumerate(parts):
            ref[pl.ds(k * size, size), :] = part[pl.ds(0, size), :]

    @pl.when(plen == 1)
    def _():
        lo_ref[...] = supply_ref[...]
        hi_ref[...] = high_ref[pl.ds(0, hi_ref.shape[0]), :]

    @pl.when(jnp.logical_and(cham, even))
    def _():
        put(hi_ref, ra_refs)

    @pl.when(jnp.logical_and(cham, odd))
    def _():
        put(lo_ref, ra_refs)

    @pl.when(jnp.logical_and(cham, ax == 0))
    def _():
        lo_ref[...] = jnp.zeros_like(lo_ref)

    @pl.when(jnp.logical_and(cham, jnp.logical_and(even, ax > 0)))
    def _():
        put(lo_ref, rb_refs)

    @pl.when(jnp.logical_and(cham, jnp.logical_and(odd, ax < n_ax - 1)))
    def _():
        put(hi_ref, rb_refs)

    @pl.when(jnp.logical_and(cham, ax == n_ax - 1))
    def _():
        for v in range(NV):
            hi_ref[pl.ds(v * n, n), :] = state_ref[v, pl.ds(CAX - 1, n, stride=CAX), :]


def add_border(v, dst_ref, scale, lo_ref, hi_ref, hl_ref, hr_ref, ul_ref, ur_ref):
    n = dst_ref.shape[1] // CAX
    left = low_half()
    dst_ref[v, pl.ds(0, n, stride=CAX), :] += scale * lo_ref[pl.ds(v * n, n), :]
    dst_ref[v, pl.ds(CAX - 1, n, stride=CAX), :] += scale * hi_ref[pl.ds(v * n, n), :]
    al = scale + scale * pltpu.roll(ul_ref[...], HALF, 1)
    ar = scale - scale * pltpu.roll(ur_ref[...], HALF, 1)
    head = pltpu.roll(hl_ref[pl.ds(v * CAX, CAX), :], HALF, 1)
    tail = pltpu.roll(hr_ref[pl.ds(v * CAX, CAX), :], HALF, 1)
    dst_ref[v, pl.ds(0, CAX), :] += jnp.where(left, al * head, 0.0)
    dst_ref[v, pl.ds((n - 1) * CAX, CAX), :] += jnp.where(left, 0.0, ar * tail)


def mixing(a_ref, mix_ref, pre_ref, heat_ref):
    width = NV * CAX
    col = lax.broadcasted_iota(jnp.int32, (CAX, 3 * width), 1)
    row = lax.broadcasted_iota(jnp.int32, (CAX, 3 * width), 0)
    inner = col % width
    species, lane = inner // CAX, inner % CAX
    for v in range(NV):
        block = jnp.zeros((CAX, 3 * width), f32)
        for k in range(NS):
            value = 0.2 * pre_ref[k] * (mix_ref[v, k] if v < NS else heat_ref[k])
            block = jnp.where(species == k, value, block)
        block = jnp.where(lane == row, block, 0.0)
        high = block.astype(jnp.bfloat16).astype(f32)
        a_ref[pl.ds(v * CAX, CAX), :] = jnp.where(col // width == 1, block - high, high)


def reactions(states, a, power_ref):
    rates = []
    for state in states:
        inv = 1.0 / jnp.maximum(state[NS], 0.5)
        some = [jnp.exp2(power_ref[pl.ds(k * CAX, CAX), :] * inv) * jnp.maximum(state[k], 0.0) for k in range(NS)]
        rates.append(jnp.concatenate(some + [jnp.zeros((CAX, LANES), f32)], axis=0))
    rate = jnp.concatenate(rates, axis=1)
    high = rate.astype(jnp.bfloat16)
    low = (rate - high.astype(f32)).astype(jnp.bfloat16)
    return jnp.dot(a, jnp.concatenate([high, high, low], axis=0), preferred_element_type=f32)


def interior(q_ref, vel_ref, a_ref, power_ref, scale, finish):
    n = q_ref.shape[1] // CAX
    left = low_half()
    sub = lax.broadcasted_iota(jnp.int32, (CAX, LANES), 0)
    bottom, top = sub == 0, sub == CAX - 1
    a = (scale * a_ref[...]).astype(jnp.bfloat16)
    c = 0.1 * scale

    def reg(ref, v, j):
        return ref[v, pl.ds(pl.multiple_of(j * CAX, CAX), CAX), :]

    def column(ref, v, j0):
        regs = [reg(ref, v, j0 + d) for d in range(NJ)]
        before = jnp.where(j0 == 0, 0.0, reg(ref, v, jnp.maximum(j0 - 1, 0)))
        after = jnp.where(j0 + NJ == n, 0.0, reg(ref, v, jnp.minimum(j0 + NJ, n - 1)))
        turned = [pltpu.roll(x, HALF, 1) for x in [before] + regs + [after]]
        lefts = [jnp.where(left, turned[d], turned[d + 1]) for d in range(NJ)]
        rights = [jnp.where(left, turned[d + 1], turned[d + 2]) for d in range(NJ)]
        return regs, lefts, rights

    def body(step, carry):
        j0 = step * NJ
        src = reactions([[reg(q_ref, v, j0 + d) for v in range(NV)] for d in range(NJ)], a, power_ref)
        _, u_left, u_right = column(vel_ref, 0, j0)
        w = [reg(vel_ref, 1, j0 + d) for d in range(NJ)]
        al = [c + c * x for x in u_left]
        ar = [c - c * x for x in u_right]
        wu = [jnp.where(bottom, 0.0, c + c * pltpu.roll(x, 1, 0)) for x in w]
        wd = [jnp.where(top, 0.0, c - c * pltpu.roll(x, CAX - 1, 0)) for x in w]
        for v in range(NV):
            regs, lefts, rights = column(q_ref, v, j0)
            for d in range(NJ):
                vertical = wu[d] * pltpu.roll(regs[d], 1, 0) + wd[d] * pltpu.roll(regs[d], CAX - 1, 0)
                new = (0.6 * scale) * regs[d] + src[v * CAX:(v + 1) * CAX, d * LANES:(d + 1) * LANES]
                finish(j0 + d, v, new + (al[d] * lefts[d] + ar[d] * rights[d]) + vertical)
        return carry

    lax.fori_loop(0, n // NJ, body, 0)


def inside_one_kernel(q_ref, vel_ref, a_ref, power_ref, out_ref):
    def finish(j, v, new):
        out_ref[v, pl.ds(pl.multiple_of(j * CAX, CAX), CAX), :] = new

    interior(q_ref, vel_ref, a_ref, power_ref, 1.0, finish)


def inside_two_kernel(q_ref, q1_ref, vel_ref, a_ref, power_ref, out_ref):
    def finish(j, v, new):
        at = pl.ds(pl.multiple_of(j * CAX, CAX), CAX)
        out_ref[v, at, :] = 0.5 * q_ref[v, at, :] + new

    interior(q1_ref, vel_ref, a_ref, power_ref, 0.5, finish)


def gather_slots(dst_ref, base, got, tables, cap):
    slots = [(k, m) for k in range(len(got)) for m in range(cap)]
    named = [jnp.broadcast_to(tables[k][pl.ds(tables[k].shape[0] - CAX + m, 1), :], (CAX, LANES)) for k, m in slots]
    for v in range(NV):
        blocks = [got[k][pl.ds((m * NV + v) * CAX, CAX), :] for k, m in slots]
        for t in range(CAX):
            at = pl.ds((v * CAX + t) * CAX, CAX)
            total = base(at)
            for name, value in zip(named, blocks):
                total = total + jnp.where(name == t, value, 0.0)
            dst_ref[at, :] = total


def border_one_kernel(n_az, n_ax, n_out, cap, s_in_ref, *rest):
    got, rest = rest[:n_out], rest[n_out:]
    hl_ref, hr_ref, part_ref, q_ref, vel_ref, supply_ref, own_in_ref, col_any, slot_any, open_any = rest[:10]
    out_refs, rest = rest[10:10 + n_out], rest[10 + n_out:]
    (q1_ref, core_ref, z_ref, own_ref, er_ref, el_ref, lo_ref, hi_ref,
     col_ref, slot_ref, open_ref, sems) = rest
    pairs = [(col_any, col_ref), (slot_any, slot_ref), (open_any, open_ref)]
    copies = [pltpu.make_async_copy(x, y, sems.at[k]) for k, (x, y) in enumerate(pairs)]
    for copy in copies:
        copy.start()
    az, _, plen = roles()
    n = q_ref.shape[1] // CAX
    rows = NV * n
    fill_ghosts(q_ref, lo_ref, hi_ref, got[:1], got[1:1 + CAX // cap], s_in_ref, supply_ref, n_ax)
    for v in range(NV):
        q1_ref[v] = part_ref[v]
        add_border(v, q1_ref, 0.1, lo_ref, hi_ref, hl_ref, hr_ref,
                   hl_ref.at[pl.ds(NV * CAX, CAX)], hr_ref.at[pl.ds(NV * CAX, CAX)])
    edges(q1_ref, er_ref, el_ref)
    for copy in copies:
        copy.wait()

    @pl.when(plen == 0)
    def _():
        core_ref[pl.ds(rows, EXT), :] = jnp.zeros((EXT, LANES), f32)
        for v in range(NV):
            core_ref[pl.ds(v * n, n), :] = q1_ref[v, pl.ds(0, n, stride=CAX), :]
        axial_rows(q1_ref, vel_ref, out_refs[:CAX // cap], (z_ref,))

    @pl.when(plen == 1)
    def _():
        gather_slots(core_ref, lambda at: own_in_ref[at, :] + got[0][at, :], got[1:], got[1:], cap)
        beside = own_in_ref[pl.ds(rows, EXT), :]
        for ref in got:
            beside = beside + ref[pl.ds(ref.shape[0] - CAX - EXT, EXT), :]
        core_ref[pl.ds(rows, EXT), :] = beside
        own_ref[...] = jnp.zeros_like(own_ref)
        used = [jnp.int32(0)] * n_out
        for b in range(n // CAX):
            tile = slot_ref[b]
            ahead = (col_ref[b] - az + n_az) % n_az
            opened = open_ref[b] != 0

            @pl.when(jnp.logical_and(opened, ahead == 0))
            def _(b=b, tile=tile):
                for v in range(NV):
                    at = pl.ds(pl.multiple_of(v * n + tile * CAX, CAX), CAX)
                    own_ref[at, :] += block(q1_ref, v, b)

            for k, ref in enumerate(out_refs):
                here = jnp.logical_and(opened, ahead == k + 1)

                @pl.when(here)
                def _(ref=ref, b=b, slot=used[k]):
                    for v in range(NV):
                        at = pl.ds(pl.multiple_of((slot * NV + v) * CAX, CAX), CAX)
                        ref[at, :] = block(q1_ref, v, b)

                used[k] = used[k] + here.astype(jnp.int32)


def tile_kernel(n_out, cap, own_ref, z_ref, *rest):
    got, tables, (step_ref,) = rest[:n_out], rest[n_out:2 * n_out], rest[2 * n_out:]
    _, _, plen = roles()

    @pl.when(plen == 0)
    def _():
        step_ref[...] = z_ref[...]

    @pl.when(plen == 1)
    def _():
        gather_slots(step_ref, lambda at: own_ref[at, :], got, tables, cap)


def add_kernel(*refs):
    refs[-1][...] = sum(ref[...] for ref in refs[:-1])


def inlet_kernel(pair_ref, far_ref, near_ref, dq_ref, out_ref):
    _, ax, plen = roles()
    rows = out_ref.shape[0]
    inlet_side = jnp.logical_and(plen == 0, ax == 0)

    @pl.when(inlet_side)
    def _():
        dq_ref[...] = 0.1 * (far_ref[...] + near_ref[...])
        out_ref[...] = dq_ref[pl.ds(0, rows), :]

    @pl.when(jnp.logical_not(inlet_side))
    def _():
        dq_ref[...] = jnp.zeros_like(dq_ref)
        out_ref[...] = pair_ref[...]


def border_two_kernel(n_ax, n_z, part_ref, q_ref, q1_ref, vel_ref, core_ref, supply_ref, step_ref, dq_ref, hl_ref, hr_ref,
                      hl0_ref, hr0_ref, *rest):
    ra_refs, rest = rest[:n_z], rest[n_z:]
    a_ref, power_ref, out_any, keep_ref, out_ref, lo_ref, hi_ref, sems = rest
    n = out_ref.shape[1] // CAX
    rows = NV * n
    _, ax, plen = roles()
    inlet_side = jnp.logical_and(ax == 0, plen == 0)
    ul_ref, ur_ref = hl0_ref.at[pl.ds(NV * CAX, CAX)], hr0_ref.at[pl.ds(NV * CAX, CAX)]
    fill_ghosts(q1_ref, lo_ref, hi_ref, ra_refs, (step_ref,), core_ref, supply_ref, n_ax)

    @pl.when(inlet_side)
    def _():
        first = lax.broadcasted_iota(jnp.int32, (n, LANES), 0) == 0
        last = lax.broadcasted_iota(jnp.int32, (n, LANES), 0) == n - 1
        left = lax.broadcasted_iota(jnp.int32, (n, LANES), 1) < HALF

        def neighbours(x, head, tail):
            before = jnp.where(first, head, pltpu.roll(x, 1, 0))
            after = jnp.where(last, tail, pltpu.roll(x, n - 1, 0))
            mid = pltpu.roll(x, HALF, 1)
            return (jnp.where(left, pltpu.roll(before, HALF, 1), mid),
                    jnp.where(left, mid, pltpu.roll(after, HALF, 1)))

        u = vel_ref[0, pl.ds(0, n, stride=CAX), :]
        w_next = vel_ref[1, pl.ds(1, n, stride=CAX), :]
        u_left, u_right = neighbours(u, ul_ref[pl.ds(0, 1), :], ur_ref[pl.ds(0, 1), :])
        state = [q1_ref[v, pl.ds(0, n, stride=CAX), :] + dq_ref[pl.ds(v * n, n), :] for v in range(NV)]
        parts = [[x[d * CAX:(d + 1) * CAX] for x in state] for d in range(n // CAX)]
        src = reactions(parts, a_ref[...].astype(jnp.bfloat16), power_ref)
        for v in range(NV):
            beside = dq_ref[pl.ds(rows + v, 1), :]
            q_left, q_right = neighbours(state[v], hl_ref[pl.ds(v * CAX, 1), :] + beside, hr_ref[pl.ds(v * CAX, 1), :] + beside)
            above = (1.0 - w_next) * q1_ref[v, pl.ds(1, n, stride=CAX), :]
            mixed = src[v * CAX:(v + 1) * CAX]
            mixed = jnp.concatenate([mixed[:, d * LANES:(d + 1) * LANES] for d in range(n // CAX)], axis=0)
            new = 0.6 * state[v] + 0.1 * ((1.0 + u_left) * q_left + (1.0 - u_right) * q_right + above) + mixed
            keep_ref[pl.ds(v * n, n), :] = 0.5 * q_ref[v, pl.ds(0, n, stride=CAX), :] + 0.5 * new

    copies = []
    for v in range(NV):
        out_ref[v] = part_ref[v]
        add_border(v, out_ref, 0.05, lo_ref, hi_ref, hl_ref, hr_ref, ul_ref, ur_ref)

        @pl.when(inlet_side)
        def _(v=v):
            w = vel_ref[1, pl.ds(0, n, stride=CAX), :]
            out_ref[v, pl.ds(1, n, stride=CAX), :] += 0.05 * ((1.0 + w) * dq_ref[pl.ds(v * n, n), :])

        @pl.when(plen == 1)
        def _(v=v):
            keep_ref[pl.ds(v * n, n), :] = out_ref[v, pl.ds(CAX - 1, n, stride=CAX), :]

        copies.append(pltpu.make_async_copy(out_ref.at[v], out_any.at[v], sems.at[v]))
        copies[-1].start()
    for copy in copies:
        copy.wait()


def last_kernel(in_any, keep_ref, core_ref, far_ref, out_any, row_ref, sem):
    _, ax, plen = roles()
    n = keep_ref.shape[0] // NV

    def patch(at, value):
        for v in range(NV):
            row_ref[v, :, 0, :] = value(pl.ds(v * n, n))
        copy = pltpu.make_async_copy(row_ref, out_any.at[:, :, pl.ds(at, 1), :], sem)
        copy.start()
        copy.wait()

    @pl.when(jnp.logical_and(ax == 0, plen == 0))
    def _():
        patch(0, lambda at: keep_ref[at, :] + 0.05 * (core_ref[at, :] + far_ref[at, :]))

    @pl.when(jnp.logical_and(ax == 0, plen == 1))
    def _():
        patch(CAX - 1, lambda at: keep_ref[at, :] + 0.05 * core_ref[at, :])


def shape(*dims):
    return jax.ShapeDtypeStruct(dims, f32)


SPACES = {"s": pltpu.SMEM, "v": pltpu.VMEM, "h": pltpu.HBM}


def call(kernel, inputs, kinds, outs, scratch=(), cost=None, to=None, aliases=None):
    return pl.pallas_call(
        kernel,
        in_specs=[pl.BlockSpec(memory_space=SPACES[k]) for k in kinds],
        out_specs=[pl.BlockSpec(memory_space=SPACES[k]) for k in (to or "v" * len(outs))],
        out_shape=outs,
        scratch_shapes=list(scratch),
        cost_estimate=cost,
        input_output_aliases=aliases or {},
        compiler_params=pltpu.CompilerParams(vmem_limit_bytes=LIMIT),
    )(*inputs)


def local(n_az, n_ax, cells, speeds, supply, mix, prefactor, activation, heat, inj_column, inj_slot, inj_open):
    size = cells.shape[-1]
    n = size // LANES
    rows = NV * n

    def view(array):
        k = array.shape[0]
        return array.reshape(k, CAX, n, LANES).transpose(0, 2, 1, 3).reshape(k, CAX * n, LANES)

    def number(i, j, p):
        return (i * n_ax + j) * 2 + p

    every = [(i, j) for i in range(n_az) for j in range(n_ax)]

    def send(x, route):
        return lax.ppermute(x, AXES, [(number(*a), number(*b)) for a, b in route])

    def ring(step):
        return [((i, j, p), ((i + step) % n_az, j, p)) for i, j in every for p in (0, 1)]

    swap = [((i, j, p), (i, j, 1 - p)) for i, j in every for p in (0, 1)]
    n_out = n_az - 1

    def mate(k, j):
        return j ^ 1 if k == 0 else ((j + 1) ^ 1) - 1 if 0 < j < n_ax - 1 else n_ax - 1 - j

    cap = CAX // 4 if n_az > 4 else CAX // 2
    pieces = CAX // cap

    def first(k):
        out = [((i, j, 1), ((i + k + 1) % n_az, j, 1)) for i, j in every]
        for i, j in every:
            along = k == 0 or (k <= pieces and 0 < j < n_ax - 1)
            out.append(((i, j, 0), (i, mate(min(k, 1), j), 0) if along else ((i + k + 1) % n_az, j, 0)))
        return out

    def compact(k):
        out = [((i, j, 1), ((i + k + 1) % n_az, j, 1)) for i, j in every]
        if k < pieces:
            return out + [((i, j, 0), (i, mate(0, j), 0)) for i, j in every]
        return out + [((i, j, 0), ((i + k + 1) % n_az, j, 0)) for i, j in every]

    q, vel = view(cells[0]), view(speeds[0])
    sup = supply.reshape(rows, LANES)
    col, slot, opened = inj_column.reshape(-1), inj_slot, inj_open
    react = (mix, prefactor, activation, heat)
    row, edge = shape(rows, LANES), shape(NV * CAX, LANES)

    whole = shape(*q.shape)
    work = pl.CostEstimate(flops=300 * q.shape[1] * LANES, transcendentals=20 * q.shape[1] * LANES,
                           bytes_accessed=12_000_000)

    raw = tuple(pltpu.with_memory_space_constraint(x, pltpu.HBM) for x in (q, vel, col, slot, opened) + react)
    wide, edge0 = shape(rows + EXT, LANES), shape((NV + 1) * CAX, LANES)
    got = call(functools.partial(first_kernel, n_az, n_out, pieces), raw, "h" * 9,
               [shape(rows + EXT + CAX, LANES)] + [shape(cap * NV * CAX + EXT + CAX, LANES)] * (n_out - 1) + [whole, shape(*vel.shape), row, wide, edge0, edge0,
                                                         shape(NV * CAX, 3 * NV * CAX), shape(NS * CAX, LANES)],
               [pltpu.SMEM(col.shape, jnp.int32)] * 3 + [pltpu.SMEM(x.shape, f32) for x in react]
               + [pltpu.SemaphoreType.DMA((8 + NV // 2,))])
    outs, (qv, velv, s0, own0, er, el, matrix, power) = got[:n_out], got[n_out:]
    ra = [send(x, first(k)) for k, x in enumerate(outs)]
    s0r = send(s0, swap)
    hl0 = send(er, ring(1))
    el, s0r = lax.optimization_barrier((el, s0r))
    hr0 = send(el, ring(-1))
    part, = call(inside_one_kernel, (qv, velv, matrix, power), "vvvv", [whole], cost=work)

    got = call(functools.partial(border_one_kernel, n_az, n_ax, n_out, cap),
               (s0r, *ra, hl0, hr0, part, qv, velv, sup, own0, col, slot, opened),
               "v" * (n_out + 11),
               [shape(cap * NV * CAX, LANES)] * n_out + [whole, wide, row, row, edge, edge],
               [pltpu.VMEM((rows, LANES), f32)] * 2 + [pltpu.SMEM(col.shape, jnp.int32)] * 3
               + [pltpu.SemaphoreType.DMA((3,))])
    outs, (q1, core, z1, own1, er, el) = got[:n_out], got[n_out:]
    down = [((i, j, 1), (i, j - 1, 1)) for i, j in every if j % 2 == 1]
    across = [((i, 2, 1), (i, 0, 0)) for i in range(n_az)]
    inner = [((i, j, 0), (i, mate(1, j), 0)) for i, j in every if 0 < j < n_ax - 1]
    rb = [send(x, compact(k)) for k, x in enumerate(outs)]
    core_in = send(core, swap)
    down0 = send(core, [((i, 2, 1), (i, 1, 0)) for i in range(n_az)])

    part, = call(inside_two_kernel, (qv, q1, velv, matrix, power), "vvvvv", [whole], cost=work)
    part, own1, late, rb = lax.optimization_barrier((part, own1, core, rb))
    down1 = send(late, [((i, 3, 1), (i, 1, 0)) for i in range(n_az)])
    step, = call(functools.partial(tile_kernel, n_out, cap), (own1, z1, *rb, *ra), "v" * (2 + 2 * n_out), [row])
    step_in = send(step, down + inner)
    er, el, core_in, step = lax.optimization_barrier((er, el, core_in, step))
    hl1, hr1 = send(er, ring(1)), send(el, ring(-1))
    pair0, = call(add_kernel, (core_in, down0, down1), "vvv", [wide])
    far0 = send(pair0, [((i, 1, 0), (i, 0, 0)) for i in range(n_az)])
    pair1, = call(add_kernel, (step, step_in), "vv", [row])
    far1 = send(pair1, across)
    pair1, hl1, hr1 = lax.optimization_barrier((pair1, hl1, hr1))

    dq, core2 = call(inlet_kernel, (pair1, far0, pair0), "vvv", [wide, row])
    core2_in = send(core2, swap)
    out, keep = call(functools.partial(border_two_kernel, n_ax, pieces),
                     (part, qv, q1, velv, core_in, sup, step_in, dq, hl1, hr1, hl0, hr0, *rb[:pieces], matrix, power),
                     "v" * (14 + pieces), [whole, row],
                     [pltpu.VMEM(q.shape, f32)] + [pltpu.VMEM((rows, LANES), f32)] * 2 + [pltpu.SemaphoreType.DMA((NV,))],
                     cost=work, to="hv")
    out, = call(last_kernel, (out.reshape(NV, n, CAX, LANES), keep, core2_in, far1), "hvvv", [shape(NV, n, CAX, LANES)],
                [pltpu.VMEM((NV, n, 1, LANES), f32), pltpu.SemaphoreType.DMA(())], to="h", aliases={0: 0})
    return out.transpose(0, 2, 1, 3).reshape(1, NV, CAX, size)


def solution(mesh):
    return jax.shard_map(
        functools.partial(local, mesh.shape["az"], mesh.shape["ax"]),
        mesh=mesh,
        in_specs=(
            P("pl", None, "ax", "az"),
            P("pl", None, "ax", "az"),
            P(None, "ax", "az"),
            P(),
            P(),
            P(),
            P(),
            P(("az", "ax"), None),
            P(("az", "ax")),
            P(("az", "ax")),
        ),
        out_specs=P("pl", None, "ax", "az"),
        check_vma=False,
    )
```

```python
import functools

import jax
import jax.numpy as jnp
from jax import lax
from jax.experimental import pallas as pl
from jax.experimental.pallas import tpu as pltpu
from jax.sharding import PartitionSpec as P

NV = 10
NS = 9
LANES = 128
CAX = 8
HALF = 64
AXES = ("az", "ax", "pl")
NJ = 8
EXT = 16
LOG2E = 1.4426950408889634
LIMIT = 16 * 1024 * 1024

f32 = jnp.float32


def roles():
    return lax.axis_index("az"), lax.axis_index("ax"), lax.axis_index("pl")


def shifts_of(n_az):
    return [n_az // 2] + [s for s in range(1, n_az) if s != n_az // 2]


def low_half():
    return lax.broadcasted_iota(jnp.int32, (CAX, LANES), 1) < HALF


def block(q_ref, v, b):
    return q_ref[v, pl.ds(CAX * CAX * b + CAX - 1, CAX, stride=CAX), :]


def axial_rows(q_ref, vel_ref, first_mate, second_mate):
    _, ax, _ = roles()
    n = q_ref.shape[1] // CAX

    def up(v, at, size):
        rows = pl.ds(CAX * at + CAX - 1, size, stride=CAX)
        return (1.0 + vel_ref[1, rows, :]) * q_ref[v, rows, :]

    def down(v, at, size):
        rows = pl.ds(CAX * at, size, stride=CAX)
        return (1.0 - vel_ref[1, rows, :]) * q_ref[v, rows, :]

    def put(refs, value):
        size = NV * n // len(refs)
        step = min(n, size) if size % n == 0 or n % size == 0 else n // 2
        for k in range(NV * n // step):
            at = k * step
            refs[at // size][pl.ds(at % size, step), :] = value(at // n, at % n, step)

    @pl.when(ax % 2 == 0)
    def _():
        put(first_mate, up)
        put(second_mate, down)

    @pl.when(ax % 2 == 1)
    def _():
        put(first_mate, down)
        put(second_mate, up)


def edges(q_ref, er_ref, el_ref):
    n = q_ref.shape[1] // CAX
    for v in range(NV):
        el_ref[pl.ds(v * CAX, CAX), :] = q_ref[v, pl.ds(0, CAX), :]
        er_ref[pl.ds(v * CAX, CAX), :] = q_ref[v, pl.ds((n - 1) * CAX, CAX), :]


def first_kernel(n_az, n_out, pieces, q_any, vel_any, col_any, slot_any, open_any, mix_any, pre_any, act_any, heat_any, *outs):
    out_refs, rest = outs[:n_out], outs[n_out:]
    (q_ref, vel_ref, s_ref, own_ref, er_ref, el_ref, a_ref, power_ref,
     col_ref, slot_ref, open_ref, mix_ref, pre_ref, act_ref, heat_ref, sems) = rest
    pairs = [(mix_any, mix_ref), (pre_any, pre_ref), (act_any, act_ref), (heat_any, heat_ref),
             (col_any, col_ref), (slot_any, slot_ref), (open_any, open_ref), (vel_any, vel_ref)]
    small = len(pairs) - 1
    pairs += [(q_any.at[pl.ds(v, 2)], q_ref.at[pl.ds(v, 2)]) for v in range(0, NV, 2)]
    copies = [pltpu.make_async_copy(x, y, sems.at[k]) for k, (x, y) in enumerate(pairs)]
    for copy in copies[small:] + copies[:small]:
        copy.start()
    az, _, plen = roles()
    n = q_ref.shape[1] // CAX
    rows = NV * n
    refs = (own_ref,) + tuple(out_refs)
    turns = [0] + shifts_of(n_az)
    beside_at = [rows] + [ref.shape[0] - CAX - EXT for ref in out_refs]

    @pl.when(plen == 1)
    def _():
        for ref in (own_ref, out_refs[0]):
            ref[pl.ds(0, rows), :] = jnp.zeros((rows, LANES), f32)
        for ref, at in zip(refs, beside_at):
            ref[pl.ds(at, EXT), :] = jnp.zeros((EXT, LANES), f32)

    for copy in copies[:small]:
        copy.wait()
    mixing(a_ref, mix_ref, pre_ref, heat_ref)
    for k in range(NS):
        power_ref[pl.ds(k * CAX, CAX), :] = jnp.full((CAX, LANES), act_ref[k] * (-LOG2E), f32)
    for copy in copies[small:]:
        copy.wait()
    edges(q_ref, er_ref, el_ref)
    el_ref[pl.ds(NV * CAX, CAX), :] = vel_ref[0, pl.ds(0, CAX), :]
    er_ref[pl.ds(NV * CAX, CAX), :] = vel_ref[0, pl.ds((n - 1) * CAX, CAX), :]

    @pl.when(plen == 0)
    def _():
        for v in range(NV):
            s_ref[pl.ds(v * n, n), :] = q_ref[v, pl.ds(0, n, stride=CAX), :]
        axial_rows(q_ref, vel_ref, out_refs[:1], out_refs[1:1 + pieces])

    @pl.when(plen == 1)
    def _():
        sub = lax.broadcasted_iota(jnp.int32, (CAX, LANES), 0)
        left = lax.broadcasted_iota(jnp.int32, (1, LANES), 1) < HALF
        blocks = n // CAX
        tables = [jnp.full((CAX, LANES), -1.0, f32)] * n_az
        used = [jnp.int32(0)] * n_az
        for b in range(blocks):
            tile, opened = slot_ref[b], open_ref[b] != 0
            ahead = (col_ref[b] - az + n_az) % n_az
            for shift, (turn, ref) in enumerate(zip(turns, refs)):
                here = jnp.logical_and(ahead == turn, opened)
                tables[shift] = jnp.where(sub == jnp.where(here, used[shift], CAX), tile.astype(f32), tables[shift])

                @pl.when(here)
                def _(ref=ref, b=b, tile=tile, shift=shift, slot=used[shift]):
                    for v in range(NV):
                        if shift < 2:
                            at = pl.ds(pl.multiple_of(v * n + tile * CAX, CAX), CAX)
                            ref[at, :] += block(q_ref, v, b)
                        else:
                            at = pl.ds(pl.multiple_of((slot * NV + v) * CAX, CAX), CAX)
                            ref[at, :] = block(q_ref, v, b)

                used[shift] = used[shift] + here.astype(jnp.int32)

            def beside(end, step, row, keep_left, b=b, tile=tile, opened=opened, ahead=ahead):
                @pl.when(jnp.logical_and(opened, tile == end))
                def _():
                    for shift, (turn, ref) in enumerate(zip(turns, refs)):
                        @pl.when(ahead == (turn + step) % n_az)
                        def _(ref=ref, at=beside_at[shift]):
                            for v in range(NV):
                                cell = q_ref[v, pl.ds(row, 1), :]
                                cell = jnp.where(left, cell, 0.0) if keep_left else jnp.where(left, 0.0, cell)
                                ref[pl.ds(at + v, 1), :] += cell

            beside(0, 1, CAX * CAX * b + CAX - 1, True)
            beside(blocks - 1, n_az - 1, CAX * CAX * (b + 1) - 1, False)
        for ref, table in zip(out_refs, tables[1:]):
            ref[pl.ds(ref.shape[0] - CAX, CAX), :] = table


def fill_ghosts(state_ref, lo_ref, hi_ref, ra_refs, rb_refs, high_ref, supply_ref, n_ax):
    _, ax, plen = roles()
    n = state_ref.shape[1] // CAX
    even = ax % 2 == 0
    odd = jnp.logical_not(even)
    cham = plen == 0

    def put(ref, parts):
        size = ref.shape[0] // len(parts)
        for k, part in enumerate(parts):
            ref[pl.ds(k * size, size), :] = part[pl.ds(0, size), :]

    @pl.when(plen == 1)
    def _():
        lo_ref[...] = supply_ref[...]
        hi_ref[...] = high_ref[pl.ds(0, hi_ref.shape[0]), :]

    @pl.when(jnp.logical_and(cham, even))
    def _():
        put(hi_ref, ra_refs)

    @pl.when(jnp.logical_and(cham, odd))
    def _():
        put(lo_ref, ra_refs)

    @pl.when(jnp.logical_and(cham, ax == 0))
    def _():
        lo_ref[...] = jnp.zeros_like(lo_ref)

    @pl.when(jnp.logical_and(cham, jnp.logical_and(even, ax > 0)))
    def _():
        put(lo_ref, rb_refs)

    @pl.when(jnp.logical_and(cham, jnp.logical_and(odd, ax < n_ax - 1)))
    def _():
        put(hi_ref, rb_refs)

    @pl.when(jnp.logical_and(cham, ax == n_ax - 1))
    def _():
        for v in range(NV):
            hi_ref[pl.ds(v * n, n), :] = state_ref[v, pl.ds(CAX - 1, n, stride=CAX), :]


def add_border(v, dst_ref, scale, lo_ref, hi_ref, hl_ref, hr_ref, ul_ref, ur_ref):
    n = dst_ref.shape[1] // CAX
    left = low_half()
    dst_ref[v, pl.ds(0, n, stride=CAX), :] += scale * lo_ref[pl.ds(v * n, n), :]
    dst_ref[v, pl.ds(CAX - 1, n, stride=CAX), :] += scale * hi_ref[pl.ds(v * n, n), :]
    al = scale + scale * pltpu.roll(ul_ref[...], HALF, 1)
    ar = scale - scale * pltpu.roll(ur_ref[...], HALF, 1)
    head = pltpu.roll(hl_ref[pl.ds(v * CAX, CAX), :], HALF, 1)
    tail = pltpu.roll(hr_ref[pl.ds(v * CAX, CAX), :], HALF, 1)
    dst_ref[v, pl.ds(0, CAX), :] += jnp.where(left, al * head, 0.0)
    dst_ref[v, pl.ds((n - 1) * CAX, CAX), :] += jnp.where(left, 0.0, ar * tail)


def mixing(a_ref, mix_ref, pre_ref, heat_ref):
    width = NV * CAX
    col = lax.broadcasted_iota(jnp.int32, (CAX, 3 * width), 1)
    row = lax.broadcasted_iota(jnp.int32, (CAX, 3 * width), 0)
    inner = col % width
    species, lane = inner // CAX, inner % CAX
    for v in range(NV):
        block = jnp.zeros((CAX, 3 * width), f32)
        for k in range(NS):
            value = 0.2 * pre_ref[k] * (mix_ref[v, k] if v < NS else heat_ref[k])
            block = jnp.where(species == k, value, block)
        block = jnp.where(lane == row, block, 0.0)
        high = block.astype(jnp.bfloat16).astype(f32)
        a_ref[pl.ds(v * CAX, CAX), :] = jnp.where(col // width == 1, block - high, high)


def reactions(states, a, power_ref):
    rates = []
    for state in states:
        inv = 1.0 / jnp.maximum(state[NS], 0.5)
        some = [jnp.exp2(power_ref[pl.ds(k * CAX, CAX), :] * inv) * jnp.maximum(state[k], 0.0) for k in range(NS)]
        rates.append(jnp.concatenate(some + [jnp.zeros((CAX, LANES), f32)], axis=0))
    rate = jnp.concatenate(rates, axis=1)
    high = rate.astype(jnp.bfloat16)
    low = (rate - high.astype(f32)).astype(jnp.bfloat16)
    return jnp.dot(a, jnp.concatenate([high, high, low], axis=0), preferred_element_type=f32)


def interior(q_ref, vel_ref, a_ref, power_ref, scale, finish):
    n = q_ref.shape[1] // CAX
    left = low_half()
    sub = lax.broadcasted_iota(jnp.int32, (CAX, LANES), 0)
    bottom, top = sub == 0, sub == CAX - 1
    a = (scale * a_ref[...]).astype(jnp.bfloat16)
    c = 0.1 * scale

    def reg(ref, v, j):
        return ref[v, pl.ds(pl.multiple_of(j * CAX, CAX), CAX), :]

    def column(ref, v, j0):
        regs = [reg(ref, v, j0 + d) for d in range(NJ)]
        before = jnp.where(j0 == 0, 0.0, reg(ref, v, jnp.maximum(j0 - 1, 0)))
        after = jnp.where(j0 + NJ == n, 0.0, reg(ref, v, jnp.minimum(j0 + NJ, n - 1)))
        turned = [pltpu.roll(x, HALF, 1) for x in [before] + regs + [after]]
        lefts = [jnp.where(left, turned[d], turned[d + 1]) for d in range(NJ)]
        rights = [jnp.where(left, turned[d + 1], turned[d + 2]) for d in range(NJ)]
        return regs, lefts, rights

    def body(step, carry):
        j0 = step * NJ
        src = reactions([[reg(q_ref, v, j0 + d) for v in range(NV)] for d in range(NJ)], a, power_ref)
        _, u_left, u_right = column(vel_ref, 0, j0)
        w = [reg(vel_ref, 1, j0 + d) for d in range(NJ)]
        al = [c + c * x for x in u_left]
        ar = [c - c * x for x in u_right]
        wu = [jnp.where(bottom, 0.0, c + c * pltpu.roll(x, 1, 0)) for x in w]
        wd = [jnp.where(top, 0.0, c - c * pltpu.roll(x, CAX - 1, 0)) for x in w]
        for v in range(NV):
            regs, lefts, rights = column(q_ref, v, j0)
            for d in range(NJ):
                vertical = wu[d] * pltpu.roll(regs[d], 1, 0) + wd[d] * pltpu.roll(regs[d], CAX - 1, 0)
                new = (0.6 * scale) * regs[d] + src[v * CAX:(v + 1) * CAX, d * LANES:(d + 1) * LANES]
                finish(j0 + d, v, new + (al[d] * lefts[d] + ar[d] * rights[d]) + vertical)
        return carry

    lax.fori_loop(0, n // NJ, body, 0)


def inside_one_kernel(q_ref, vel_ref, a_ref, power_ref, out_ref):
    def finish(j, v, new):
        out_ref[v, pl.ds(pl.multiple_of(j * CAX, CAX), CAX), :] = new

    interior(q_ref, vel_ref, a_ref, power_ref, 1.0, finish)


def inside_two_kernel(q_ref, q1_ref, vel_ref, a_ref, power_ref, out_ref):
    def finish(j, v, new):
        at = pl.ds(pl.multiple_of(j * CAX, CAX), CAX)
        out_ref[v, at, :] = 0.5 * q_ref[v, at, :] + new

    interior(q1_ref, vel_ref, a_ref, power_ref, 0.5, finish)


def gather_slots(dst_ref, base, got, tables, cap):
    slots = [(k, m) for k in range(len(got)) for m in range(cap)]
    named = [jnp.broadcast_to(tables[k][pl.ds(tables[k].shape[0] - CAX + m, 1), :], (CAX, LANES)) for k, m in slots]
    for v in range(NV):
        blocks = [got[k][pl.ds((m * NV + v) * CAX, CAX), :] for k, m in slots]
        for t in range(CAX):
            at = pl.ds((v * CAX + t) * CAX, CAX)
            total = base(at)
            for name, value in zip(named, blocks):
                total = total + jnp.where(name == t, value, 0.0)
            dst_ref[at, :] = total


def border_one_kernel(n_az, n_ax, n_out, cap, s_in_ref, *rest):
    got, rest = rest[:n_out], rest[n_out:]
    hl_ref, hr_ref, part_ref, q_ref, vel_ref, supply_ref, own_in_ref, col_any, slot_any, open_any = rest[:10]
    out_refs, rest = rest[10:10 + n_out], rest[10 + n_out:]
    (q1_ref, core_ref, z_ref, own_ref, er_ref, el_ref, lo_ref, hi_ref,
     col_ref, slot_ref, open_ref, sems) = rest
    pairs = [(col_any, col_ref), (slot_any, slot_ref), (open_any, open_ref)]
    copies = [pltpu.make_async_copy(x, y, sems.at[k]) for k, (x, y) in enumerate(pairs)]
    for copy in copies:
        copy.start()
    az, _, plen = roles()
    n = q_ref.shape[1] // CAX
    rows = NV * n
    fill_ghosts(q_ref, lo_ref, hi_ref, got[:1], got[1:1 + CAX // cap], s_in_ref, supply_ref, n_ax)
    for v in range(NV):
        q1_ref[v] = part_ref[v]
        add_border(v, q1_ref, 0.1, lo_ref, hi_ref, hl_ref, hr_ref,
                   hl_ref.at[pl.ds(NV * CAX, CAX)], hr_ref.at[pl.ds(NV * CAX, CAX)])
    edges(q1_ref, er_ref, el_ref)
    for copy in copies:
        copy.wait()

    @pl.when(plen == 0)
    def _():
        core_ref[pl.ds(rows, EXT), :] = jnp.zeros((EXT, LANES), f32)
        for v in range(NV):
            core_ref[pl.ds(v * n, n), :] = q1_ref[v, pl.ds(0, n, stride=CAX), :]
        axial_rows(q1_ref, vel_ref, out_refs[:CAX // cap], (z_ref,))

    @pl.when(plen == 1)
    def _():
        gather_slots(core_ref, lambda at: own_in_ref[at, :] + got[0][at, :], got[1:], got[1:], cap)
        beside = own_in_ref[pl.ds(rows, EXT), :]
        for ref in got:
            beside = beside + ref[pl.ds(ref.shape[0] - CAX - EXT, EXT), :]
        core_ref[pl.ds(rows, EXT), :] = beside
        own_ref[...] = jnp.zeros_like(own_ref)
        used = [jnp.int32(0)] * n_out
        for b in range(n // CAX):
            tile = slot_ref[b]
            ahead = (col_ref[b] - az + n_az) % n_az
            opened = open_ref[b] != 0

            @pl.when(jnp.logical_and(opened, ahead == 0))
            def _(b=b, tile=tile):
                for v in range(NV):
                    at = pl.ds(pl.multiple_of(v * n + tile * CAX, CAX), CAX)
                    own_ref[at, :] += block(q1_ref, v, b)

            for k, ref in enumerate(out_refs):
                here = jnp.logical_and(opened, ahead == shifts_of(n_az)[k])

                @pl.when(here)
                def _(ref=ref, b=b, slot=used[k]):
                    for v in range(NV):
                        at = pl.ds(pl.multiple_of((slot * NV + v) * CAX, CAX), CAX)
                        ref[at, :] = block(q1_ref, v, b)

                used[k] = used[k] + here.astype(jnp.int32)


def tile_kernel(n_out, cap, own_ref, z_ref, *rest):
    got, tables, (step_ref,) = rest[:n_out], rest[n_out:2 * n_out], rest[2 * n_out:]
    _, _, plen = roles()

    @pl.when(plen == 0)
    def _():
        step_ref[...] = z_ref[...]

    @pl.when(plen == 1)
    def _():
        gather_slots(step_ref, lambda at: own_ref[at, :], got, tables, cap)


def add_kernel(*refs):
    refs[-1][...] = sum(ref[...] for ref in refs[:-1])


def inlet_kernel(pair_ref, far_ref, near_ref, dq_ref, out_ref):
    _, ax, plen = roles()
    rows = out_ref.shape[0]
    inlet_side = jnp.logical_and(plen == 0, ax == 0)

    @pl.when(inlet_side)
    def _():
        dq_ref[...] = 0.1 * (far_ref[...] + near_ref[...])
        out_ref[...] = dq_ref[pl.ds(0, rows), :]

    @pl.when(jnp.logical_not(inlet_side))
    def _():
        dq_ref[...] = jnp.zeros_like(dq_ref)
        out_ref[...] = pair_ref[...]


def border_two_kernel(n_ax, n_z, part_ref, q_ref, q1_ref, vel_ref, core_ref, supply_ref, step_ref, dq_ref, hl_ref, hr_ref,
                      hl0_ref, hr0_ref, *rest):
    ra_refs, rest = rest[:n_z], rest[n_z:]
    a_ref, power_ref, out_any, keep_ref, out_ref, lo_ref, hi_ref, sems = rest
    n = out_ref.shape[1] // CAX
    rows = NV * n
    _, ax, plen = roles()
    inlet_side = jnp.logical_and(ax == 0, plen == 0)
    ul_ref, ur_ref = hl0_ref.at[pl.ds(NV * CAX, CAX)], hr0_ref.at[pl.ds(NV * CAX, CAX)]
    fill_ghosts(q1_ref, lo_ref, hi_ref, ra_refs, (step_ref,), core_ref, supply_ref, n_ax)

    @pl.when(inlet_side)
    def _():
        first = lax.broadcasted_iota(jnp.int32, (n, LANES), 0) == 0
        last = lax.broadcasted_iota(jnp.int32, (n, LANES), 0) == n - 1
        left = lax.broadcasted_iota(jnp.int32, (n, LANES), 1) < HALF

        def neighbours(x, head, tail):
            before = jnp.where(first, head, pltpu.roll(x, 1, 0))
            after = jnp.where(last, tail, pltpu.roll(x, n - 1, 0))
            mid = pltpu.roll(x, HALF, 1)
            return (jnp.where(left, pltpu.roll(before, HALF, 1), mid),
                    jnp.where(left, mid, pltpu.roll(after, HALF, 1)))

        u = vel_ref[0, pl.ds(0, n, stride=CAX), :]
        w_next = vel_ref[1, pl.ds(1, n, stride=CAX), :]
        u_left, u_right = neighbours(u, ul_ref[pl.ds(0, 1), :], ur_ref[pl.ds(0, 1), :])
        state = [q1_ref[v, pl.ds(0, n, stride=CAX), :] + dq_ref[pl.ds(v * n, n), :] for v in range(NV)]
        parts = [[x[d * CAX:(d + 1) * CAX] for x in state] for d in range(n // CAX)]
        src = reactions(parts, a_ref[...].astype(jnp.bfloat16), power_ref)
        for v in range(NV):
            beside = dq_ref[pl.ds(rows + v, 1), :]
            q_left, q_right = neighbours(state[v], hl_ref[pl.ds(v * CAX, 1), :] + beside, hr_ref[pl.ds(v * CAX, 1), :] + beside)
            above = (1.0 - w_next) * q1_ref[v, pl.ds(1, n, stride=CAX), :]
            mixed = src[v * CAX:(v + 1) * CAX]
            mixed = jnp.concatenate([mixed[:, d * LANES:(d + 1) * LANES] for d in range(n // CAX)], axis=0)
            new = 0.6 * state[v] + 0.1 * ((1.0 + u_left) * q_left + (1.0 - u_right) * q_right + above) + mixed
            keep_ref[pl.ds(v * n, n), :] = 0.5 * q_ref[v, pl.ds(0, n, stride=CAX), :] + 0.5 * new

    copies = []
    for v in range(NV):
        out_ref[v] = part_ref[v]
        add_border(v, out_ref, 0.05, lo_ref, hi_ref, hl_ref, hr_ref, ul_ref, ur_ref)

        @pl.when(inlet_side)
        def _(v=v):
            w = vel_ref[1, pl.ds(0, n, stride=CAX), :]
            out_ref[v, pl.ds(1, n, stride=CAX), :] += 0.05 * ((1.0 + w) * dq_ref[pl.ds(v * n, n), :])

        @pl.when(plen == 1)
        def _(v=v):
            keep_ref[pl.ds(v * n, n), :] = out_ref[v, pl.ds(CAX - 1, n, stride=CAX), :]

        copies.append(pltpu.make_async_copy(out_ref.at[v], out_any.at[v], sems.at[v]))
        copies[-1].start()
    for copy in copies:
        copy.wait()


def last_kernel(in_any, keep_ref, core_ref, far_ref, out_any, row_ref, sem):
    _, ax, plen = roles()
    n = keep_ref.shape[0] // NV

    def patch(at, value):
        for v in range(NV):
            row_ref[v, :, 0, :] = value(pl.ds(v * n, n))
        copy = pltpu.make_async_copy(row_ref, out_any.at[:, :, pl.ds(at, 1), :], sem)
        copy.start()
        copy.wait()

    @pl.when(jnp.logical_and(ax == 0, plen == 0))
    def _():
        patch(0, lambda at: keep_ref[at, :] + 0.05 * (core_ref[at, :] + far_ref[at, :]))

    @pl.when(jnp.logical_and(ax == 0, plen == 1))
    def _():
        patch(CAX - 1, lambda at: keep_ref[at, :] + 0.05 * core_ref[at, :])


def shape(*dims):
    return jax.ShapeDtypeStruct(dims, f32)


SPACES = {"s": pltpu.SMEM, "v": pltpu.VMEM, "h": pltpu.HBM}


def call(kernel, inputs, kinds, outs, scratch=(), cost=None, to=None, aliases=None):
    return pl.pallas_call(
        kernel,
        in_specs=[pl.BlockSpec(memory_space=SPACES[k]) for k in kinds],
        out_specs=[pl.BlockSpec(memory_space=SPACES[k]) for k in (to or "v" * len(outs))],
        out_shape=outs,
        scratch_shapes=list(scratch),
        cost_estimate=cost,
        input_output_aliases=aliases or {},
        compiler_params=pltpu.CompilerParams(vmem_limit_bytes=LIMIT),
    )(*inputs)


def local(n_az, n_ax, cells, speeds, supply, mix, prefactor, activation, heat, inj_column, inj_slot, inj_open):
    size = cells.shape[-1]
    n = size // LANES
    rows = NV * n

    def view(array):
        k = array.shape[0]
        return array.reshape(k, CAX, n, LANES).transpose(0, 2, 1, 3).reshape(k, CAX * n, LANES)

    def number(i, j, p):
        return (i * n_ax + j) * 2 + p

    every = [(i, j) for i in range(n_az) for j in range(n_ax)]

    def send(x, route):
        return lax.ppermute(x, AXES, [(number(*a), number(*b)) for a, b in route])

    def ring(step):
        return [((i, j, p), ((i + step) % n_az, j, p)) for i, j in every for p in (0, 1)]

    swap = [((i, j, p), (i, j, 1 - p)) for i, j in every for p in (0, 1)]
    n_out = n_az - 1

    def mate(k, j):
        return j ^ 1 if k == 0 else ((j + 1) ^ 1) - 1 if 0 < j < n_ax - 1 else n_ax - 1 - j

    cap = CAX // 4 if n_az > 4 else CAX // 2
    pieces = CAX // cap

    shifts = shifts_of(n_az)

    def first(k):
        out = [((i, j, 1), ((i + shifts[k]) % n_az, j, 1)) for i, j in every]
        for i, j in every:
            inside = 0 < j < n_ax - 1
            if k == 0 or (k <= pieces and (inside or k % 2 == 0)):
                to = (i, mate(min(k, 1), j), 0)
            else:
                to = (i ^ 1, j, 0)
            out.append(((i, j, 0), to))
        return out

    def compact(k):
        out = [((i, j, 1), ((i + shifts[k]) % n_az, j, 1)) for i, j in every]
        return out + [((i, j, 0), (i, mate(0, j), 0) if k < pieces else (i ^ 1, j, 0)) for i, j in every]

    q, vel = view(cells[0]), view(speeds[0])
    sup = supply.reshape(rows, LANES)
    col, slot, opened = inj_column.reshape(-1), inj_slot, inj_open
    react = (mix, prefactor, activation, heat)
    row, edge = shape(rows, LANES), shape(NV * CAX, LANES)

    whole = shape(*q.shape)
    work = pl.CostEstimate(flops=300 * q.shape[1] * LANES, transcendentals=20 * q.shape[1] * LANES,
                           bytes_accessed=12_000_000)

    raw = tuple(pltpu.with_memory_space_constraint(x, pltpu.HBM) for x in (q, vel, col, slot, opened) + react)
    wide, edge0 = shape(rows + EXT, LANES), shape((NV + 1) * CAX, LANES)
    got = call(functools.partial(first_kernel, n_az, n_out, pieces), raw, "h" * 9,
               [shape(rows + EXT + CAX, LANES)] + [shape(cap * NV * CAX + EXT + CAX, LANES)] * (n_out - 1) + [whole, shape(*vel.shape), row, wide, edge0, edge0,
                                                         shape(NV * CAX, 3 * NV * CAX), shape(NS * CAX, LANES)],
               [pltpu.SMEM(col.shape, jnp.int32)] * 3 + [pltpu.SMEM(x.shape, f32) for x in react]
               + [pltpu.SemaphoreType.DMA((8 + NV // 2,))])
    outs, (qv, velv, s0, own0, er, el, matrix, power) = got[:n_out], got[n_out:]
    ra = [send(x, first(k)) for k, x in enumerate(outs)]
    s0r = send(s0, swap)
    hl0 = send(er, ring(1))
    el, s0r = lax.optimization_barrier((el, s0r))
    hr0 = send(el, ring(-1))
    part, = call(inside_one_kernel, (qv, velv, matrix, power), "vvvv", [whole], cost=work)

    got = call(functools.partial(border_one_kernel, n_az, n_ax, n_out, cap),
               (s0r, *ra, hl0, hr0, part, qv, velv, sup, own0, col, slot, opened),
               "v" * (n_out + 11),
               [shape(cap * NV * CAX, LANES)] * n_out + [whole, wide, row, row, edge, edge],
               [pltpu.VMEM((rows, LANES), f32)] * 2 + [pltpu.SMEM(col.shape, jnp.int32)] * 3
               + [pltpu.SemaphoreType.DMA((3,))])
    outs, (q1, core, z1, own1, er, el) = got[:n_out], got[n_out:]
    down = [((i, j, 1), (i, j - 1, 1)) for i, j in every if j % 2 == 1]
    across = [((i, 2, 1), (i, 0, 0)) for i in range(n_az)]
    inner = [((i, j, 0), (i, mate(1, j), 0)) for i, j in every if 0 < j < n_ax - 1]
    rb = [send(x, compact(k)) for k, x in enumerate(outs)]
    core_in = send(core, swap)
    down0 = send(core, [((i, 3, 1), (i, 1, 0)) for i in range(n_az)])

    part, = call(inside_two_kernel, (qv, q1, velv, matrix, power), "vvvvv", [whole], cost=work)
    part, own1, late, rb = lax.optimization_barrier((part, own1, core, rb))
    down1 = send(late, [((i, 2, 1), (i, 1, 0)) for i in range(n_az)])
    step, = call(functools.partial(tile_kernel, n_out, cap), (own1, z1, *rb, *ra), "v" * (2 + 2 * n_out), [row])
    step_in = send(step, down + inner)
    er, el, core_in, step = lax.optimization_barrier((er, el, core_in, step))
    hl1, hr1 = send(er, ring(1)), send(el, ring(-1))
    pair0, = call(add_kernel, (core_in, down0, down1), "vvv", [wide])
    far0 = send(pair0, [((i, 1, 0), (i, 0, 0)) for i in range(n_az)])
    pair1, = call(add_kernel, (step, step_in), "vv", [row])
    far1 = send(pair1, across)
    pair1, hl1, hr1 = lax.optimization_barrier((pair1, hl1, hr1))

    dq, core2 = call(inlet_kernel, (pair1, far0, pair0), "vvv", [wide, row])
    core2_in = send(core2, swap)
    out, keep = call(functools.partial(border_two_kernel, n_ax, pieces),
                     (part, qv, q1, velv, core_in, sup, step_in, dq, hl1, hr1, hl0, hr0, *rb[:pieces], matrix, power),
                     "v" * (14 + pieces), [whole, row],
                     [pltpu.VMEM(q.shape, f32)] + [pltpu.VMEM((rows, LANES), f32)] * 2 + [pltpu.SemaphoreType.DMA((NV,))],
                     cost=work, to="hv")
    out, = call(last_kernel, (out.reshape(NV, n, CAX, LANES), keep, core2_in, far1), "hvvv", [shape(NV, n, CAX, LANES)],
                [pltpu.VMEM((NV, n, 1, LANES), f32), pltpu.SemaphoreType.DMA(())], to="h", aliases={0: 0})
    return out.transpose(0, 2, 1, 3).reshape(1, NV, CAX, size)


def solution(mesh):
    return jax.shard_map(
        functools.partial(local, mesh.shape["az"], mesh.shape["ax"]),
        mesh=mesh,
        in_specs=(
            P("pl", None, "ax", "az"),
            P("pl", None, "ax", "az"),
            P(None, "ax", "az"),
            P(),
            P(),
            P(),
            P(),
            P(("az", "ax"), None),
            P(("az", "ax")),
            P(("az", "ax")),
        ),
        out_specs=P("pl", None, "ax", "az"),
        check_vma=False,
    )
```

```python
import functools

import jax
import jax.numpy as jnp
from jax import lax
from jax.experimental import pallas as pl
from jax.experimental.pallas import tpu as pltpu
from jax.sharding import PartitionSpec as P

NV = 10
NS = 9
LANES = 128
CAX = 8
HALF = 64
AXES = ("az", "ax", "pl")
NJ = 8
EXT = 16
LOG2E = 1.4426950408889634
LIMIT = 16 * 1024 * 1024

f32 = jnp.float32


def roles():
    return lax.axis_index("az"), lax.axis_index("ax"), lax.axis_index("pl")


def shifts_of(n_az):
    return [n_az // 2] + [s for s in range(1, n_az) if s != n_az // 2]


def low_half():
    return lax.broadcasted_iota(jnp.int32, (CAX, LANES), 1) < HALF


def block(q_ref, v, b):
    return q_ref[v, pl.ds(CAX * CAX * b + CAX - 1, CAX, stride=CAX), :]


def axial_rows(q_ref, vel_ref, first_mate, second_mate):
    _, ax, _ = roles()
    n = q_ref.shape[1] // CAX

    def up(v, at, size):
        rows = pl.ds(CAX * at + CAX - 1, size, stride=CAX)
        return (1.0 + vel_ref[1, rows, :]) * q_ref[v, rows, :]

    def down(v, at, size):
        rows = pl.ds(CAX * at, size, stride=CAX)
        return (1.0 - vel_ref[1, rows, :]) * q_ref[v, rows, :]

    def put(refs, value):
        size = NV * n // len(refs)
        step = min(n, size) if size % n == 0 or n % size == 0 else n // 2
        for k in range(NV * n // step):
            at = k * step
            refs[at // size][pl.ds(at % size, step), :] = value(at // n, at % n, step)

    @pl.when(ax % 2 == 0)
    def _():
        put(first_mate, up)
        put(second_mate, down)

    @pl.when(ax % 2 == 1)
    def _():
        put(first_mate, down)
        put(second_mate, up)


def edges(q_ref, er_ref, el_ref):
    n = q_ref.shape[1] // CAX
    for v in range(NV):
        el_ref[pl.ds(v * CAX, CAX), :] = q_ref[v, pl.ds(0, CAX), :]
        er_ref[pl.ds(v * CAX, CAX), :] = q_ref[v, pl.ds((n - 1) * CAX, CAX), :]


def first_kernel(n_az, n_out, pieces, q_any, vel_any, col_any, slot_any, open_any, mix_any, pre_any, act_any, heat_any, *outs):
    out_refs, rest = outs[:n_out], outs[n_out:]
    (q_ref, vel_ref, s_ref, own_ref, er_ref, el_ref, a_ref, power_ref,
     col_ref, slot_ref, open_ref, mix_ref, pre_ref, act_ref, heat_ref, sems) = rest
    pairs = [(mix_any, mix_ref), (pre_any, pre_ref), (act_any, act_ref), (heat_any, heat_ref),
             (col_any, col_ref), (slot_any, slot_ref), (open_any, open_ref), (vel_any, vel_ref)]
    small = len(pairs) - 1
    pairs += [(q_any.at[pl.ds(v, 2)], q_ref.at[pl.ds(v, 2)]) for v in range(0, NV, 2)]
    copies = [pltpu.make_async_copy(x, y, sems.at[k]) for k, (x, y) in enumerate(pairs)]
    for copy in copies[small:] + copies[:small]:
        copy.start()
    az, _, plen = roles()
    n = q_ref.shape[1] // CAX
    rows = NV * n
    refs = (own_ref,) + tuple(out_refs)
    turns = [0] + shifts_of(n_az)
    beside_at = [rows] + [ref.shape[0] - CAX - EXT for ref in out_refs]

    @pl.when(plen == 1)
    def _():
        for ref in (own_ref, out_refs[0]):
            ref[pl.ds(0, rows), :] = jnp.zeros((rows, LANES), f32)
        for ref, at in zip(refs, beside_at):
            ref[pl.ds(at, EXT), :] = jnp.zeros((EXT, LANES), f32)

    for copy in copies[:small]:
        copy.wait()
    mixing(a_ref, mix_ref, pre_ref, heat_ref)
    for k in range(NS):
        power_ref[pl.ds(k * CAX, CAX), :] = jnp.full((CAX, LANES), act_ref[k] * (-LOG2E), f32)
    for copy in copies[small:]:
        copy.wait()
    edges(q_ref, er_ref, el_ref)
    el_ref[pl.ds(NV * CAX, CAX), :] = vel_ref[0, pl.ds(0, CAX), :]
    er_ref[pl.ds(NV * CAX, CAX), :] = vel_ref[0, pl.ds((n - 1) * CAX, CAX), :]

    @pl.when(plen == 0)
    def _():
        for v in range(NV):
            s_ref[pl.ds(v * n, n), :] = q_ref[v, pl.ds(0, n, stride=CAX), :]
        axial_rows(q_ref, vel_ref, out_refs[:1], out_refs[1:1 + pieces])

    @pl.when(plen == 1)
    def _():
        sub = lax.broadcasted_iota(jnp.int32, (CAX, LANES), 0)
        left = lax.broadcasted_iota(jnp.int32, (1, LANES), 1) < HALF
        blocks = n // CAX
        tables = [jnp.full((CAX, LANES), -1.0, f32)] * n_az
        used = [jnp.int32(0)] * n_az
        for b in range(blocks):
            tile, opened = slot_ref[b], open_ref[b] != 0
            ahead = (col_ref[b] - az + n_az) % n_az
            for shift, (turn, ref) in enumerate(zip(turns, refs)):
                here = jnp.logical_and(ahead == turn, opened)
                tables[shift] = jnp.where(sub == jnp.where(here, used[shift], CAX), tile.astype(f32), tables[shift])

                @pl.when(here)
                def _(ref=ref, b=b, tile=tile, shift=shift, slot=used[shift]):
                    for v in range(NV):
                        if shift < 2:
                            at = pl.ds(pl.multiple_of(v * n + tile * CAX, CAX), CAX)
                            ref[at, :] += block(q_ref, v, b)
                        else:
                            at = pl.ds(pl.multiple_of((slot * NV + v) * CAX, CAX), CAX)
                            ref[at, :] = block(q_ref, v, b)

                used[shift] = used[shift] + here.astype(jnp.int32)

            def beside(end, step, row, keep_left, b=b, tile=tile, opened=opened, ahead=ahead):
                @pl.when(jnp.logical_and(opened, tile == end))
                def _():
                    for shift, (turn, ref) in enumerate(zip(turns, refs)):
                        @pl.when(ahead == (turn + step) % n_az)
                        def _(ref=ref, at=beside_at[shift]):
                            for v in range(NV):
                                cell = q_ref[v, pl.ds(row, 1), :]
                                cell = jnp.where(left, cell, 0.0) if keep_left else jnp.where(left, 0.0, cell)
                                ref[pl.ds(at + v, 1), :] += cell

            beside(0, 1, CAX * CAX * b + CAX - 1, True)
            beside(blocks - 1, n_az - 1, CAX * CAX * (b + 1) - 1, False)
        for ref, table in zip(out_refs, tables[1:]):
            ref[pl.ds(ref.shape[0] - CAX, CAX), :] = table


def fill_ghosts(state_ref, lo_ref, hi_ref, ra_refs, rb_refs, high_ref, supply_ref, n_ax):
    _, ax, plen = roles()
    n = state_ref.shape[1] // CAX
    even = ax % 2 == 0
    odd = jnp.logical_not(even)
    cham = plen == 0

    def put(ref, parts):
        size = ref.shape[0] // len(parts)
        for k, part in enumerate(parts):
            ref[pl.ds(k * size, size), :] = part[pl.ds(0, size), :]

    @pl.when(plen == 1)
    def _():
        lo_ref[...] = supply_ref[...]
        hi_ref[...] = high_ref[pl.ds(0, hi_ref.shape[0]), :]

    @pl.when(jnp.logical_and(cham, even))
    def _():
        put(hi_ref, ra_refs)

    @pl.when(jnp.logical_and(cham, odd))
    def _():
        put(lo_ref, ra_refs)

    @pl.when(jnp.logical_and(cham, ax == 0))
    def _():
        lo_ref[...] = jnp.zeros_like(lo_ref)

    @pl.when(jnp.logical_and(cham, jnp.logical_and(even, ax > 0)))
    def _():
        put(lo_ref, rb_refs)

    @pl.when(jnp.logical_and(cham, jnp.logical_and(odd, ax < n_ax - 1)))
    def _():
        put(hi_ref, rb_refs)

    @pl.when(jnp.logical_and(cham, ax == n_ax - 1))
    def _():
        for v in range(NV):
            hi_ref[pl.ds(v * n, n), :] = state_ref[v, pl.ds(CAX - 1, n, stride=CAX), :]


def add_border(v, dst_ref, scale, lo_ref, hi_ref, hl_ref, hr_ref, ul_ref, ur_ref):
    n = dst_ref.shape[1] // CAX
    left = low_half()
    dst_ref[v, pl.ds(0, n, stride=CAX), :] += scale * lo_ref[pl.ds(v * n, n), :]
    dst_ref[v, pl.ds(CAX - 1, n, stride=CAX), :] += scale * hi_ref[pl.ds(v * n, n), :]
    al = scale + scale * pltpu.roll(ul_ref[...], HALF, 1)
    ar = scale - scale * pltpu.roll(ur_ref[...], HALF, 1)
    head = pltpu.roll(hl_ref[pl.ds(v * CAX, CAX), :], HALF, 1)
    tail = pltpu.roll(hr_ref[pl.ds(v * CAX, CAX), :], HALF, 1)
    dst_ref[v, pl.ds(0, CAX), :] += jnp.where(left, al * head, 0.0)
    dst_ref[v, pl.ds((n - 1) * CAX, CAX), :] += jnp.where(left, 0.0, ar * tail)


def mixing(a_ref, mix_ref, pre_ref, heat_ref):
    width = NV * CAX
    col = lax.broadcasted_iota(jnp.int32, (CAX, 3 * width), 1)
    row = lax.broadcasted_iota(jnp.int32, (CAX, 3 * width), 0)
    inner = col % width
    species, lane = inner // CAX, inner % CAX
    for v in range(NV):
        block = jnp.zeros((CAX, 3 * width), f32)
        for k in range(NS):
            value = 0.2 * pre_ref[k] * (mix_ref[v, k] if v < NS else heat_ref[k])
            block = jnp.where(species == k, value, block)
        block = jnp.where(lane == row, block, 0.0)
        high = block.astype(jnp.bfloat16).astype(f32)
        a_ref[pl.ds(v * CAX, CAX), :] = jnp.where(col // width == 1, block - high, high)


def reactions(states, a, power_ref):
    rates = []
    for state in states:
        inv = 1.0 / jnp.maximum(state[NS], 0.5)
        some = [jnp.exp2(power_ref[pl.ds(k * CAX, CAX), :] * inv) * jnp.maximum(state[k], 0.0) for k in range(NS)]
        rates.append(jnp.concatenate(some + [jnp.zeros((CAX, LANES), f32)], axis=0))
    rate = jnp.concatenate(rates, axis=1)
    high = rate.astype(jnp.bfloat16)
    low = (rate - high.astype(f32)).astype(jnp.bfloat16)
    return jnp.dot(a, jnp.concatenate([high, high, low], axis=0), preferred_element_type=f32)


def interior(q_ref, vel_ref, a_ref, power_ref, scale, finish):
    n = q_ref.shape[1] // CAX
    left = low_half()
    sub = lax.broadcasted_iota(jnp.int32, (CAX, LANES), 0)
    bottom, top = sub == 0, sub == CAX - 1
    a = (scale * a_ref[...]).astype(jnp.bfloat16)
    c = 0.1 * scale

    def reg(ref, v, j):
        return ref[v, pl.ds(pl.multiple_of(j * CAX, CAX), CAX), :]

    def column(ref, v, j0):
        regs = [reg(ref, v, j0 + d) for d in range(NJ)]
        before = jnp.where(j0 == 0, 0.0, reg(ref, v, jnp.maximum(j0 - 1, 0)))
        after = jnp.where(j0 + NJ == n, 0.0, reg(ref, v, jnp.minimum(j0 + NJ, n - 1)))
        turned = [pltpu.roll(x, HALF, 1) for x in [before] + regs + [after]]
        lefts = [jnp.where(left, turned[d], turned[d + 1]) for d in range(NJ)]
        rights = [jnp.where(left, turned[d + 1], turned[d + 2]) for d in range(NJ)]
        return regs, lefts, rights

    def body(step, carry):
        j0 = step * NJ
        src = reactions([[reg(q_ref, v, j0 + d) for v in range(NV)] for d in range(NJ)], a, power_ref)
        _, u_left, u_right = column(vel_ref, 0, j0)
        w = [reg(vel_ref, 1, j0 + d) for d in range(NJ)]
        al = [c + c * x for x in u_left]
        ar = [c - c * x for x in u_right]
        wu = [jnp.where(bottom, 0.0, c + c * pltpu.roll(x, 1, 0)) for x in w]
        wd = [jnp.where(top, 0.0, c - c * pltpu.roll(x, CAX - 1, 0)) for x in w]
        for v in range(NV):
            regs, lefts, rights = column(q_ref, v, j0)
            for d in range(NJ):
                vertical = wu[d] * pltpu.roll(regs[d], 1, 0) + wd[d] * pltpu.roll(regs[d], CAX - 1, 0)
                new = (0.6 * scale) * regs[d] + src[v * CAX:(v + 1) * CAX, d * LANES:(d + 1) * LANES]
                finish(j0 + d, v, new + (al[d] * lefts[d] + ar[d] * rights[d]) + vertical)
        return carry

    lax.fori_loop(0, n // NJ, body, 0)


def inside_one_kernel(q_ref, vel_ref, a_ref, power_ref, out_ref):
    def finish(j, v, new):
        out_ref[v, pl.ds(pl.multiple_of(j * CAX, CAX), CAX), :] = new

    interior(q_ref, vel_ref, a_ref, power_ref, 1.0, finish)


def inside_two_kernel(q_ref, q1_ref, vel_ref, a_ref, power_ref, out_ref):
    def finish(j, v, new):
        at = pl.ds(pl.multiple_of(j * CAX, CAX), CAX)
        out_ref[v, at, :] = 0.5 * q_ref[v, at, :] + new

    interior(q1_ref, vel_ref, a_ref, power_ref, 0.5, finish)


def gather_slots(dst_ref, base, got, tables, cap):
    slots = [(k, m) for k in range(len(got)) for m in range(cap)]
    named = [jnp.broadcast_to(tables[k][pl.ds(tables[k].shape[0] - CAX + m, 1), :], (CAX, LANES)) for k, m in slots]
    for v in range(NV):
        blocks = [got[k][pl.ds((m * NV + v) * CAX, CAX), :] for k, m in slots]
        for t in range(CAX):
            at = pl.ds((v * CAX + t) * CAX, CAX)
            total = base(at)
            for name, value in zip(named, blocks):
                total = total + jnp.where(name == t, value, 0.0)
            dst_ref[at, :] = total


def border_one_kernel(n_az, n_ax, n_out, cap, s_in_ref, *rest):
    got, rest = rest[:n_out], rest[n_out:]
    hl_ref, hr_ref, part_ref, q_ref, vel_ref, supply_ref, own_in_ref, col_any, slot_any, open_any = rest[:10]
    out_refs, rest = rest[10:10 + n_out], rest[10 + n_out:]
    (q1_ref, core_ref, z_ref, own_ref, er_ref, el_ref, lo_ref, hi_ref,
     col_ref, slot_ref, open_ref, sems) = rest
    pairs = [(col_any, col_ref), (slot_any, slot_ref), (open_any, open_ref)]
    copies = [pltpu.make_async_copy(x, y, sems.at[k]) for k, (x, y) in enumerate(pairs)]
    for copy in copies:
        copy.start()
    az, _, plen = roles()
    n = q_ref.shape[1] // CAX
    rows = NV * n
    fill_ghosts(q_ref, lo_ref, hi_ref, got[:1], got[1:1 + CAX // cap], s_in_ref, supply_ref, n_ax)
    for v in range(NV):
        q1_ref[v] = part_ref[v]
        add_border(v, q1_ref, 0.1, lo_ref, hi_ref, hl_ref, hr_ref,
                   hl_ref.at[pl.ds(NV * CAX, CAX)], hr_ref.at[pl.ds(NV * CAX, CAX)])
    edges(q1_ref, er_ref, el_ref)
    for copy in copies:
        copy.wait()

    @pl.when(plen == 0)
    def _():
        core_ref[pl.ds(rows, EXT), :] = jnp.zeros((EXT, LANES), f32)
        for v in range(NV):
            core_ref[pl.ds(v * n, n), :] = q1_ref[v, pl.ds(0, n, stride=CAX), :]
        axial_rows(q1_ref, vel_ref, out_refs[:CAX // cap], (z_ref,))

    @pl.when(plen == 1)
    def _():
        gather_slots(core_ref, lambda at: own_in_ref[at, :] + got[0][at, :], got[1:], got[1:], cap)
        beside = own_in_ref[pl.ds(rows, EXT), :]
        for ref in got:
            beside = beside + ref[pl.ds(ref.shape[0] - CAX - EXT, EXT), :]
        core_ref[pl.ds(rows, EXT), :] = beside
        own_ref[...] = jnp.zeros_like(own_ref)
        used = [jnp.int32(0)] * n_out
        for b in range(n // CAX):
            tile = slot_ref[b]
            ahead = (col_ref[b] - az + n_az) % n_az
            opened = open_ref[b] != 0

            @pl.when(jnp.logical_and(opened, ahead == 0))
            def _(b=b, tile=tile):
                for v in range(NV):
                    at = pl.ds(pl.multiple_of(v * n + tile * CAX, CAX), CAX)
                    own_ref[at, :] += block(q1_ref, v, b)

            for k, ref in enumerate(out_refs):
                here = jnp.logical_and(opened, ahead == shifts_of(n_az)[k])

                @pl.when(here)
                def _(ref=ref, b=b, slot=used[k]):
                    for v in range(NV):
                        at = pl.ds(pl.multiple_of((slot * NV + v) * CAX, CAX), CAX)
                        ref[at, :] = block(q1_ref, v, b)

                used[k] = used[k] + here.astype(jnp.int32)


def tile_kernel(n_out, cap, own_ref, z_ref, *rest):
    got, tables, (step_ref,) = rest[:n_out], rest[n_out:2 * n_out], rest[2 * n_out:]
    _, _, plen = roles()

    @pl.when(plen == 0)
    def _():
        step_ref[...] = z_ref[...]

    @pl.when(plen == 1)
    def _():
        gather_slots(step_ref, lambda at: own_ref[at, :], got, tables, cap)


def add_kernel(*refs):
    refs[-1][...] = sum(ref[...] for ref in refs[:-1])


def inlet_kernel(pair_ref, far_ref, near_ref, dq_ref, out_ref):
    _, ax, plen = roles()
    rows = out_ref.shape[0]
    inlet_side = jnp.logical_and(plen == 0, ax == 0)

    @pl.when(inlet_side)
    def _():
        dq_ref[...] = 0.1 * (far_ref[...] + near_ref[...])
        out_ref[...] = dq_ref[pl.ds(0, rows), :]

    @pl.when(jnp.logical_not(inlet_side))
    def _():
        dq_ref[...] = jnp.zeros_like(dq_ref)
        out_ref[...] = pair_ref[...]


def border_two_kernel(n_ax, n_z, part_ref, q_ref, q1_ref, vel_ref, core_ref, supply_ref, step_ref, dq_ref, hl_ref, hr_ref,
                      hl0_ref, hr0_ref, *rest):
    ra_refs, rest = rest[:n_z], rest[n_z:]
    a_ref, power_ref, out_any, keep_ref, out_ref, lo_ref, hi_ref, sems = rest
    n = out_ref.shape[1] // CAX
    rows = NV * n
    _, ax, plen = roles()
    inlet_side = jnp.logical_and(ax == 0, plen == 0)
    ul_ref, ur_ref = hl0_ref.at[pl.ds(NV * CAX, CAX)], hr0_ref.at[pl.ds(NV * CAX, CAX)]
    fill_ghosts(q1_ref, lo_ref, hi_ref, ra_refs, (step_ref,), core_ref, supply_ref, n_ax)

    @pl.when(inlet_side)
    def _():
        first = lax.broadcasted_iota(jnp.int32, (n, LANES), 0) == 0
        last = lax.broadcasted_iota(jnp.int32, (n, LANES), 0) == n - 1
        left = lax.broadcasted_iota(jnp.int32, (n, LANES), 1) < HALF

        def neighbours(x, head, tail):
            before = jnp.where(first, head, pltpu.roll(x, 1, 0))
            after = jnp.where(last, tail, pltpu.roll(x, n - 1, 0))
            mid = pltpu.roll(x, HALF, 1)
            return (jnp.where(left, pltpu.roll(before, HALF, 1), mid),
                    jnp.where(left, mid, pltpu.roll(after, HALF, 1)))

        u = vel_ref[0, pl.ds(0, n, stride=CAX), :]
        w_next = vel_ref[1, pl.ds(1, n, stride=CAX), :]
        u_left, u_right = neighbours(u, ul_ref[pl.ds(0, 1), :], ur_ref[pl.ds(0, 1), :])
        state = [q1_ref[v, pl.ds(0, n, stride=CAX), :] + dq_ref[pl.ds(v * n, n), :] for v in range(NV)]
        parts = [[x[d * CAX:(d + 1) * CAX] for x in state] for d in range(n // CAX)]
        src = reactions(parts, a_ref[...].astype(jnp.bfloat16), power_ref)
        for v in range(NV):
            beside = dq_ref[pl.ds(rows + v, 1), :]
            q_left, q_right = neighbours(state[v], hl_ref[pl.ds(v * CAX, 1), :] + beside, hr_ref[pl.ds(v * CAX, 1), :] + beside)
            above = (1.0 - w_next) * q1_ref[v, pl.ds(1, n, stride=CAX), :]
            mixed = src[v * CAX:(v + 1) * CAX]
            mixed = jnp.concatenate([mixed[:, d * LANES:(d + 1) * LANES] for d in range(n // CAX)], axis=0)
            new = 0.6 * state[v] + 0.1 * ((1.0 + u_left) * q_left + (1.0 - u_right) * q_right + above) + mixed
            keep_ref[pl.ds(v * n, n), :] = 0.5 * q_ref[v, pl.ds(0, n, stride=CAX), :] + 0.5 * new

    copies = []
    for v in range(NV):
        out_ref[v] = part_ref[v]
        add_border(v, out_ref, 0.05, lo_ref, hi_ref, hl_ref, hr_ref, ul_ref, ur_ref)

        @pl.when(inlet_side)
        def _(v=v):
            w = vel_ref[1, pl.ds(0, n, stride=CAX), :]
            out_ref[v, pl.ds(1, n, stride=CAX), :] += 0.05 * ((1.0 + w) * dq_ref[pl.ds(v * n, n), :])

        @pl.when(plen == 1)
        def _(v=v):
            keep_ref[pl.ds(v * n, n), :] = out_ref[v, pl.ds(CAX - 1, n, stride=CAX), :]

        copies.append(pltpu.make_async_copy(out_ref.at[v], out_any.at[v], sems.at[v]))
        copies[-1].start()
    for copy in copies:
        copy.wait()


def last_kernel(in_any, keep_ref, core_ref, far_ref, out_any, row_ref, sem):
    _, ax, plen = roles()
    n = keep_ref.shape[0] // NV

    def patch(at, value):
        for v in range(NV):
            row_ref[v, :, 0, :] = value(pl.ds(v * n, n))
        copy = pltpu.make_async_copy(row_ref, out_any.at[:, :, pl.ds(at, 1), :], sem)
        copy.start()
        copy.wait()

    @pl.when(jnp.logical_and(ax == 0, plen == 0))
    def _():
        patch(0, lambda at: keep_ref[at, :] + 0.05 * (core_ref[at, :] + far_ref[at, :]))

    @pl.when(jnp.logical_and(ax == 0, plen == 1))
    def _():
        patch(CAX - 1, lambda at: keep_ref[at, :] + 0.05 * core_ref[at, :])


def shape(*dims):
    return jax.ShapeDtypeStruct(dims, f32)


SPACES = {"s": pltpu.SMEM, "v": pltpu.VMEM, "h": pltpu.HBM}


def call(kernel, inputs, kinds, outs, scratch=(), cost=None, to=None, aliases=None):
    return pl.pallas_call(
        kernel,
        in_specs=[pl.BlockSpec(memory_space=SPACES[k]) for k in kinds],
        out_specs=[pl.BlockSpec(memory_space=SPACES[k]) for k in (to or "v" * len(outs))],
        out_shape=outs,
        scratch_shapes=list(scratch),
        cost_estimate=cost,
        input_output_aliases=aliases or {},
        compiler_params=pltpu.CompilerParams(vmem_limit_bytes=LIMIT),
    )(*inputs)


def local(n_az, n_ax, cells, speeds, supply, mix, prefactor, activation, heat, inj_column, inj_slot, inj_open):
    size = cells.shape[-1]
    n = size // LANES
    rows = NV * n

    def view(array):
        k = array.shape[0]
        return array.reshape(k, CAX, n, LANES).transpose(0, 2, 1, 3).reshape(k, CAX * n, LANES)

    def number(i, j, p):
        return (i * n_ax + j) * 2 + p

    every = [(i, j) for i in range(n_az) for j in range(n_ax)]

    def send(x, route):
        return lax.ppermute(x, AXES, [(number(*a), number(*b)) for a, b in route])

    def ring(step):
        return [((i, j, p), ((i + step) % n_az, j, p)) for i, j in every for p in (0, 1)]

    swap = [((i, j, p), (i, j, 1 - p)) for i, j in every for p in (0, 1)]
    n_out = n_az - 1

    def mate(k, j):
        return j ^ 1 if k == 0 else ((j + 1) ^ 1) - 1 if 0 < j < n_ax - 1 else n_ax - 1 - j

    cap = CAX // 4 if n_az > 4 else CAX // 2
    pieces = CAX // cap

    shifts = shifts_of(n_az)

    def first(k):
        out = [((i, j, 1), ((i + shifts[k]) % n_az, j, 1)) for i, j in every]
        for i, j in every:
            inside = 0 < j < n_ax - 1
            if k == 0 or (k <= pieces and (inside or k % 2 == 0)):
                to = (i, mate(min(k, 1), j), 0)
            else:
                to = (i ^ 1, j, 0)
            out.append(((i, j, 0), to))
        return out

    def compact(k):
        out = [((i, j, 1), ((i + shifts[k]) % n_az, j, 1)) for i, j in every]
        return out + [((i, j, 0), (i, mate(0, j), 0) if k < pieces else (i ^ 1, j, 0)) for i, j in every]

    q, vel = view(cells[0]), view(speeds[0])
    sup = supply.reshape(rows, LANES)
    col, slot, opened = inj_column.reshape(-1), inj_slot, inj_open
    react = (mix, prefactor, activation, heat)
    row, edge = shape(rows, LANES), shape(NV * CAX, LANES)

    whole = shape(*q.shape)
    work = pl.CostEstimate(flops=300 * q.shape[1] * LANES, transcendentals=20 * q.shape[1] * LANES,
                           bytes_accessed=12_000_000)

    raw = tuple(pltpu.with_memory_space_constraint(x, pltpu.HBM) for x in (q, vel, col, slot, opened) + react)
    wide, edge0 = shape(rows + EXT, LANES), shape((NV + 1) * CAX, LANES)
    got = call(functools.partial(first_kernel, n_az, n_out, pieces), raw, "h" * 9,
               [shape(rows + EXT + CAX, LANES)] + [shape(cap * NV * CAX + EXT + CAX, LANES)] * (n_out - 1) + [whole, shape(*vel.shape), row, wide, edge0, edge0,
                                                         shape(NV * CAX, 3 * NV * CAX), shape(NS * CAX, LANES)],
               [pltpu.SMEM(col.shape, jnp.int32)] * 3 + [pltpu.SMEM(x.shape, f32) for x in react]
               + [pltpu.SemaphoreType.DMA((8 + NV // 2,))])
    outs, (qv, velv, s0, own0, er, el, matrix, power) = got[:n_out], got[n_out:]
    ra = [send(x, first(k)) for k, x in enumerate(outs)]
    s0r = send(s0, swap)
    hl0 = send(er, ring(1))
    el, s0r = lax.optimization_barrier((el, s0r))
    hr0 = send(el, ring(-1))
    part, = call(inside_one_kernel, (qv, velv, matrix, power), "vvvv", [whole], cost=work)

    got = call(functools.partial(border_one_kernel, n_az, n_ax, n_out, cap),
               (s0r, *ra, hl0, hr0, part, qv, velv, sup, own0, col, slot, opened),
               "v" * (n_out + 11),
               [shape(cap * NV * CAX, LANES)] * n_out + [whole, wide, row, row, edge, edge],
               [pltpu.VMEM((rows, LANES), f32)] * 2 + [pltpu.SMEM(col.shape, jnp.int32)] * 3
               + [pltpu.SemaphoreType.DMA((3,))])
    outs, (q1, core, z1, own1, er, el) = got[:n_out], got[n_out:]
    down = [((i, j, 1), (i, j - 1, 1)) for i, j in every if j % 2 == 1]
    across = [((i, 2, 1), (i, 0, 0)) for i in range(n_az)]
    inner = [((i, j, 0), (i, mate(1, j), 0)) for i, j in every if 0 < j < n_ax - 1]
    rb = [send(x, compact(k)) for k, x in enumerate(outs)]
    core_in = send(core, swap)
    down0 = send(core, [((i, j, 1), (i, j - 1, 0)) for i, j in every if j % 2 == 1])

    part, = call(inside_two_kernel, (qv, q1, velv, matrix, power), "vvvvv", [whole], cost=work)
    part, own1 = lax.optimization_barrier((part, own1))
    step, = call(functools.partial(tile_kernel, n_out, cap), (own1, z1, *rb, *ra), "v" * (2 + 2 * n_out), [row])
    step_in = send(step, down + inner)
    er, el, core_in, step = lax.optimization_barrier((er, el, core_in, step))
    hl1, hr1 = send(er, ring(1)), send(el, ring(-1))
    pair0, = call(add_kernel, (core_in, down0), "vv", [wide])
    far0 = send(pair0, [((i, 2, 0), (i, 0, 0)) for i in range(n_az)])
    pair1, = call(add_kernel, (step, step_in), "vv", [row])
    far1 = send(pair1, across)
    pair1, hl1, hr1 = lax.optimization_barrier((pair1, hl1, hr1))

    dq, core2 = call(inlet_kernel, (pair1, far0, pair0), "vvv", [wide, row])
    core2_in = send(core2, swap)
    out, keep = call(functools.partial(border_two_kernel, n_ax, pieces),
                     (part, qv, q1, velv, core_in, sup, step_in, dq, hl1, hr1, hl0, hr0, *rb[:pieces], matrix, power),
                     "v" * (14 + pieces), [whole, row],
                     [pltpu.VMEM(q.shape, f32)] + [pltpu.VMEM((rows, LANES), f32)] * 2 + [pltpu.SemaphoreType.DMA((NV,))],
                     cost=work, to="hv")
    out, = call(last_kernel, (out.reshape(NV, n, CAX, LANES), keep, core2_in, far1), "hvvv", [shape(NV, n, CAX, LANES)],
                [pltpu.VMEM((NV, n, 1, LANES), f32), pltpu.SemaphoreType.DMA(())], to="h", aliases={0: 0})
    return out.transpose(0, 2, 1, 3).reshape(1, NV, CAX, size)


def solution(mesh):
    return jax.shard_map(
        functools.partial(local, mesh.shape["az"], mesh.shape["ax"]),
        mesh=mesh,
        in_specs=(
            P("pl", None, "ax", "az"),
            P("pl", None, "ax", "az"),
            P(None, "ax", "az"),
            P(),
            P(),
            P(),
            P(),
            P(("az", "ax"), None),
            P(("az", "ax")),
            P(("az", "ax")),
        ),
        out_specs=P("pl", None, "ax", "az"),
        check_vma=False,
    )
```

```python
import functools

import jax
import jax.numpy as jnp
from jax import lax
from jax.experimental import pallas as pl
from jax.experimental.pallas import tpu as pltpu
from jax.sharding import PartitionSpec as P

NV = 10
NS = 9
LANES = 128
CAX = 8
HALF = 64
AXES = ("az", "ax", "pl")
NJ = 8
EXT = 16
LOG2E = 1.4426950408889634
LIMIT = 16 * 1024 * 1024

f32 = jnp.float32


def roles():
    return lax.axis_index("az"), lax.axis_index("ax"), lax.axis_index("pl")


def shifts_of(n_az):
    return [n_az // 2] + [s for s in range(1, n_az) if s != n_az // 2]


def low_half():
    return lax.broadcasted_iota(jnp.int32, (CAX, LANES), 1) < HALF


def block(q_ref, v, b):
    return q_ref[v, pl.ds(CAX * CAX * b + CAX - 1, CAX, stride=CAX), :]


def axial_rows(q_ref, vel_ref, first_mate, second_mate):
    _, ax, _ = roles()
    n = q_ref.shape[1] // CAX

    def up(v, at, size):
        rows = pl.ds(CAX * at + CAX - 1, size, stride=CAX)
        return (1.0 + vel_ref[1, rows, :]) * q_ref[v, rows, :]

    def down(v, at, size):
        rows = pl.ds(CAX * at, size, stride=CAX)
        return (1.0 - vel_ref[1, rows, :]) * q_ref[v, rows, :]

    def put(refs, value):
        size = NV * n // len(refs)
        step = min(n, size) if size % n == 0 or n % size == 0 else n // 2
        for k in range(NV * n // step):
            at = k * step
            refs[at // size][pl.ds(at % size, step), :] = value(at // n, at % n, step)

    @pl.when(ax % 2 == 0)
    def _():
        put(first_mate, up)
        put(second_mate, down)

    @pl.when(ax % 2 == 1)
    def _():
        put(first_mate, down)
        put(second_mate, up)


def edges(q_ref, er_ref, el_ref):
    n = q_ref.shape[1] // CAX
    for v in range(NV):
        el_ref[pl.ds(v * CAX, CAX), :] = q_ref[v, pl.ds(0, CAX), :]
        er_ref[pl.ds(v * CAX, CAX), :] = q_ref[v, pl.ds((n - 1) * CAX, CAX), :]


def first_kernel(n_az, n_out, pieces, q_any, vel_any, col_any, slot_any, open_any, mix_any, pre_any, act_any, heat_any, *outs):
    out_refs, rest = outs[:n_out], outs[n_out:]
    (q_ref, vel_ref, s_ref, own_ref, er_ref, el_ref, a_ref, power_ref,
     col_ref, slot_ref, open_ref, mix_ref, pre_ref, act_ref, heat_ref, sems) = rest
    pairs = [(mix_any, mix_ref), (pre_any, pre_ref), (act_any, act_ref), (heat_any, heat_ref),
             (col_any, col_ref), (slot_any, slot_ref), (open_any, open_ref), (vel_any, vel_ref)]
    small = len(pairs) - 1
    pairs += [(q_any.at[pl.ds(v, 2)], q_ref.at[pl.ds(v, 2)]) for v in range(0, NV, 2)]
    copies = [pltpu.make_async_copy(x, y, sems.at[k]) for k, (x, y) in enumerate(pairs)]
    for copy in copies[small:] + copies[:small]:
        copy.start()
    az, _, plen = roles()
    n = q_ref.shape[1] // CAX
    rows = NV * n
    refs = (own_ref,) + tuple(out_refs)
    turns = [0] + shifts_of(n_az)
    beside_at = [rows] + [ref.shape[0] - CAX - EXT for ref in out_refs]

    @pl.when(plen == 1)
    def _():
        for ref in (own_ref, out_refs[0]):
            ref[pl.ds(0, rows), :] = jnp.zeros((rows, LANES), f32)
        for ref, at in zip(refs, beside_at):
            ref[pl.ds(at, EXT), :] = jnp.zeros((EXT, LANES), f32)

    for copy in copies[:small]:
        copy.wait()
    mixing(a_ref, mix_ref, pre_ref, heat_ref)
    for k in range(NS):
        power_ref[pl.ds(k * CAX, CAX), :] = jnp.full((CAX, LANES), act_ref[k] * (-LOG2E), f32)
    for copy in copies[small:]:
        copy.wait()
    edges(q_ref, er_ref, el_ref)
    el_ref[pl.ds(NV * CAX, CAX), :] = vel_ref[0, pl.ds(0, CAX), :]
    er_ref[pl.ds(NV * CAX, CAX), :] = vel_ref[0, pl.ds((n - 1) * CAX, CAX), :]

    @pl.when(plen == 0)
    def _():
        for v in range(NV):
            s_ref[pl.ds(v * n, n), :] = q_ref[v, pl.ds(0, n, stride=CAX), :]
        axial_rows(q_ref, vel_ref, out_refs[:1], out_refs[1:1 + pieces])

    @pl.when(plen == 1)
    def _():
        sub = lax.broadcasted_iota(jnp.int32, (CAX, LANES), 0)
        left = lax.broadcasted_iota(jnp.int32, (1, LANES), 1) < HALF
        blocks = n // CAX
        tables = [jnp.full((CAX, LANES), -1.0, f32)] * n_az
        used = [jnp.int32(0)] * n_az
        for b in range(blocks):
            tile, opened = slot_ref[b], open_ref[b] != 0
            ahead = (col_ref[b] - az + n_az) % n_az
            for shift, (turn, ref) in enumerate(zip(turns, refs)):
                here = jnp.logical_and(ahead == turn, opened)
                tables[shift] = jnp.where(sub == jnp.where(here, used[shift], CAX), tile.astype(f32), tables[shift])

                @pl.when(here)
                def _(ref=ref, b=b, tile=tile, shift=shift, slot=used[shift]):
                    for v in range(NV):
                        if shift < 2:
                            at = pl.ds(pl.multiple_of(v * n + tile * CAX, CAX), CAX)
                            ref[at, :] += block(q_ref, v, b)
                        else:
                            at = pl.ds(pl.multiple_of((slot * NV + v) * CAX, CAX), CAX)
                            ref[at, :] = block(q_ref, v, b)

                used[shift] = used[shift] + here.astype(jnp.int32)

            def beside(end, step, row, keep_left, b=b, tile=tile, opened=opened, ahead=ahead):
                @pl.when(jnp.logical_and(opened, tile == end))
                def _():
                    for shift, (turn, ref) in enumerate(zip(turns, refs)):
                        @pl.when(ahead == (turn + step) % n_az)
                        def _(ref=ref, at=beside_at[shift]):
                            for v in range(NV):
                                cell = q_ref[v, pl.ds(row, 1), :]
                                cell = jnp.where(left, cell, 0.0) if keep_left else jnp.where(left, 0.0, cell)
                                ref[pl.ds(at + v, 1), :] += cell

            beside(0, 1, CAX * CAX * b + CAX - 1, True)
            beside(blocks - 1, n_az - 1, CAX * CAX * (b + 1) - 1, False)
        for ref, table in zip(out_refs, tables[1:]):
            ref[pl.ds(ref.shape[0] - CAX, CAX), :] = table


def fill_ghosts(state_ref, lo_ref, hi_ref, ra_refs, rb_refs, high_ref, supply_ref, n_ax):
    _, ax, plen = roles()
    n = state_ref.shape[1] // CAX
    even = ax % 2 == 0
    odd = jnp.logical_not(even)
    cham = plen == 0

    def put(ref, parts):
        size = ref.shape[0] // len(parts)
        for k, part in enumerate(parts):
            ref[pl.ds(k * size, size), :] = part[pl.ds(0, size), :]

    @pl.when(plen == 1)
    def _():
        lo_ref[...] = supply_ref[...]
        hi_ref[...] = high_ref[pl.ds(0, hi_ref.shape[0]), :]

    @pl.when(jnp.logical_and(cham, even))
    def _():
        put(hi_ref, ra_refs)

    @pl.when(jnp.logical_and(cham, odd))
    def _():
        put(lo_ref, ra_refs)

    @pl.when(jnp.logical_and(cham, ax == 0))
    def _():
        lo_ref[...] = jnp.zeros_like(lo_ref)

    @pl.when(jnp.logical_and(cham, jnp.logical_and(even, ax > 0)))
    def _():
        put(lo_ref, rb_refs)

    @pl.when(jnp.logical_and(cham, jnp.logical_and(odd, ax < n_ax - 1)))
    def _():
        put(hi_ref, rb_refs)

    @pl.when(jnp.logical_and(cham, ax == n_ax - 1))
    def _():
        for v in range(NV):
            hi_ref[pl.ds(v * n, n), :] = state_ref[v, pl.ds(CAX - 1, n, stride=CAX), :]


def add_border(v, dst_ref, scale, lo_ref, hi_ref, hl_ref, hr_ref, ul_ref, ur_ref):
    n = dst_ref.shape[1] // CAX
    left = low_half()
    dst_ref[v, pl.ds(0, n, stride=CAX), :] += scale * lo_ref[pl.ds(v * n, n), :]
    dst_ref[v, pl.ds(CAX - 1, n, stride=CAX), :] += scale * hi_ref[pl.ds(v * n, n), :]
    al = scale + scale * pltpu.roll(ul_ref[...], HALF, 1)
    ar = scale - scale * pltpu.roll(ur_ref[...], HALF, 1)
    head = pltpu.roll(hl_ref[pl.ds(v * CAX, CAX), :], HALF, 1)
    tail = pltpu.roll(hr_ref[pl.ds(v * CAX, CAX), :], HALF, 1)
    dst_ref[v, pl.ds(0, CAX), :] += jnp.where(left, al * head, 0.0)
    dst_ref[v, pl.ds((n - 1) * CAX, CAX), :] += jnp.where(left, 0.0, ar * tail)


def mixing(a_ref, mix_ref, pre_ref, heat_ref):
    width = NV * CAX
    col = lax.broadcasted_iota(jnp.int32, (CAX, 3 * width), 1)
    row = lax.broadcasted_iota(jnp.int32, (CAX, 3 * width), 0)
    inner = col % width
    species, lane = inner // CAX, inner % CAX
    for v in range(NV):
        block = jnp.zeros((CAX, 3 * width), f32)
        for k in range(NS):
            value = 0.2 * pre_ref[k] * (mix_ref[v, k] if v < NS else heat_ref[k])
            block = jnp.where(species == k, value, block)
        block = jnp.where(lane == row, block, 0.0)
        high = block.astype(jnp.bfloat16).astype(f32)
        a_ref[pl.ds(v * CAX, CAX), :] = jnp.where(col // width == 1, block - high, high)


def reactions(states, a, power_ref):
    rates = []
    for state in states:
        inv = 1.0 / jnp.maximum(state[NS], 0.5)
        some = [jnp.exp2(power_ref[pl.ds(k * CAX, CAX), :] * inv) * jnp.maximum(state[k], 0.0) for k in range(NS)]
        rates.append(jnp.concatenate(some + [jnp.zeros((CAX, LANES), f32)], axis=0))
    rate = jnp.concatenate(rates, axis=1)
    high = rate.astype(jnp.bfloat16)
    low = (rate - high.astype(f32)).astype(jnp.bfloat16)
    return jnp.dot(a, jnp.concatenate([high, high, low], axis=0), preferred_element_type=f32)


def interior(q_ref, vel_ref, a_ref, power_ref, scale, finish):
    n = q_ref.shape[1] // CAX
    left = low_half()
    sub = lax.broadcasted_iota(jnp.int32, (CAX, LANES), 0)
    bottom, top = sub == 0, sub == CAX - 1
    a = (scale * a_ref[...]).astype(jnp.bfloat16)
    c = 0.1 * scale

    def reg(ref, v, j):
        return ref[v, pl.ds(pl.multiple_of(j * CAX, CAX), CAX), :]

    def column(ref, v, j0):
        regs = [reg(ref, v, j0 + d) for d in range(NJ)]
        before = jnp.where(j0 == 0, 0.0, reg(ref, v, jnp.maximum(j0 - 1, 0)))
        after = jnp.where(j0 + NJ == n, 0.0, reg(ref, v, jnp.minimum(j0 + NJ, n - 1)))
        turned = [pltpu.roll(x, HALF, 1) for x in [before] + regs + [after]]
        lefts = [jnp.where(left, turned[d], turned[d + 1]) for d in range(NJ)]
        rights = [jnp.where(left, turned[d + 1], turned[d + 2]) for d in range(NJ)]
        return regs, lefts, rights

    def body(step, carry):
        j0 = step * NJ
        src = reactions([[reg(q_ref, v, j0 + d) for v in range(NV)] for d in range(NJ)], a, power_ref)
        _, u_left, u_right = column(vel_ref, 0, j0)
        w = [reg(vel_ref, 1, j0 + d) for d in range(NJ)]
        al = [c + c * x for x in u_left]
        ar = [c - c * x for x in u_right]
        wu = [jnp.where(bottom, 0.0, c + c * pltpu.roll(x, 1, 0)) for x in w]
        wd = [jnp.where(top, 0.0, c - c * pltpu.roll(x, CAX - 1, 0)) for x in w]
        for v in range(NV):
            regs, lefts, rights = column(q_ref, v, j0)
            for d in range(NJ):
                vertical = wu[d] * pltpu.roll(regs[d], 1, 0) + wd[d] * pltpu.roll(regs[d], CAX - 1, 0)
                new = (0.6 * scale) * regs[d] + src[v * CAX:(v + 1) * CAX, d * LANES:(d + 1) * LANES]
                finish(j0 + d, v, new + (al[d] * lefts[d] + ar[d] * rights[d]) + vertical)
        return carry

    lax.fori_loop(0, n // NJ, body, 0)


def inside_one_kernel(q_ref, vel_ref, a_ref, power_ref, out_ref):
    def finish(j, v, new):
        out_ref[v, pl.ds(pl.multiple_of(j * CAX, CAX), CAX), :] = new

    interior(q_ref, vel_ref, a_ref, power_ref, 1.0, finish)


def inside_two_kernel(q_ref, q1_ref, vel_ref, a_ref, power_ref, out_ref):
    def finish(j, v, new):
        at = pl.ds(pl.multiple_of(j * CAX, CAX), CAX)
        out_ref[v, at, :] = 0.5 * q_ref[v, at, :] + new

    interior(q1_ref, vel_ref, a_ref, power_ref, 0.5, finish)


def gather_slots(dst_ref, base, got, tables, cap):
    slots = [(k, m) for k in range(len(got)) for m in range(cap)]
    named = [jnp.broadcast_to(tables[k][pl.ds(tables[k].shape[0] - CAX + m, 1), :], (CAX, LANES)) for k, m in slots]
    for v in range(NV):
        blocks = [got[k][pl.ds((m * NV + v) * CAX, CAX), :] for k, m in slots]
        for t in range(CAX):
            at = pl.ds((v * CAX + t) * CAX, CAX)
            total = base(at)
            for name, value in zip(named, blocks):
                total = total + jnp.where(name == t, value, 0.0)
            dst_ref[at, :] = total


def border_one_kernel(n_az, n_ax, n_out, cap, s_in_ref, *rest):
    got, rest = rest[:n_out], rest[n_out:]
    hl_ref, hr_ref, part_ref, q_ref, vel_ref, supply_ref, own_in_ref, col_any, slot_any, open_any = rest[:10]
    out_refs, rest = rest[10:10 + n_out], rest[10 + n_out:]
    (q1_ref, core_ref, z_ref, own_ref, er_ref, el_ref, lo_ref, hi_ref,
     col_ref, slot_ref, open_ref, sems) = rest
    pairs = [(col_any, col_ref), (slot_any, slot_ref), (open_any, open_ref)]
    copies = [pltpu.make_async_copy(x, y, sems.at[k]) for k, (x, y) in enumerate(pairs)]
    for copy in copies:
        copy.start()
    az, _, plen = roles()
    n = q_ref.shape[1] // CAX
    rows = NV * n
    fill_ghosts(q_ref, lo_ref, hi_ref, got[:1], got[1:1 + CAX // cap], s_in_ref, supply_ref, n_ax)
    for v in range(NV):
        q1_ref[v] = part_ref[v]
        add_border(v, q1_ref, 0.1, lo_ref, hi_ref, hl_ref, hr_ref,
                   hl_ref.at[pl.ds(NV * CAX, CAX)], hr_ref.at[pl.ds(NV * CAX, CAX)])
    edges(q1_ref, er_ref, el_ref)
    for copy in copies:
        copy.wait()

    @pl.when(plen == 0)
    def _():
        core_ref[pl.ds(rows, EXT), :] = jnp.zeros((EXT, LANES), f32)
        for v in range(NV):
            core_ref[pl.ds(v * n, n), :] = q1_ref[v, pl.ds(0, n, stride=CAX), :]
        axial_rows(q1_ref, vel_ref, (z_ref,), out_refs[:CAX // cap])

    @pl.when(plen == 1)
    def _():
        gather_slots(core_ref, lambda at: own_in_ref[at, :] + got[0][at, :], got[1:], got[1:], cap)
        beside = own_in_ref[pl.ds(rows, EXT), :]
        for ref in got:
            beside = beside + ref[pl.ds(ref.shape[0] - CAX - EXT, EXT), :]
        core_ref[pl.ds(rows, EXT), :] = beside
        own_ref[...] = jnp.zeros_like(own_ref)
        used = [jnp.int32(0)] * n_out
        for b in range(n // CAX):
            tile = slot_ref[b]
            ahead = (col_ref[b] - az + n_az) % n_az
            opened = open_ref[b] != 0

            @pl.when(jnp.logical_and(opened, ahead == 0))
            def _(b=b, tile=tile):
                for v in range(NV):
                    at = pl.ds(pl.multiple_of(v * n + tile * CAX, CAX), CAX)
                    own_ref[at, :] += block(q1_ref, v, b)

            for k, ref in enumerate(out_refs):
                here = jnp.logical_and(opened, ahead == shifts_of(n_az)[k])

                @pl.when(here)
                def _(ref=ref, b=b, slot=used[k]):
                    for v in range(NV):
                        at = pl.ds(pl.multiple_of((slot * NV + v) * CAX, CAX), CAX)
                        ref[at, :] = block(q1_ref, v, b)

                used[k] = used[k] + here.astype(jnp.int32)


def tile_kernel(n_out, cap, own_ref, *rest):
    got, tables, (step_ref,) = rest[:n_out], rest[n_out:2 * n_out], rest[2 * n_out:]
    _, _, plen = roles()

    @pl.when(plen == 0)
    def _():
        step_ref[...] = jnp.zeros_like(step_ref)

    @pl.when(plen == 1)
    def _():
        gather_slots(step_ref, lambda at: own_ref[at, :], got, tables, cap)


def add_kernel(*refs):
    refs[-1][...] = sum(ref[...] for ref in refs[:-1])


def inlet_kernel(pair_ref, far_ref, near_ref, dq_ref, out_ref):
    _, ax, plen = roles()
    rows = out_ref.shape[0]
    inlet_side = jnp.logical_and(plen == 0, ax == 0)

    @pl.when(inlet_side)
    def _():
        dq_ref[...] = 0.1 * (far_ref[...] + near_ref[...])
        out_ref[...] = dq_ref[pl.ds(0, rows), :]

    @pl.when(jnp.logical_not(inlet_side))
    def _():
        dq_ref[...] = jnp.zeros_like(dq_ref)
        out_ref[...] = pair_ref[...]


def border_two_kernel(n_ax, n_z, part_ref, q_ref, q1_ref, vel_ref, core_ref, supply_ref, ra_ref, dq_ref, hl_ref, hr_ref,
                      hl0_ref, hr0_ref, *rest):
    rb_refs, rest = rest[:n_z], rest[n_z:]
    a_ref, power_ref, out_any, keep_ref, out_ref, lo_ref, hi_ref, sems = rest
    n = out_ref.shape[1] // CAX
    rows = NV * n
    _, ax, plen = roles()
    inlet_side = jnp.logical_and(ax == 0, plen == 0)
    ul_ref, ur_ref = hl0_ref.at[pl.ds(NV * CAX, CAX)], hr0_ref.at[pl.ds(NV * CAX, CAX)]
    fill_ghosts(q1_ref, lo_ref, hi_ref, (ra_ref,), rb_refs, core_ref, supply_ref, n_ax)

    @pl.when(inlet_side)
    def _():
        first = lax.broadcasted_iota(jnp.int32, (n, LANES), 0) == 0
        last = lax.broadcasted_iota(jnp.int32, (n, LANES), 0) == n - 1
        left = lax.broadcasted_iota(jnp.int32, (n, LANES), 1) < HALF

        def neighbours(x, head, tail):
            before = jnp.where(first, head, pltpu.roll(x, 1, 0))
            after = jnp.where(last, tail, pltpu.roll(x, n - 1, 0))
            mid = pltpu.roll(x, HALF, 1)
            return (jnp.where(left, pltpu.roll(before, HALF, 1), mid),
                    jnp.where(left, mid, pltpu.roll(after, HALF, 1)))

        u = vel_ref[0, pl.ds(0, n, stride=CAX), :]
        w_next = vel_ref[1, pl.ds(1, n, stride=CAX), :]
        u_left, u_right = neighbours(u, ul_ref[pl.ds(0, 1), :], ur_ref[pl.ds(0, 1), :])
        state = [q1_ref[v, pl.ds(0, n, stride=CAX), :] + dq_ref[pl.ds(v * n, n), :] for v in range(NV)]
        parts = [[x[d * CAX:(d + 1) * CAX] for x in state] for d in range(n // CAX)]
        src = reactions(parts, a_ref[...].astype(jnp.bfloat16), power_ref)
        for v in range(NV):
            beside = dq_ref[pl.ds(rows + v, 1), :]
            q_left, q_right = neighbours(state[v], hl_ref[pl.ds(v * CAX, 1), :] + beside, hr_ref[pl.ds(v * CAX, 1), :] + beside)
            above = (1.0 - w_next) * q1_ref[v, pl.ds(1, n, stride=CAX), :]
            mixed = src[v * CAX:(v + 1) * CAX]
            mixed = jnp.concatenate([mixed[:, d * LANES:(d + 1) * LANES] for d in range(n // CAX)], axis=0)
            new = 0.6 * state[v] + 0.1 * ((1.0 + u_left) * q_left + (1.0 - u_right) * q_right + above) + mixed
            keep_ref[pl.ds(v * n, n), :] = 0.5 * q_ref[v, pl.ds(0, n, stride=CAX), :] + 0.5 * new

    copies = []
    for v in range(NV):
        out_ref[v] = part_ref[v]
        add_border(v, out_ref, 0.05, lo_ref, hi_ref, hl_ref, hr_ref, ul_ref, ur_ref)

        @pl.when(inlet_side)
        def _(v=v):
            w = vel_ref[1, pl.ds(0, n, stride=CAX), :]
            out_ref[v, pl.ds(1, n, stride=CAX), :] += 0.05 * ((1.0 + w) * dq_ref[pl.ds(v * n, n), :])

        @pl.when(plen == 1)
        def _(v=v):
            keep_ref[pl.ds(v * n, n), :] = out_ref[v, pl.ds(CAX - 1, n, stride=CAX), :]

        copies.append(pltpu.make_async_copy(out_ref.at[v], out_any.at[v], sems.at[v]))
        copies[-1].start()
    for copy in copies:
        copy.wait()


def last_kernel(in_any, keep_ref, core_ref, far_ref, out_any, row_ref, sem):
    _, ax, plen = roles()
    n = keep_ref.shape[0] // NV

    def patch(at, value):
        for v in range(NV):
            row_ref[v, :, 0, :] = value(pl.ds(v * n, n))
        copy = pltpu.make_async_copy(row_ref, out_any.at[:, :, pl.ds(at, 1), :], sem)
        copy.start()
        copy.wait()

    @pl.when(jnp.logical_and(ax == 0, plen == 0))
    def _():
        patch(0, lambda at: keep_ref[at, :] + 0.05 * (core_ref[at, :] + far_ref[at, :]))

    @pl.when(jnp.logical_and(ax == 0, plen == 1))
    def _():
        patch(CAX - 1, lambda at: keep_ref[at, :] + 0.05 * core_ref[at, :])


def shape(*dims):
    return jax.ShapeDtypeStruct(dims, f32)


SPACES = {"s": pltpu.SMEM, "v": pltpu.VMEM, "h": pltpu.HBM}


def call(kernel, inputs, kinds, outs, scratch=(), cost=None, to=None, aliases=None):
    return pl.pallas_call(
        kernel,
        in_specs=[pl.BlockSpec(memory_space=SPACES[k]) for k in kinds],
        out_specs=[pl.BlockSpec(memory_space=SPACES[k]) for k in (to or "v" * len(outs))],
        out_shape=outs,
        scratch_shapes=list(scratch),
        cost_estimate=cost,
        input_output_aliases=aliases or {},
        compiler_params=pltpu.CompilerParams(vmem_limit_bytes=LIMIT),
    )(*inputs)


def local(n_az, n_ax, cells, speeds, supply, mix, prefactor, activation, heat, inj_column, inj_slot, inj_open):
    size = cells.shape[-1]
    n = size // LANES
    rows = NV * n

    def view(array):
        k = array.shape[0]
        return array.reshape(k, CAX, n, LANES).transpose(0, 2, 1, 3).reshape(k, CAX * n, LANES)

    def number(i, j, p):
        return (i * n_ax + j) * 2 + p

    every = [(i, j) for i in range(n_az) for j in range(n_ax)]

    def send(x, route):
        return lax.ppermute(x, AXES, [(number(*a), number(*b)) for a, b in route])

    def ring(step):
        return [((i, j, p), ((i + step) % n_az, j, p)) for i, j in every for p in (0, 1)]

    swap = [((i, j, p), (i, j, 1 - p)) for i, j in every for p in (0, 1)]
    n_out = n_az - 1

    def mate(k, j):
        return j ^ 1 if k == 0 else ((j + 1) ^ 1) - 1 if 0 < j < n_ax - 1 else n_ax - 1 - j

    cap = CAX // 4 if n_az > 4 else CAX // 2
    pieces = CAX // cap

    shifts = shifts_of(n_az)

    def first(k):
        out = [((i, j, 1), ((i + shifts[k]) % n_az, j, 1)) for i, j in every]
        for i, j in every:
            inside = 0 < j < n_ax - 1
            if k == 0 or (k <= pieces and (inside or k % 2 == 0)):
                to = (i, mate(min(k, 1), j), 0)
            else:
                to = (i ^ 1, j, 0)
            out.append(((i, j, 0), to))
        return out

    def compact(k):
        out = [((i, j, 1), ((i + shifts[k]) % n_az, j, 1)) for i, j in every]
        for i, j in every:
            if k >= pieces or 0 < j < n_ax - 1:
                to = (i, mate(int(k < pieces), j), 0)
            else:
                to = (i ^ (1 if k % 2 == 0 else n_az // 2), j, 0)
            out.append(((i, j, 0), to))
        return out

    q, vel = view(cells[0]), view(speeds[0])
    sup = supply.reshape(rows, LANES)
    col, slot, opened = inj_column.reshape(-1), inj_slot, inj_open
    react = (mix, prefactor, activation, heat)
    row, edge = shape(rows, LANES), shape(NV * CAX, LANES)

    whole = shape(*q.shape)
    work = pl.CostEstimate(flops=300 * q.shape[1] * LANES, transcendentals=20 * q.shape[1] * LANES,
                           bytes_accessed=12_000_000)

    raw = tuple(pltpu.with_memory_space_constraint(x, pltpu.HBM) for x in (q, vel, col, slot, opened) + react)
    wide, edge0 = shape(rows + EXT, LANES), shape((NV + 1) * CAX, LANES)
    got = call(functools.partial(first_kernel, n_az, n_out, pieces), raw, "h" * 9,
               [shape(rows + EXT + CAX, LANES)] + [shape(cap * NV * CAX + EXT + CAX, LANES)] * (n_out - 1) + [whole, shape(*vel.shape), row, wide, edge0, edge0,
                                                         shape(NV * CAX, 3 * NV * CAX), shape(NS * CAX, LANES)],
               [pltpu.SMEM(col.shape, jnp.int32)] * 3 + [pltpu.SMEM(x.shape, f32) for x in react]
               + [pltpu.SemaphoreType.DMA((8 + NV // 2,))])
    outs, (qv, velv, s0, own0, er, el, matrix, power) = got[:n_out], got[n_out:]
    ra = [send(x, first(k)) for k, x in enumerate(outs)]
    s0r = send(s0, swap)
    hl0 = send(er, ring(1))
    el, s0r = lax.optimization_barrier((el, s0r))
    hr0 = send(el, ring(-1))
    part, = call(inside_one_kernel, (qv, velv, matrix, power), "vvvv", [whole], cost=work)

    got = call(functools.partial(border_one_kernel, n_az, n_ax, n_out, cap),
               (s0r, *ra, hl0, hr0, part, qv, velv, sup, own0, col, slot, opened),
               "v" * (n_out + 11),
               [shape(cap * NV * CAX, LANES)] * n_out + [whole, wide, row, row, edge, edge],
               [pltpu.VMEM((rows, LANES), f32)] * 2 + [pltpu.SMEM(col.shape, jnp.int32)] * 3
               + [pltpu.SemaphoreType.DMA((3,))])
    outs, (q1, core, z1, own1, er, el) = got[:n_out], got[n_out:]
    down = [((i, j, 1), (i, j - 1, 1)) for i, j in every if j % 2 == 1]
    across = [((i, 2, 1), (i, 0, 0)) for i in range(n_az)]
    rb = [send(x, compact(k)) for k, x in enumerate(outs)]
    core_in = send(core, swap)
    down0 = send(core, [((i, j, 1), (i, j - 1, 0)) for i, j in every if j % 2 == 1])

    part, = call(inside_two_kernel, (qv, q1, velv, matrix, power), "vvvvv", [whole], cost=work)
    part, own1 = lax.optimization_barrier((part, own1))
    step, = call(functools.partial(tile_kernel, n_out, cap), (own1, *rb, *ra), "v" * (1 + 2 * n_out), [row])
    step_in = send(step, down)
    er, el, core_in, step = lax.optimization_barrier((er, el, core_in, step))
    hl1, hr1 = send(er, ring(1)), send(el, ring(-1))
    pair0, = call(add_kernel, (core_in, down0), "vv", [wide])
    far0 = send(pair0, [((i, 2, 0), (i, 0, 0)) for i in range(n_az)])
    pair1, = call(add_kernel, (step, step_in), "vv", [row])
    far1 = send(pair1, across)
    z1, pair1 = lax.optimization_barrier((z1, pair1))
    z1_in = send(z1, [((i, j, 0), (i, mate(0, j), 0)) for i, j in every])

    dq, core2 = call(inlet_kernel, (pair1, far0, pair0), "vvv", [wide, row])
    core2_in = send(core2, swap)
    out, keep = call(functools.partial(border_two_kernel, n_ax, pieces),
                     (part, qv, q1, velv, core_in, sup, z1_in, dq, hl1, hr1, hl0, hr0, *rb[:pieces], matrix, power),
                     "v" * (14 + pieces), [whole, row],
                     [pltpu.VMEM(q.shape, f32)] + [pltpu.VMEM((rows, LANES), f32)] * 2 + [pltpu.SemaphoreType.DMA((NV,))],
                     cost=work, to="hv")
    out, = call(last_kernel, (out.reshape(NV, n, CAX, LANES), keep, core2_in, far1), "hvvv", [shape(NV, n, CAX, LANES)],
                [pltpu.VMEM((NV, n, 1, LANES), f32), pltpu.SemaphoreType.DMA(())], to="h", aliases={0: 0})
    return out.transpose(0, 2, 1, 3).reshape(1, NV, CAX, size)


def solution(mesh):
    return jax.shard_map(
        functools.partial(local, mesh.shape["az"], mesh.shape["ax"]),
        mesh=mesh,
        in_specs=(
            P("pl", None, "ax", "az"),
            P("pl", None, "ax", "az"),
            P(None, "ax", "az"),
            P(),
            P(),
            P(),
            P(),
            P(("az", "ax"), None),
            P(("az", "ax")),
            P(("az", "ax")),
        ),
        out_specs=P("pl", None, "ax", "az"),
        check_vma=False,
    )
```

```python
import functools

import jax
import jax.numpy as jnp
from jax import lax
from jax.experimental import pallas as pl
from jax.experimental.pallas import tpu as pltpu
from jax.sharding import PartitionSpec as P

NV = 10
NS = 9
LANES = 128
CAX = 8
HALF = 64
AXES = ("az", "ax", "pl")
NJ = 8
EXT = 16
LOG2E = 1.4426950408889634
LIMIT = 16 * 1024 * 1024

f32 = jnp.float32


def roles():
    return lax.axis_index("az"), lax.axis_index("ax"), lax.axis_index("pl")


def shifts_of(n_az):
    return [n_az // 2] + [s for s in range(1, n_az) if s != n_az // 2]


def low_half():
    return lax.broadcasted_iota(jnp.int32, (CAX, LANES), 1) < HALF


def block(q_ref, v, b):
    return q_ref[v, pl.ds(CAX * CAX * b + CAX - 1, CAX, stride=CAX), :]


def axial_rows(q_ref, vel_ref, first_mate, second_mate):
    _, ax, _ = roles()
    n = q_ref.shape[1] // CAX

    def up(v, at, size):
        rows = pl.ds(CAX * at + CAX - 1, size, stride=CAX)
        return (1.0 + vel_ref[1, rows, :]) * q_ref[v, rows, :]

    def down(v, at, size):
        rows = pl.ds(CAX * at, size, stride=CAX)
        return (1.0 - vel_ref[1, rows, :]) * q_ref[v, rows, :]

    def put(refs, value):
        size = NV * n // len(refs)
        step = min(n, size) if size % n == 0 or n % size == 0 else n // 2
        for k in range(NV * n // step):
            at = k * step
            refs[at // size][pl.ds(at % size, step), :] = value(at // n, at % n, step)

    @pl.when(ax % 2 == 0)
    def _():
        put(first_mate, up)
        put(second_mate, down)

    @pl.when(ax % 2 == 1)
    def _():
        put(first_mate, down)
        put(second_mate, up)


def edges(q_ref, er_ref, el_ref):
    n = q_ref.shape[1] // CAX
    for v in range(NV):
        el_ref[pl.ds(v * CAX, CAX), :] = q_ref[v, pl.ds(0, CAX), :]
        er_ref[pl.ds(v * CAX, CAX), :] = q_ref[v, pl.ds((n - 1) * CAX, CAX), :]


def first_kernel(n_az, n_out, pieces, q_any, vel_any, col_any, slot_any, open_any, mix_any, pre_any, act_any, heat_any, *outs):
    out_refs, rest = outs[:n_out], outs[n_out:]
    (q_ref, vel_ref, s_ref, own_ref, er_ref, el_ref, a_ref, power_ref,
     col_ref, slot_ref, open_ref, mix_ref, pre_ref, act_ref, heat_ref, sems) = rest
    pairs = [(mix_any, mix_ref), (pre_any, pre_ref), (act_any, act_ref), (heat_any, heat_ref),
             (col_any, col_ref), (slot_any, slot_ref), (open_any, open_ref), (vel_any, vel_ref)]
    small = len(pairs) - 1
    pairs += [(q_any.at[pl.ds(v, 2)], q_ref.at[pl.ds(v, 2)]) for v in range(0, NV, 2)]
    copies = [pltpu.make_async_copy(x, y, sems.at[k]) for k, (x, y) in enumerate(pairs)]
    for copy in copies[small:] + copies[:small]:
        copy.start()
    az, _, plen = roles()
    n = q_ref.shape[1] // CAX
    rows = NV * n
    refs = (own_ref,) + tuple(out_refs)
    turns = [0] + shifts_of(n_az)
    beside_at = [rows] + [ref.shape[0] - CAX - EXT for ref in out_refs]

    @pl.when(plen == 1)
    def _():
        for ref in (own_ref, out_refs[0]):
            ref[pl.ds(0, rows), :] = jnp.zeros((rows, LANES), f32)
        for ref, at in zip(refs, beside_at):
            ref[pl.ds(at, EXT), :] = jnp.zeros((EXT, LANES), f32)

    for copy in copies[:small]:
        copy.wait()
    mixing(a_ref, mix_ref, pre_ref, heat_ref)
    for k in range(NS):
        power_ref[pl.ds(k * CAX, CAX), :] = jnp.full((CAX, LANES), act_ref[k] * (-LOG2E), f32)
    for copy in copies[small:]:
        copy.wait()
    edges(q_ref, er_ref, el_ref)
    el_ref[pl.ds(NV * CAX, CAX), :] = vel_ref[0, pl.ds(0, CAX), :]
    er_ref[pl.ds(NV * CAX, CAX), :] = vel_ref[0, pl.ds((n - 1) * CAX, CAX), :]

    @pl.when(plen == 0)
    def _():
        for v in range(NV):
            s_ref[pl.ds(v * n, n), :] = q_ref[v, pl.ds(0, n, stride=CAX), :]
        axial_rows(q_ref, vel_ref, out_refs[:1], out_refs[1:1 + pieces])

    @pl.when(plen == 1)
    def _():
        sub = lax.broadcasted_iota(jnp.int32, (CAX, LANES), 0)
        left = lax.broadcasted_iota(jnp.int32, (1, LANES), 1) < HALF
        blocks = n // CAX
        tables = [jnp.full((CAX, LANES), -1.0, f32)] * n_az
        used = [jnp.int32(0)] * n_az
        for b in range(blocks):
            tile, opened = slot_ref[b], open_ref[b] != 0
            ahead = (col_ref[b] - az + n_az) % n_az
            for shift, (turn, ref) in enumerate(zip(turns, refs)):
                here = jnp.logical_and(ahead == turn, opened)
                tables[shift] = jnp.where(sub == jnp.where(here, used[shift], CAX), tile.astype(f32), tables[shift])

                @pl.when(here)
                def _(ref=ref, b=b, tile=tile, shift=shift, slot=used[shift]):
                    for v in range(NV):
                        if shift < 2:
                            at = pl.ds(pl.multiple_of(v * n + tile * CAX, CAX), CAX)
                            ref[at, :] += block(q_ref, v, b)
                        else:
                            at = pl.ds(pl.multiple_of((slot * NV + v) * CAX, CAX), CAX)
                            ref[at, :] = block(q_ref, v, b)

                used[shift] = used[shift] + here.astype(jnp.int32)

            def beside(end, step, row, keep_left, b=b, tile=tile, opened=opened, ahead=ahead):
                @pl.when(jnp.logical_and(opened, tile == end))
                def _():
                    for shift, (turn, ref) in enumerate(zip(turns, refs)):
                        @pl.when(ahead == (turn + step) % n_az)
                        def _(ref=ref, at=beside_at[shift]):
                            for v in range(NV):
                                cell = q_ref[v, pl.ds(row, 1), :]
                                cell = jnp.where(left, cell, 0.0) if keep_left else jnp.where(left, 0.0, cell)
                                ref[pl.ds(at + v, 1), :] += cell

            beside(0, 1, CAX * CAX * b + CAX - 1, True)
            beside(blocks - 1, n_az - 1, CAX * CAX * (b + 1) - 1, False)
        for ref, table in zip(out_refs, tables[1:]):
            ref[pl.ds(ref.shape[0] - CAX, CAX), :] = table


def fill_ghosts(state_ref, lo_ref, hi_ref, ra_refs, rb_refs, high_ref, supply_ref, n_ax):
    _, ax, plen = roles()
    n = state_ref.shape[1] // CAX
    even = ax % 2 == 0
    odd = jnp.logical_not(even)
    cham = plen == 0

    def put(ref, parts):
        size = ref.shape[0] // len(parts)
        for k, part in enumerate(parts):
            ref[pl.ds(k * size, size), :] = part[pl.ds(0, size), :]

    @pl.when(plen == 1)
    def _():
        lo_ref[...] = supply_ref[...]
        hi_ref[...] = high_ref[pl.ds(0, hi_ref.shape[0]), :]

    @pl.when(jnp.logical_and(cham, even))
    def _():
        put(hi_ref, ra_refs)

    @pl.when(jnp.logical_and(cham, odd))
    def _():
        put(lo_ref, ra_refs)

    @pl.when(jnp.logical_and(cham, ax == 0))
    def _():
        lo_ref[...] = jnp.zeros_like(lo_ref)

    @pl.when(jnp.logical_and(cham, jnp.logical_and(even, ax > 0)))
    def _():
        put(lo_ref, rb_refs)

    @pl.when(jnp.logical_and(cham, jnp.logical_and(odd, ax < n_ax - 1)))
    def _():
        put(hi_ref, rb_refs)

    @pl.when(jnp.logical_and(cham, ax == n_ax - 1))
    def _():
        for v in range(NV):
            hi_ref[pl.ds(v * n, n), :] = state_ref[v, pl.ds(CAX - 1, n, stride=CAX), :]


def add_border(v, dst_ref, scale, lo_ref, hi_ref, hl_ref, hr_ref, ul_ref, ur_ref):
    n = dst_ref.shape[1] // CAX
    left = low_half()
    dst_ref[v, pl.ds(0, n, stride=CAX), :] += scale * lo_ref[pl.ds(v * n, n), :]
    dst_ref[v, pl.ds(CAX - 1, n, stride=CAX), :] += scale * hi_ref[pl.ds(v * n, n), :]
    al = scale + scale * pltpu.roll(ul_ref[...], HALF, 1)
    ar = scale - scale * pltpu.roll(ur_ref[...], HALF, 1)
    head = pltpu.roll(hl_ref[pl.ds(v * CAX, CAX), :], HALF, 1)
    tail = pltpu.roll(hr_ref[pl.ds(v * CAX, CAX), :], HALF, 1)
    dst_ref[v, pl.ds(0, CAX), :] += jnp.where(left, al * head, 0.0)
    dst_ref[v, pl.ds((n - 1) * CAX, CAX), :] += jnp.where(left, 0.0, ar * tail)


def mixing(a_ref, mix_ref, pre_ref, heat_ref):
    width = NV * CAX
    col = lax.broadcasted_iota(jnp.int32, (CAX, 3 * width), 1)
    row = lax.broadcasted_iota(jnp.int32, (CAX, 3 * width), 0)
    inner = col % width
    species, lane = inner // CAX, inner % CAX
    for v in range(NV):
        block = jnp.zeros((CAX, 3 * width), f32)
        for k in range(NS):
            value = 0.2 * pre_ref[k] * (mix_ref[v, k] if v < NS else heat_ref[k])
            block = jnp.where(species == k, value, block)
        block = jnp.where(lane == row, block, 0.0)
        high = block.astype(jnp.bfloat16).astype(f32)
        a_ref[pl.ds(v * CAX, CAX), :] = jnp.where(col // width == 1, block - high, high)


def reactions(states, a, power_ref):
    rates = []
    for state in states:
        inv = 1.0 / jnp.maximum(state[NS], 0.5)
        some = [jnp.exp2(power_ref[pl.ds(k * CAX, CAX), :] * inv) * jnp.maximum(state[k], 0.0) for k in range(NS)]
        rates.append(jnp.concatenate(some + [jnp.zeros((CAX, LANES), f32)], axis=0))
    rate = jnp.concatenate(rates, axis=1)
    high = rate.astype(jnp.bfloat16)
    low = (rate - high.astype(f32)).astype(jnp.bfloat16)
    return jnp.dot(a, jnp.concatenate([high, high, low], axis=0), preferred_element_type=f32)


def interior(q_ref, vel_ref, a_ref, power_ref, scale, finish):
    n = q_ref.shape[1] // CAX
    left = low_half()
    sub = lax.broadcasted_iota(jnp.int32, (CAX, LANES), 0)
    bottom, top = sub == 0, sub == CAX - 1
    a = (scale * a_ref[...]).astype(jnp.bfloat16)
    c = 0.1 * scale

    def reg(ref, v, j):
        return ref[v, pl.ds(pl.multiple_of(j * CAX, CAX), CAX), :]

    def column(ref, v, j0):
        regs = [reg(ref, v, j0 + d) for d in range(NJ)]
        before = jnp.where(j0 == 0, 0.0, reg(ref, v, jnp.maximum(j0 - 1, 0)))
        after = jnp.where(j0 + NJ == n, 0.0, reg(ref, v, jnp.minimum(j0 + NJ, n - 1)))
        turned = [pltpu.roll(x, HALF, 1) for x in [before] + regs + [after]]
        lefts = [jnp.where(left, turned[d], turned[d + 1]) for d in range(NJ)]
        rights = [jnp.where(left, turned[d + 1], turned[d + 2]) for d in range(NJ)]
        return regs, lefts, rights

    def body(step, carry):
        j0 = step * NJ
        src = reactions([[reg(q_ref, v, j0 + d) for v in range(NV)] for d in range(NJ)], a, power_ref)
        _, u_left, u_right = column(vel_ref, 0, j0)
        w = [reg(vel_ref, 1, j0 + d) for d in range(NJ)]
        al = [c + c * x for x in u_left]
        ar = [c - c * x for x in u_right]
        wu = [jnp.where(bottom, 0.0, c + c * pltpu.roll(x, 1, 0)) for x in w]
        wd = [jnp.where(top, 0.0, c - c * pltpu.roll(x, CAX - 1, 0)) for x in w]
        for v in range(NV):
            regs, lefts, rights = column(q_ref, v, j0)
            for d in range(NJ):
                vertical = wu[d] * pltpu.roll(regs[d], 1, 0) + wd[d] * pltpu.roll(regs[d], CAX - 1, 0)
                new = (0.6 * scale) * regs[d] + src[v * CAX:(v + 1) * CAX, d * LANES:(d + 1) * LANES]
                finish(j0 + d, v, new + (al[d] * lefts[d] + ar[d] * rights[d]) + vertical)
        return carry

    lax.fori_loop(0, n // NJ, body, 0)


def inside_one_kernel(q_ref, vel_ref, a_ref, power_ref, out_ref):
    def finish(j, v, new):
        out_ref[v, pl.ds(pl.multiple_of(j * CAX, CAX), CAX), :] = new

    interior(q_ref, vel_ref, a_ref, power_ref, 1.0, finish)


def inside_two_kernel(q_ref, q1_ref, vel_ref, a_ref, power_ref, out_ref):
    def finish(j, v, new):
        at = pl.ds(pl.multiple_of(j * CAX, CAX), CAX)
        out_ref[v, at, :] = 0.5 * q_ref[v, at, :] + new

    interior(q1_ref, vel_ref, a_ref, power_ref, 0.5, finish)


def gather_slots(dst_ref, base, got, tables, cap):
    slots = [(k, m) for k in range(len(got)) for m in range(cap)]
    named = [jnp.broadcast_to(tables[k][pl.ds(tables[k].shape[0] - CAX + m, 1), :], (CAX, LANES)) for k, m in slots]
    for v in range(NV):
        blocks = [got[k][pl.ds((m * NV + v) * CAX, CAX), :] for k, m in slots]
        for t in range(CAX):
            at = pl.ds((v * CAX + t) * CAX, CAX)
            total = base(at)
            for name, value in zip(named, blocks):
                total = total + jnp.where(name == t, value, 0.0)
            dst_ref[at, :] = total


def border_one_kernel(n_az, n_ax, n_out, cap, s_in_ref, *rest):
    got, rest = rest[:n_out], rest[n_out:]
    hl_ref, hr_ref, part_ref, q_ref, vel_ref, supply_ref, own_in_ref, col_any, slot_any, open_any = rest[:10]
    out_refs, rest = rest[10:10 + n_out], rest[10 + n_out:]
    (q1_ref, core_ref, z_ref, own_ref, er_ref, el_ref, lo_ref, hi_ref,
     col_ref, slot_ref, open_ref, sems) = rest
    pairs = [(col_any, col_ref), (slot_any, slot_ref), (open_any, open_ref)]
    copies = [pltpu.make_async_copy(x, y, sems.at[k]) for k, (x, y) in enumerate(pairs)]
    for copy in copies:
        copy.start()
    az, _, plen = roles()
    n = q_ref.shape[1] // CAX
    rows = NV * n
    fill_ghosts(q_ref, lo_ref, hi_ref, got[:1], got[1:1 + CAX // cap], s_in_ref, supply_ref, n_ax)
    for v in range(NV):
        q1_ref[v] = part_ref[v]
        add_border(v, q1_ref, 0.1, lo_ref, hi_ref, hl_ref, hr_ref,
                   hl_ref.at[pl.ds(NV * CAX, CAX)], hr_ref.at[pl.ds(NV * CAX, CAX)])
    edges(q1_ref, er_ref, el_ref)
    for copy in copies:
        copy.wait()

    @pl.when(plen == 0)
    def _():
        core_ref[pl.ds(rows, EXT), :] = jnp.zeros((EXT, LANES), f32)
        for v in range(NV):
            core_ref[pl.ds(v * n, n), :] = q1_ref[v, pl.ds(0, n, stride=CAX), :]
        axial_rows(q1_ref, vel_ref, out_refs[:CAX // cap], (z_ref,))

    @pl.when(plen == 1)
    def _():
        gather_slots(core_ref, lambda at: own_in_ref[at, :] + got[0][at, :], got[1:], got[1:], cap)
        beside = own_in_ref[pl.ds(rows, EXT), :]
        for ref in got:
            beside = beside + ref[pl.ds(ref.shape[0] - CAX - EXT, EXT), :]
        core_ref[pl.ds(rows, EXT), :] = beside
        own_ref[...] = jnp.zeros_like(own_ref)
        used = [jnp.int32(0)] * n_out
        for b in range(n // CAX):
            tile = slot_ref[b]
            ahead = (col_ref[b] - az + n_az) % n_az
            opened = open_ref[b] != 0

            @pl.when(jnp.logical_and(opened, ahead == 0))
            def _(b=b, tile=tile):
                for v in range(NV):
                    at = pl.ds(pl.multiple_of(v * n + tile * CAX, CAX), CAX)
                    own_ref[at, :] += block(q1_ref, v, b)

            for k, ref in enumerate(out_refs):
                here = jnp.logical_and(opened, ahead == shifts_of(n_az)[k])

                @pl.when(here)
                def _(ref=ref, b=b, slot=used[k]):
                    for v in range(NV):
                        at = pl.ds(pl.multiple_of((slot * NV + v) * CAX, CAX), CAX)
                        ref[at, :] = block(q1_ref, v, b)

                used[k] = used[k] + here.astype(jnp.int32)


def tile_kernel(n_out, cap, own_ref, z_ref, *rest):
    got, tables, (step_ref,) = rest[:n_out], rest[n_out:2 * n_out], rest[2 * n_out:]
    _, _, plen = roles()

    @pl.when(plen == 0)
    def _():
        step_ref[...] = z_ref[...]

    @pl.when(plen == 1)
    def _():
        gather_slots(step_ref, lambda at: own_ref[at, :], got, tables, cap)


def add_kernel(*refs):
    refs[-1][...] = sum(ref[...] for ref in refs[:-1])


def inlet_kernel(pair_ref, far_ref, near_ref, dq_ref, out_ref):
    _, ax, plen = roles()
    rows = out_ref.shape[0]
    inlet_side = jnp.logical_and(plen == 0, ax == 0)

    @pl.when(inlet_side)
    def _():
        dq_ref[...] = 0.1 * (far_ref[...] + near_ref[...])
        out_ref[...] = dq_ref[pl.ds(0, rows), :]

    @pl.when(jnp.logical_not(inlet_side))
    def _():
        dq_ref[...] = jnp.zeros_like(dq_ref)
        out_ref[...] = pair_ref[...]


def border_two_kernel(n_ax, n_z, part_ref, q_ref, q1_ref, vel_ref, core_ref, supply_ref, step_ref, dq_ref, hl_ref, hr_ref,
                      hl0_ref, hr0_ref, *rest):
    ra_refs, rest = rest[:n_z], rest[n_z:]
    a_ref, power_ref, out_any, keep_ref, out_ref, lo_ref, hi_ref, sems = rest
    n = out_ref.shape[1] // CAX
    rows = NV * n
    _, ax, plen = roles()
    inlet_side = jnp.logical_and(ax == 0, plen == 0)
    ul_ref, ur_ref = hl0_ref.at[pl.ds(NV * CAX, CAX)], hr0_ref.at[pl.ds(NV * CAX, CAX)]
    fill_ghosts(q1_ref, lo_ref, hi_ref, ra_refs, (step_ref,), core_ref, supply_ref, n_ax)

    @pl.when(inlet_side)
    def _():
        first = lax.broadcasted_iota(jnp.int32, (n, LANES), 0) == 0
        last = lax.broadcasted_iota(jnp.int32, (n, LANES), 0) == n - 1
        left = lax.broadcasted_iota(jnp.int32, (n, LANES), 1) < HALF

        def neighbours(x, head, tail):
            before = jnp.where(first, head, pltpu.roll(x, 1, 0))
            after = jnp.where(last, tail, pltpu.roll(x, n - 1, 0))
            mid = pltpu.roll(x, HALF, 1)
            return (jnp.where(left, pltpu.roll(before, HALF, 1), mid),
                    jnp.where(left, mid, pltpu.roll(after, HALF, 1)))

        u = vel_ref[0, pl.ds(0, n, stride=CAX), :]
        w_next = vel_ref[1, pl.ds(1, n, stride=CAX), :]
        u_left, u_right = neighbours(u, ul_ref[pl.ds(0, 1), :], ur_ref[pl.ds(0, 1), :])
        state = [q1_ref[v, pl.ds(0, n, stride=CAX), :] + dq_ref[pl.ds(v * n, n), :] for v in range(NV)]
        parts = [[x[d * CAX:(d + 1) * CAX] for x in state] for d in range(n // CAX)]
        src = reactions(parts, a_ref[...].astype(jnp.bfloat16), power_ref)
        for v in range(NV):
            beside = dq_ref[pl.ds(rows + v, 1), :]
            q_left, q_right = neighbours(state[v], hl_ref[pl.ds(v * CAX, 1), :] + beside, hr_ref[pl.ds(v * CAX, 1), :] + beside)
            above = (1.0 - w_next) * q1_ref[v, pl.ds(1, n, stride=CAX), :]
            mixed = src[v * CAX:(v + 1) * CAX]
            mixed = jnp.concatenate([mixed[:, d * LANES:(d + 1) * LANES] for d in range(n // CAX)], axis=0)
            new = 0.6 * state[v] + 0.1 * ((1.0 + u_left) * q_left + (1.0 - u_right) * q_right + above) + mixed
            keep_ref[pl.ds(v * n, n), :] = 0.5 * q_ref[v, pl.ds(0, n, stride=CAX), :] + 0.5 * new

    copies = []
    for v in range(NV):
        out_ref[v] = part_ref[v]
        add_border(v, out_ref, 0.05, lo_ref, hi_ref, hl_ref, hr_ref, ul_ref, ur_ref)

        @pl.when(inlet_side)
        def _(v=v):
            w = vel_ref[1, pl.ds(0, n, stride=CAX), :]
            out_ref[v, pl.ds(1, n, stride=CAX), :] += 0.05 * ((1.0 + w) * dq_ref[pl.ds(v * n, n), :])

        @pl.when(plen == 1)
        def _(v=v):
            keep_ref[pl.ds(v * n, n), :] = out_ref[v, pl.ds(CAX - 1, n, stride=CAX), :]

        copies.append(pltpu.make_async_copy(out_ref.at[v], out_any.at[v], sems.at[v]))
        copies[-1].start()
    for copy in copies:
        copy.wait()


def last_kernel(in_any, keep_ref, core_ref, far_ref, out_any, row_ref, sem):
    _, ax, plen = roles()
    n = keep_ref.shape[0] // NV

    def patch(at, value):
        for v in range(NV):
            row_ref[v, :, 0, :] = value(pl.ds(v * n, n))
        copy = pltpu.make_async_copy(row_ref, out_any.at[:, :, pl.ds(at, 1), :], sem)
        copy.start()
        copy.wait()

    @pl.when(jnp.logical_and(ax == 0, plen == 0))
    def _():
        patch(0, lambda at: keep_ref[at, :] + 0.05 * (core_ref[at, :] + far_ref[at, :]))

    @pl.when(jnp.logical_and(ax == 0, plen == 1))
    def _():
        patch(CAX - 1, lambda at: keep_ref[at, :] + 0.05 * core_ref[at, :])


def shape(*dims):
    return jax.ShapeDtypeStruct(dims, f32)


SPACES = {"s": pltpu.SMEM, "v": pltpu.VMEM, "h": pltpu.HBM}


def call(kernel, inputs, kinds, outs, scratch=(), cost=None, to=None, aliases=None):
    return pl.pallas_call(
        kernel,
        in_specs=[pl.BlockSpec(memory_space=SPACES[k]) for k in kinds],
        out_specs=[pl.BlockSpec(memory_space=SPACES[k]) for k in (to or "v" * len(outs))],
        out_shape=outs,
        scratch_shapes=list(scratch),
        cost_estimate=cost,
        input_output_aliases=aliases or {},
        compiler_params=pltpu.CompilerParams(vmem_limit_bytes=LIMIT),
    )(*inputs)


def local(n_az, n_ax, cells, speeds, supply, mix, prefactor, activation, heat, inj_column, inj_slot, inj_open):
    size = cells.shape[-1]
    n = size // LANES
    rows = NV * n

    def view(array):
        k = array.shape[0]
        return array.reshape(k, CAX, n, LANES).transpose(0, 2, 1, 3).reshape(k, CAX * n, LANES)

    def number(i, j, p):
        return (i * n_ax + j) * 2 + p

    every = [(i, j) for i in range(n_az) for j in range(n_ax)]

    def send(x, route):
        return lax.ppermute(x, AXES, [(number(*a), number(*b)) for a, b in route])

    def ring(step):
        return [((i, j, p), ((i + step) % n_az, j, p)) for i, j in every for p in (0, 1)]

    swap = [((i, j, p), (i, j, 1 - p)) for i, j in every for p in (0, 1)]
    n_out = n_az - 1

    def mate(k, j):
        return j ^ 1 if k == 0 else ((j + 1) ^ 1) - 1 if 0 < j < n_ax - 1 else n_ax - 1 - j

    cap = CAX // 4 if n_az > 4 else CAX // 2
    pieces = CAX // cap

    shifts = shifts_of(n_az)

    def first(k):
        out = [((i, j, 1), ((i + shifts[k]) % n_az, j, 1)) for i, j in every]
        for i, j in every:
            inside = 0 < j < n_ax - 1
            if k == 0 or (k <= pieces and (inside or k % 2 == 0)):
                to = (i, mate(min(k, 1), j), 0)
            else:
                to = (i ^ 1, j, 0)
            out.append(((i, j, 0), to))
        return out

    def compact(k):
        out = [((i, j, 1), ((i + shifts[k]) % n_az, j, 1)) for i, j in every]
        return out + [((i, j, 0), (i, mate(0, j), 0) if k < pieces else (i ^ 1, j, 0)) for i, j in every]

    q, vel = view(cells[0]), view(speeds[0])
    sup = supply.reshape(rows, LANES)
    col, slot, opened = inj_column.reshape(-1), inj_slot, inj_open
    react = (mix, prefactor, activation, heat)
    row, edge = shape(rows, LANES), shape(NV * CAX, LANES)

    whole = shape(*q.shape)
    work = pl.CostEstimate(flops=300 * q.shape[1] * LANES, transcendentals=20 * q.shape[1] * LANES,
                           bytes_accessed=12_000_000)

    raw = tuple(pltpu.with_memory_space_constraint(x, pltpu.HBM) for x in (q, vel, col, slot, opened) + react)
    wide, edge0 = shape(rows + EXT, LANES), shape((NV + 1) * CAX, LANES)
    got = call(functools.partial(first_kernel, n_az, n_out, pieces), raw, "h" * 9,
               [shape(rows + EXT + CAX, LANES)] + [shape(cap * NV * CAX + EXT + CAX, LANES)] * (n_out - 1) + [whole, shape(*vel.shape), row, wide, edge0, edge0,
                                                         shape(NV * CAX, 3 * NV * CAX), shape(NS * CAX, LANES)],
               [pltpu.SMEM(col.shape, jnp.int32)] * 3 + [pltpu.SMEM(x.shape, f32) for x in react]
               + [pltpu.SemaphoreType.DMA((8 + NV // 2,))])
    outs, (qv, velv, s0, own0, er, el, matrix, power) = got[:n_out], got[n_out:]
    ra = [send(x, first(k)) for k, x in enumerate(outs)]
    s0r = send(s0, swap)
    hl0 = send(er, ring(1))
    el, s0r = lax.optimization_barrier((el, s0r))
    hr0 = send(el, ring(-1))
    part, = call(inside_one_kernel, (qv, velv, matrix, power), "vvvv", [whole], cost=work)

    got = call(functools.partial(border_one_kernel, n_az, n_ax, n_out, cap),
               (s0r, *ra, hl0, hr0, part, qv, velv, sup, own0, col, slot, opened),
               "v" * (n_out + 11),
               [shape(cap * NV * CAX, LANES)] * n_out + [whole, wide, row, row, edge, edge],
               [pltpu.VMEM((rows, LANES), f32)] * 2 + [pltpu.SMEM(col.shape, jnp.int32)] * 3
               + [pltpu.SemaphoreType.DMA((3,))])
    outs, (q1, core, z1, own1, er, el) = got[:n_out], got[n_out:]
    down = [((i, j, 1), (i, j - 1, 1)) for i, j in every if j % 2 == 1]
    across = [((i, 2, 1), (i, 0, 0)) for i in range(n_az)]
    inner = [((i, j, 0), (i, mate(1, j), 0)) for i, j in every if 0 < j < n_ax - 1]
    rb = [send(x, compact(k)) for k, x in enumerate(outs)]
    core_in = send(core, swap)
    down0, down1 = [send(core, [((i, j, 1), (i, 1, 0)) for i in range(n_az)]) for j in (3, 2)]

    part, = call(inside_two_kernel, (qv, q1, velv, matrix, power), "vvvvv", [whole], cost=work)
    part, own1 = lax.optimization_barrier((part, own1))
    step, = call(functools.partial(tile_kernel, n_out, cap), (own1, z1, *rb, *ra), "v" * (2 + 2 * n_out), [row])
    step_in = send(step, down + inner)
    er, el, core_in, step = lax.optimization_barrier((er, el, core_in, step))
    hl1, hr1 = send(er, ring(1)), send(el, ring(-1))
    pair0, = call(add_kernel, (core_in, down0, down1), "vvv", [wide])
    far0 = send(pair0, [((i, 1, 0), (i, 0, 0)) for i in range(n_az)])
    pair1, = call(add_kernel, (step, step_in), "vv", [row])
    far1 = send(pair1, across)
    pair1, hl1, hr1 = lax.optimization_barrier((pair1, hl1, hr1))

    dq, core2 = call(inlet_kernel, (pair1, far0, pair0), "vvv", [wide, row])
    core2_in = send(core2, swap)
    out, keep = call(functools.partial(border_two_kernel, n_ax, pieces),
                     (part, qv, q1, velv, core_in, sup, step_in, dq, hl1, hr1, hl0, hr0, *rb[:pieces], matrix, power),
                     "v" * (14 + pieces), [whole, row],
                     [pltpu.VMEM(q.shape, f32)] + [pltpu.VMEM((rows, LANES), f32)] * 2 + [pltpu.SemaphoreType.DMA((NV,))],
                     cost=work, to="hv")
    out, = call(last_kernel, (out.reshape(NV, n, CAX, LANES), keep, core2_in, far1), "hvvv", [shape(NV, n, CAX, LANES)],
                [pltpu.VMEM((NV, n, 1, LANES), f32), pltpu.SemaphoreType.DMA(())], to="h", aliases={0: 0})
    return out.transpose(0, 2, 1, 3).reshape(1, NV, CAX, size)


def solution(mesh):
    return jax.shard_map(
        functools.partial(local, mesh.shape["az"], mesh.shape["ax"]),
        mesh=mesh,
        in_specs=(
            P("pl", None, "ax", "az"),
            P("pl", None, "ax", "az"),
            P(None, "ax", "az"),
            P(),
            P(),
            P(),
            P(),
            P(("az", "ax"), None),
            P(("az", "ax")),
            P(("az", "ax")),
        ),
        out_specs=P("pl", None, "ax", "az"),
        check_vma=False,
    )
```

```python
import functools

import jax
import jax.numpy as jnp
from jax import lax
from jax.experimental import pallas as pl
from jax.experimental.pallas import tpu as pltpu
from jax.sharding import PartitionSpec as P

NV = 10
NS = 9
LANES = 128
CAX = 8
HALF = 64
AXES = ("az", "ax", "pl")
NJ = 8
EXT = 16
LOG2E = 1.4426950408889634
LIMIT = 16 * 1024 * 1024

f32 = jnp.float32


def roles():
    return lax.axis_index("az"), lax.axis_index("ax"), lax.axis_index("pl")


def shifts_of(n_az):
    return [n_az // 2] + [s for s in range(1, n_az) if s != n_az // 2]


def low_half():
    return lax.broadcasted_iota(jnp.int32, (CAX, LANES), 1) < HALF


def block(q_ref, v, b):
    return q_ref[v, pl.ds(CAX * CAX * b + CAX - 1, CAX, stride=CAX), :]


def axial_rows(q_ref, vel_ref, first_mate, second_mate):
    _, ax, _ = roles()
    n = q_ref.shape[1] // CAX

    def up(v, at, size):
        rows = pl.ds(CAX * at + CAX - 1, size, stride=CAX)
        return (1.0 + vel_ref[1, rows, :]) * q_ref[v, rows, :]

    def down(v, at, size):
        rows = pl.ds(CAX * at, size, stride=CAX)
        return (1.0 - vel_ref[1, rows, :]) * q_ref[v, rows, :]

    def put(refs, value):
        size = NV * n // len(refs)
        step = min(n, size) if size % n == 0 or n % size == 0 else n // 2
        for k in range(NV * n // step):
            at = k * step
            refs[at // size][pl.ds(at % size, step), :] = value(at // n, at % n, step)

    @pl.when(ax % 2 == 0)
    def _():
        put(first_mate, up)
        put(second_mate, down)

    @pl.when(ax % 2 == 1)
    def _():
        put(first_mate, down)
        put(second_mate, up)


def edges(q_ref, er_ref, el_ref):
    n = q_ref.shape[1] // CAX
    for v in range(NV):
        el_ref[pl.ds(v * CAX, CAX), :] = q_ref[v, pl.ds(0, CAX), :]
        er_ref[pl.ds(v * CAX, CAX), :] = q_ref[v, pl.ds((n - 1) * CAX, CAX), :]


def first_kernel(n_az, n_out, pieces, q_any, vel_any, col_any, slot_any, open_any, mix_any, pre_any, act_any, heat_any, *outs):
    out_refs, rest = outs[:n_out], outs[n_out:]
    (q_ref, vel_ref, s_ref, own_ref, er_ref, el_ref, a_ref, power_ref,
     col_ref, slot_ref, open_ref, mix_ref, pre_ref, act_ref, heat_ref, sems) = rest
    pairs = [(mix_any, mix_ref), (pre_any, pre_ref), (act_any, act_ref), (heat_any, heat_ref),
             (col_any, col_ref), (slot_any, slot_ref), (open_any, open_ref), (vel_any, vel_ref)]
    small = len(pairs) - 1
    pairs += [(q_any.at[pl.ds(v, 2)], q_ref.at[pl.ds(v, 2)]) for v in range(0, NV, 2)]
    copies = [pltpu.make_async_copy(x, y, sems.at[k]) for k, (x, y) in enumerate(pairs)]
    for copy in copies[small:] + copies[:small]:
        copy.start()
    az, _, plen = roles()
    n = q_ref.shape[1] // CAX
    rows = NV * n
    refs = (own_ref,) + tuple(out_refs)
    turns = [0] + shifts_of(n_az)
    beside_at = [rows] + [ref.shape[0] - CAX - EXT for ref in out_refs]

    @pl.when(plen == 1)
    def _():
        for ref in (own_ref, out_refs[0]):
            ref[pl.ds(0, rows), :] = jnp.zeros((rows, LANES), f32)
        for ref, at in zip(refs, beside_at):
            ref[pl.ds(at, EXT), :] = jnp.zeros((EXT, LANES), f32)

    for copy in copies[:small]:
        copy.wait()
    mixing(a_ref, mix_ref, pre_ref, heat_ref)
    for k in range(NS):
        power_ref[pl.ds(k * CAX, CAX), :] = jnp.full((CAX, LANES), act_ref[k] * (-LOG2E), f32)
    for copy in copies[small:]:
        copy.wait()
    edges(q_ref, er_ref, el_ref)
    el_ref[pl.ds(NV * CAX, CAX), :] = vel_ref[0, pl.ds(0, CAX), :]
    er_ref[pl.ds(NV * CAX, CAX), :] = vel_ref[0, pl.ds((n - 1) * CAX, CAX), :]

    @pl.when(plen == 0)
    def _():
        for v in range(NV):
            s_ref[pl.ds(v * n, n), :] = q_ref[v, pl.ds(0, n, stride=CAX), :]
        axial_rows(q_ref, vel_ref, out_refs[:1], out_refs[1:1 + pieces])

    @pl.when(plen == 1)
    def _():
        sub = lax.broadcasted_iota(jnp.int32, (CAX, LANES), 0)
        left = lax.broadcasted_iota(jnp.int32, (1, LANES), 1) < HALF
        blocks = n // CAX
        tables = [jnp.full((CAX, LANES), -1.0, f32)] * n_az
        used = [jnp.int32(0)] * n_az
        for b in range(blocks):
            tile, opened = slot_ref[b], open_ref[b] != 0
            ahead = (col_ref[b] - az + n_az) % n_az
            for shift, (turn, ref) in enumerate(zip(turns, refs)):
                here = jnp.logical_and(ahead == turn, opened)
                tables[shift] = jnp.where(sub == jnp.where(here, used[shift], CAX), tile.astype(f32), tables[shift])

                @pl.when(here)
                def _(ref=ref, b=b, tile=tile, shift=shift, slot=used[shift]):
                    for v in range(NV):
                        if shift < 2:
                            at = pl.ds(pl.multiple_of(v * n + tile * CAX, CAX), CAX)
                            ref[at, :] += block(q_ref, v, b)
                        else:
                            at = pl.ds(pl.multiple_of((slot * NV + v) * CAX, CAX), CAX)
                            ref[at, :] = block(q_ref, v, b)

                used[shift] = used[shift] + here.astype(jnp.int32)

            def beside(end, step, row, keep_left, b=b, tile=tile, opened=opened, ahead=ahead):
                @pl.when(jnp.logical_and(opened, tile == end))
                def _():
                    for shift, (turn, ref) in enumerate(zip(turns, refs)):
                        @pl.when(ahead == (turn + step) % n_az)
                        def _(ref=ref, at=beside_at[shift]):
                            for v in range(NV):
                                cell = q_ref[v, pl.ds(row, 1), :]
                                cell = jnp.where(left, cell, 0.0) if keep_left else jnp.where(left, 0.0, cell)
                                ref[pl.ds(at + v, 1), :] += cell

            beside(0, 1, CAX * CAX * b + CAX - 1, True)
            beside(blocks - 1, n_az - 1, CAX * CAX * (b + 1) - 1, False)
        for ref, table in zip(out_refs, tables[1:]):
            ref[pl.ds(ref.shape[0] - CAX, CAX), :] = table


def fill_ghosts(state_ref, lo_ref, hi_ref, ra_refs, rb_refs, high_ref, supply_ref, n_ax):
    _, ax, plen = roles()
    n = state_ref.shape[1] // CAX
    even = ax % 2 == 0
    odd = jnp.logical_not(even)
    cham = plen == 0

    def put(ref, parts):
        size = ref.shape[0] // len(parts)
        for k, part in enumerate(parts):
            ref[pl.ds(k * size, size), :] = part[pl.ds(0, size), :]

    @pl.when(plen == 1)
    def _():
        lo_ref[...] = supply_ref[...]
        hi_ref[...] = high_ref[pl.ds(0, hi_ref.shape[0]), :]

    @pl.when(jnp.logical_and(cham, even))
    def _():
        put(hi_ref, ra_refs)

    @pl.when(jnp.logical_and(cham, odd))
    def _():
        put(lo_ref, ra_refs)

    @pl.when(jnp.logical_and(cham, ax == 0))
    def _():
        lo_ref[...] = jnp.zeros_like(lo_ref)

    @pl.when(jnp.logical_and(cham, jnp.logical_and(even, ax > 0)))
    def _():
        put(lo_ref, rb_refs)

    @pl.when(jnp.logical_and(cham, jnp.logical_and(odd, ax < n_ax - 1)))
    def _():
        put(hi_ref, rb_refs)

    @pl.when(jnp.logical_and(cham, ax == n_ax - 1))
    def _():
        for v in range(NV):
            hi_ref[pl.ds(v * n, n), :] = state_ref[v, pl.ds(CAX - 1, n, stride=CAX), :]


def add_border(v, dst_ref, scale, lo_ref, hi_ref, hl_ref, hr_ref, ul_ref, ur_ref):
    n = dst_ref.shape[1] // CAX
    left = low_half()
    dst_ref[v, pl.ds(0, n, stride=CAX), :] += scale * lo_ref[pl.ds(v * n, n), :]
    dst_ref[v, pl.ds(CAX - 1, n, stride=CAX), :] += scale * hi_ref[pl.ds(v * n, n), :]
    al = scale + scale * pltpu.roll(ul_ref[...], HALF, 1)
    ar = scale - scale * pltpu.roll(ur_ref[...], HALF, 1)
    head = pltpu.roll(hl_ref[pl.ds(v * CAX, CAX), :], HALF, 1)
    tail = pltpu.roll(hr_ref[pl.ds(v * CAX, CAX), :], HALF, 1)
    dst_ref[v, pl.ds(0, CAX), :] += jnp.where(left, al * head, 0.0)
    dst_ref[v, pl.ds((n - 1) * CAX, CAX), :] += jnp.where(left, 0.0, ar * tail)


def mixing(a_ref, mix_ref, pre_ref, heat_ref):
    width = NV * CAX
    col = lax.broadcasted_iota(jnp.int32, (CAX, 3 * width), 1)
    row = lax.broadcasted_iota(jnp.int32, (CAX, 3 * width), 0)
    inner = col % width
    species, lane = inner // CAX, inner % CAX
    for v in range(NV):
        block = jnp.zeros((CAX, 3 * width), f32)
        for k in range(NS):
            value = 0.2 * pre_ref[k] * (mix_ref[v, k] if v < NS else heat_ref[k])
            block = jnp.where(species == k, value, block)
        block = jnp.where(lane == row, block, 0.0)
        high = block.astype(jnp.bfloat16).astype(f32)
        a_ref[pl.ds(v * CAX, CAX), :] = jnp.where(col // width == 1, block - high, high)


def reactions(states, a, power_ref):
    rates = []
    for state in states:
        inv = 1.0 / jnp.maximum(state[NS], 0.5)
        some = [jnp.exp2(power_ref[pl.ds(k * CAX, CAX), :] * inv) * jnp.maximum(state[k], 0.0) for k in range(NS)]
        rates.append(jnp.concatenate(some + [jnp.zeros((CAX, LANES), f32)], axis=0))
    rate = jnp.concatenate(rates, axis=1)
    high = rate.astype(jnp.bfloat16)
    low = (rate - high.astype(f32)).astype(jnp.bfloat16)
    return jnp.dot(a, jnp.concatenate([high, high, low], axis=0), preferred_element_type=f32)


def interior(q_ref, vel_ref, a_ref, power_ref, scale, finish):
    n = q_ref.shape[1] // CAX
    left = low_half()
    sub = lax.broadcasted_iota(jnp.int32, (CAX, LANES), 0)
    bottom, top = sub == 0, sub == CAX - 1
    a = (scale * a_ref[...]).astype(jnp.bfloat16)
    c = 0.1 * scale

    def reg(ref, v, j):
        return ref[v, pl.ds(pl.multiple_of(j * CAX, CAX), CAX), :]

    def column(ref, v, j0):
        regs = [reg(ref, v, j0 + d) for d in range(NJ)]
        before = jnp.where(j0 == 0, 0.0, reg(ref, v, jnp.maximum(j0 - 1, 0)))
        after = jnp.where(j0 + NJ == n, 0.0, reg(ref, v, jnp.minimum(j0 + NJ, n - 1)))
        turned = [pltpu.roll(x, HALF, 1) for x in [before] + regs + [after]]
        lefts = [jnp.where(left, turned[d], turned[d + 1]) for d in range(NJ)]
        rights = [jnp.where(left, turned[d + 1], turned[d + 2]) for d in range(NJ)]
        return regs, lefts, rights

    def body(step, carry):
        j0 = step * NJ
        src = reactions([[reg(q_ref, v, j0 + d) for v in range(NV)] for d in range(NJ)], a, power_ref)
        _, u_left, u_right = column(vel_ref, 0, j0)
        w = [reg(vel_ref, 1, j0 + d) for d in range(NJ)]
        al = [c + c * x for x in u_left]
        ar = [c - c * x for x in u_right]
        wu = [jnp.where(bottom, 0.0, c + c * pltpu.roll(x, 1, 0)) for x in w]
        wd = [jnp.where(top, 0.0, c - c * pltpu.roll(x, CAX - 1, 0)) for x in w]
        for v in range(NV):
            regs, lefts, rights = column(q_ref, v, j0)
            for d in range(NJ):
                vertical = wu[d] * pltpu.roll(regs[d], 1, 0) + wd[d] * pltpu.roll(regs[d], CAX - 1, 0)
                new = (0.6 * scale) * regs[d] + src[v * CAX:(v + 1) * CAX, d * LANES:(d + 1) * LANES]
                finish(j0 + d, v, new + (al[d] * lefts[d] + ar[d] * rights[d]) + vertical)
        return carry

    lax.fori_loop(0, n // NJ, body, 0)


def inside_one_kernel(q_ref, vel_ref, a_ref, power_ref, out_ref):
    def finish(j, v, new):
        out_ref[v, pl.ds(pl.multiple_of(j * CAX, CAX), CAX), :] = new

    interior(q_ref, vel_ref, a_ref, power_ref, 1.0, finish)


def inside_two_kernel(q_ref, q1_ref, vel_ref, a_ref, power_ref, out_ref):
    def finish(j, v, new):
        at = pl.ds(pl.multiple_of(j * CAX, CAX), CAX)
        out_ref[v, at, :] = 0.5 * q_ref[v, at, :] + new

    interior(q1_ref, vel_ref, a_ref, power_ref, 0.5, finish)


def gather_slots(dst_ref, base, got, tables, cap):
    slots = [(k, m) for k in range(len(got)) for m in range(cap)]
    named = [jnp.broadcast_to(tables[k][pl.ds(tables[k].shape[0] - CAX + m, 1), :], (CAX, LANES)) for k, m in slots]
    for v in range(NV):
        blocks = [got[k][pl.ds((m * NV + v) * CAX, CAX), :] for k, m in slots]
        for t in range(CAX):
            at = pl.ds((v * CAX + t) * CAX, CAX)
            total = base(at)
            for name, value in zip(named, blocks):
                total = total + jnp.where(name == t, value, 0.0)
            dst_ref[at, :] = total


def border_one_kernel(n_az, n_ax, n_out, cap, s_in_ref, *rest):
    got, rest = rest[:n_out], rest[n_out:]
    hl_ref, hr_ref, part_ref, q_ref, vel_ref, supply_ref, own_in_ref, col_any, slot_any, open_any = rest[:10]
    out_refs, rest = rest[10:10 + n_out], rest[10 + n_out:]
    (q1_ref, core_ref, z_ref, own_ref, er_ref, el_ref, lo_ref, hi_ref,
     col_ref, slot_ref, open_ref, sems) = rest
    pairs = [(col_any, col_ref), (slot_any, slot_ref), (open_any, open_ref)]
    copies = [pltpu.make_async_copy(x, y, sems.at[k]) for k, (x, y) in enumerate(pairs)]
    for copy in copies:
        copy.start()
    az, _, plen = roles()
    n = q_ref.shape[1] // CAX
    rows = NV * n
    fill_ghosts(q_ref, lo_ref, hi_ref, got[:1], got[1:1 + CAX // cap], s_in_ref, supply_ref, n_ax)
    for v in range(NV):
        q1_ref[v] = part_ref[v]
        add_border(v, q1_ref, 0.1, lo_ref, hi_ref, hl_ref, hr_ref,
                   hl_ref.at[pl.ds(NV * CAX, CAX)], hr_ref.at[pl.ds(NV * CAX, CAX)])
    edges(q1_ref, er_ref, el_ref)
    for copy in copies:
        copy.wait()

    @pl.when(plen == 0)
    def _():
        core_ref[pl.ds(rows, EXT), :] = jnp.zeros((EXT, LANES), f32)
        for v in range(NV):
            core_ref[pl.ds(v * n, n), :] = q1_ref[v, pl.ds(0, n, stride=CAX), :]
        axial_rows(q1_ref, vel_ref, out_refs[:CAX // cap], (z_ref,))

    @pl.when(plen == 1)
    def _():
        gather_slots(core_ref, lambda at: own_in_ref[at, :] + got[0][at, :], got[1:], got[1:], cap)
        beside = own_in_ref[pl.ds(rows, EXT), :]
        for ref in got:
            beside = beside + ref[pl.ds(ref.shape[0] - CAX - EXT, EXT), :]
        core_ref[pl.ds(rows, EXT), :] = beside
        own_ref[...] = jnp.zeros_like(own_ref)
        used = [jnp.int32(0)] * n_out
        for b in range(n // CAX):
            tile = slot_ref[b]
            ahead = (col_ref[b] - az + n_az) % n_az
            opened = open_ref[b] != 0

            @pl.when(jnp.logical_and(opened, ahead == 0))
            def _(b=b, tile=tile):
                for v in range(NV):
                    at = pl.ds(pl.multiple_of(v * n + tile * CAX, CAX), CAX)
                    own_ref[at, :] += block(q1_ref, v, b)

            for k, ref in enumerate(out_refs):
                here = jnp.logical_and(opened, ahead == shifts_of(n_az)[k])

                @pl.when(here)
                def _(ref=ref, b=b, slot=used[k]):
                    for v in range(NV):
                        at = pl.ds(pl.multiple_of((slot * NV + v) * CAX, CAX), CAX)
                        ref[at, :] = block(q1_ref, v, b)

                used[k] = used[k] + here.astype(jnp.int32)


def tile_kernel(n_out, cap, own_ref, z_ref, *rest):
    got, tables, (step_ref,) = rest[:n_out], rest[n_out:2 * n_out], rest[2 * n_out:]
    _, _, plen = roles()

    @pl.when(plen == 0)
    def _():
        step_ref[...] = z_ref[...]

    @pl.when(plen == 1)
    def _():
        gather_slots(step_ref, lambda at: own_ref[at, :], got, tables, cap)


def add_kernel(*refs):
    refs[-1][...] = sum(ref[...] for ref in refs[:-1])


def inlet_kernel(pair_ref, far_ref, near_ref, dq_ref, out_ref):
    _, ax, plen = roles()
    rows = out_ref.shape[0]
    inlet_side = jnp.logical_and(plen == 0, ax == 0)

    @pl.when(inlet_side)
    def _():
        dq_ref[...] = 0.1 * (far_ref[...] + near_ref[...])
        out_ref[...] = dq_ref[pl.ds(0, rows), :]

    @pl.when(jnp.logical_not(inlet_side))
    def _():
        dq_ref[...] = jnp.zeros_like(dq_ref)
        out_ref[...] = pair_ref[...]


def border_two_kernel(n_ax, n_z, part_ref, q_ref, q1_ref, vel_ref, core_ref, supply_ref, step_ref, dq_ref, hl_ref, hr_ref,
                      hl0_ref, hr0_ref, *rest):
    ra_refs, rest = rest[:n_z], rest[n_z:]
    a_ref, power_ref, out_any, keep_ref, out_ref, lo_ref, hi_ref, sems = rest
    n = out_ref.shape[1] // CAX
    rows = NV * n
    _, ax, plen = roles()
    inlet_side = jnp.logical_and(ax == 0, plen == 0)
    ul_ref, ur_ref = hl0_ref.at[pl.ds(NV * CAX, CAX)], hr0_ref.at[pl.ds(NV * CAX, CAX)]
    fill_ghosts(q1_ref, lo_ref, hi_ref, ra_refs, (step_ref,), core_ref, supply_ref, n_ax)

    @pl.when(inlet_side)
    def _():
        first = lax.broadcasted_iota(jnp.int32, (n, LANES), 0) == 0
        last = lax.broadcasted_iota(jnp.int32, (n, LANES), 0) == n - 1
        left = lax.broadcasted_iota(jnp.int32, (n, LANES), 1) < HALF

        def neighbours(x, head, tail):
            before = jnp.where(first, head, pltpu.roll(x, 1, 0))
            after = jnp.where(last, tail, pltpu.roll(x, n - 1, 0))
            mid = pltpu.roll(x, HALF, 1)
            return (jnp.where(left, pltpu.roll(before, HALF, 1), mid),
                    jnp.where(left, mid, pltpu.roll(after, HALF, 1)))

        u = vel_ref[0, pl.ds(0, n, stride=CAX), :]
        w_next = vel_ref[1, pl.ds(1, n, stride=CAX), :]
        u_left, u_right = neighbours(u, ul_ref[pl.ds(0, 1), :], ur_ref[pl.ds(0, 1), :])
        state = [q1_ref[v, pl.ds(0, n, stride=CAX), :] + dq_ref[pl.ds(v * n, n), :] for v in range(NV)]
        parts = [[x[d * CAX:(d + 1) * CAX] for x in state] for d in range(n // CAX)]
        src = reactions(parts, a_ref[...].astype(jnp.bfloat16), power_ref)
        for v in range(NV):
            beside = dq_ref[pl.ds(rows + v, 1), :]
            q_left, q_right = neighbours(state[v], hl_ref[pl.ds(v * CAX, 1), :] + beside, hr_ref[pl.ds(v * CAX, 1), :] + beside)
            above = (1.0 - w_next) * q1_ref[v, pl.ds(1, n, stride=CAX), :]
            mixed = src[v * CAX:(v + 1) * CAX]
            mixed = jnp.concatenate([mixed[:, d * LANES:(d + 1) * LANES] for d in range(n // CAX)], axis=0)
            new = 0.6 * state[v] + 0.1 * ((1.0 + u_left) * q_left + (1.0 - u_right) * q_right + above) + mixed
            keep_ref[pl.ds(v * n, n), :] = 0.5 * q_ref[v, pl.ds(0, n, stride=CAX), :] + 0.5 * new

    copies = []
    for v in range(NV):
        out_ref[v] = part_ref[v]
        add_border(v, out_ref, 0.05, lo_ref, hi_ref, hl_ref, hr_ref, ul_ref, ur_ref)

        @pl.when(inlet_side)
        def _(v=v):
            w = vel_ref[1, pl.ds(0, n, stride=CAX), :]
            out_ref[v, pl.ds(1, n, stride=CAX), :] += 0.05 * ((1.0 + w) * dq_ref[pl.ds(v * n, n), :])

        @pl.when(plen == 1)
        def _(v=v):
            keep_ref[pl.ds(v * n, n), :] = out_ref[v, pl.ds(CAX - 1, n, stride=CAX), :]

        copies.append(pltpu.make_async_copy(out_ref.at[v], out_any.at[v], sems.at[v]))
        copies[-1].start()
    for copy in copies:
        copy.wait()


def last_kernel(in_any, keep_ref, core_ref, far_ref, out_any, row_ref, sem):
    _, ax, plen = roles()
    n = keep_ref.shape[0] // NV

    def patch(at, value):
        for v in range(NV):
            row_ref[v, :, 0, :] = value(pl.ds(v * n, n))
        copy = pltpu.make_async_copy(row_ref, out_any.at[:, :, pl.ds(at, 1), :], sem)
        copy.start()
        copy.wait()

    @pl.when(jnp.logical_and(ax == 0, plen == 0))
    def _():
        patch(0, lambda at: keep_ref[at, :] + 0.05 * (core_ref[at, :] + far_ref[at, :]))

    @pl.when(jnp.logical_and(ax == 0, plen == 1))
    def _():
        patch(CAX - 1, lambda at: keep_ref[at, :] + 0.05 * core_ref[at, :])


def shape(*dims):
    return jax.ShapeDtypeStruct(dims, f32)


SPACES = {"s": pltpu.SMEM, "v": pltpu.VMEM, "h": pltpu.HBM}


def call(kernel, inputs, kinds, outs, scratch=(), cost=None, to=None, aliases=None):
    return pl.pallas_call(
        kernel,
        in_specs=[pl.BlockSpec(memory_space=SPACES[k]) for k in kinds],
        out_specs=[pl.BlockSpec(memory_space=SPACES[k]) for k in (to or "v" * len(outs))],
        out_shape=outs,
        scratch_shapes=list(scratch),
        cost_estimate=cost,
        input_output_aliases=aliases or {},
        compiler_params=pltpu.CompilerParams(vmem_limit_bytes=LIMIT),
    )(*inputs)


def local(n_az, n_ax, cells, speeds, supply, mix, prefactor, activation, heat, inj_column, inj_slot, inj_open):
    size = cells.shape[-1]
    n = size // LANES
    rows = NV * n

    def view(array):
        k = array.shape[0]
        return array.reshape(k, CAX, n, LANES).transpose(0, 2, 1, 3).reshape(k, CAX * n, LANES)

    def number(i, j, p):
        return (i * n_ax + j) * 2 + p

    every = [(i, j) for i in range(n_az) for j in range(n_ax)]

    def send(x, route):
        return lax.ppermute(x, AXES, [(number(*a), number(*b)) for a, b in route])

    def ring(step):
        return [((i, j, p), ((i + step) % n_az, j, p)) for i, j in every for p in (0, 1)]

    swap = [((i, j, p), (i, j, 1 - p)) for i, j in every for p in (0, 1)]
    n_out = n_az - 1

    def mate(k, j):
        return j ^ 1 if k == 0 else ((j + 1) ^ 1) - 1 if 0 < j < n_ax - 1 else n_ax - 1 - j

    cap = CAX // 4 if n_az > 4 else CAX // 2
    pieces = CAX // cap

    shifts = shifts_of(n_az)

    def first(k):
        out = [((i, j, 1), ((i + shifts[k]) % n_az, j, 1)) for i, j in every]
        for i, j in every:
            inside = 0 < j < n_ax - 1
            if k == 0 or (k <= pieces and (inside or k % 2 == 0)):
                to = (i, mate(min(k, 1), j), 0)
            else:
                to = (i ^ 1, j, 0)
            out.append(((i, j, 0), to))
        return out

    def compact(k):
        out = [((i, j, 1), ((i + shifts[k]) % n_az, j, 1)) for i, j in every]
        return out + [((i, j, 0), (i, mate(0, j), 0) if k < pieces else (i ^ 1, j, 0)) for i, j in every]

    q, vel = view(cells[0]), view(speeds[0])
    sup = supply.reshape(rows, LANES)
    col, slot, opened = inj_column.reshape(-1), inj_slot, inj_open
    react = (mix, prefactor, activation, heat)
    row, edge = shape(rows, LANES), shape(NV * CAX, LANES)

    whole = shape(*q.shape)
    work = pl.CostEstimate(flops=300 * q.shape[1] * LANES, transcendentals=20 * q.shape[1] * LANES,
                           bytes_accessed=12_000_000)

    raw = tuple(pltpu.with_memory_space_constraint(x, pltpu.HBM) for x in (q, vel, col, slot, opened) + react)
    wide, edge0 = shape(rows + EXT, LANES), shape((NV + 1) * CAX, LANES)
    got = call(functools.partial(first_kernel, n_az, n_out, pieces), raw, "h" * 9,
               [shape(rows + EXT + CAX, LANES)] + [shape(cap * NV * CAX + EXT + CAX, LANES)] * (n_out - 1) + [whole, shape(*vel.shape), row, wide, edge0, edge0,
                                                         shape(NV * CAX, 3 * NV * CAX), shape(NS * CAX, LANES)],
               [pltpu.SMEM(col.shape, jnp.int32)] * 3 + [pltpu.SMEM(x.shape, f32) for x in react]
               + [pltpu.SemaphoreType.DMA((8 + NV // 2,))])
    outs, (qv, velv, s0, own0, er, el, matrix, power) = got[:n_out], got[n_out:]
    ra = [send(x, first(k)) for k, x in enumerate(outs)]
    s0r = send(s0, swap)
    hl0 = send(er, ring(1))
    el, s0r = lax.optimization_barrier((el, s0r))
    hr0 = send(el, ring(-1))
    part, = call(inside_one_kernel, (qv, velv, matrix, power), "vvvv", [whole], cost=work)

    got = call(functools.partial(border_one_kernel, n_az, n_ax, n_out, cap),
               (s0r, *ra, hl0, hr0, part, qv, velv, sup, own0, col, slot, opened),
               "v" * (n_out + 11),
               [shape(cap * NV * CAX, LANES)] * n_out + [whole, wide, row, row, edge, edge],
               [pltpu.VMEM((rows, LANES), f32)] * 2 + [pltpu.SMEM(col.shape, jnp.int32)] * 3
               + [pltpu.SemaphoreType.DMA((3,))])
    outs, (q1, core, z1, own1, er, el) = got[:n_out], got[n_out:]
    down = [((i, j, 1), (i, j - 1, 1)) for i, j in every if j % 2 == 1]
    across = [((i, 2, 1), (i, 0, 0)) for i in range(n_az)]
    inner = [((i, j, 0), (i, mate(1, j), 0)) for i, j in every if 0 < j < n_ax - 1]
    rb = [send(x, compact(k)) for k, x in enumerate(outs)]
    core_in = send(core, swap)
    down0 = send(core, [((i, j, 1), (i, j - 1, 0)) for i, j in every if j % 2 == 1])

    part, = call(inside_two_kernel, (qv, q1, velv, matrix, power), "vvvvv", [whole], cost=work)
    part, down0 = lax.optimization_barrier((part, down0))
    pair0, = call(add_kernel, (core_in, down0), "vv", [wide])
    part, own1, pair0 = lax.optimization_barrier((part, own1, pair0))
    far0 = send(pair0, [((i, 2, 0), (i, 0, 0)) for i in range(n_az)])
    step, = call(functools.partial(tile_kernel, n_out, cap), (own1, z1, *rb, *ra), "v" * (2 + 2 * n_out), [row])
    step_in = send(step, down + inner)
    er, el, step = lax.optimization_barrier((er, el, step))
    hl1, hr1 = send(er, ring(1)), send(el, ring(-1))
    pair1, = call(add_kernel, (step, step_in), "vv", [row])
    far1 = send(pair1, across)
    pair1, hl1, hr1 = lax.optimization_barrier((pair1, hl1, hr1))

    dq, core2 = call(inlet_kernel, (pair1, far0, pair0), "vvv", [wide, row])
    core2_in = send(core2, swap)
    out, keep = call(functools.partial(border_two_kernel, n_ax, pieces),
                     (part, qv, q1, velv, core_in, sup, step_in, dq, hl1, hr1, hl0, hr0, *rb[:pieces], matrix, power),
                     "v" * (14 + pieces), [whole, row],
                     [pltpu.VMEM(q.shape, f32)] + [pltpu.VMEM((rows, LANES), f32)] * 2 + [pltpu.SemaphoreType.DMA((NV,))],
                     cost=work, to="hv")
    out, = call(last_kernel, (out.reshape(NV, n, CAX, LANES), keep, core2_in, far1), "hvvv", [shape(NV, n, CAX, LANES)],
                [pltpu.VMEM((NV, n, 1, LANES), f32), pltpu.SemaphoreType.DMA(())], to="h", aliases={0: 0})
    return out.transpose(0, 2, 1, 3).reshape(1, NV, CAX, size)


def solution(mesh):
    return jax.shard_map(
        functools.partial(local, mesh.shape["az"], mesh.shape["ax"]),
        mesh=mesh,
        in_specs=(
            P("pl", None, "ax", "az"),
            P("pl", None, "ax", "az"),
            P(None, "ax", "az"),
            P(),
            P(),
            P(),
            P(),
            P(("az", "ax"), None),
            P(("az", "ax")),
            P(("az", "ax")),
        ),
        out_specs=P("pl", None, "ax", "az"),
        check_vma=False,
    )
```

```python
import functools

import jax
import jax.numpy as jnp
from jax import lax
from jax.experimental import pallas as pl
from jax.experimental.pallas import tpu as pltpu
from jax.sharding import PartitionSpec as P

NV = 10
NS = 9
LANES = 128
CAX = 8
HALF = 64
AXES = ("az", "ax", "pl")
NJ = 8
EXT = 16
LOG2E = 1.4426950408889634
LIMIT = 16 * 1024 * 1024

f32 = jnp.float32


def roles():
    return lax.axis_index("az"), lax.axis_index("ax"), lax.axis_index("pl")


def shifts_of(n_az):
    return [n_az // 2] + [s for s in range(1, n_az) if s != n_az // 2]


def low_half():
    return lax.broadcasted_iota(jnp.int32, (CAX, LANES), 1) < HALF


def block(q_ref, v, b):
    return q_ref[v, pl.ds(CAX * CAX * b + CAX - 1, CAX, stride=CAX), :]


def axial_rows(q_ref, vel_ref, first_mate, second_mate):
    _, ax, _ = roles()
    n = q_ref.shape[1] // CAX

    def up(v, at, size):
        rows = pl.ds(CAX * at + CAX - 1, size, stride=CAX)
        return (1.0 + vel_ref[1, rows, :]) * q_ref[v, rows, :]

    def down(v, at, size):
        rows = pl.ds(CAX * at, size, stride=CAX)
        return (1.0 - vel_ref[1, rows, :]) * q_ref[v, rows, :]

    def put(refs, value):
        size = NV * n // len(refs)
        step = min(n, size) if size % n == 0 or n % size == 0 else n // 2
        for k in range(NV * n // step):
            at = k * step
            refs[at // size][pl.ds(at % size, step), :] = value(at // n, at % n, step)

    @pl.when(ax % 2 == 0)
    def _():
        put(first_mate, up)
        put(second_mate, down)

    @pl.when(ax % 2 == 1)
    def _():
        put(first_mate, down)
        put(second_mate, up)


def edges(q_ref, er_ref, el_ref):
    n = q_ref.shape[1] // CAX
    for v in range(NV):
        el_ref[pl.ds(v * CAX, CAX), :] = q_ref[v, pl.ds(0, CAX), :]
        er_ref[pl.ds(v * CAX, CAX), :] = q_ref[v, pl.ds((n - 1) * CAX, CAX), :]


def first_kernel(n_az, n_out, pieces, q_any, vel_any, col_any, slot_any, open_any, mix_any, pre_any, act_any, heat_any, *outs):
    out_refs, rest = outs[:n_out], outs[n_out:]
    (q_ref, vel_ref, s_ref, own_ref, er_ref, el_ref, a_ref, power_ref,
     col_ref, slot_ref, open_ref, mix_ref, pre_ref, act_ref, heat_ref, sems) = rest
    pairs = [(mix_any, mix_ref), (pre_any, pre_ref), (act_any, act_ref), (heat_any, heat_ref),
             (col_any, col_ref), (slot_any, slot_ref), (open_any, open_ref), (vel_any, vel_ref)]
    small = len(pairs) - 1
    pairs += [(q_any.at[pl.ds(v, 2)], q_ref.at[pl.ds(v, 2)]) for v in range(0, NV, 2)]
    copies = [pltpu.make_async_copy(x, y, sems.at[k]) for k, (x, y) in enumerate(pairs)]
    for copy in copies[small:] + copies[:small]:
        copy.start()
    az, _, plen = roles()
    n = q_ref.shape[1] // CAX
    rows = NV * n
    refs = (own_ref,) + tuple(out_refs)
    turns = [0] + shifts_of(n_az)
    beside_at = [rows] + [ref.shape[0] - CAX - EXT for ref in out_refs]

    @pl.when(plen == 1)
    def _():
        for ref in (own_ref, out_refs[0]):
            ref[pl.ds(0, rows), :] = jnp.zeros((rows, LANES), f32)
        for ref, at in zip(refs, beside_at):
            ref[pl.ds(at, EXT), :] = jnp.zeros((EXT, LANES), f32)

    for copy in copies[:small]:
        copy.wait()
    mixing(a_ref, mix_ref, pre_ref, heat_ref)
    for k in range(NS):
        power_ref[pl.ds(k * CAX, CAX), :] = jnp.full((CAX, LANES), act_ref[k] * (-LOG2E), f32)
    for copy in copies[small:]:
        copy.wait()
    edges(q_ref, er_ref, el_ref)
    el_ref[pl.ds(NV * CAX, CAX), :] = vel_ref[0, pl.ds(0, CAX), :]
    er_ref[pl.ds(NV * CAX, CAX), :] = vel_ref[0, pl.ds((n - 1) * CAX, CAX), :]

    @pl.when(plen == 0)
    def _():
        for v in range(NV):
            s_ref[pl.ds(v * n, n), :] = q_ref[v, pl.ds(0, n, stride=CAX), :]
        axial_rows(q_ref, vel_ref, out_refs[:1], out_refs[1:1 + pieces])

    @pl.when(plen == 1)
    def _():
        sub = lax.broadcasted_iota(jnp.int32, (CAX, LANES), 0)
        left = lax.broadcasted_iota(jnp.int32, (1, LANES), 1) < HALF
        blocks = n // CAX
        tables = [jnp.full((CAX, LANES), -1.0, f32)] * n_az
        used = [jnp.int32(0)] * n_az
        for b in range(blocks):
            tile, opened = slot_ref[b], open_ref[b] != 0
            ahead = (col_ref[b] - az + n_az) % n_az
            for shift, (turn, ref) in enumerate(zip(turns, refs)):
                here = jnp.logical_and(ahead == turn, opened)
                tables[shift] = jnp.where(sub == jnp.where(here, used[shift], CAX), tile.astype(f32), tables[shift])

                @pl.when(here)
                def _(ref=ref, b=b, tile=tile, shift=shift, slot=used[shift]):
                    for v in range(NV):
                        if shift < 2:
                            at = pl.ds(pl.multiple_of(v * n + tile * CAX, CAX), CAX)
                            ref[at, :] += block(q_ref, v, b)
                        else:
                            at = pl.ds(pl.multiple_of((slot * NV + v) * CAX, CAX), CAX)
                            ref[at, :] = block(q_ref, v, b)

                used[shift] = used[shift] + here.astype(jnp.int32)

            def beside(end, step, row, keep_left, b=b, tile=tile, opened=opened, ahead=ahead):
                @pl.when(jnp.logical_and(opened, tile == end))
                def _():
                    for shift, (turn, ref) in enumerate(zip(turns, refs)):
                        @pl.when(ahead == (turn + step) % n_az)
                        def _(ref=ref, at=beside_at[shift]):
                            for v in range(NV):
                                cell = q_ref[v, pl.ds(row, 1), :]
                                cell = jnp.where(left, cell, 0.0) if keep_left else jnp.where(left, 0.0, cell)
                                ref[pl.ds(at + v, 1), :] += cell

            beside(0, 1, CAX * CAX * b + CAX - 1, True)
            beside(blocks - 1, n_az - 1, CAX * CAX * (b + 1) - 1, False)
        for ref, table in zip(out_refs, tables[1:]):
            ref[pl.ds(ref.shape[0] - CAX, CAX), :] = table


def fill_ghosts(state_ref, lo_ref, hi_ref, ra_refs, rb_refs, high_ref, supply_ref, n_ax):
    _, ax, plen = roles()
    n = state_ref.shape[1] // CAX
    even = ax % 2 == 0
    odd = jnp.logical_not(even)
    cham = plen == 0

    def put(ref, parts):
        size = ref.shape[0] // len(parts)
        for k, part in enumerate(parts):
            ref[pl.ds(k * size, size), :] = part[pl.ds(0, size), :]

    @pl.when(plen == 1)
    def _():
        lo_ref[...] = supply_ref[...]
        hi_ref[...] = high_ref[pl.ds(0, hi_ref.shape[0]), :]

    @pl.when(jnp.logical_and(cham, even))
    def _():
        put(hi_ref, ra_refs)

    @pl.when(jnp.logical_and(cham, odd))
    def _():
        put(lo_ref, ra_refs)

    @pl.when(jnp.logical_and(cham, ax == 0))
    def _():
        lo_ref[...] = jnp.zeros_like(lo_ref)

    @pl.when(jnp.logical_and(cham, jnp.logical_and(even, ax > 0)))
    def _():
        put(lo_ref, rb_refs)

    @pl.when(jnp.logical_and(cham, jnp.logical_and(odd, ax < n_ax - 1)))
    def _():
        put(hi_ref, rb_refs)

    @pl.when(jnp.logical_and(cham, ax == n_ax - 1))
    def _():
        for v in range(NV):
            hi_ref[pl.ds(v * n, n), :] = state_ref[v, pl.ds(CAX - 1, n, stride=CAX), :]


def add_border(v, dst_ref, scale, lo_ref, hi_ref, hl_ref, hr_ref, ul_ref, ur_ref):
    n = dst_ref.shape[1] // CAX
    left = low_half()
    dst_ref[v, pl.ds(0, n, stride=CAX), :] += scale * lo_ref[pl.ds(v * n, n), :]
    dst_ref[v, pl.ds(CAX - 1, n, stride=CAX), :] += scale * hi_ref[pl.ds(v * n, n), :]
    al = scale + scale * pltpu.roll(ul_ref[...], HALF, 1)
    ar = scale - scale * pltpu.roll(ur_ref[...], HALF, 1)
    head = pltpu.roll(hl_ref[pl.ds(v * CAX, CAX), :], HALF, 1)
    tail = pltpu.roll(hr_ref[pl.ds(v * CAX, CAX), :], HALF, 1)
    dst_ref[v, pl.ds(0, CAX), :] += jnp.where(left, al * head, 0.0)
    dst_ref[v, pl.ds((n - 1) * CAX, CAX), :] += jnp.where(left, 0.0, ar * tail)


def mixing(a_ref, mix_ref, pre_ref, heat_ref):
    width = NV * CAX
    col = lax.broadcasted_iota(jnp.int32, (CAX, 3 * width), 1)
    row = lax.broadcasted_iota(jnp.int32, (CAX, 3 * width), 0)
    inner = col % width
    species, lane = inner // CAX, inner % CAX
    for v in range(NV):
        block = jnp.zeros((CAX, 3 * width), f32)
        for k in range(NS):
            value = 0.2 * pre_ref[k] * (mix_ref[v, k] if v < NS else heat_ref[k])
            block = jnp.where(species == k, value, block)
        block = jnp.where(lane == row, block, 0.0)
        high = block.astype(jnp.bfloat16).astype(f32)
        a_ref[pl.ds(v * CAX, CAX), :] = jnp.where(col // width == 1, block - high, high)


def reactions(states, a, power_ref):
    rates = []
    for state in states:
        inv = 1.0 / jnp.maximum(state[NS], 0.5)
        some = [jnp.exp2(power_ref[pl.ds(k * CAX, CAX), :] * inv) * jnp.maximum(state[k], 0.0) for k in range(NS)]
        rates.append(jnp.concatenate(some + [jnp.zeros((CAX, LANES), f32)], axis=0))
    rate = jnp.concatenate(rates, axis=1)
    high = rate.astype(jnp.bfloat16)
    low = (rate - high.astype(f32)).astype(jnp.bfloat16)
    return jnp.dot(a, jnp.concatenate([high, high, low], axis=0), preferred_element_type=f32)


def interior(q_ref, vel_ref, a_ref, power_ref, scale, finish):
    n = q_ref.shape[1] // CAX
    left = low_half()
    sub = lax.broadcasted_iota(jnp.int32, (CAX, LANES), 0)
    bottom, top = sub == 0, sub == CAX - 1
    a = (scale * a_ref[...]).astype(jnp.bfloat16)
    c = 0.1 * scale

    def reg(ref, v, j):
        return ref[v, pl.ds(pl.multiple_of(j * CAX, CAX), CAX), :]

    def column(ref, v, j0):
        regs = [reg(ref, v, j0 + d) for d in range(NJ)]
        before = jnp.where(j0 == 0, 0.0, reg(ref, v, jnp.maximum(j0 - 1, 0)))
        after = jnp.where(j0 + NJ == n, 0.0, reg(ref, v, jnp.minimum(j0 + NJ, n - 1)))
        turned = [pltpu.roll(x, HALF, 1) for x in [before] + regs + [after]]
        lefts = [jnp.where(left, turned[d], turned[d + 1]) for d in range(NJ)]
        rights = [jnp.where(left, turned[d + 1], turned[d + 2]) for d in range(NJ)]
        return regs, lefts, rights

    def body(step, carry):
        j0 = step * NJ
        src = reactions([[reg(q_ref, v, j0 + d) for v in range(NV)] for d in range(NJ)], a, power_ref)
        _, u_left, u_right = column(vel_ref, 0, j0)
        w = [reg(vel_ref, 1, j0 + d) for d in range(NJ)]
        al = [c + c * x for x in u_left]
        ar = [c - c * x for x in u_right]
        wu = [jnp.where(bottom, 0.0, c + c * pltpu.roll(x, 1, 0)) for x in w]
        wd = [jnp.where(top, 0.0, c - c * pltpu.roll(x, CAX - 1, 0)) for x in w]
        for v in range(NV):
            regs, lefts, rights = column(q_ref, v, j0)
            for d in range(NJ):
                vertical = wu[d] * pltpu.roll(regs[d], 1, 0) + wd[d] * pltpu.roll(regs[d], CAX - 1, 0)
                new = (0.6 * scale) * regs[d] + src[v * CAX:(v + 1) * CAX, d * LANES:(d + 1) * LANES]
                finish(j0 + d, v, new + (al[d] * lefts[d] + ar[d] * rights[d]) + vertical)
        return carry

    lax.fori_loop(0, n // NJ, body, 0)


def inside_one_kernel(q_ref, vel_ref, a_ref, power_ref, out_ref):
    def finish(j, v, new):
        out_ref[v, pl.ds(pl.multiple_of(j * CAX, CAX), CAX), :] = new

    interior(q_ref, vel_ref, a_ref, power_ref, 1.0, finish)


def inside_two_kernel(q_ref, q1_ref, vel_ref, a_ref, power_ref, out_ref):
    def finish(j, v, new):
        at = pl.ds(pl.multiple_of(j * CAX, CAX), CAX)
        out_ref[v, at, :] = 0.5 * q_ref[v, at, :] + new

    interior(q1_ref, vel_ref, a_ref, power_ref, 0.5, finish)


def gather_slots(dst_ref, base, got, tables, cap):
    slots = [(k, m) for k in range(len(got)) for m in range(cap)]
    named = [jnp.broadcast_to(tables[k][pl.ds(tables[k].shape[0] - CAX + m, 1), :], (CAX, LANES)) for k, m in slots]
    for v in range(NV):
        blocks = [got[k][pl.ds((m * NV + v) * CAX, CAX), :] for k, m in slots]
        for t in range(CAX):
            at = pl.ds((v * CAX + t) * CAX, CAX)
            total = base(at)
            for name, value in zip(named, blocks):
                total = total + jnp.where(name == t, value, 0.0)
            dst_ref[at, :] = total


def border_one_kernel(n_az, n_ax, n_out, cap, s_in_ref, *rest):
    got, rest = rest[:n_out], rest[n_out:]
    hl_ref, hr_ref, part_ref, q_ref, vel_ref, supply_ref, own_in_ref, col_any, slot_any, open_any = rest[:10]
    out_refs, rest = rest[10:10 + n_out], rest[10 + n_out:]
    (q1_ref, core_ref, z_ref, own_ref, er_ref, el_ref, lo_ref, hi_ref,
     col_ref, slot_ref, open_ref, sems) = rest
    pairs = [(col_any, col_ref), (slot_any, slot_ref), (open_any, open_ref)]
    copies = [pltpu.make_async_copy(x, y, sems.at[k]) for k, (x, y) in enumerate(pairs)]
    for copy in copies:
        copy.start()
    az, _, plen = roles()
    n = q_ref.shape[1] // CAX
    rows = NV * n
    fill_ghosts(q_ref, lo_ref, hi_ref, got[:1], got[1:1 + CAX // cap], s_in_ref, supply_ref, n_ax)
    for v in range(NV):
        q1_ref[v] = part_ref[v]
        add_border(v, q1_ref, 0.1, lo_ref, hi_ref, hl_ref, hr_ref,
                   hl_ref.at[pl.ds(NV * CAX, CAX)], hr_ref.at[pl.ds(NV * CAX, CAX)])
    edges(q1_ref, er_ref, el_ref)
    for copy in copies:
        copy.wait()

    @pl.when(plen == 0)
    def _():
        core_ref[pl.ds(rows, EXT), :] = jnp.zeros((EXT, LANES), f32)
        for v in range(NV):
            core_ref[pl.ds(v * n, n), :] = q1_ref[v, pl.ds(0, n, stride=CAX), :]
        axial_rows(q1_ref, vel_ref, out_refs[n_out - CAX // cap:], (z_ref,))

    @pl.when(plen == 1)
    def _():
        gather_slots(core_ref, lambda at: own_in_ref[at, :] + got[0][at, :], got[1:], got[1:], cap)
        beside = own_in_ref[pl.ds(rows, EXT), :]
        for ref in got:
            beside = beside + ref[pl.ds(ref.shape[0] - CAX - EXT, EXT), :]
        core_ref[pl.ds(rows, EXT), :] = beside
        own_ref[...] = jnp.zeros_like(own_ref)
        used = [jnp.int32(0)] * n_out
        for b in range(n // CAX):
            tile = slot_ref[b]
            ahead = (col_ref[b] - az + n_az) % n_az
            opened = open_ref[b] != 0

            @pl.when(jnp.logical_and(opened, ahead == 0))
            def _(b=b, tile=tile):
                for v in range(NV):
                    at = pl.ds(pl.multiple_of(v * n + tile * CAX, CAX), CAX)
                    own_ref[at, :] += block(q1_ref, v, b)

            for k, ref in enumerate(out_refs):
                here = jnp.logical_and(opened, ahead == shifts_of(n_az)[k])

                @pl.when(here)
                def _(ref=ref, b=b, slot=used[k]):
                    for v in range(NV):
                        at = pl.ds(pl.multiple_of((slot * NV + v) * CAX, CAX), CAX)
                        ref[at, :] = block(q1_ref, v, b)

                used[k] = used[k] + here.astype(jnp.int32)


def tile_kernel(n_out, cap, own_ref, z_ref, *rest):
    got, tables, (step_ref,) = rest[:n_out], rest[n_out:2 * n_out], rest[2 * n_out:]
    _, _, plen = roles()

    @pl.when(plen == 0)
    def _():
        step_ref[...] = z_ref[...]

    @pl.when(plen == 1)
    def _():
        gather_slots(step_ref, lambda at: own_ref[at, :], got, tables, cap)


def add_kernel(*refs):
    refs[-1][...] = sum(ref[...] for ref in refs[:-1])


def inlet_kernel(pair_ref, far_ref, near_ref, dq_ref, out_ref):
    _, ax, plen = roles()
    rows = out_ref.shape[0]
    inlet_side = jnp.logical_and(plen == 0, ax == 0)

    @pl.when(inlet_side)
    def _():
        dq_ref[...] = 0.1 * (far_ref[...] + near_ref[...])
        out_ref[...] = dq_ref[pl.ds(0, rows), :]

    @pl.when(jnp.logical_not(inlet_side))
    def _():
        dq_ref[...] = jnp.zeros_like(dq_ref)
        out_ref[...] = pair_ref[...]


def border_two_kernel(n_ax, n_z, part_ref, q_ref, q1_ref, vel_ref, core_ref, supply_ref, step_ref, dq_ref, hl_ref, hr_ref,
                      hl0_ref, hr0_ref, *rest):
    ra_refs, rest = rest[:n_z], rest[n_z:]
    a_ref, power_ref, out_any, keep_ref, out_ref, lo_ref, hi_ref, sems = rest
    n = out_ref.shape[1] // CAX
    rows = NV * n
    _, ax, plen = roles()
    inlet_side = jnp.logical_and(ax == 0, plen == 0)
    ul_ref, ur_ref = hl0_ref.at[pl.ds(NV * CAX, CAX)], hr0_ref.at[pl.ds(NV * CAX, CAX)]
    fill_ghosts(q1_ref, lo_ref, hi_ref, ra_refs, (step_ref,), core_ref, supply_ref, n_ax)

    @pl.when(inlet_side)
    def _():
        first = lax.broadcasted_iota(jnp.int32, (n, LANES), 0) == 0
        last = lax.broadcasted_iota(jnp.int32, (n, LANES), 0) == n - 1
        left = lax.broadcasted_iota(jnp.int32, (n, LANES), 1) < HALF

        def neighbours(x, head, tail):
            before = jnp.where(first, head, pltpu.roll(x, 1, 0))
            after = jnp.where(last, tail, pltpu.roll(x, n - 1, 0))
            mid = pltpu.roll(x, HALF, 1)
            return (jnp.where(left, pltpu.roll(before, HALF, 1), mid),
                    jnp.where(left, mid, pltpu.roll(after, HALF, 1)))

        u = vel_ref[0, pl.ds(0, n, stride=CAX), :]
        w_next = vel_ref[1, pl.ds(1, n, stride=CAX), :]
        u_left, u_right = neighbours(u, ul_ref[pl.ds(0, 1), :], ur_ref[pl.ds(0, 1), :])
        state = [q1_ref[v, pl.ds(0, n, stride=CAX), :] + dq_ref[pl.ds(v * n, n), :] for v in range(NV)]
        parts = [[x[d * CAX:(d + 1) * CAX] for x in state] for d in range(n // CAX)]
        src = reactions(parts, a_ref[...].astype(jnp.bfloat16), power_ref)
        for v in range(NV):
            beside = dq_ref[pl.ds(rows + v, 1), :]
            q_left, q_right = neighbours(state[v], hl_ref[pl.ds(v * CAX, 1), :] + beside, hr_ref[pl.ds(v * CAX, 1), :] + beside)
            above = (1.0 - w_next) * q1_ref[v, pl.ds(1, n, stride=CAX), :]
            mixed = src[v * CAX:(v + 1) * CAX]
            mixed = jnp.concatenate([mixed[:, d * LANES:(d + 1) * LANES] for d in range(n // CAX)], axis=0)
            new = 0.6 * state[v] + 0.1 * ((1.0 + u_left) * q_left + (1.0 - u_right) * q_right + above) + mixed
            keep_ref[pl.ds(v * n, n), :] = 0.5 * q_ref[v, pl.ds(0, n, stride=CAX), :] + 0.5 * new

    copies = []
    for v in range(NV):
        out_ref[v] = part_ref[v]
        add_border(v, out_ref, 0.05, lo_ref, hi_ref, hl_ref, hr_ref, ul_ref, ur_ref)

        @pl.when(inlet_side)
        def _(v=v):
            w = vel_ref[1, pl.ds(0, n, stride=CAX), :]
            out_ref[v, pl.ds(1, n, stride=CAX), :] += 0.05 * ((1.0 + w) * dq_ref[pl.ds(v * n, n), :])

        @pl.when(plen == 1)
        def _(v=v):
            keep_ref[pl.ds(v * n, n), :] = out_ref[v, pl.ds(CAX - 1, n, stride=CAX), :]

        copies.append(pltpu.make_async_copy(out_ref.at[v], out_any.at[v], sems.at[v]))
        copies[-1].start()
    for copy in copies:
        copy.wait()


def last_kernel(in_any, keep_ref, core_ref, far_ref, out_any, row_ref, sem):
    _, ax, plen = roles()
    n = keep_ref.shape[0] // NV

    def patch(at, value):
        for v in range(NV):
            row_ref[v, :, 0, :] = value(pl.ds(v * n, n))
        copy = pltpu.make_async_copy(row_ref, out_any.at[:, :, pl.ds(at, 1), :], sem)
        copy.start()
        copy.wait()

    @pl.when(jnp.logical_and(ax == 0, plen == 0))
    def _():
        patch(0, lambda at: keep_ref[at, :] + 0.05 * (core_ref[at, :] + far_ref[at, :]))

    @pl.when(jnp.logical_and(ax == 0, plen == 1))
    def _():
        patch(CAX - 1, lambda at: keep_ref[at, :] + 0.05 * core_ref[at, :])


def shape(*dims):
    return jax.ShapeDtypeStruct(dims, f32)


SPACES = {"s": pltpu.SMEM, "v": pltpu.VMEM, "h": pltpu.HBM}


def call(kernel, inputs, kinds, outs, scratch=(), cost=None, to=None, aliases=None):
    return pl.pallas_call(
        kernel,
        in_specs=[pl.BlockSpec(memory_space=SPACES[k]) for k in kinds],
        out_specs=[pl.BlockSpec(memory_space=SPACES[k]) for k in (to or "v" * len(outs))],
        out_shape=outs,
        scratch_shapes=list(scratch),
        cost_estimate=cost,
        input_output_aliases=aliases or {},
        compiler_params=pltpu.CompilerParams(vmem_limit_bytes=LIMIT),
    )(*inputs)


def local(n_az, n_ax, cells, speeds, supply, mix, prefactor, activation, heat, inj_column, inj_slot, inj_open):
    size = cells.shape[-1]
    n = size // LANES
    rows = NV * n

    def view(array):
        k = array.shape[0]
        return array.reshape(k, CAX, n, LANES).transpose(0, 2, 1, 3).reshape(k, CAX * n, LANES)

    def number(i, j, p):
        return (i * n_ax + j) * 2 + p

    every = [(i, j) for i in range(n_az) for j in range(n_ax)]

    def send(x, route):
        return lax.ppermute(x, AXES, [(number(*a), number(*b)) for a, b in route])

    def ring(step):
        return [((i, j, p), ((i + step) % n_az, j, p)) for i, j in every for p in (0, 1)]

    swap = [((i, j, p), (i, j, 1 - p)) for i, j in every for p in (0, 1)]
    n_out = n_az - 1

    def mate(k, j):
        return j ^ 1 if k == 0 else ((j + 1) ^ 1) - 1 if 0 < j < n_ax - 1 else n_ax - 1 - j

    cap = CAX // 4 if n_az > 4 else CAX // 2
    pieces = CAX // cap

    shifts = shifts_of(n_az)

    def first(k):
        out = [((i, j, 1), ((i + shifts[k]) % n_az, j, 1)) for i, j in every]
        for i, j in every:
            inside = 0 < j < n_ax - 1
            if k == 0 or (k <= pieces and (inside or k % 2 == 0)):
                to = (i, mate(min(k, 1), j), 0)
            else:
                to = (i ^ 1, j, 0)
            out.append(((i, j, 0), to))
        return out

    def compact(k):
        out = [((i, j, 1), ((i + shifts[k]) % n_az, j, 1)) for i, j in every]
        return out + [((i, j, 0), (i, mate(0, j), 0) if k >= n_out - pieces else (i ^ 1, j, 0))
                      for i, j in every]

    q, vel = view(cells[0]), view(speeds[0])
    sup = supply.reshape(rows, LANES)
    col, slot, opened = inj_column.reshape(-1), inj_slot, inj_open
    react = (mix, prefactor, activation, heat)
    row, edge = shape(rows, LANES), shape(NV * CAX, LANES)

    whole = shape(*q.shape)
    work = pl.CostEstimate(flops=300 * q.shape[1] * LANES, transcendentals=20 * q.shape[1] * LANES,
                           bytes_accessed=12_000_000)

    raw = tuple(pltpu.with_memory_space_constraint(x, pltpu.HBM) for x in (q, vel, col, slot, opened) + react)
    wide, edge0 = shape(rows + EXT, LANES), shape((NV + 1) * CAX, LANES)
    got = call(functools.partial(first_kernel, n_az, n_out, pieces), raw, "h" * 9,
               [shape(rows + EXT + CAX, LANES)] + [shape(cap * NV * CAX + EXT + CAX, LANES)] * (n_out - 1) + [whole, shape(*vel.shape), row, wide, edge0, edge0,
                                                         shape(NV * CAX, 3 * NV * CAX), shape(NS * CAX, LANES)],
               [pltpu.SMEM(col.shape, jnp.int32)] * 3 + [pltpu.SMEM(x.shape, f32) for x in react]
               + [pltpu.SemaphoreType.DMA((8 + NV // 2,))])
    outs, (qv, velv, s0, own0, er, el, matrix, power) = got[:n_out], got[n_out:]
    ra = [send(x, first(k)) for k, x in enumerate(outs)]
    s0r = send(s0, swap)
    hl0 = send(er, ring(1))
    el, s0r = lax.optimization_barrier((el, s0r))
    hr0 = send(el, ring(-1))
    part, = call(inside_one_kernel, (qv, velv, matrix, power), "vvvv", [whole], cost=work)

    got = call(functools.partial(border_one_kernel, n_az, n_ax, n_out, cap),
               (s0r, *ra, hl0, hr0, part, qv, velv, sup, own0, col, slot, opened),
               "v" * (n_out + 11),
               [shape(cap * NV * CAX, LANES)] * n_out + [whole, wide, row, row, edge, edge],
               [pltpu.VMEM((rows, LANES), f32)] * 2 + [pltpu.SMEM(col.shape, jnp.int32)] * 3
               + [pltpu.SemaphoreType.DMA((3,))])
    outs, (q1, core, z1, own1, er, el) = got[:n_out], got[n_out:]
    down = [((i, j, 1), (i, j - 1, 1)) for i, j in every if j % 2 == 1]
    across = [((i, 2, 1), (i, 0, 0)) for i in range(n_az)]
    inner = [((i, j, 0), (i, mate(1, j), 0)) for i, j in every if 0 < j < n_ax - 1]
    rb = [send(x, compact(k)) for k, x in enumerate(outs)]
    core_in = send(core, swap)
    down0 = send(core, [((i, j, 1), (i, j - 1, 0)) for i, j in every if j % 2 == 1])

    part, = call(inside_two_kernel, (qv, q1, velv, matrix, power), "vvvvv", [whole], cost=work)
    part, down0 = lax.optimization_barrier((part, down0))
    pair0, = call(add_kernel, (core_in, down0), "vv", [wide])
    part, own1, pair0 = lax.optimization_barrier((part, own1, pair0))
    far0 = send(pair0, [((i, 2, 0), (i, 0, 0)) for i in range(n_az)])
    step, = call(functools.partial(tile_kernel, n_out, cap), (own1, z1, *rb, *ra), "v" * (2 + 2 * n_out), [row])
    step_in = send(step, down + inner)
    er, el, step = lax.optimization_barrier((er, el, step))
    hl1, hr1 = send(er, ring(1)), send(el, ring(-1))
    pair1, = call(add_kernel, (step, step_in), "vv", [row])
    far1 = send(pair1, across)
    pair1, hl1, hr1 = lax.optimization_barrier((pair1, hl1, hr1))

    dq, core2 = call(inlet_kernel, (pair1, far0, pair0), "vvv", [wide, row])
    core2_in = send(core2, swap)
    out, keep = call(functools.partial(border_two_kernel, n_ax, pieces),
                     (part, qv, q1, velv, core_in, sup, step_in, dq, hl1, hr1, hl0, hr0, *rb[n_out - pieces:], matrix, power),
                     "v" * (14 + pieces), [whole, row],
                     [pltpu.VMEM(q.shape, f32)] + [pltpu.VMEM((rows, LANES), f32)] * 2 + [pltpu.SemaphoreType.DMA((NV,))],
                     cost=work, to="hv")
    out, = call(last_kernel, (out.reshape(NV, n, CAX, LANES), keep, core2_in, far1), "hvvv", [shape(NV, n, CAX, LANES)],
                [pltpu.VMEM((NV, n, 1, LANES), f32), pltpu.SemaphoreType.DMA(())], to="h", aliases={0: 0})
    return out.transpose(0, 2, 1, 3).reshape(1, NV, CAX, size)


def solution(mesh):
    return jax.shard_map(
        functools.partial(local, mesh.shape["az"], mesh.shape["ax"]),
        mesh=mesh,
        in_specs=(
            P("pl", None, "ax", "az"),
            P("pl", None, "ax", "az"),
            P(None, "ax", "az"),
            P(),
            P(),
            P(),
            P(),
            P(("az", "ax"), None),
            P(("az", "ax")),
            P(("az", "ax")),
        ),
        out_specs=P("pl", None, "ax", "az"),
        check_vma=False,
    )
```

```python
import functools

import jax
import jax.numpy as jnp
from jax import lax
from jax.experimental import pallas as pl
from jax.experimental.pallas import tpu as pltpu
from jax.sharding import PartitionSpec as P

NV = 10
NS = 9
LANES = 128
CAX = 8
HALF = 64
AXES = ("az", "ax", "pl")
NJ = 8
EXT = 16
LOG2E = 1.4426950408889634
LIMIT = 16 * 1024 * 1024

f32 = jnp.float32


def roles():
    return lax.axis_index("az"), lax.axis_index("ax"), lax.axis_index("pl")


def shifts_of(n_az):
    return [n_az // 2] + [s for s in range(1, n_az) if s != n_az // 2]


def low_half():
    return lax.broadcasted_iota(jnp.int32, (CAX, LANES), 1) < HALF


def block(q_ref, v, b):
    return q_ref[v, pl.ds(CAX * CAX * b + CAX - 1, CAX, stride=CAX), :]


def axial_rows(q_ref, vel_ref, first_mate, second_mate):
    _, ax, _ = roles()
    n = q_ref.shape[1] // CAX

    def up(v, at, size):
        rows = pl.ds(CAX * at + CAX - 1, size, stride=CAX)
        return (1.0 + vel_ref[1, rows, :]) * q_ref[v, rows, :]

    def down(v, at, size):
        rows = pl.ds(CAX * at, size, stride=CAX)
        return (1.0 - vel_ref[1, rows, :]) * q_ref[v, rows, :]

    def put(refs, value):
        size = NV * n // len(refs)
        step = min(n, size) if size % n == 0 or n % size == 0 else n // 2
        for k in range(NV * n // step):
            at = k * step
            refs[at // size][pl.ds(at % size, step), :] = value(at // n, at % n, step)

    @pl.when(ax % 2 == 0)
    def _():
        put(first_mate, up)
        put(second_mate, down)

    @pl.when(ax % 2 == 1)
    def _():
        put(first_mate, down)
        put(second_mate, up)


def edges(q_ref, er_ref, el_ref):
    n = q_ref.shape[1] // CAX
    for v in range(NV):
        el_ref[pl.ds(v * CAX, CAX), :] = q_ref[v, pl.ds(0, CAX), :]
        er_ref[pl.ds(v * CAX, CAX), :] = q_ref[v, pl.ds((n - 1) * CAX, CAX), :]


def first_kernel(n_az, n_out, pieces, q_any, vel_any, col_any, slot_any, open_any, mix_any, pre_any, act_any, heat_any, *outs):
    out_refs, rest = outs[:n_out], outs[n_out:]
    (q_ref, vel_ref, s_ref, own_ref, er_ref, el_ref, a_ref, power_ref,
     col_ref, slot_ref, open_ref, mix_ref, pre_ref, act_ref, heat_ref, sems) = rest
    pairs = [(mix_any, mix_ref), (pre_any, pre_ref), (act_any, act_ref), (heat_any, heat_ref),
             (col_any, col_ref), (slot_any, slot_ref), (open_any, open_ref), (vel_any, vel_ref)]
    small = len(pairs) - 1
    pairs += [(q_any.at[pl.ds(v, 2)], q_ref.at[pl.ds(v, 2)]) for v in range(0, NV, 2)]
    copies = [pltpu.make_async_copy(x, y, sems.at[k]) for k, (x, y) in enumerate(pairs)]
    for copy in copies[small:] + copies[:small]:
        copy.start()
    az, _, plen = roles()
    n = q_ref.shape[1] // CAX
    rows = NV * n
    refs = (own_ref,) + tuple(out_refs)
    turns = [0] + shifts_of(n_az)
    beside_at = [rows] + [ref.shape[0] - CAX - EXT for ref in out_refs]

    @pl.when(plen == 1)
    def _():
        for ref in (own_ref, out_refs[0]):
            ref[pl.ds(0, rows), :] = jnp.zeros((rows, LANES), f32)
        for ref, at in zip(refs, beside_at):
            ref[pl.ds(at, EXT), :] = jnp.zeros((EXT, LANES), f32)

    for copy in copies[:small]:
        copy.wait()
    mixing(a_ref, mix_ref, pre_ref, heat_ref)
    for k in range(NS):
        power_ref[pl.ds(k * CAX, CAX), :] = jnp.full((CAX, LANES), act_ref[k] * (-LOG2E), f32)
    for copy in copies[small:]:
        copy.wait()
    edges(q_ref, er_ref, el_ref)
    el_ref[pl.ds(NV * CAX, CAX), :] = vel_ref[0, pl.ds(0, CAX), :]
    er_ref[pl.ds(NV * CAX, CAX), :] = vel_ref[0, pl.ds((n - 1) * CAX, CAX), :]

    @pl.when(plen == 0)
    def _():
        for v in range(NV):
            s_ref[pl.ds(v * n, n), :] = q_ref[v, pl.ds(0, n, stride=CAX), :]
        axial_rows(q_ref, vel_ref, out_refs[:1], out_refs[1:1 + pieces])

    @pl.when(plen == 1)
    def _():
        sub = lax.broadcasted_iota(jnp.int32, (CAX, LANES), 0)
        left = lax.broadcasted_iota(jnp.int32, (1, LANES), 1) < HALF
        blocks = n // CAX
        tables = [jnp.full((CAX, LANES), -1.0, f32)] * n_az
        used = [jnp.int32(0)] * n_az
        for b in range(blocks):
            tile, opened = slot_ref[b], open_ref[b] != 0
            ahead = (col_ref[b] - az + n_az) % n_az
            for shift, (turn, ref) in enumerate(zip(turns, refs)):
                here = jnp.logical_and(ahead == turn, opened)
                tables[shift] = jnp.where(sub == jnp.where(here, used[shift], CAX), tile.astype(f32), tables[shift])

                @pl.when(here)
                def _(ref=ref, b=b, tile=tile, shift=shift, slot=used[shift]):
                    for v in range(NV):
                        if shift < 2:
                            at = pl.ds(pl.multiple_of(v * n + tile * CAX, CAX), CAX)
                            ref[at, :] += block(q_ref, v, b)
                        else:
                            at = pl.ds(pl.multiple_of((slot * NV + v) * CAX, CAX), CAX)
                            ref[at, :] = block(q_ref, v, b)

                used[shift] = used[shift] + here.astype(jnp.int32)

            def beside(end, step, row, keep_left, b=b, tile=tile, opened=opened, ahead=ahead):
                @pl.when(jnp.logical_and(opened, tile == end))
                def _():
                    for shift, (turn, ref) in enumerate(zip(turns, refs)):
                        @pl.when(ahead == (turn + step) % n_az)
                        def _(ref=ref, at=beside_at[shift]):
                            for v in range(NV):
                                cell = q_ref[v, pl.ds(row, 1), :]
                                cell = jnp.where(left, cell, 0.0) if keep_left else jnp.where(left, 0.0, cell)
                                ref[pl.ds(at + v, 1), :] += cell

            beside(0, 1, CAX * CAX * b + CAX - 1, True)
            beside(blocks - 1, n_az - 1, CAX * CAX * (b + 1) - 1, False)
        for ref, table in zip(out_refs, tables[1:]):
            ref[pl.ds(ref.shape[0] - CAX, CAX), :] = table


def fill_ghosts(state_ref, lo_ref, hi_ref, ra_refs, rb_refs, high_ref, supply_ref, n_ax):
    _, ax, plen = roles()
    n = state_ref.shape[1] // CAX
    even = ax % 2 == 0
    odd = jnp.logical_not(even)
    cham = plen == 0

    def put(ref, parts):
        size = ref.shape[0] // len(parts)
        for k, part in enumerate(parts):
            ref[pl.ds(k * size, size), :] = part[pl.ds(0, size), :]

    @pl.when(plen == 1)
    def _():
        lo_ref[...] = supply_ref[...]
        hi_ref[...] = high_ref[pl.ds(0, hi_ref.shape[0]), :]

    @pl.when(jnp.logical_and(cham, even))
    def _():
        put(hi_ref, ra_refs)

    @pl.when(jnp.logical_and(cham, odd))
    def _():
        put(lo_ref, ra_refs)

    @pl.when(jnp.logical_and(cham, ax == 0))
    def _():
        lo_ref[...] = jnp.zeros_like(lo_ref)

    @pl.when(jnp.logical_and(cham, jnp.logical_and(even, ax > 0)))
    def _():
        put(lo_ref, rb_refs)

    @pl.when(jnp.logical_and(cham, jnp.logical_and(odd, ax < n_ax - 1)))
    def _():
        put(hi_ref, rb_refs)

    @pl.when(jnp.logical_and(cham, ax == n_ax - 1))
    def _():
        for v in range(NV):
            hi_ref[pl.ds(v * n, n), :] = state_ref[v, pl.ds(CAX - 1, n, stride=CAX), :]


def add_border(v, dst_ref, scale, lo_ref, hi_ref, hl_ref, hr_ref, ul_ref, ur_ref):
    n = dst_ref.shape[1] // CAX
    left = low_half()
    dst_ref[v, pl.ds(0, n, stride=CAX), :] += scale * lo_ref[pl.ds(v * n, n), :]
    dst_ref[v, pl.ds(CAX - 1, n, stride=CAX), :] += scale * hi_ref[pl.ds(v * n, n), :]
    al = scale + scale * pltpu.roll(ul_ref[...], HALF, 1)
    ar = scale - scale * pltpu.roll(ur_ref[...], HALF, 1)
    head = pltpu.roll(hl_ref[pl.ds(v * CAX, CAX), :], HALF, 1)
    tail = pltpu.roll(hr_ref[pl.ds(v * CAX, CAX), :], HALF, 1)
    dst_ref[v, pl.ds(0, CAX), :] += jnp.where(left, al * head, 0.0)
    dst_ref[v, pl.ds((n - 1) * CAX, CAX), :] += jnp.where(left, 0.0, ar * tail)


def mixing(a_ref, mix_ref, pre_ref, heat_ref):
    width = NV * CAX
    col = lax.broadcasted_iota(jnp.int32, (CAX, 3 * width), 1)
    row = lax.broadcasted_iota(jnp.int32, (CAX, 3 * width), 0)
    inner = col % width
    species, lane = inner // CAX, inner % CAX
    for v in range(NV):
        block = jnp.zeros((CAX, 3 * width), f32)
        for k in range(NS):
            value = 0.2 * pre_ref[k] * (mix_ref[v, k] if v < NS else heat_ref[k])
            block = jnp.where(species == k, value, block)
        block = jnp.where(lane == row, block, 0.0)
        high = block.astype(jnp.bfloat16).astype(f32)
        a_ref[pl.ds(v * CAX, CAX), :] = jnp.where(col // width == 1, block - high, high)


def reactions(states, a, power_ref):
    rates = []
    for state in states:
        inv = 1.0 / jnp.maximum(state[NS], 0.5)
        some = [jnp.exp2(power_ref[pl.ds(k * CAX, CAX), :] * inv) * jnp.maximum(state[k], 0.0) for k in range(NS)]
        rates.append(jnp.concatenate(some + [jnp.zeros((CAX, LANES), f32)], axis=0))
    rate = jnp.concatenate(rates, axis=1)
    high = rate.astype(jnp.bfloat16)
    low = (rate - high.astype(f32)).astype(jnp.bfloat16)
    return jnp.dot(a, jnp.concatenate([high, high, low], axis=0), preferred_element_type=f32)


def interior(q_ref, vel_ref, a_ref, power_ref, scale, finish):
    n = q_ref.shape[1] // CAX
    left = low_half()
    sub = lax.broadcasted_iota(jnp.int32, (CAX, LANES), 0)
    bottom, top = sub == 0, sub == CAX - 1
    a = (scale * a_ref[...]).astype(jnp.bfloat16)
    c = 0.1 * scale

    def reg(ref, v, j):
        return ref[v, pl.ds(pl.multiple_of(j * CAX, CAX), CAX), :]

    def column(ref, v, j0):
        regs = [reg(ref, v, j0 + d) for d in range(NJ)]
        before = jnp.where(j0 == 0, 0.0, reg(ref, v, jnp.maximum(j0 - 1, 0)))
        after = jnp.where(j0 + NJ == n, 0.0, reg(ref, v, jnp.minimum(j0 + NJ, n - 1)))
        turned = [pltpu.roll(x, HALF, 1) for x in [before] + regs + [after]]
        lefts = [jnp.where(left, turned[d], turned[d + 1]) for d in range(NJ)]
        rights = [jnp.where(left, turned[d + 1], turned[d + 2]) for d in range(NJ)]
        return regs, lefts, rights

    def body(step, carry):
        j0 = step * NJ
        src = reactions([[reg(q_ref, v, j0 + d) for v in range(NV)] for d in range(NJ)], a, power_ref)
        _, u_left, u_right = column(vel_ref, 0, j0)
        w = [reg(vel_ref, 1, j0 + d) for d in range(NJ)]
        al = [c + c * x for x in u_left]
        ar = [c - c * x for x in u_right]
        wu = [jnp.where(bottom, 0.0, c + c * pltpu.roll(x, 1, 0)) for x in w]
        wd = [jnp.where(top, 0.0, c - c * pltpu.roll(x, CAX - 1, 0)) for x in w]
        for v in range(NV):
            regs, lefts, rights = column(q_ref, v, j0)
            for d in range(NJ):
                vertical = wu[d] * pltpu.roll(regs[d], 1, 0) + wd[d] * pltpu.roll(regs[d], CAX - 1, 0)
                new = (0.6 * scale) * regs[d] + src[v * CAX:(v + 1) * CAX, d * LANES:(d + 1) * LANES]
                finish(j0 + d, v, new + (al[d] * lefts[d] + ar[d] * rights[d]) + vertical)
        return carry

    lax.fori_loop(0, n // NJ, body, 0)


def inside_one_kernel(q_ref, vel_ref, a_ref, power_ref, out_ref):
    def finish(j, v, new):
        out_ref[v, pl.ds(pl.multiple_of(j * CAX, CAX), CAX), :] = new

    interior(q_ref, vel_ref, a_ref, power_ref, 1.0, finish)


def inside_two_kernel(q_ref, q1_ref, vel_ref, a_ref, power_ref, out_ref):
    def finish(j, v, new):
        at = pl.ds(pl.multiple_of(j * CAX, CAX), CAX)
        out_ref[v, at, :] = 0.5 * q_ref[v, at, :] + new

    interior(q1_ref, vel_ref, a_ref, power_ref, 0.5, finish)


def gather_slots(dst_ref, base, got, tables, cap):
    slots = [(k, m) for k in range(len(got)) for m in range(cap)]
    named = [jnp.broadcast_to(tables[k][pl.ds(tables[k].shape[0] - CAX + m, 1), :], (CAX, LANES)) for k, m in slots]
    for v in range(NV):
        blocks = [got[k][pl.ds((m * NV + v) * CAX, CAX), :] for k, m in slots]
        for t in range(CAX):
            at = pl.ds((v * CAX + t) * CAX, CAX)
            total = base(at)
            for name, value in zip(named, blocks):
                total = total + jnp.where(name == t, value, 0.0)
            dst_ref[at, :] = total


def border_one_kernel(n_az, n_ax, n_out, cap, s_in_ref, *rest):
    got, rest = rest[:n_out], rest[n_out:]
    hl_ref, hr_ref, part_ref, q_ref, vel_ref, supply_ref, own_in_ref, col_any, slot_any, open_any = rest[:10]
    out_refs, rest = rest[10:10 + n_out], rest[10 + n_out:]
    (q1_ref, core_ref, z_ref, own_ref, er_ref, el_ref, lo_ref, hi_ref,
     col_ref, slot_ref, open_ref, sems) = rest
    pairs = [(col_any, col_ref), (slot_any, slot_ref), (open_any, open_ref)]
    copies = [pltpu.make_async_copy(x, y, sems.at[k]) for k, (x, y) in enumerate(pairs)]
    for copy in copies:
        copy.start()
    az, _, plen = roles()
    n = q_ref.shape[1] // CAX
    rows = NV * n
    fill_ghosts(q_ref, lo_ref, hi_ref, got[:1], got[1:1 + CAX // cap], s_in_ref, supply_ref, n_ax)
    for v in range(NV):
        q1_ref[v] = part_ref[v]
        add_border(v, q1_ref, 0.1, lo_ref, hi_ref, hl_ref, hr_ref,
                   hl_ref.at[pl.ds(NV * CAX, CAX)], hr_ref.at[pl.ds(NV * CAX, CAX)])
    edges(q1_ref, er_ref, el_ref)
    for copy in copies:
        copy.wait()

    @pl.when(plen == 0)
    def _():
        core_ref[pl.ds(rows, EXT), :] = jnp.zeros((EXT, LANES), f32)
        for v in range(NV):
            core_ref[pl.ds(v * n, n), :] = q1_ref[v, pl.ds(0, n, stride=CAX), :]
        axial_rows(q1_ref, vel_ref, out_refs[n_out - CAX // cap:], (z_ref,))

    @pl.when(plen == 1)
    def _():
        gather_slots(core_ref, lambda at: own_in_ref[at, :] + got[0][at, :], got[1:], got[1:], cap)
        beside = own_in_ref[pl.ds(rows, EXT), :]
        for ref in got:
            beside = beside + ref[pl.ds(ref.shape[0] - CAX - EXT, EXT), :]
        core_ref[pl.ds(rows, EXT), :] = beside
        own_ref[...] = jnp.zeros_like(own_ref)
        used = [jnp.int32(0)] * n_out
        for b in range(n // CAX):
            tile = slot_ref[b]
            ahead = (col_ref[b] - az + n_az) % n_az
            opened = open_ref[b] != 0

            @pl.when(jnp.logical_and(opened, ahead == 0))
            def _(b=b, tile=tile):
                for v in range(NV):
                    at = pl.ds(pl.multiple_of(v * n + tile * CAX, CAX), CAX)
                    own_ref[at, :] += block(q1_ref, v, b)

            for k, ref in enumerate(out_refs):
                here = jnp.logical_and(opened, ahead == shifts_of(n_az)[k])

                @pl.when(here)
                def _(ref=ref, b=b, slot=used[k]):
                    for v in range(NV):
                        at = pl.ds(pl.multiple_of((slot * NV + v) * CAX, CAX), CAX)
                        ref[at, :] = block(q1_ref, v, b)

                used[k] = used[k] + here.astype(jnp.int32)


def tile_kernel(n_out, cap, own_ref, z_ref, *rest):
    got, tables, (step_ref,) = rest[:n_out], rest[n_out:2 * n_out], rest[2 * n_out:]
    _, _, plen = roles()

    @pl.when(plen == 0)
    def _():
        step_ref[...] = z_ref[...]

    @pl.when(plen == 1)
    def _():
        gather_slots(step_ref, lambda at: own_ref[at, :], got, tables, cap)


def add_kernel(*refs):
    refs[-1][...] = sum(ref[...] for ref in refs[:-1])


def inlet_kernel(pair_ref, far_ref, near_ref, dq_ref, out_ref):
    _, ax, plen = roles()
    rows = out_ref.shape[0]
    inlet_side = jnp.logical_and(plen == 0, ax == 0)

    @pl.when(inlet_side)
    def _():
        dq_ref[...] = 0.1 * (far_ref[...] + near_ref[...])
        out_ref[...] = dq_ref[pl.ds(0, rows), :]

    @pl.when(jnp.logical_not(inlet_side))
    def _():
        dq_ref[...] = jnp.zeros_like(dq_ref)
        out_ref[...] = pair_ref[...]


def border_two_kernel(n_ax, n_z, part_ref, q_ref, q1_ref, vel_ref, core_ref, supply_ref, step_ref, dq_ref, hl_ref, hr_ref,
                      hl0_ref, hr0_ref, *rest):
    ra_refs, rest = rest[:n_z], rest[n_z:]
    a_ref, power_ref, out_any, keep_ref, out_ref, lo_ref, hi_ref, sems = rest
    n = out_ref.shape[1] // CAX
    rows = NV * n
    _, ax, plen = roles()
    inlet_side = jnp.logical_and(ax == 0, plen == 0)
    ul_ref, ur_ref = hl0_ref.at[pl.ds(NV * CAX, CAX)], hr0_ref.at[pl.ds(NV * CAX, CAX)]
    fill_ghosts(q1_ref, lo_ref, hi_ref, ra_refs, (step_ref,), core_ref, supply_ref, n_ax)

    @pl.when(inlet_side)
    def _():
        first = lax.broadcasted_iota(jnp.int32, (n, LANES), 0) == 0
        last = lax.broadcasted_iota(jnp.int32, (n, LANES), 0) == n - 1
        left = lax.broadcasted_iota(jnp.int32, (n, LANES), 1) < HALF

        def neighbours(x, head, tail):
            before = jnp.where(first, head, pltpu.roll(x, 1, 0))
            after = jnp.where(last, tail, pltpu.roll(x, n - 1, 0))
            mid = pltpu.roll(x, HALF, 1)
            return (jnp.where(left, pltpu.roll(before, HALF, 1), mid),
                    jnp.where(left, mid, pltpu.roll(after, HALF, 1)))

        u = vel_ref[0, pl.ds(0, n, stride=CAX), :]
        w_next = vel_ref[1, pl.ds(1, n, stride=CAX), :]
        u_left, u_right = neighbours(u, ul_ref[pl.ds(0, 1), :], ur_ref[pl.ds(0, 1), :])
        state = [q1_ref[v, pl.ds(0, n, stride=CAX), :] + dq_ref[pl.ds(v * n, n), :] for v in range(NV)]
        parts = [[x[d * CAX:(d + 1) * CAX] for x in state] for d in range(n // CAX)]
        src = reactions(parts, a_ref[...].astype(jnp.bfloat16), power_ref)
        for v in range(NV):
            beside = dq_ref[pl.ds(rows + v, 1), :]
            q_left, q_right = neighbours(state[v], hl_ref[pl.ds(v * CAX, 1), :] + beside, hr_ref[pl.ds(v * CAX, 1), :] + beside)
            above = (1.0 - w_next) * q1_ref[v, pl.ds(1, n, stride=CAX), :]
            mixed = src[v * CAX:(v + 1) * CAX]
            mixed = jnp.concatenate([mixed[:, d * LANES:(d + 1) * LANES] for d in range(n // CAX)], axis=0)
            new = 0.6 * state[v] + 0.1 * ((1.0 + u_left) * q_left + (1.0 - u_right) * q_right + above) + mixed
            keep_ref[pl.ds(v * n, n), :] = 0.5 * q_ref[v, pl.ds(0, n, stride=CAX), :] + 0.5 * new

    copies = []
    for v in range(NV):
        out_ref[v] = part_ref[v]
        add_border(v, out_ref, 0.05, lo_ref, hi_ref, hl_ref, hr_ref, ul_ref, ur_ref)

        @pl.when(inlet_side)
        def _(v=v):
            w = vel_ref[1, pl.ds(0, n, stride=CAX), :]
            out_ref[v, pl.ds(1, n, stride=CAX), :] += 0.05 * ((1.0 + w) * dq_ref[pl.ds(v * n, n), :])

        @pl.when(plen == 1)
        def _(v=v):
            keep_ref[pl.ds(v * n, n), :] = out_ref[v, pl.ds(CAX - 1, n, stride=CAX), :]

        copies.append(pltpu.make_async_copy(out_ref.at[v], out_any.at[v], sems.at[v]))
        copies[-1].start()
    for copy in copies:
        copy.wait()


def last_kernel(in_any, keep_ref, core_ref, far_ref, out_any, row_ref, sem):
    _, ax, plen = roles()
    n = keep_ref.shape[0] // NV

    def patch(at, value):
        for v in range(NV):
            row_ref[v, :, 0, :] = value(pl.ds(v * n, n))
        copy = pltpu.make_async_copy(row_ref, out_any.at[:, :, pl.ds(at, 1), :], sem)
        copy.start()
        copy.wait()

    @pl.when(jnp.logical_and(ax == 0, plen == 0))
    def _():
        patch(0, lambda at: keep_ref[at, :] + 0.05 * (core_ref[at, :] + far_ref[at, :]))

    @pl.when(jnp.logical_and(ax == 0, plen == 1))
    def _():
        patch(CAX - 1, lambda at: keep_ref[at, :] + 0.05 * core_ref[at, :])


def shape(*dims):
    return jax.ShapeDtypeStruct(dims, f32)


SPACES = {"s": pltpu.SMEM, "v": pltpu.VMEM, "h": pltpu.HBM}


def call(kernel, inputs, kinds, outs, scratch=(), cost=None, to=None, aliases=None):
    return pl.pallas_call(
        kernel,
        in_specs=[pl.BlockSpec(memory_space=SPACES[k]) for k in kinds],
        out_specs=[pl.BlockSpec(memory_space=SPACES[k]) for k in (to or "v" * len(outs))],
        out_shape=outs,
        scratch_shapes=list(scratch),
        cost_estimate=cost,
        input_output_aliases=aliases or {},
        compiler_params=pltpu.CompilerParams(vmem_limit_bytes=LIMIT),
    )(*inputs)


def local(n_az, n_ax, cells, speeds, supply, mix, prefactor, activation, heat, inj_column, inj_slot, inj_open):
    size = cells.shape[-1]
    n = size // LANES
    rows = NV * n

    def view(array):
        k = array.shape[0]
        return array.reshape(k, CAX, n, LANES).transpose(0, 2, 1, 3).reshape(k, CAX * n, LANES)

    def number(i, j, p):
        return (i * n_ax + j) * 2 + p

    every = [(i, j) for i in range(n_az) for j in range(n_ax)]

    def send(x, route):
        return lax.ppermute(x, AXES, [(number(*a), number(*b)) for a, b in route])

    def ring(step):
        return [((i, j, p), ((i + step) % n_az, j, p)) for i, j in every for p in (0, 1)]

    swap = [((i, j, p), (i, j, 1 - p)) for i, j in every for p in (0, 1)]
    n_out = n_az - 1

    def mate(k, j):
        return j ^ 1 if k == 0 else ((j + 1) ^ 1) - 1 if 0 < j < n_ax - 1 else n_ax - 1 - j

    cap = CAX // 4 if n_az > 4 else CAX // 2
    pieces = CAX // cap

    shifts = shifts_of(n_az)

    def first(k):
        out = [((i, j, 1), ((i + shifts[k]) % n_az, j, 1)) for i, j in every]
        for i, j in every:
            inside = 0 < j < n_ax - 1
            if k == 0 or (k <= pieces and (inside or k % 2 == 0)):
                to = (i, mate(min(k, 1), j), 0)
            else:
                to = (i ^ 1, j, 0)
            out.append(((i, j, 0), to))
        return out

    def compact(k):
        out = [((i, j, 1), ((i + shifts[k]) % n_az, j, 1)) for i, j in every]
        return out + [((i, j, 0), (i, mate(0, j), 0) if k >= n_out - pieces else (i ^ (n_az // 2), j, 0))
                      for i, j in every]

    q, vel = view(cells[0]), view(speeds[0])
    sup = supply.reshape(rows, LANES)
    col, slot, opened = inj_column.reshape(-1), inj_slot, inj_open
    react = (mix, prefactor, activation, heat)
    row, edge = shape(rows, LANES), shape(NV * CAX, LANES)

    whole = shape(*q.shape)
    work = pl.CostEstimate(flops=300 * q.shape[1] * LANES, transcendentals=20 * q.shape[1] * LANES,
                           bytes_accessed=12_000_000)

    raw = tuple(pltpu.with_memory_space_constraint(x, pltpu.HBM) for x in (q, vel, col, slot, opened) + react)
    wide, edge0 = shape(rows + EXT, LANES), shape((NV + 1) * CAX, LANES)
    got = call(functools.partial(first_kernel, n_az, n_out, pieces), raw, "h" * 9,
               [shape(rows + EXT + CAX, LANES)] + [shape(cap * NV * CAX + EXT + CAX, LANES)] * (n_out - 1) + [whole, shape(*vel.shape), row, wide, edge0, edge0,
                                                         shape(NV * CAX, 3 * NV * CAX), shape(NS * CAX, LANES)],
               [pltpu.SMEM(col.shape, jnp.int32)] * 3 + [pltpu.SMEM(x.shape, f32) for x in react]
               + [pltpu.SemaphoreType.DMA((8 + NV // 2,))])
    outs, (qv, velv, s0, own0, er, el, matrix, power) = got[:n_out], got[n_out:]
    ra = [send(x, first(k)) for k, x in enumerate(outs)]
    s0r = send(s0, swap)
    hl0 = send(er, ring(1))
    el, s0r = lax.optimization_barrier((el, s0r))
    hr0 = send(el, ring(-1))
    part, = call(inside_one_kernel, (qv, velv, matrix, power), "vvvv", [whole], cost=work)

    got = call(functools.partial(border_one_kernel, n_az, n_ax, n_out, cap),
               (s0r, *ra, hl0, hr0, part, qv, velv, sup, own0, col, slot, opened),
               "v" * (n_out + 11),
               [shape(cap * NV * CAX, LANES)] * n_out + [whole, wide, row, row, edge, edge],
               [pltpu.VMEM((rows, LANES), f32)] * 2 + [pltpu.SMEM(col.shape, jnp.int32)] * 3
               + [pltpu.SemaphoreType.DMA((3,))])
    outs, (q1, core, z1, own1, er, el) = got[:n_out], got[n_out:]
    down = [((i, j, 1), (i, j - 1, 1)) for i, j in every if j % 2 == 1]
    across = [((i, 2, 1), (i, 0, 0)) for i in range(n_az)]
    inner = [((i, j, 0), (i, mate(1, j), 0)) for i, j in every if 0 < j < n_ax - 1]
    rb = [send(x, compact(k)) for k, x in enumerate(outs)]
    core_in = send(core, swap)
    down0 = send(core, [((i, j, 1), (i, j - 1, 0)) for i, j in every if j % 2 == 1])

    part, = call(inside_two_kernel, (qv, q1, velv, matrix, power), "vvvvv", [whole], cost=work)
    part, down0 = lax.optimization_barrier((part, down0))
    pair0, = call(add_kernel, (core_in, down0), "vv", [wide])
    part, own1, pair0 = lax.optimization_barrier((part, own1, pair0))
    far0 = send(pair0, [((i, 2, 0), (i, 0, 0)) for i in range(n_az)])
    step, = call(functools.partial(tile_kernel, n_out, cap), (own1, z1, *rb, *ra), "v" * (2 + 2 * n_out), [row])
    step_in = send(step, down + inner)
    er, el, step = lax.optimization_barrier((er, el, step))
    hl1, hr1 = send(er, ring(1)), send(el, ring(-1))
    pair1, = call(add_kernel, (step, step_in), "vv", [row])
    far1 = send(pair1, across)
    pair1, hl1, hr1 = lax.optimization_barrier((pair1, hl1, hr1))

    dq, core2 = call(inlet_kernel, (pair1, far0, pair0), "vvv", [wide, row])
    core2_in = send(core2, swap)
    out, keep = call(functools.partial(border_two_kernel, n_ax, pieces),
                     (part, qv, q1, velv, core_in, sup, step_in, dq, hl1, hr1, hl0, hr0, *rb[n_out - pieces:], matrix, power),
                     "v" * (14 + pieces), [whole, row],
                     [pltpu.VMEM(q.shape, f32)] + [pltpu.VMEM((rows, LANES), f32)] * 2 + [pltpu.SemaphoreType.DMA((NV,))],
                     cost=work, to="hv")
    out, = call(last_kernel, (out.reshape(NV, n, CAX, LANES), keep, core2_in, far1), "hvvv", [shape(NV, n, CAX, LANES)],
                [pltpu.VMEM((NV, n, 1, LANES), f32), pltpu.SemaphoreType.DMA(())], to="h", aliases={0: 0})
    return out.transpose(0, 2, 1, 3).reshape(1, NV, CAX, size)


def solution(mesh):
    return jax.shard_map(
        functools.partial(local, mesh.shape["az"], mesh.shape["ax"]),
        mesh=mesh,
        in_specs=(
            P("pl", None, "ax", "az"),
            P("pl", None, "ax", "az"),
            P(None, "ax", "az"),
            P(),
            P(),
            P(),
            P(),
            P(("az", "ax"), None),
            P(("az", "ax")),
            P(("az", "ax")),
        ),
        out_specs=P("pl", None, "ax", "az"),
        check_vma=False,
    )
```
